32 devices in a mesh: expert: 8 (over y, x, core), shard: 4 (over z).
Axes of the slice: x: 2, y: 2, z: 4, core: 2. Of those that a mesh axis runs over, the one named last changes fastest.
Arguments:
- inputs: bfloat16 [32768, 768], P(('expert', 'shard')), may hold values from -4.5 to 4.5
- norm_gain: bfloat16 [768], P('shard'), may hold values from 0.25 to 1.75
- query_weight: bfloat16 [768, 768], P('shard'), may hold values from -0.21875 to 0.21875
- key_weight: bfloat16 [768, 768], P('shard'), may hold values from -0.21875 to 0.21875
- value_weight: bfloat16 [768, 768], P('shard'), may hold values from -0.21875 to 0.21875
- merge_weight: bfloat16 [768, 768], P('shard'), may hold values from -6 to 6
- bias_table: bfloat16 [32, 12], P(None, 'shard'), may hold values from -4 to 4
- expert_gain: bfloat16 [768], P('shard'), may hold values from 0.25 to 1.75
- router_weight: bfloat16 [768, 16], P('shard'), may hold values from -0.21875 to 0.21875
- up_weight: bfloat16 [16, 768, 3072], P('expert'), may hold values from -0.21875 to 0.21875
- down_weight: bfloat16 [16, 3072, 768], P('expert'), may hold values from -0.109375 to 0.109375
- routes: int32 [32768, 2], P(('expert', 'shard')), may hold values from 0 to 15, all different within a row; in each aligned block of 1024 rows (0 to 1023, 1024 to 2047, ...) at most 160 rows name the same one
- cotangent: bfloat16 [32768, 768], P(('expert', 'shard')), may hold values from -6 to 6
Outputs:
- output: bfloat16 [32768, 768], P(('expert', 'shard'))
- input_gradient: float32 [32768, 768], P(('expert', 'shard'))
- norm_gradient: float32 [768], P('shard')
- query_gradient: float32 [768, 768], P('shard')
- key_gradient: float32 [768, 768], P('shard')
- value_gradient: float32 [768, 768], P('shard')
- merge_gradient: float32 [768, 768], P('shard')
- table_gradient: float32 [32, 12], P(None, 'shard')
- gain_gradient: float32 [768], P('shard')
- router_gradient: float32 [768, 16], P('shard')
- up_gradient: float32 [16, 768, 3072], P('expert', None, 'shard')
- down_gradient: float32 [16, 3072, 768], P('expert', 'shard')
The draws below stay inside these ranges and needn't reach their ends.
Inputs may be any that keep to these rules, and one draw needn't show every extreme that they name: In each aligned block of 1024 tokens (the tokens of one device) every expert is named by at most 160 routes, and by exactly 160 in some block; the 2 routes of a token name different experts; every expert is named by some token.
All inputs are finite; a program needn't handle non-finite values.
Results may differ from the reference program's by a relative error of at most 0.02.
Values may be sent and summed in bfloat16 or wider, within the bound.
No kernel may reach another device: no remote copies, remote signals or barrier semaphores. Data moves between devices by JAX's collectives and lax.ppermute only.
A program may use at most 448 MiB of HBM per device.

```python
import math
import jax
import jax.numpy as jnp
import numpy as np
from jax import lax

D = 768
HEADS = 12
HEAD_DIM = 64
FF = 3072
TOP = 2
BUCKETS = 32
MAX_DIST = 128
TOK_DEV = 1024
EXPERTS = 16
CAP = 160
TOKENS = 32768


def steps_of(stream_key, shape, shards, low, high):
    loudness = 1.0
    for position, shards_of in shards:
        draws = jax.random.uniform(jax.random.fold_in(jax.random.fold_in(stream_key, 6), position), (shards_of,), jnp.float32, low / len(shards), high / len(shards))
        loudness = loudness * jnp.repeat(jnp.exp(draws), shape[position] // shards_of).reshape((-1,) + (1,) * (len(shape) - 1 - position))
    return loudness


def deal_out(own_key, own, number, rows, number_of, top, bound, slope):
    order = jax.random.permutation(own_key, number_of)
    crowded, usual = portions_of(number_of, rows * top, bound, slope, True), portions_of(number_of, rows * top, bound, slope, False)
    places = jnp.arange(number_of)

    def named(lengths, turn):
        used = int((lengths > 0).sum())
        fixed = max(1, used // 4)
        passed = fixed + (places - fixed + turn * (used - fixed)) % max(1, number_of - fixed)
        return jnp.zeros((number_of,), jnp.int32).at[order[jnp.where(places < fixed, places, passed)]].set(jnp.asarray(lengths, jnp.int32))

    lengths = jnp.where(number % 4 == 0, named(crowded, number // 4), named(usual, number - number // 4 - 1))
    mixed = jax.random.permutation(jax.random.fold_in(own, 3), number_of)
    source_of, receiver = mixed[0:number_of // 2 * 2:2], mixed[1:number_of // 2 * 2:2]
    slack = jnp.minimum(lengths[source_of] - 1, bound - lengths[receiver]) // 2
    slack = jnp.where((source_of == order[0]) | (receiver == order[0]) | (lengths[receiver] == 0), 0, jnp.maximum(slack, 0))
    passed = jax.random.randint(jax.random.fold_in(own, 4), (number_of // 2,), 0, 1 << 20) % (slack + 1)
    lengths = lengths.at[source_of].add(-passed).at[receiver].add(passed)
    items = jnp.searchsorted(jnp.cumsum(lengths), jnp.arange(rows * top), side="right").astype(jnp.int32)
    listing = items.reshape(top, rows).T
    listing = listing[jax.random.permutation(jax.random.fold_in(own, 1), rows)]
    turn = jax.random.randint(jax.random.fold_in(own, 2), (rows, 1), 0, top)
    return jnp.take_along_axis(listing, (jnp.arange(top)[None, :] + turn) % top, axis=1)


def portions_of(amount, total, most, lean, full):
    portions = [(1 << 20) // math.isqrt(grade ** lean) + 1 for grade in range(1, amount + 1)]
    largest = most if full else min(most, max(-(-total // amount), total * portions[0] // sum(portions)))
    least = 1 if total - largest >= amount - 1 else 0
    counts, spare = [largest] + [least] * (amount - 1), total - largest - least * (amount - 1)
    while spare > 0:
        candidates = [i for i in range(1, amount) if counts[i] < largest] or [i for i in range(1, amount) if counts[i] < most]
        mass, remaining = sum([portions[i] for i in candidates]), spare
        for i in candidates:
            addition = min(most - counts[i], max(1, remaining * portions[i] // mass), spare)
            counts[i] = counts[i] + addition
            spare = spare - addition
    return np.array(counts)


def bell_draw(rng, shape, scale, limit, cuts=(), kind=jnp.bfloat16):
    entries = jax.random.normal(rng, shape, jnp.float32) * scale
    if len(cuts) > 0:
        entries = steps_of(rng, shape, cuts, -0.22, 0.18) * entries
    return jnp.clip(entries, min=-limit, max=limit).astype(kind)


def setup_inputs(seed: int = 0) -> dict:
    splits = jax.random.split(jax.random.key(seed), 14)
    inputs = bell_draw(splits[0], (TOKENS, D), 1.0, 4.5, ((0, 32),))
    norm_gain = jnp.clip(1.0 + 0.15 * jax.random.normal(splits[1], (D,), jnp.float32), 0.25, 1.75).astype(jnp.bfloat16)
    query_weight = bell_draw(splits[2], (D, D), D ** -0.5, 0.21875, ((0, 4),))
    key_weight = bell_draw(splits[3], (D, D), D ** -0.5, 0.21875, ((0, 4),))
    value_weight = bell_draw(splits[4], (D, D), D ** -0.5, 0.21875, ((0, 4),))
    merge_weight = bell_draw(splits[5], (D, D), (max(1, 2 * D // TOK_DEV)) ** -0.5, 6.0, ((0, 4),))
    bias_table = bell_draw(splits[6], (BUCKETS, HEADS), 1.0, 4.0, ((1, 4),))
    expert_gain = jnp.clip(1.0 + 0.15 * jax.random.normal(splits[7], (D,), jnp.float32), 0.25, 1.75).astype(jnp.bfloat16)
    router_weight = bell_draw(splits[8], (D, EXPERTS), D ** -0.5, 0.21875, ((0, 4),))
    up_weight = bell_draw(splits[9], (EXPERTS, D, FF), D ** -0.5, 0.21875, ((0, 8),))
    down_weight = bell_draw(splits[10], (EXPERTS, FF, D), FF ** -0.5, 0.109375, ((0, 8),))
    routes_keys = jax.random.split(jax.random.fold_in(splits[11], 1), TOKENS // TOK_DEV)
    routes_turns = jax.random.permutation(jax.random.fold_in(splits[11], 3), TOKENS // TOK_DEV)
    routes = jax.vmap(lambda own, number: deal_out(jax.random.fold_in(splits[11], 2), own, number, TOK_DEV, EXPERTS, TOP, CAP, 2))(routes_keys, routes_turns).reshape((TOKENS, TOP))
    cotangent = bell_draw(splits[12], (TOKENS, D), 1.0, 6.0, ((0, 32),))
    return dict(inputs=inputs, norm_gain=norm_gain, query_weight=query_weight, key_weight=key_weight, value_weight=value_weight, merge_weight=merge_weight, bias_table=bias_table, expert_gain=expert_gain, router_weight=router_weight, up_weight=up_weight, down_weight=down_weight, routes=routes, cotangent=cotangent)


epsilon = 1e-06

@jax.custom_vjp
def low(v):
    return lax.optimization_barrier(v.astype(jnp.bfloat16)).astype(jnp.float32)

@jax.custom_vjp
def low_back(v):
    return v

def low_keep(v):
    return (low(v), None)

def low_pass(kept, grad):
    return (grad,)

def back_keep(v):
    return (v, None)

def back_low(kept, grad):
    return (low(grad),)
low.defvjp(low_keep, low_pass)
low_back.defvjp(back_keep, back_low)

def bucket_hot(length):
    distance = np.arange(length)
    half_count = BUCKETS // 2
    clipped = np.maximum(distance, half_count)
    spread = np.log(clipped / half_count) / np.log(MAX_DIST / half_count) * (BUCKETS - half_count)
    far_bucket = np.minimum(half_count + np.floor(spread).astype(np.int32), BUCKETS - 1)
    bucket = np.where(distance < half_count, distance, far_bucket)
    return (bucket[:, None] == np.arange(BUCKETS)[None, :]).astype(np.float32)

def matmul(left, right):
    return jnp.dot(left, right, precision=lax.Precision.HIGHEST)

def rms_scale(values, gain_values):
    return values * lax.rsqrt(lax.optimization_barrier(jnp.mean(values * values, axis=-1, keepdims=True)) + epsilon) * gain_values

def attend_sequence(queries, keys_in, values_in, relative):
    length = queries.shape[0]
    query_heads = queries.reshape(length, HEADS, HEAD_DIM)
    key_heads = keys_in.reshape(length, HEADS, HEAD_DIM)
    value_heads = values_in.reshape(length, HEADS, HEAD_DIM)
    positions = jnp.arange(length, dtype=jnp.int32)
    distance = positions[:, None] - positions[None, :]
    bias_block = relative[:, jnp.clip(distance, 0, length - 1)]
    scores = jnp.einsum('qhd,khd->hqk', query_heads, key_heads, precision=lax.Precision.HIGHEST) * 0.125 + bias_block
    scores = low_back(scores)
    scores = jnp.where(distance[None] >= 0, scores, -1e+30)
    weights = jax.nn.softmax(scores, axis=-1)
    mixed = jnp.einsum('hqk,khd->qhd', low(weights), value_heads, precision=lax.Precision.HIGHEST)
    return mixed.reshape(length, HEADS * HEAD_DIM)

def expert_apply(row_block, weight_in, weight_out):
    pre_hidden = low_back(matmul(row_block, weight_in))
    hidden = low(jax.nn.gelu(pre_hidden, approximate=True))
    return low_back(low(matmul(hidden, weight_out)))

def group_slots(group_routes):
    flat_routes = group_routes.reshape(-1)
    flat_hot = (flat_routes[:, None] == jnp.arange(EXPERTS, dtype=jnp.int32)[None, :]).astype(jnp.int32)
    earlier = jnp.cumsum(flat_hot, axis=0, dtype=jnp.int32) - flat_hot
    slot_index = flat_routes * CAP + lax.optimization_barrier(jnp.sum(earlier * flat_hot, axis=1, dtype=jnp.int32))
    route_ids = jnp.arange(flat_routes.shape[0], dtype=jnp.int32)
    route_of_slot = jnp.zeros((EXPERTS * CAP,), jnp.int32).at[slot_index].set(route_ids)
    filled = jnp.zeros((EXPERTS * CAP,), jnp.int32).at[slot_index].set(1)
    return (slot_index, route_of_slot, filled)

def pick_rows(group_rows, route_of_slot, filled):
    return jnp.where(filled[:, None] > 0, group_rows[route_of_slot // TOP], 0.0)

def take_slots(group_out, slot_index):
    return group_out[slot_index]

def forward(features, norm_gain, query_weight, key_weight, value_weight, merge_weight, bias_table, expert_gain, router_weight, up_weight, down_weight, routes):
    token_count = features.shape[0]
    seq_count = token_count // TOK_DEV
    normed = low(rms_scale(features, norm_gain))
    queries = low_back(low(matmul(normed, query_weight)))
    keys_all = low_back(low(matmul(normed, key_weight)))
    values_all = low_back(low(matmul(normed, value_weight)))
    bucket_table = jnp.asarray(bucket_hot(TOK_DEV), dtype=jnp.float32)
    relative = matmul(bucket_table, bias_table).T

    def per_sequence(members):
        return jax.checkpoint(attend_sequence)(members[0], members[1], members[2], relative)
    attended = lax.map(per_sequence, (queries.reshape(seq_count, TOK_DEV, D), keys_all.reshape(seq_count, TOK_DEV, D), values_all.reshape(seq_count, TOK_DEV, D)))
    attended = low_back(low(attended.reshape(token_count, D)))
    resid = features + low_back(matmul(attended, merge_weight))
    routed = low(rms_scale(resid, expert_gain))
    logits = low_back(matmul(routed, router_weight))
    chosen = jnp.take_along_axis(logits, routes, axis=1)
    gate_values = jax.nn.softmax(chosen, axis=1)
    slot_index, route_of_slot, filled = jax.vmap(group_slots)(routes.reshape(seq_count, TOK_DEV * TOP))
    row_table = jax.vmap(pick_rows)(routed.reshape(seq_count, TOK_DEV, D), route_of_slot, filled)
    row_table = low_back(row_table)
    row_table = row_table.reshape(seq_count, EXPERTS, CAP, D).transpose(1, 0, 2, 3).reshape(EXPERTS, seq_count * CAP, D)

    def per_expert(members):
        return jax.checkpoint(expert_apply)(members[0], members[1], members[2])
    produced = lax.map(per_expert, (row_table, up_weight, down_weight))
    produced = produced.reshape(EXPERTS, seq_count, CAP, D).transpose(1, 0, 2, 3).reshape(seq_count, EXPERTS * CAP, D)
    picked = jax.vmap(take_slots)(produced, slot_index).reshape(token_count, TOP, D)
    return resid + lax.optimization_barrier(jnp.sum(gate_values[:, :, None] * picked, axis=1))

def reference(inputs, norm_gain, query_weight, key_weight, value_weight, merge_weight, bias_table, expert_gain, router_weight, up_weight, down_weight, routes, cotangent):

    def wrapped(features, gain_one, weight_q, weight_k, weight_v, weight_m, table, gain_two, weight_r, weight_up, weight_down):
        return forward(features, gain_one, weight_q, weight_k, weight_v, weight_m, table, gain_two, weight_r, weight_up, weight_down, routes)
    result, pullback = jax.vjp(wrapped, inputs.astype(jnp.float32), norm_gain.astype(jnp.float32), query_weight.astype(jnp.float32), key_weight.astype(jnp.float32), value_weight.astype(jnp.float32), merge_weight.astype(jnp.float32), bias_table.astype(jnp.float32), expert_gain.astype(jnp.float32), router_weight.astype(jnp.float32), up_weight.astype(jnp.float32), down_weight.astype(jnp.float32))
    grads = pullback(cotangent.astype(jnp.float32))
    return (result.astype(jnp.bfloat16), grads[0], grads[1], grads[2], grads[3], grads[4], grads[5], grads[6], grads[7], grads[8], grads[9], grads[10])
```

```python
from functools import partial, reduce

import jax
import jax.numpy as jnp
import numpy as np
from jax import lax
from jax.experimental import pallas as pl
from jax.experimental.pallas import tpu as pltpu
from jax.sharding import PartitionSpec as P

BUCKETS = 32
MAX_DIST = 128


epsilon = 1e-06
masked_score = -1e30


def bucket_hot(length):
    distance = np.arange(length)
    half_count = BUCKETS // 2
    clipped = np.maximum(distance, half_count)
    spread = np.log(clipped / half_count) / np.log(MAX_DIST / half_count) * (BUCKETS - half_count)
    far_bucket = np.minimum(half_count + np.floor(spread).astype(np.int32), BUCKETS - 1)
    bucket = np.where(distance < half_count, distance, far_bucket)
    return (bucket[:, None] == np.arange(BUCKETS)[None, :]).astype(np.float32)


def rms_parts(values, gain_values):
    inverse = lax.rsqrt(jnp.mean(values * values, axis=-1, keepdims=True) + epsilon)
    unit_rows = values * inverse
    return (unit_rows * gain_values, unit_rows, inverse)


def rms_back(grad_rows, unit_rows, inverse, gain_values):
    scaled = grad_rows * gain_values
    gain_grad = jnp.sum(grad_rows * unit_rows, axis=0)
    inner = jnp.mean(scaled * unit_rows, axis=-1, keepdims=True)
    return (inverse * (scaled - unit_rows * inner), gain_grad)


def dot_nt(a, b):
    return lax.dot_general(a, b, (((1,), (1,)), ((), ())), preferred_element_type=jnp.float32)

def dot_nn(a, b):
    return lax.dot_general(a, b, (((1,), (0,)), ((), ())), preferred_element_type=jnp.float32)

def near_tiles(near_ref, head, block):
    spread = jnp.broadcast_to(near_ref[0, head:head + 1, :], (block, block))
    spread = pltpu.roll(spread, 0, 1, stride=1, stride_axis=0)
    key_at = lax.broadcasted_iota(jnp.int32, (block, block), 0)
    query_at = lax.broadcasted_iota(jnp.int32, (block, block), 1)
    return (jnp.where(query_at >= key_at, spread, masked_score), jnp.where(query_at < key_at, spread, 0.0), query_at < key_at)

def diagonal_sums(tile):
    block = tile.shape[1]
    total = tile[:8]
    for start in range(8, block, 8):
        total = total + pltpu.roll(tile[start:start + 8], block - start, 1)
    row = lax.broadcasted_iota(jnp.int32, total.shape, 0)
    for step in (1, 2, 4):
        total = jnp.where((row & step) != 0, pltpu.roll(total, block - step, 1), total)
    return jnp.sum(total, axis=0, keepdims=True)

def head_part(rows, head, size):
    lane = lax.broadcasted_iota(jnp.int32, rows.shape, 1)
    return jnp.where((lane >= head * size) & (lane < (head + 1) * size), rows, jnp.zeros_like(rows))

def attend_kernel(query_ref, key_ref, value_ref, near_ref, out_ref, total_ref, *, block, size, scale):
    length, lanes = query_ref.shape
    heads = lanes // size
    count = length // block
    flipped = value_ref[...].T
    tiles = [near_tiles(near_ref, head, block) for head in range(heads)]
    for i in range(count):
        rows = pl.ds(i * block, block)
        query_rows = query_ref[rows, :] * jnp.bfloat16(scale)
        parts = []
        for head in range(heads):
            query_part = head_part(query_rows, head, size)
            scores = []
            for j in range(i + 1):
                tile = dot_nt(key_ref[pl.ds(j * block, block), :], query_part)
                if j == i:
                    tile = tile + tiles[head][0]
                elif j == i - 1:
                    tile = tile + tiles[head][1]
                scores.append(tile)
            top = reduce(jnp.maximum, scores)
            top = jnp.max(top, axis=0, keepdims=True)
            mixed = None
            total = None
            for j in range(i + 1):
                weights = jnp.exp(scores[j] - top)
                sums = jnp.sum(weights, axis=0, keepdims=True)
                part = dot_nn(flipped[head * size:(head + 1) * size, j * block:(j + 1) * block], weights.astype(jnp.bfloat16))
                mixed = part if mixed is None else mixed + part
                total = sums if total is None else total + sums
            parts.append(mixed / total)
            total_ref[0, head:head + 1, rows] = top + jnp.log(total)
        out_ref[rows, :] = jnp.concatenate(parts, axis=0).T.astype(out_ref.dtype)

def attend(queries, keys, values, near, size, block):
    length, width = queries.shape
    lanes = 128
    heads = lanes // size
    groups = width // lanes
    column = pl.BlockSpec((length, lanes), lambda g: (0, g))
    head_rows = pl.BlockSpec((1, heads, block), lambda g: (g, 0, 0))
    return pl.pallas_call(
        partial(attend_kernel, block=block, size=size, scale=size ** -0.5),
        grid=(groups,),
        in_specs=[column, column, column, head_rows],
        out_specs=[column, pl.BlockSpec((1, heads, length), lambda g: (g, 0, 0))],
        out_shape=[jax.ShapeDtypeStruct((length, width), jnp.bfloat16), jax.ShapeDtypeStruct((groups, heads, length), jnp.float32)],
        compiler_params=pltpu.CompilerParams(vmem_limit_bytes=48 << 20),
        name="attend",
    )(queries, keys, values, near)

def attend_back_kernel(query_ref, key_ref, value_ref, grad_ref, out_ref, total_ref, near_ref, dq_ref, dk_ref, dv_ref, dist_ref, key_acc, value_acc, *, block, size, scale):
    length, lanes = query_ref.shape
    heads = lanes // size
    count = length // block
    flipped = key_ref[...].T
    tiles = [near_tiles(near_ref, head, block) for head in range(heads)]
    near_acc = [None] * heads
    far_acc = [None] * heads
    for i in range(count):
        rows = pl.ds(i * block, block)
        query_rows = query_ref[rows, :] * jnp.bfloat16(scale)
        grad_rows = grad_ref[rows, :]
        products = (grad_rows.astype(jnp.float32) * out_ref[rows, :].astype(jnp.float32)).T
        query_parts = [head_part(query_rows, head, size) for head in range(heads)]
        grad_parts = [head_part(grad_rows, head, size) for head in range(heads)]
        inner = [jnp.sum(products[head * size:(head + 1) * size], axis=0, keepdims=True) for head in range(heads)]
        query_stack = jnp.concatenate(query_parts, axis=0)
        grad_stack = jnp.concatenate(grad_parts, axis=0)
        query_grads = [None] * heads
        for j in range(i + 1):
            cols = pl.ds(j * block, block)
            weight_list = []
            score_list = []
            for head in range(heads):
                tile = dot_nt(key_ref[cols, :], query_parts[head])
                if j == i:
                    tile = tile + tiles[head][0]
                elif j == i - 1:
                    tile = tile + tiles[head][1]
                weights = jnp.exp(tile - total_ref[0, head:head + 1, rows])
                grads = dot_nt(value_ref[cols, :], grad_parts[head])
                score_grads = weights * (grads - inner[head])
                low = score_grads.astype(jnp.bfloat16)
                weight_list.append(weights.astype(jnp.bfloat16))
                score_list.append(low)
                part = dot_nn(flipped[head * size:(head + 1) * size, j * block:(j + 1) * block], low)
                query_grads[head] = part if query_grads[head] is None else query_grads[head] + part
                if j == i:
                    near_acc[head] = score_grads if near_acc[head] is None else near_acc[head] + score_grads
                else:
                    far = score_grads
                    if j == i - 1:
                        close = jnp.where(tiles[head][2], score_grads, 0.0)
                        near_acc[head] = near_acc[head] + close
                        far = score_grads - close
                    far = jnp.sum(far, axis=0, keepdims=True)
                    far_acc[head] = far if far_acc[head] is None else far_acc[head] + far
            value_part = dot_nn(jnp.concatenate(weight_list, axis=1), grad_stack)
            key_part = dot_nn(jnp.concatenate(score_list, axis=1), query_stack)
            if j == i:
                value_acc[cols, :] = value_part
                key_acc[cols, :] = key_part
            else:
                value_acc[cols, :] += value_part
                key_acc[cols, :] += key_part
        dq_ref[rows, :] = (jnp.concatenate(query_grads, axis=0) * scale).T.astype(dq_ref.dtype)
    dk_ref[...] = key_acc[...].astype(dk_ref.dtype)
    dv_ref[...] = value_acc[...].astype(dv_ref.dtype)
    for head in range(heads):
        dist_ref[0, head:head + 1, :] = diagonal_sums(near_acc[head])
        dist_ref[0, heads + head:heads + head + 1, :] = far_acc[head]

def attend_back(queries, keys, values, grads, outs, totals, near, size, block):
    length, width = queries.shape
    lanes = 128
    heads = lanes // size
    groups = width // lanes
    column = pl.BlockSpec((length, lanes), lambda g: (0, g))
    head_rows = pl.BlockSpec((1, heads, block), lambda g: (g, 0, 0))
    return pl.pallas_call(
        partial(attend_back_kernel, block=block, size=size, scale=size ** -0.5),
        grid=(groups,),
        in_specs=[column] * 5 + [pl.BlockSpec((1, heads, length), lambda g: (g, 0, 0)), head_rows],
        out_specs=[column, column, column, pl.BlockSpec((1, 2 * heads, block), lambda g: (g, 0, 0))],
        out_shape=[jax.ShapeDtypeStruct((length, width), jnp.bfloat16)] * 3 + [jax.ShapeDtypeStruct((groups, 2 * heads, block), jnp.float32)],
        scratch_shapes=[pltpu.VMEM((length, lanes), jnp.float32)] * 2,
        compiler_params=pltpu.CompilerParams(vmem_limit_bytes=56 << 20),
        name="attend_back",
    )(queries, keys, values, grads, outs, totals, near)


def local(
    inputs,
    norm_gain,
    query_weight,
    key_weight,
    value_weight,
    merge_weight,
    bias_table,
    expert_gain,
    router_weight,
    up_weight,
    down_weight,
    routes,
    cotangent,
):
    gathered = (
        lax.all_gather(norm_gain, "shard", axis=0, tiled=True),
        lax.all_gather(query_weight, "shard", axis=0, tiled=True),
        lax.all_gather(key_weight, "shard", axis=0, tiled=True),
        lax.all_gather(value_weight, "shard", axis=0, tiled=True),
        lax.all_gather(merge_weight, "shard", axis=0, tiled=True),
        lax.all_gather(bias_table, "shard", axis=1, tiled=True),
        lax.all_gather(expert_gain, "shard", axis=0, tiled=True),
        lax.all_gather(router_weight, "shard", axis=0, tiled=True),
    )
    gain_one = gathered[0].astype(jnp.float32)
    query_full = gathered[1]
    key_full = gathered[2]
    value_full = gathered[3]
    merge_full = gathered[4]
    table_full = gathered[5].astype(jnp.float32)
    gain_two = gathered[6].astype(jnp.float32)
    router_full = gathered[7]
    token_count, width = inputs.shape
    head_count = table_full.shape[1]
    head_size = width // head_count
    route_count = routes.shape[1]
    local_count = up_weight.shape[0]
    owner_count = lax.axis_size("expert")
    expert_count = router_full.shape[1]
    capacity = (5 * token_count * route_count + 4 * expert_count - 1) // (4 * expert_count)
    slot_total = local_count * owner_count * capacity
    pair_count = token_count * route_count
    features = inputs.astype(jnp.float32)
    normed, unit_one, inverse_one = rms_parts(features, gain_one)
    normed_low = normed.astype(jnp.bfloat16)
    queries = jnp.dot(normed_low, query_full, preferred_element_type=jnp.float32).astype(jnp.bfloat16)
    keys = jnp.dot(normed_low, key_full, preferred_element_type=jnp.float32).astype(jnp.bfloat16)
    values = jnp.dot(normed_low, value_full, preferred_element_type=jnp.float32).astype(jnp.bfloat16)
    block = 256
    hot = bucket_hot(token_count)
    assert hot[block:, -1].all()
    near_hot = jnp.asarray(hot[:block] - hot[-1:], dtype=jnp.float32)
    group_heads = 128 // head_size
    near = jnp.dot(near_hot, table_full, precision=lax.Precision.HIGHEST).T.reshape(
        head_count // group_heads, group_heads, block
    )
    attended, log_totals = attend(queries, keys, values, near, head_size, block)
    branch = jnp.dot(attended, merge_full, preferred_element_type=jnp.float32)
    resid = features + branch
    routed, unit_two, inverse_two = rms_parts(resid, gain_two)
    routed_low = routed.astype(jnp.bfloat16)
    logits = jnp.dot(routed_low, router_full, preferred_element_type=jnp.float32)
    expert_ids = jnp.arange(expert_count, dtype=jnp.int32)
    route_hot = routes[:, :, None] == expert_ids[None, None, :]
    chosen = jnp.sum(jnp.where(route_hot, logits[:, None, :], 0.0), axis=-1)
    chosen_exp = jnp.exp(chosen - jnp.max(chosen, axis=1, keepdims=True))
    gate_values = chosen_exp / jnp.sum(chosen_exp, axis=1, keepdims=True)
    flat_routes = routes.reshape(-1)
    flat_hot = (flat_routes[:, None] == expert_ids[None, :]).astype(jnp.bfloat16)
    pair_ids = jnp.arange(pair_count, dtype=jnp.int32)
    lower_table = (pair_ids[None, :] < pair_ids[:, None]).astype(jnp.bfloat16)
    earlier = jnp.dot(lower_table, flat_hot, preferred_element_type=jnp.float32)
    position = jnp.sum(earlier * flat_hot.astype(jnp.float32), axis=1).astype(jnp.int32)
    slot_index = (
        flat_routes % local_count * owner_count + flat_routes // local_count
    ) * capacity + position
    slot_ids = jnp.arange(slot_total, dtype=jnp.int32)
    pair_hot = (slot_ids[:, None] == slot_index[None, :]).astype(jnp.bfloat16)
    token_hot = jnp.sum(
        pair_hot.reshape(slot_total, token_count, route_count), axis=2, dtype=jnp.bfloat16
    )
    send_rows = jnp.dot(token_hot, routed_low, preferred_element_type=jnp.float32).astype(
        jnp.bfloat16
    )
    arrived = lax.all_to_all(
        send_rows.reshape(local_count, owner_count, capacity, width),
        "expert",
        split_axis=1,
        concat_axis=1,
        tiled=True,
    )
    expert_rows = arrived.reshape(local_count, owner_count * capacity, width)
    pre_hidden = jnp.einsum(
        "erd,edf->erf", expert_rows, up_weight, preferred_element_type=jnp.float32
    )
    hidden = jax.nn.gelu(pre_hidden, approximate=True).astype(jnp.bfloat16)
    produced = jnp.einsum(
        "erf,efd->erd", hidden, down_weight, preferred_element_type=jnp.float32
    ).astype(jnp.bfloat16)
    returned = lax.all_to_all(
        produced.reshape(local_count, owner_count, capacity, width),
        "expert",
        split_axis=1,
        concat_axis=1,
        tiled=True,
    )
    picked = jnp.einsum(
        "sp,sd->pd",
        pair_hot,
        returned.reshape(slot_total, width),
        preferred_element_type=jnp.float32,
    ).reshape(token_count, route_count, width)
    result = resid + jnp.sum(gate_values[:, :, None] * picked, axis=1)
    output = result.astype(jnp.bfloat16)
    grad_result = cotangent.astype(jnp.float32)
    grad_gates = jnp.sum(grad_result[:, None, :] * picked, axis=-1)
    grad_chosen = gate_values * (
        grad_gates - jnp.sum(gate_values * grad_gates, axis=1, keepdims=True)
    )
    grad_logits = jnp.sum(jnp.where(route_hot, grad_chosen[:, :, None], 0.0), axis=1).astype(
        jnp.bfloat16
    )
    grad_picked = (
        (gate_values[:, :, None] * grad_result[:, None, :])
        .astype(jnp.bfloat16)
        .reshape(pair_count, width)
    )
    grad_send = jnp.dot(pair_hot, grad_picked, preferred_element_type=jnp.float32).astype(
        jnp.bfloat16
    )
    grad_arrived = lax.all_to_all(
        grad_send.reshape(local_count, owner_count, capacity, width),
        "expert",
        split_axis=1,
        concat_axis=1,
        tiled=True,
    )
    grad_produced = grad_arrived.reshape(local_count, owner_count * capacity, width)
    grad_hidden = jnp.einsum(
        "erd,efd->erf", grad_produced, down_weight, preferred_element_type=jnp.float32
    )
    activation, gelu_back = jax.vjp(partial(jax.nn.gelu, approximate=True), pre_hidden)
    hidden_again = activation.astype(jnp.bfloat16)
    grad_pre = gelu_back(grad_hidden)[0].astype(jnp.bfloat16)
    up_grad = jnp.einsum("erd,erf->edf", expert_rows, grad_pre, preferred_element_type=jnp.float32)
    down_grad = jnp.einsum(
        "erf,erd->efd", hidden_again, grad_produced, preferred_element_type=jnp.float32
    )
    grad_rows = jnp.einsum(
        "erf,edf->erd", grad_pre, up_weight, preferred_element_type=jnp.float32
    ).astype(jnp.bfloat16)
    returned_grads = lax.all_to_all(
        grad_rows.reshape(local_count, owner_count, capacity, width),
        "expert",
        split_axis=1,
        concat_axis=1,
        tiled=True,
    )
    grad_routed = jnp.einsum(
        "st,sd->td",
        token_hot,
        returned_grads.reshape(slot_total, width),
        preferred_element_type=jnp.float32,
    )
    grad_routed = grad_routed + jnp.einsum(
        "te,de->td", grad_logits, router_full, preferred_element_type=jnp.float32
    )
    router_grad = jnp.einsum(
        "td,te->de", routed_low, grad_logits, preferred_element_type=jnp.float32
    )
    grad_norm_two, gain_grad = rms_back(grad_routed, unit_two, inverse_two, gain_two)
    grad_resid = grad_result + grad_norm_two
    grad_branch = grad_resid.astype(jnp.bfloat16)
    merge_grad = jnp.einsum("ti,to->io", attended, grad_branch, preferred_element_type=jnp.float32)
    grad_attended = jnp.einsum(
        "to,io->ti", grad_branch, merge_full, preferred_element_type=jnp.float32
    ).astype(jnp.bfloat16)
    grad_queries, grad_keys, grad_values, distances = attend_back(
        queries, keys, values, grad_attended, attended, log_totals, near, head_size, block
    )
    close_sums = distances[:, :group_heads].reshape(head_count, block)
    far_sums = jnp.sum(distances[:, group_heads:].reshape(head_count, block), axis=1)
    table_grad = jnp.einsum(
        "nb,hn->bh", jnp.asarray(hot[:block]), close_sums, precision=lax.Precision.HIGHEST
    )
    table_grad = table_grad + jnp.asarray(hot[-1:]).T * far_sums[None, :]
    query_grad = jnp.einsum(
        "ti,to->io", normed_low, grad_queries, preferred_element_type=jnp.float32
    )
    key_grad = jnp.einsum("ti,to->io", normed_low, grad_keys, preferred_element_type=jnp.float32)
    value_grad = jnp.einsum(
        "ti,to->io", normed_low, grad_values, preferred_element_type=jnp.float32
    )
    grad_normed = jnp.einsum(
        "to,io->ti", grad_queries, query_full, preferred_element_type=jnp.float32
    )
    grad_normed = grad_normed + jnp.einsum(
        "to,io->ti", grad_keys, key_full, preferred_element_type=jnp.float32
    )
    grad_normed = grad_normed + jnp.einsum(
        "to,io->ti", grad_values, value_full, preferred_element_type=jnp.float32
    )
    grad_norm_one, norm_grad = rms_back(grad_normed, unit_one, inverse_one, gain_one)
    input_gradient = grad_resid + grad_norm_one
    everything = (
        lax.psum_scatter(
            norm_grad.astype(jnp.bfloat16), "shard", scatter_dimension=0, tiled=True
        ).astype(jnp.float32),
        lax.psum_scatter(
            query_grad.astype(jnp.bfloat16), "shard", scatter_dimension=0, tiled=True
        ).astype(jnp.float32),
        lax.psum_scatter(
            key_grad.astype(jnp.bfloat16), "shard", scatter_dimension=0, tiled=True
        ).astype(jnp.float32),
        lax.psum_scatter(
            value_grad.astype(jnp.bfloat16), "shard", scatter_dimension=0, tiled=True
        ).astype(jnp.float32),
        lax.psum_scatter(
            merge_grad.astype(jnp.bfloat16), "shard", scatter_dimension=0, tiled=True
        ).astype(jnp.float32),
        lax.psum_scatter(
            table_grad.astype(jnp.bfloat16), "shard", scatter_dimension=1, tiled=True
        ).astype(jnp.float32),
        lax.psum_scatter(
            gain_grad.astype(jnp.bfloat16), "shard", scatter_dimension=0, tiled=True
        ).astype(jnp.float32),
        lax.psum_scatter(
            router_grad.astype(jnp.bfloat16), "shard", scatter_dimension=0, tiled=True
        ).astype(jnp.float32),
        lax.psum_scatter(
            up_grad.astype(jnp.bfloat16), "shard", scatter_dimension=2, tiled=True
        ).astype(jnp.float32),
        lax.psum_scatter(
            down_grad.astype(jnp.bfloat16), "shard", scatter_dimension=1, tiled=True
        ).astype(jnp.float32),
    )
    layer_parts = everything[:8]
    up_part = everything[8]
    down_part = everything[9]
    totals = (
        lax.psum(layer_parts[0].astype(jnp.bfloat16), "expert").astype(jnp.float32),
        lax.psum(layer_parts[1].astype(jnp.bfloat16), "expert").astype(jnp.float32),
        lax.psum(layer_parts[2].astype(jnp.bfloat16), "expert").astype(jnp.float32),
        lax.psum(layer_parts[3].astype(jnp.bfloat16), "expert").astype(jnp.float32),
        lax.psum(layer_parts[4].astype(jnp.bfloat16), "expert").astype(jnp.float32),
        lax.psum(layer_parts[5].astype(jnp.bfloat16), "expert").astype(jnp.float32),
        lax.psum(layer_parts[6].astype(jnp.bfloat16), "expert").astype(jnp.float32),
        lax.psum(layer_parts[7].astype(jnp.bfloat16), "expert").astype(jnp.float32),
    )
    return (
        output,
        input_gradient,
        totals[0],
        totals[1],
        totals[2],
        totals[3],
        totals[4],
        totals[5],
        totals[6],
        totals[7],
        up_part,
        down_part,
    )


def solution(mesh):
    in_specs = (
        P(("expert", "shard"), None),
        P("shard"),
        P("shard", None),
        P("shard", None),
        P("shard", None),
        P("shard", None),
        P(None, "shard"),
        P("shard"),
        P("shard", None),
        P("expert", None, None),
        P("expert", None, None),
        P(("expert", "shard"), None),
        P(("expert", "shard"), None),
    )
    out_specs = (
        P(("expert", "shard"), None),
        P(("expert", "shard"), None),
        P("shard"),
        P("shard", None),
        P("shard", None),
        P("shard", None),
        P("shard", None),
        P(None, "shard"),
        P("shard"),
        P("shard", None),
        P("expert", None, "shard"),
        P("expert", "shard", None),
    )
    return jax.shard_map(local, mesh=mesh, in_specs=in_specs, out_specs=out_specs, check_vma=False)
```

```python
from functools import partial, reduce

import jax
import jax.numpy as jnp
import numpy as np
from jax import lax
from jax.experimental import pallas as pl
from jax.experimental.pallas import tpu as pltpu
from jax.sharding import PartitionSpec as P

BUCKETS = 32
MAX_DIST = 128


epsilon = 1e-06
masked_score = -1e30


def bucket_hot(length):
    distance = np.arange(length)
    half_count = BUCKETS // 2
    clipped = np.maximum(distance, half_count)
    spread = np.log(clipped / half_count) / np.log(MAX_DIST / half_count) * (BUCKETS - half_count)
    far_bucket = np.minimum(half_count + np.floor(spread).astype(np.int32), BUCKETS - 1)
    bucket = np.where(distance < half_count, distance, far_bucket)
    return (bucket[:, None] == np.arange(BUCKETS)[None, :]).astype(np.float32)


def dot_nt(a, b):
    return lax.dot_general(a, b, (((1,), (1,)), ((), ())), preferred_element_type=jnp.float32)

def dot_nn(a, b):
    return lax.dot_general(a, b, (((1,), (0,)), ((), ())), preferred_element_type=jnp.float32)

def dot_tn(a, b):
    return lax.dot_general(a, b, (((0,), (0,)), ((), ())), preferred_element_type=jnp.float32)


def slot_kernel(routes_ref, base_ref, slots_ref, *, experts):
    tokens = routes_ref.shape[1]
    expert = lax.broadcasted_iota(jnp.int32, (experts, tokens), 0)
    hits = [routes_ref[c:c + 1, :] == expert for c in range(2)]
    hot = jnp.where(hits[0] | hits[1], 1.0, 0.0).astype(jnp.bfloat16)
    earlier = lax.broadcasted_iota(jnp.int32, (tokens, tokens), 0)
    later = lax.broadcasted_iota(jnp.int32, (tokens, tokens), 1)
    before = jnp.where(earlier < later, 1.0, 0.0).astype(jnp.bfloat16)
    counts = dot_nn(hot, before)
    for c in range(2):
        position = jnp.sum(jnp.where(hits[c], counts, 0.0), axis=0, keepdims=True)
        slots_ref[c:c + 1, :] = base_ref[c:c + 1, :] + position.astype(jnp.int32)

def find_slots(routes, base, experts):
    return pl.pallas_call(
        partial(slot_kernel, experts=experts),
        out_shape=jax.ShapeDtypeStruct(routes.shape, jnp.int32),
        name="find_slots",
    )(routes, base)


def dispatch_kernel(slots_ref, rows_ref, *refs, start, gated):
    out_ref = refs[-2] if gated else refs[-1]
    block, tokens = out_ref.shape[0], rows_ref.shape[0]
    slot = lax.broadcasted_iota(jnp.int32, (block, tokens), 0) + (pl.program_id(0) * block + start)
    hits = [slot == slots_ref[c:c + 1, :] for c in range(2)]
    hot = jnp.where(hits[0] | hits[1], 1.0, 0.0).astype(jnp.bfloat16)
    out_ref[...] = dot_nn(hot, rows_ref[...]).astype(out_ref.dtype)
    if gated:
        gates_ref, gate_ref = refs[0], refs[-1]
        gate = jnp.where(hits[0], gates_ref[0:1, :], jnp.where(hits[1], gates_ref[1:2, :], 0.0))
        column = jnp.sum(gate, axis=1, keepdims=True)
        gate_ref[...] = jnp.broadcast_to(column, (block, 128)).T[0:1, :]

def dispatch(slots, rows, start, count, gates=None, block=256):
    tokens, width = rows.shape
    gated = gates is not None
    whole = lambda shape: pl.BlockSpec(shape, lambda i: (0, 0))
    out_shape = jax.ShapeDtypeStruct((count, width), rows.dtype)
    out_spec = pl.BlockSpec((block, width), lambda i: (i, 0))
    if gated:
        out_shape = [out_shape, jax.ShapeDtypeStruct((1, count), jnp.float32)]
        out_spec = [out_spec, pl.BlockSpec((1, block), lambda i: (0, i))]
    return pl.pallas_call(
        partial(dispatch_kernel, start=start, gated=gated),
        grid=(count // block,),
        in_specs=[whole(slots.shape), whole(rows.shape)] + ([whole(gates.shape)] if gated else []),
        out_specs=out_spec,
        out_shape=out_shape,
        name="dispatch",
    )(slots, rows, *([gates] if gated else []))


def gelu_pair(v):
    c = np.float32(np.sqrt(2.0 / np.pi))
    a = np.float32(0.044715)
    square = v * v
    half = 0.5 * jnp.tanh(v * (c * a * square + c)) + 0.5
    value = v * half
    slope = half + value * (1.0 - half) * (6.0 * c * a * square + 2.0 * c)
    return value, slope


def first_kernel(rows_ref, cot_ref, gate_ref, up_ref, act_ref, slope_ref, down_grad_ref, grad_ref, *, chunk):
    rows, width = rows_ref.shape
    @pl.when(pl.program_id(0) == 0)
    def _():
        column = jnp.broadcast_to(gate_ref[...], (128, rows)).T
        for start in range(0, width, 128):
            part = cot_ref[:, start:start + 128].astype(jnp.float32) * column
            grad_ref[:, start:start + 128] = part.astype(jnp.bfloat16)
    up = up_ref[0]
    for start in range(0, rows, chunk):
        pre = dot_nn(rows_ref[start:start + chunk, :], up)
        value, slope = gelu_pair(pre)
        act_ref[start:start + chunk, :] = value.astype(jnp.bfloat16)
        slope_ref[start:start + chunk, :] = slope.astype(jnp.bfloat16)
    down_grad_ref[...] = dot_tn(act_ref[...], grad_ref[...]).astype(jnp.bfloat16)

def expert_first(rows_in, cot, gate, up, which, tile=512, chunk=256):
    rows, width = rows_in.shape
    hidden = up.shape[2]
    fixed = pl.BlockSpec((rows, width), lambda i: (0, 0))
    column = pl.BlockSpec((rows, tile), lambda i: (0, i))
    return pl.pallas_call(
        partial(first_kernel, chunk=chunk),
        grid=(hidden // tile,),
        in_specs=[fixed, fixed, pl.BlockSpec((1, rows), lambda i: (0, 0)), pl.BlockSpec((1, width, tile), lambda i: (which, 0, i))],
        out_specs=[column, column, pl.BlockSpec((tile, width), lambda i: (i, 0)), fixed],
        out_shape=[jax.ShapeDtypeStruct((rows, hidden), jnp.bfloat16)] * 2 + [jax.ShapeDtypeStruct((hidden, width), jnp.bfloat16), jax.ShapeDtypeStruct((rows, width), jnp.bfloat16)],
        compiler_params=pltpu.CompilerParams(vmem_limit_bytes=56 << 20),
        name="expert_first",
    )(rows_in, cot, gate, up)


def second_kernel(rows_ref, grad_ref, act_ref, slope_ref, up_ref, down_ref, made_ref, back_ref, up_grad_ref, turned, made_acc, back_acc):
    step = pl.program_id(0)
    @pl.when(step == 0)
    def _():
        turned[...] = rows_ref[...].T
    up = up_ref[0]
    down = down_ref[0]
    grads = dot_nt(grad_ref[...], down)
    low = (slope_ref[...].astype(jnp.float32) * grads).astype(jnp.bfloat16)
    up_grad_ref[...] = dot_nn(turned[...], low).astype(jnp.bfloat16)
    back = dot_nt(low, up)
    made = dot_nn(act_ref[...], down)
    last = pl.num_programs(0) - 1
    @pl.when(step == 0)
    def _():
        made_acc[...] = made
        back_acc[...] = back
    @pl.when((step > 0) & (step < last))
    def _():
        made_acc[...] += made
        back_acc[...] += back
    @pl.when(step == last)
    def _():
        made_ref[...] = (made_acc[...] + made).astype(jnp.bfloat16)
        back_ref[...] = (back_acc[...] + back).astype(jnp.bfloat16)

def expert_second(rows_in, grad, act, slope, up, down, which, tile=512):
    rows, width = rows_in.shape
    hidden = up.shape[2]
    fixed = pl.BlockSpec((rows, width), lambda i: (0, 0))
    column = pl.BlockSpec((rows, tile), lambda i: (0, i))
    return pl.pallas_call(
        second_kernel,
        grid=(hidden // tile,),
        in_specs=[fixed, fixed, column, column, pl.BlockSpec((1, width, tile), lambda i: (which, 0, i)), pl.BlockSpec((1, tile, width), lambda i: (which, i, 0))],
        out_specs=[fixed, fixed, pl.BlockSpec((width, tile), lambda i: (0, i))],
        out_shape=[jax.ShapeDtypeStruct((rows, width), jnp.bfloat16)] * 2 + [jax.ShapeDtypeStruct((width, hidden), jnp.bfloat16)],
        scratch_shapes=[pltpu.VMEM((width, rows), jnp.bfloat16), pltpu.VMEM((rows, width), jnp.float32), pltpu.VMEM((rows, width), jnp.float32)],
        compiler_params=pltpu.CompilerParams(vmem_limit_bytes=60 << 20),
        name="expert_second",
    )(rows_in, grad, act, slope, up, down)


def spread(row, block):
    return jnp.broadcast_to(row, (128, block)).T

def out_kernel(slots_ref, routes_ref, gates_ref, resid_ref, cot_ref, first_ref, second_ref, out_ref, logit_ref):
    block = out_ref.shape[0]
    half = first_ref.shape[0]
    lane = lax.broadcasted_iota(jnp.int32, (block, 128), 1)
    cot = cot_ref[...].astype(jnp.float32)
    result = resid_ref[...]
    gates, inner = [], []
    for c in range(2):
        slot = spread(slots_ref[c:c + 1, :], block)
        gate = spread(gates_ref[c:c + 1, :], block)[:, 0:1]
        hots = [jnp.where(slot == lane + k * 128, 1.0, 0.0).astype(jnp.bfloat16) for k in range(2 * half // 128)]
        count = half // 128
        picked = dot_nn(jnp.concatenate(hots[:count], axis=1), first_ref[...]) + dot_nn(jnp.concatenate(hots[count:], axis=1), second_ref[...])
        result = result + gate * picked
        gates.append(gate)
        inner.append(jnp.sum(cot * picked, axis=1, keepdims=True))
    out_ref[...] = result.astype(out_ref.dtype)
    middle = gates[0] * inner[0] + gates[1] * inner[1]
    logit = jnp.zeros((block, 128), jnp.float32)
    for c in range(2):
        route = spread(routes_ref[c:c + 1, :], block)
        logit = logit + jnp.where(route == lane, gates[c] * (inner[c] - middle), 0.0)
    logit_ref[...] = logit.astype(jnp.bfloat16)

def combine_out(slots, routes, gates, resid, cot, first, second, block=256):
    tokens, width = resid.shape
    small = pl.BlockSpec((2, block), lambda i: (0, i))
    rows = pl.BlockSpec((block, width), lambda i: (i, 0))
    fixed = pl.BlockSpec(first.shape, lambda i: (0, 0))
    return pl.pallas_call(
        out_kernel,
        grid=(tokens // block,),
        in_specs=[small, small, small, rows, rows, fixed, fixed],
        out_specs=[rows, pl.BlockSpec((block, 128), lambda i: (i, 0))],
        out_shape=[jax.ShapeDtypeStruct((tokens, width), jnp.bfloat16), jax.ShapeDtypeStruct((tokens, 128), jnp.bfloat16)],
        compiler_params=pltpu.CompilerParams(vmem_limit_bytes=48 << 20),
        name="combine_out",
    )(slots, routes, gates, resid, cot, first, second)


def back_kernel(slots_ref, logit_ref, router_ref, gain_ref, resid_ref, cot_ref, first_ref, second_ref, grad_ref, low_ref, gain_grad_ref, *, eps):
    block, width = grad_ref.shape
    half = first_ref.shape[0]
    lane = lax.broadcasted_iota(jnp.int32, (block, 128), 1)
    slots = [spread(slots_ref[c:c + 1, :], block) for c in range(2)]
    hots = [jnp.where((slots[0] == lane + k * 128) | (slots[1] == lane + k * 128), 1.0, 0.0).astype(jnp.bfloat16) for k in range(2 * half // 128)]
    count = half // 128
    grads = dot_nn(jnp.concatenate(hots[:count], axis=1), first_ref[...]) + dot_nn(jnp.concatenate(hots[count:], axis=1), second_ref[...])
    grads = grads + dot_nt(logit_ref[...], router_ref[...])
    resid = resid_ref[...]
    inverse = lax.rsqrt(jnp.mean(resid * resid, axis=1, keepdims=True) + eps)
    unit = resid * inverse
    @pl.when(pl.program_id(0) == 0)
    def _():
        gain_grad_ref[...] = jnp.zeros_like(gain_grad_ref)
    gain_grad_ref[...] += jnp.sum(grads * unit, axis=0, keepdims=True)
    scaled = grads * gain_ref[...]
    inner = jnp.mean(scaled * unit, axis=1, keepdims=True)
    total = cot_ref[...].astype(jnp.float32) + inverse * (scaled - unit * inner)
    grad_ref[...] = total
    low_ref[...] = total.astype(jnp.bfloat16)

def combine_back(slots, logit, router, gain, resid, cot, first, second, eps, block=256):
    tokens, width = resid.shape
    rows = pl.BlockSpec((block, width), lambda i: (i, 0))
    whole = lambda shape: pl.BlockSpec(shape, lambda i: (0, 0))
    return pl.pallas_call(
        partial(back_kernel, eps=eps),
        grid=(tokens // block,),
        in_specs=[pl.BlockSpec((2, block), lambda i: (0, i)), pl.BlockSpec((block, 128), lambda i: (i, 0)), whole(router.shape), whole(gain.shape), rows, rows, whole(first.shape), whole(second.shape)],
        out_specs=[rows, rows, whole((1, width))],
        out_shape=[jax.ShapeDtypeStruct((tokens, width), jnp.float32), jax.ShapeDtypeStruct((tokens, width), jnp.bfloat16), jax.ShapeDtypeStruct((1, width), jnp.float32)],
        compiler_params=pltpu.CompilerParams(vmem_limit_bytes=48 << 20),
        name="combine_back",
    )(slots, logit, router, gain, resid, cot, first, second)


def near_tiles(near_ref, head, block):
    spread = jnp.broadcast_to(near_ref[0, head:head + 1, :], (block, block))
    spread = pltpu.roll(spread, 0, 1, stride=1, stride_axis=0)
    key_at = lax.broadcasted_iota(jnp.int32, (block, block), 0)
    query_at = lax.broadcasted_iota(jnp.int32, (block, block), 1)
    return (jnp.where(query_at >= key_at, spread, masked_score), jnp.where(query_at < key_at, spread, 0.0), query_at < key_at)

def diagonal_sums(tile):
    block = tile.shape[1]
    total = tile[:8]
    for start in range(8, block, 8):
        total = total + pltpu.roll(tile[start:start + 8], block - start, 1)
    row = lax.broadcasted_iota(jnp.int32, total.shape, 0)
    for step in (1, 2, 4):
        total = jnp.where((row & step) != 0, pltpu.roll(total, block - step, 1), total)
    return jnp.sum(total, axis=0, keepdims=True)

def head_part(rows, head, size):
    lane = lax.broadcasted_iota(jnp.int32, rows.shape, 1)
    return jnp.where((lane >= head * size) & (lane < (head + 1) * size), rows, jnp.zeros_like(rows))

def attend_kernel(query_ref, key_ref, value_ref, near_ref, out_ref, total_ref, *, block, size, scale):
    length, lanes = query_ref.shape
    heads = lanes // size
    count = length // block
    flipped = value_ref[...].T
    tiles = [near_tiles(near_ref, head, block) for head in range(heads)]
    for i in range(count):
        rows = pl.ds(i * block, block)
        query_rows = query_ref[rows, :] * jnp.bfloat16(scale)
        parts = []
        for head in range(heads):
            query_part = head_part(query_rows, head, size)
            scores = []
            for j in range(i + 1):
                tile = dot_nt(key_ref[pl.ds(j * block, block), :], query_part)
                if j == i:
                    tile = tile + tiles[head][0]
                elif j == i - 1:
                    tile = tile + tiles[head][1]
                scores.append(tile)
            top = reduce(jnp.maximum, scores)
            top = jnp.max(top, axis=0, keepdims=True)
            mixed = None
            total = None
            for j in range(i + 1):
                weights = jnp.exp(scores[j] - top)
                sums = jnp.sum(weights, axis=0, keepdims=True)
                part = dot_nn(flipped[head * size:(head + 1) * size, j * block:(j + 1) * block], weights.astype(jnp.bfloat16))
                mixed = part if mixed is None else mixed + part
                total = sums if total is None else total + sums
            parts.append(mixed / total)
            total_ref[0, head:head + 1, rows] = top + jnp.log(total)
        out_ref[rows, :] = jnp.concatenate(parts, axis=0).T.astype(out_ref.dtype)

def attend(queries, keys, values, near, size, block):
    length, width = queries.shape
    lanes = 128
    heads = lanes // size
    groups = width // lanes
    column = pl.BlockSpec((length, lanes), lambda g: (0, g))
    head_rows = pl.BlockSpec((1, heads, block), lambda g: (g, 0, 0))
    return pl.pallas_call(
        partial(attend_kernel, block=block, size=size, scale=size ** -0.5),
        grid=(groups,),
        in_specs=[column, column, column, head_rows],
        out_specs=[column, pl.BlockSpec((1, heads, length), lambda g: (g, 0, 0))],
        out_shape=[jax.ShapeDtypeStruct((length, width), jnp.bfloat16), jax.ShapeDtypeStruct((groups, heads, length), jnp.float32)],
        compiler_params=pltpu.CompilerParams(vmem_limit_bytes=48 << 20),
        name="attend",
    )(queries, keys, values, near)

def attend_back_kernel(query_ref, key_ref, value_ref, grad_ref, out_ref, total_ref, near_ref, dq_ref, dk_ref, dv_ref, dist_ref, key_acc, value_acc, *, block, size, scale):
    length, lanes = query_ref.shape
    heads = lanes // size
    count = length // block
    flipped = key_ref[...].T
    tiles = [near_tiles(near_ref, head, block) for head in range(heads)]
    near_acc = [None] * heads
    far_acc = [None] * heads
    for i in range(count):
        rows = pl.ds(i * block, block)
        query_rows = query_ref[rows, :] * jnp.bfloat16(scale)
        grad_rows = grad_ref[rows, :]
        products = (grad_rows.astype(jnp.float32) * out_ref[rows, :].astype(jnp.float32)).T
        query_parts = [head_part(query_rows, head, size) for head in range(heads)]
        grad_parts = [head_part(grad_rows, head, size) for head in range(heads)]
        inner = [jnp.sum(products[head * size:(head + 1) * size], axis=0, keepdims=True) for head in range(heads)]
        query_stack = jnp.concatenate(query_parts, axis=0)
        grad_stack = jnp.concatenate(grad_parts, axis=0)
        query_grads = [None] * heads
        for j in range(i + 1):
            cols = pl.ds(j * block, block)
            weight_list = []
            score_list = []
            for head in range(heads):
                tile = dot_nt(key_ref[cols, :], query_parts[head])
                if j == i:
                    tile = tile + tiles[head][0]
                elif j == i - 1:
                    tile = tile + tiles[head][1]
                weights = jnp.exp(tile - total_ref[0, head:head + 1, rows])
                grads = dot_nt(value_ref[cols, :], grad_parts[head])
                score_grads = weights * (grads - inner[head])
                low = score_grads.astype(jnp.bfloat16)
                weight_list.append(weights.astype(jnp.bfloat16))
                score_list.append(low)
                part = dot_nn(flipped[head * size:(head + 1) * size, j * block:(j + 1) * block], low)
                query_grads[head] = part if query_grads[head] is None else query_grads[head] + part
                if j == i:
                    near_acc[head] = score_grads if near_acc[head] is None else near_acc[head] + score_grads
                else:
                    far = score_grads
                    if j == i - 1:
                        close = jnp.where(tiles[head][2], score_grads, 0.0)
                        near_acc[head] = near_acc[head] + close
                        far = score_grads - close
                    far = jnp.sum(far, axis=0, keepdims=True)
                    far_acc[head] = far if far_acc[head] is None else far_acc[head] + far
            value_part = dot_nn(jnp.concatenate(weight_list, axis=1), grad_stack)
            key_part = dot_nn(jnp.concatenate(score_list, axis=1), query_stack)
            if j == i:
                value_acc[cols, :] = value_part
                key_acc[cols, :] = key_part
            else:
                value_acc[cols, :] += value_part
                key_acc[cols, :] += key_part
        dq_ref[rows, :] = (jnp.concatenate(query_grads, axis=0) * scale).T.astype(dq_ref.dtype)
    dk_ref[...] = key_acc[...].astype(dk_ref.dtype)
    dv_ref[...] = value_acc[...].astype(dv_ref.dtype)
    for head in range(heads):
        dist_ref[0, head:head + 1, :] = diagonal_sums(near_acc[head])
        dist_ref[0, heads + head:heads + head + 1, :] = far_acc[head]

def attend_back(queries, keys, values, grads, outs, totals, near, size, block):
    length, width = queries.shape
    lanes = 128
    heads = lanes // size
    groups = width // lanes
    column = pl.BlockSpec((length, lanes), lambda g: (0, g))
    head_rows = pl.BlockSpec((1, heads, block), lambda g: (g, 0, 0))
    return pl.pallas_call(
        partial(attend_back_kernel, block=block, size=size, scale=size ** -0.5),
        grid=(groups,),
        in_specs=[column] * 5 + [pl.BlockSpec((1, heads, length), lambda g: (g, 0, 0)), head_rows],
        out_specs=[column, column, column, pl.BlockSpec((1, 2 * heads, block), lambda g: (g, 0, 0))],
        out_shape=[jax.ShapeDtypeStruct((length, width), jnp.bfloat16)] * 3 + [jax.ShapeDtypeStruct((groups, 2 * heads, block), jnp.float32)],
        scratch_shapes=[pltpu.VMEM((length, lanes), jnp.float32)] * 2,
        compiler_params=pltpu.CompilerParams(vmem_limit_bytes=56 << 20),
        name="attend_back",
    )(queries, keys, values, grads, outs, totals, near)


def project_kernel(inputs_ref, gain_ref, query_ref, key_ref, value_ref, low_ref, *out_refs, eps):
    rows = inputs_ref[...].astype(jnp.float32)
    inverse = lax.rsqrt(jnp.mean(rows * rows, axis=1, keepdims=True) + eps)
    low = (rows * inverse * gain_ref[...]).astype(jnp.bfloat16)
    low_ref[...] = low
    for weight_ref, out_ref in zip((query_ref, key_ref, value_ref), out_refs):
        out_ref[...] = dot_nn(low, weight_ref[...]).astype(jnp.bfloat16)

def project(inputs, gain, query, key, value, eps, block=256):
    tokens, width = inputs.shape
    rows = pl.BlockSpec((block, width), lambda i: (i, 0))
    whole = lambda shape: pl.BlockSpec(shape, lambda i: (0, 0))
    return pl.pallas_call(
        partial(project_kernel, eps=eps),
        grid=(tokens // block,),
        in_specs=[rows, whole(gain.shape)] + [whole(query.shape)] * 3,
        out_specs=[rows] * 4,
        out_shape=[jax.ShapeDtypeStruct((tokens, width), jnp.bfloat16)] * 4,
        compiler_params=pltpu.CompilerParams(vmem_limit_bytes=40 << 20),
        name="project",
    )(inputs, gain, query, key, value)


def settle_kernel(mixed_ref, merge_ref, inputs_ref, gain_ref, router_ref, routes_ref, resid_ref, low_ref, gates_ref, *, eps):
    block = mixed_ref.shape[0]
    resid = inputs_ref[...].astype(jnp.float32) + dot_nn(mixed_ref[...], merge_ref[...])
    resid_ref[...] = resid
    inverse = lax.rsqrt(jnp.mean(resid * resid, axis=1, keepdims=True) + eps)
    low = (resid * inverse * gain_ref[...]).astype(jnp.bfloat16)
    low_ref[...] = low
    logits = dot_nt(router_ref[...], low)
    expert = lax.broadcasted_iota(jnp.int32, logits.shape, 0)
    chosen = [jnp.sum(jnp.where(routes_ref[c:c + 1, :] == expert, logits, 0.0), axis=0, keepdims=True) for c in range(2)]
    top = jnp.maximum(chosen[0], chosen[1])
    powers = [jnp.exp(value - top) for value in chosen]
    total = powers[0] + powers[1]
    for c in range(2):
        gates_ref[c:c + 1, :] = powers[c] / total

def settle(mixed, merge, inputs, gain, router, routes, eps, block=256):
    tokens, width = inputs.shape
    rows = pl.BlockSpec((block, width), lambda i: (i, 0))
    whole = lambda shape: pl.BlockSpec(shape, lambda i: (0, 0))
    small = pl.BlockSpec((2, block), lambda i: (0, i))
    return pl.pallas_call(
        partial(settle_kernel, eps=eps),
        grid=(tokens // block,),
        in_specs=[rows, whole(merge.shape), rows, whole(gain.shape), whole(router.shape), small],
        out_specs=[rows, rows, small],
        out_shape=[jax.ShapeDtypeStruct((tokens, width), jnp.float32), jax.ShapeDtypeStruct((tokens, width), jnp.bfloat16), jax.ShapeDtypeStruct((2, tokens), jnp.float32)],
        compiler_params=pltpu.CompilerParams(vmem_limit_bytes=40 << 20),
        name="settle",
    )(mixed, merge, inputs, gain, router, routes)


def finish_kernel(dq_ref, dk_ref, dv_ref, query_ref, key_ref, value_ref, gain_ref, inputs_ref, resid_grad_ref, out_ref, gain_grad_ref, *, eps):
    grads = dot_nt(dq_ref[...], query_ref[...]) + dot_nt(dk_ref[...], key_ref[...]) + dot_nt(dv_ref[...], value_ref[...])
    rows = inputs_ref[...].astype(jnp.float32)
    inverse = lax.rsqrt(jnp.mean(rows * rows, axis=1, keepdims=True) + eps)
    unit = rows * inverse
    @pl.when(pl.program_id(0) == 0)
    def _():
        gain_grad_ref[...] = jnp.zeros_like(gain_grad_ref)
    gain_grad_ref[...] += jnp.sum(grads * unit, axis=0, keepdims=True)
    scaled = grads * gain_ref[...]
    inner = jnp.mean(scaled * unit, axis=1, keepdims=True)
    out_ref[...] = resid_grad_ref[...] + inverse * (scaled - unit * inner)

def finish(dq, dk, dv, query, key, value, gain, inputs, resid_grad, eps, block=256):
    tokens, width = inputs.shape
    rows = pl.BlockSpec((block, width), lambda i: (i, 0))
    whole = lambda shape: pl.BlockSpec(shape, lambda i: (0, 0))
    return pl.pallas_call(
        partial(finish_kernel, eps=eps),
        grid=(tokens // block,),
        in_specs=[rows] * 3 + [whole(query.shape)] * 3 + [whole(gain.shape), rows, rows],
        out_specs=[rows, whole((1, width))],
        out_shape=[jax.ShapeDtypeStruct((tokens, width), jnp.float32), jax.ShapeDtypeStruct((1, width), jnp.float32)],
        compiler_params=pltpu.CompilerParams(vmem_limit_bytes=40 << 20),
        name="finish",
    )(dq, dk, dv, query, key, value, gain, inputs, resid_grad)


def exchange(rows, bit):
    count = lax.axis_size("expert")
    return lax.ppermute(rows, "expert", [(i, i ^ bit) for i in range(count)])


def shift(rows, step):
    count = lax.axis_size("shard")
    return lax.ppermute(rows, "shard", [(i, (i + step) % count) for i in range(count)])


def gather_line(rows):
    count = lax.axis_size("shard")
    me = lax.axis_index("shard")
    out = jnp.zeros((count,) + rows.shape, rows.dtype)
    out = lax.dynamic_update_index_in_dim(out, rows, me, 0)
    for step in range(1, count):
        out = lax.dynamic_update_index_in_dim(out, shift(rows, step), (me - step) % count, 0)
    return out


def add_low(left, right):
    return (left.astype(jnp.float32) + right.astype(jnp.float32)).astype(jnp.bfloat16)


def reduce_stack(stack, bits):
    me = lax.axis_index("expert")
    for bit in bits:
        half = stack.shape[1] // 2
        side = (me // bit) % 2
        keep = lax.dynamic_slice_in_dim(stack, side * half, half, 1)
        send = lax.dynamic_slice_in_dim(stack, (1 - side) * half, half, 1)
        stack = add_low(keep, exchange(send, bit))
    count = lax.axis_size("shard")
    place = lax.axis_index("shard")
    total = lax.dynamic_index_in_dim(stack, place, 0, False).astype(jnp.float32)
    for step in range(1, count):
        send = lax.dynamic_index_in_dim(stack, (place + step) % count, 0, False)
        total = total + shift(send, step).astype(jnp.float32)
    piece = total.astype(jnp.bfloat16)
    for bit in reversed(bits):
        other = exchange(piece, bit)
        side = (me // bit) % 2
        piece = jnp.where(
            side == 0, jnp.concatenate([piece, other]), jnp.concatenate([other, piece])
        )
    return piece


def share_rows(rows, owners):
    count, width = rows.shape
    return lax.all_to_all(
        rows.reshape(owners, count // owners, width), "expert", 0, 0, tiled=True
    ).reshape(count, width)


def local(
    inputs,
    norm_gain,
    query_weight,
    key_weight,
    value_weight,
    merge_weight,
    bias_table,
    expert_gain,
    router_weight,
    up_weight,
    down_weight,
    routes,
    cotangent,
):
    f32, bf16 = jnp.float32, jnp.bfloat16
    tokens, width = inputs.shape
    owners = lax.axis_size("expert")
    shards = lax.axis_size("shard")
    me = lax.axis_index("expert")
    part = query_weight.shape[0]
    piece = part // owners
    local_heads = bias_table.shape[1]
    heads = local_heads * shards
    size = width // heads
    experts = router_weight.shape[1]
    local_count = up_weight.shape[0]
    capacity = (5 * tokens * routes.shape[1] + 4 * experts - 1) // (4 * experts)
    rows = owners * capacity

    small = jnp.concatenate(
        [norm_gain, expert_gain, router_weight.reshape(-1), bias_table.reshape(-1)]
    )
    small_rows = 8 * owners
    small = jnp.pad(small, (0, small_rows * width - small.shape[0])).reshape(small_rows, width)
    slices = [
        lax.dynamic_slice_in_dim(weight, me * piece, piece, 0)
        for weight in (query_weight, key_weight, value_weight)
    ] + [lax.dynamic_slice_in_dim(small, me * 8, 8, 0)]
    lined = gather_line(jnp.concatenate(slices))
    gathered = lax.all_gather(lined, "expert", axis=0, tiled=False)
    merge_full = lax.all_gather(merge_weight, "shard", axis=0, tiled=True)

    def whole_weight(index):
        block = gathered[:, :, index * piece : (index + 1) * piece]
        return block.transpose(1, 0, 2, 3).reshape(width, width)

    query_full, key_full, value_full = (whole_weight(index) for index in range(3))
    small_full = gathered[:, :, 3 * piece :].transpose(1, 0, 2, 3).reshape(shards, small_rows * width)
    gain_one = small_full[:, :part].reshape(1, width).astype(f32)
    gain_two = small_full[:, part : 2 * part].reshape(1, width).astype(f32)
    router_at = 2 * part + part * experts
    router_full = small_full[:, 2 * part : router_at].reshape(width, experts)
    table_full = small_full[:, router_at : router_at + BUCKETS * local_heads]
    table_full = table_full.reshape(shards, BUCKETS, local_heads).transpose(1, 0, 2)
    table_full = table_full.reshape(BUCKETS, heads).astype(f32)

    routes_line = routes.T
    base = (routes_line % local_count * owners + routes_line // local_count) * capacity
    slots = find_slots(routes_line, base, experts)
    cot_rows = [dispatch(slots, cotangent, index * rows, rows) for index in range(local_count)]

    low_one, queries, keys, values = project(
        inputs, gain_one, query_full, key_full, value_full, epsilon
    )
    block = 256
    hot = bucket_hot(tokens)
    assert hot[block:, -1].all()
    near_hot = jnp.asarray(hot[:block] - hot[-1:], dtype=f32)
    group = 128 // size
    near = jnp.dot(near_hot, table_full, precision=lax.Precision.HIGHEST).T
    near = near.reshape(heads // group, group, block)
    attended, totals = attend(queries, keys, values, near, size, block)
    resid, low_two, gates = settle(
        attended, merge_full, inputs, gain_two, router_full.T, routes_line, epsilon
    )

    made, back, up_grads, down_grads = [], [], [], []
    for index in range(local_count):
        rows_out, gate_out = dispatch(slots, low_two, index * rows, rows, gates)
        rows_in = share_rows(rows_out, owners)
        gate_in = lax.all_to_all(
            gate_out.reshape(owners, 1, capacity), "expert", 0, 0, tiled=True
        ).reshape(1, rows)
        cot_in = share_rows(cot_rows[index], owners)
        act, slope, down_grad, grad_in = expert_first(rows_in, cot_in, gate_in, up_weight, index)
        down_grads.append(lax.psum_scatter(down_grad, "shard", scatter_dimension=0, tiled=True))
        made_rows, back_rows, up_grad = expert_second(
            rows_in, grad_in, act, slope, up_weight, down_weight, index
        )
        up_grads.append(lax.psum_scatter(up_grad, "shard", scatter_dimension=1, tiled=True))
        made.append(share_rows(made_rows, owners))
        back.append(share_rows(back_rows, owners))
    output, logit_grad = combine_out(slots, routes_line, gates, resid, cotangent, *made)
    router_wide = jnp.pad(router_full, ((0, 0), (0, 128 - experts)))
    resid_grad, branch, gain_grad = combine_back(
        slots, logit_grad, router_wide, gain_two, resid, cotangent, *back, epsilon
    )

    def weight_grad(left, right):
        return jnp.einsum("ti,to->io", left, right, preferred_element_type=f32).astype(bf16)

    router_grad = weight_grad(low_two, logit_grad[:, :experts])
    merge_grad = weight_grad(attended, branch)
    mixed_grad = jnp.einsum(
        "to,io->ti", branch, merge_full, preferred_element_type=f32
    ).astype(bf16)
    grad_queries, grad_keys, grad_values, distances = attend_back(
        queries, keys, values, mixed_grad, attended, totals, near, size, block
    )
    close_sums = distances[:, :group].reshape(heads, block)
    far_sums = jnp.sum(distances[:, group:].reshape(heads, block), axis=1)
    table_grad = jnp.einsum(
        "nb,hn->bh", jnp.asarray(hot[:block]), close_sums, precision=lax.Precision.HIGHEST
    )
    table_grad = table_grad + jnp.asarray(hot[-1:]).T * far_sums[None, :]
    input_gradient, norm_grad = finish(
        grad_queries, grad_keys, grad_values, query_full, key_full, value_full,
        gain_one, inputs, resid_grad, epsilon,
    )

    def by_shard(grad):
        return grad.reshape(shards, part, width)

    small_grad = jnp.concatenate(
        [
            norm_grad.reshape(shards, part).astype(bf16),
            gain_grad.reshape(shards, part).astype(bf16),
            router_grad.reshape(shards, part * experts),
            table_grad.reshape(BUCKETS, shards, local_heads)
            .transpose(1, 0, 2)
            .reshape(shards, BUCKETS * local_heads)
            .astype(bf16),
        ],
        axis=1,
    )
    used = small_grad.shape[1]
    small_grad = jnp.pad(small_grad, ((0, 0), (0, small_rows * width - used)))
    small_grad = small_grad.reshape(shards, small_rows, width)
    bits = [1 << level for level in range(owners.bit_length() - 1)]
    first_stack = jnp.concatenate(
        [by_shard(weight_grad(low_one, grad)) for grad in (grad_queries, grad_keys)], axis=1
    )
    second_stack = jnp.concatenate(
        [by_shard(weight_grad(low_one, grad_values)), by_shard(merge_grad), small_grad], axis=1
    )
    first_sum = reduce_stack(first_stack, bits).astype(f32)
    second_sum = reduce_stack(second_stack, bits[:1] + bits[:0:-1]).astype(f32)
    small_sum = second_sum[2 * part :].reshape(-1)
    return (
        output,
        input_gradient,
        small_sum[:part],
        first_sum[:part],
        first_sum[part:],
        second_sum[:part],
        second_sum[part : 2 * part],
        small_sum[router_at : router_at + BUCKETS * local_heads].reshape(BUCKETS, local_heads),
        small_sum[part : 2 * part],
        small_sum[2 * part : router_at].reshape(part, experts),
        jnp.stack([grad.astype(f32) for grad in up_grads]),
        jnp.stack([grad.astype(f32) for grad in down_grads]),
    )


def solution(mesh):
    in_specs = (
        P(("expert", "shard"), None),
        P("shard"),
        P("shard", None),
        P("shard", None),
        P("shard", None),
        P("shard", None),
        P(None, "shard"),
        P("shard"),
        P("shard", None),
        P("expert", None, None),
        P("expert", None, None),
        P(("expert", "shard"), None),
        P(("expert", "shard"), None),
    )
    out_specs = (
        P(("expert", "shard"), None),
        P(("expert", "shard"), None),
        P("shard"),
        P("shard", None),
        P("shard", None),
        P("shard", None),
        P("shard", None),
        P(None, "shard"),
        P("shard"),
        P("shard", None),
        P("expert", None, "shard"),
        P("expert", "shard", None),
    )
    return jax.shard_map(local, mesh=mesh, in_specs=in_specs, out_specs=out_specs, check_vma=False)
```

```python
from functools import partial, reduce

import jax
import jax.numpy as jnp
import numpy as np
from jax import lax
from jax.experimental import pallas as pl
from jax.experimental.pallas import tpu as pltpu
from jax.sharding import PartitionSpec as P


BUCKETS = 32
MAX_DIST = 128


epsilon = 1e-06
masked_score = -1e30


def bucket_hot(length):
    distance = np.arange(length)
    half_count = BUCKETS // 2
    clipped = np.maximum(distance, half_count)
    spread = np.log(clipped / half_count) / np.log(MAX_DIST / half_count) * (BUCKETS - half_count)
    far_bucket = np.minimum(half_count + np.floor(spread).astype(np.int32), BUCKETS - 1)
    bucket = np.where(distance < half_count, distance, far_bucket)
    return (bucket[:, None] == np.arange(BUCKETS)[None, :]).astype(np.float32)


def dot_nt(a, b):
    return lax.dot_general(a, b, (((1,), (1,)), ((), ())), preferred_element_type=jnp.float32)


def dot_nn(a, b):
    return lax.dot_general(a, b, (((1,), (0,)), ((), ())), preferred_element_type=jnp.float32)


def dot_tn(a, b):
    return lax.dot_general(a, b, (((0,), (0,)), ((), ())), preferred_element_type=jnp.float32)


def slot_kernel(routes_ref, base_ref, slots_ref, *, experts):
    tokens = routes_ref.shape[1]
    expert = lax.broadcasted_iota(jnp.int32, (experts, tokens), 0)
    hits = [routes_ref[c:c + 1, :] == expert for c in range(2)]
    hot = jnp.where(hits[0] | hits[1], 1.0, 0.0).astype(jnp.bfloat16)
    earlier = lax.broadcasted_iota(jnp.int32, (tokens, tokens), 0)
    later = lax.broadcasted_iota(jnp.int32, (tokens, tokens), 1)
    before = jnp.where(earlier < later, 1.0, 0.0).astype(jnp.bfloat16)
    counts = dot_nn(hot, before)
    for c in range(2):
        position = jnp.sum(jnp.where(hits[c], counts, 0.0), axis=0, keepdims=True)
        slots_ref[c:c + 1, :] = base_ref[c:c + 1, :] + position.astype(jnp.int32)


def find_slots(routes, base, experts):
    return pl.pallas_call(
        partial(slot_kernel, experts=experts),
        out_shape=jax.ShapeDtypeStruct(routes.shape, jnp.int32),
        name="find_slots",
    )(routes, base)


def dispatch_kernel(slots_ref, rows_ref, *refs, start):
    out_ref = refs[-1]
    block, tokens = out_ref.shape[0], rows_ref.shape[0]
    slot = lax.broadcasted_iota(jnp.int32, (block, tokens), 0) + (pl.program_id(0) * block + start)
    hot = jnp.where((slot == slots_ref[0:1, :]) | (slot == slots_ref[1:2, :]), 1.0, 0.0)
    out_ref[...] = dot_nn(hot.astype(jnp.bfloat16), rows_ref[...]).astype(out_ref.dtype)


def dispatch(slots, rows, start, count, after=(), block=256):
    _, width = rows.shape
    whole = lambda shape: pl.BlockSpec(shape, lambda i: (0, 0))
    return pl.pallas_call(
        partial(dispatch_kernel, start=start),
        grid=(count // block,),
        in_specs=[whole(slots.shape), whole(rows.shape)] + [pl.BlockSpec(memory_space=pl.ANY)] * len(after),
        out_specs=pl.BlockSpec((block, width), lambda i: (i, 0)),
        out_shape=jax.ShapeDtypeStruct((count, width), rows.dtype),
        name="dispatch",
    )(slots, rows, *after)


def dispatch_all_kernel(slots_ref, routes_ref, rows_ref, out_ref, other_ref, *, owners, capacity):
    block, tokens = out_ref.shape[1], rows_ref.shape[0]
    row = lax.broadcasted_iota(jnp.int32, (block, tokens), 0)
    slot = row + pl.program_id(0) * capacity
    for index in range(1, block // capacity):
        slot = slot + jnp.where(row >= index * capacity, (owners - 1) * capacity, 0)
    hits = [slot == slots_ref[c:c + 1, :] for c in range(2)]
    hot = jnp.where(hits[0] | hits[1], 1.0, 0.0).astype(jnp.bfloat16)
    out_ref[0] = dot_nn(hot, rows_ref[...]).astype(out_ref.dtype)
    other = jnp.where(hits[0], routes_ref[1:2, :], jnp.where(hits[1], routes_ref[0:1, :], 0.0))
    column = jnp.sum(other, axis=1, keepdims=True)
    other_ref[0] = jnp.broadcast_to(column, (block, 128)).T[0:1, :]


def dispatch_all(slots, routes, rows, owners, capacity, local_count):
    _, width = rows.shape
    block = local_count * capacity
    whole = lambda shape: pl.BlockSpec(shape, lambda i: (0, 0))
    return pl.pallas_call(
        partial(dispatch_all_kernel, owners=owners, capacity=capacity),
        grid=(owners,),
        in_specs=[whole(slots.shape), whole(routes.shape), whole(rows.shape)],
        out_specs=[pl.BlockSpec((1, block, width), lambda i: (i, 0, 0)), pl.BlockSpec((1, 1, block), lambda i: (i, 0, 0))],
        out_shape=[jax.ShapeDtypeStruct((owners, block, width), rows.dtype), jax.ShapeDtypeStruct((owners, 1, block), jnp.float32)],
        name="dispatch_all",
    )(slots, routes, rows)


def gelu_pair(v):
    c = np.float32(np.sqrt(2.0 / np.pi))
    a = np.float32(0.044715)
    square = v * v
    half = 0.5 * jnp.tanh(v * (c * a * square + c)) + 0.5
    value = v * half
    slope = half + value * (1.0 - half) * (6.0 * c * a * square + 2.0 * c)
    return value, slope


def first_kernel(owner_ref, rows_ref, cot_ref, other_ref, router_ref, up_ref, *refs, chunk, index, local_count):
    act_ref, slope_ref, down_grad_ref, grad_ref = refs[-4:]
    rows, width = rows_ref.shape
    @pl.when(pl.program_id(0) == 0)
    def _():
        logits = dot_nt(router_ref[...], rows_ref[...])
        expert = lax.broadcasted_iota(jnp.int32, logits.shape, 0)
        mine = owner_ref[0] * local_count + index
        own = jnp.sum(jnp.where(expert == mine, logits, 0.0), axis=0, keepdims=True)
        other = other_ref[...].astype(jnp.int32)
        other = jnp.sum(jnp.where(expert == other, logits, 0.0), axis=0, keepdims=True)
        top = jnp.maximum(own, other)
        own = jnp.exp(own - top)
        gate = own / (own + jnp.exp(other - top))
        column = jnp.broadcast_to(gate, (128, rows)).T
        for start in range(0, width, 128):
            part = cot_ref[:, :, start:start + 128].reshape(rows, 128).astype(jnp.float32) * column
            grad_ref[:, start:start + 128] = part.astype(jnp.bfloat16)
    up = up_ref[0]
    for start in range(0, rows, chunk):
        pre = dot_nn(rows_ref[start:start + chunk, :], up)
        value, slope = gelu_pair(pre)
        act_ref[start:start + chunk, :] = value.astype(jnp.bfloat16)
        slope_ref[start:start + chunk, :] = slope.astype(jnp.bfloat16)
    down_grad_ref[0] = dot_tn(act_ref[...], grad_ref[...]).astype(jnp.bfloat16)


def expert_first(owner, rows_in, cot, other, router, up, index, local_count, shards, into=None, after=(), chunk=640):
    rows, width = rows_in.shape
    hidden = up.shape[2]
    tile = hidden // shards
    owners, _, capacity, _ = cot.shape
    fixed = pl.BlockSpec((rows, width), lambda i: (0, 0))
    column = pl.BlockSpec((rows, tile), lambda i: (0, i))
    chunk = chunk if rows % chunk == 0 else rows // 2
    operands = [owner, rows_in, cot, other, router, up]
    place, aliases = 0, {}
    grad_shape = jax.ShapeDtypeStruct((shards, tile, width), jnp.bfloat16)
    if into is not None:
        aliases = {len(operands): 2}
        operands.append(into)
        place, grad_shape = 1, jax.ShapeDtypeStruct(into.shape, into.dtype)
    operands += list(after)
    return pl.pallas_call(
        partial(first_kernel, chunk=chunk, index=index, local_count=local_count),
        grid=(shards,),
        in_specs=[
            pl.BlockSpec(memory_space=pltpu.SMEM),
            fixed,
            pl.BlockSpec((owners, None, capacity, width), lambda i: (0, index, 0, 0)),
            pl.BlockSpec((1, rows), lambda i: (0, 0)),
            pl.BlockSpec(router.shape, lambda i: (0, 0)),
            pl.BlockSpec((1, width, tile), lambda i: (index, 0, i)),
        ]
        + [pl.BlockSpec(memory_space=pl.ANY)] * (len(operands) - 6),
        out_specs=[column, column, pl.BlockSpec((1, tile, width), lambda i: (i, place, 0)), fixed],
        out_shape=[jax.ShapeDtypeStruct((rows, hidden), jnp.bfloat16)] * 2 + [grad_shape, jax.ShapeDtypeStruct((rows, width), jnp.bfloat16)],
        input_output_aliases=aliases,
        compiler_params=pltpu.CompilerParams(vmem_limit_bytes=60 << 20),
        name="expert_first",
    )(*operands)


def second_kernel(rows_ref, grad_ref, act_ref, slope_ref, up_ref, down_ref, *refs):
    made_ref, up_grad_ref, turned, made_acc, back_acc = refs[-5:]
    step = pl.program_id(0)
    owners, _, capacity, width = made_ref.shape
    @pl.when(step == 0)
    def _():
        turned[...] = rows_ref[...].T
    up = up_ref[0]
    down = down_ref[0]
    grads = dot_nt(grad_ref[...], down)
    low = (slope_ref[...].astype(jnp.float32) * grads).astype(jnp.bfloat16)
    up_grad_ref[0] = dot_nn(turned[...], low).astype(jnp.bfloat16)
    back = dot_nt(low, up)
    made = dot_nn(act_ref[...], down)
    last = pl.num_programs(0) - 1
    @pl.when(step == 0)
    def _():
        made_acc[...] = made
        back_acc[...] = back
    @pl.when((step > 0) & (step < last))
    def _():
        made_acc[...] += made
        back_acc[...] += back
    @pl.when(step == last)
    def _():
        made_ref[:, 0] = (made_acc[...] + made).astype(jnp.bfloat16).reshape(owners, capacity, width)
        made_ref[:, 1] = (back_acc[...] + back).astype(jnp.bfloat16).reshape(owners, capacity, width)


def expert_second(rows_in, grad, act, slope, up, down, index, owners, shards, wide, after=()):
    rows, width = rows_in.shape
    hidden = up.shape[2]
    tile = hidden // shards
    fixed = pl.BlockSpec((rows, width), lambda i: (0, 0))
    column = pl.BlockSpec((rows, tile), lambda i: (0, i))
    made_shape = (owners, 2, rows // owners, width)
    return pl.pallas_call(
        second_kernel,
        grid=(shards,),
        in_specs=[fixed, fixed, column, column, pl.BlockSpec((1, width, tile), lambda i: (index, 0, i)), pl.BlockSpec((1, tile, width), lambda i: (index, i, 0))]
        + [pl.BlockSpec(memory_space=pl.ANY)] * len(after),
        out_specs=[pl.BlockSpec(made_shape, lambda i: (0, 0, 0, 0)), pl.BlockSpec((1, width, tile), lambda i: (i, 0, 0))],
        out_shape=[jax.ShapeDtypeStruct(made_shape, jnp.bfloat16), jax.ShapeDtypeStruct((shards, wide, tile), jnp.bfloat16)],
        scratch_shapes=[pltpu.VMEM((width, rows), jnp.bfloat16), pltpu.VMEM((rows, width), jnp.float32), pltpu.VMEM((rows, width), jnp.float32)],
        compiler_params=pltpu.CompilerParams(vmem_limit_bytes=62 << 20),
        name="expert_second",
    )(rows_in, grad, act, slope, up, down, *after)


def spread(row, block):
    return jnp.broadcast_to(row, (128, block)).T


def pick(slots, lane, back_refs):
    picked = None
    for index, back_ref in enumerate(back_refs):
        owners, capacity, width = back_ref.shape
        half = owners * capacity
        hots = []
        for start in range(index * half, (index + 1) * half, 128):
            hit = reduce(jnp.logical_or, [slot == lane + start for slot in slots])
            hots.append(jnp.where(hit, 1.0, 0.0).astype(jnp.bfloat16))
        part = dot_nn(jnp.concatenate(hots, axis=1), back_ref[...].reshape(half, width))
        picked = part if picked is None else picked + part
    return picked


def out_kernel(slots_ref, routes_ref, gates_ref, resid_ref, cot_ref, *refs):
    back_refs, (out_ref, logit_ref) = refs[:-2], refs[-2:]
    block = out_ref.shape[0]
    lane = lax.broadcasted_iota(jnp.int32, (block, 128), 1)
    cot = cot_ref[...].astype(jnp.float32)
    result = resid_ref[...]
    gates, inner = [], []
    for c in range(2):
        slot = spread(slots_ref[c:c + 1, :], block)
        gate = spread(gates_ref[c:c + 1, :], block)[:, 0:1]
        picked = pick([slot], lane, back_refs)
        result = result + gate * picked
        gates.append(gate)
        inner.append(jnp.sum(cot * picked, axis=1, keepdims=True))
    out_ref[...] = result.astype(out_ref.dtype)
    middle = gates[0] * inner[0] + gates[1] * inner[1]
    logit = jnp.zeros((block, 128), jnp.float32)
    for c in range(2):
        route = spread(routes_ref[c:c + 1, :], block)
        logit = logit + jnp.where(route == lane, gates[c] * (inner[c] - middle), 0.0)
    logit_ref[...] = logit.astype(jnp.bfloat16)


def returned_spec(returned, which):
    owners, _, capacity, width = returned.shape
    return pl.BlockSpec((owners, None, capacity, width), lambda i: (0, which, 0, 0))


def combine_out(slots, routes, gates, resid, cot, returned, block=256):
    tokens, width = resid.shape
    small = pl.BlockSpec((2, block), lambda i: (0, i))
    rows = pl.BlockSpec((block, width), lambda i: (i, 0))
    return pl.pallas_call(
        out_kernel,
        grid=(tokens // block,),
        in_specs=[small, small, small, rows, rows] + [returned_spec(part, 0) for part in returned],
        out_specs=[rows, pl.BlockSpec((block, 128), lambda i: (i, 0))],
        out_shape=[jax.ShapeDtypeStruct((tokens, width), jnp.bfloat16), jax.ShapeDtypeStruct((tokens, 128), jnp.bfloat16)],
        compiler_params=pltpu.CompilerParams(vmem_limit_bytes=48 << 20),
        name="combine_out",
    )(slots, routes, gates, resid, cot, *returned)


def back_kernel(slots_ref, logit_ref, router_ref, gain_ref, resid_ref, cot_ref, merge_ref, *refs, eps):
    back_refs, (grad_ref, low_ref, mixed_ref, gain_grad_ref) = refs[:-4], refs[-4:]
    block, _ = grad_ref.shape
    lane = lax.broadcasted_iota(jnp.int32, (block, 128), 1)
    grads = pick([spread(slots_ref[c:c + 1, :], block) for c in range(2)], lane, back_refs)
    grads = grads + dot_nn(logit_ref[...], router_ref[...])
    resid = resid_ref[...]
    inverse = lax.rsqrt(jnp.mean(resid * resid, axis=1, keepdims=True) + eps)
    unit = resid * inverse
    @pl.when(pl.program_id(0) == 0)
    def _():
        gain_grad_ref[...] = jnp.zeros_like(gain_grad_ref)
    gain_grad_ref[...] += jnp.sum(grads * unit, axis=0, keepdims=True)
    scaled = grads * gain_ref[...]
    inner = jnp.mean(scaled * unit, axis=1, keepdims=True)
    total = cot_ref[...].astype(jnp.float32) + inverse * (scaled - unit * inner)
    grad_ref[...] = total
    low = total.astype(jnp.bfloat16)
    low_ref[...] = low
    mixed_ref[...] = dot_nt(low, merge_ref[...]).astype(jnp.bfloat16)


def combine_back(slots, logit, router, gain, resid, cot, merge, returned, eps, block=256):
    tokens, width = resid.shape
    rows = pl.BlockSpec((block, width), lambda i: (i, 0))
    whole = lambda shape: pl.BlockSpec(shape, lambda i: (0, 0))
    low = jax.ShapeDtypeStruct((tokens, width), jnp.bfloat16)
    return pl.pallas_call(
        partial(back_kernel, eps=eps),
        grid=(tokens // block,),
        in_specs=[pl.BlockSpec((2, block), lambda i: (0, i)), pl.BlockSpec((block, 128), lambda i: (i, 0)), whole(router.shape), whole(gain.shape), rows, rows, whole(merge.shape)]
        + [returned_spec(part, 1) for part in returned],
        out_specs=[rows, rows, rows, whole((1, width))],
        out_shape=[jax.ShapeDtypeStruct((tokens, width), jnp.float32), low, low, jax.ShapeDtypeStruct((1, width), jnp.float32)],
        compiler_params=pltpu.CompilerParams(vmem_limit_bytes=48 << 20),
        name="combine_back",
    )(slots, logit, router, gain, resid, cot, merge, *returned)


def near_tiles(near_ref, head, block):
    spread = jnp.broadcast_to(near_ref[0, head:head + 1, :], (block, block))
    spread = pltpu.roll(spread, 0, 1, stride=1, stride_axis=0)
    key_at = lax.broadcasted_iota(jnp.int32, (block, block), 0)
    query_at = lax.broadcasted_iota(jnp.int32, (block, block), 1)
    return (jnp.where(query_at >= key_at, spread, masked_score), jnp.where(query_at < key_at, spread, 0.0), query_at < key_at)


def diagonal_sums(tile):
    block = tile.shape[1]
    total = tile[:8]
    for start in range(8, block, 8):
        total = total + pltpu.roll(tile[start:start + 8], block - start, 1)
    row = lax.broadcasted_iota(jnp.int32, total.shape, 0)
    for step in (1, 2, 4):
        total = jnp.where((row & step) != 0, pltpu.roll(total, block - step, 1), total)
    return jnp.sum(total, axis=0, keepdims=True)


def head_part(rows, head, size):
    lane = lax.broadcasted_iota(jnp.int32, rows.shape, 1)
    return jnp.where((lane >= head * size) & (lane < (head + 1) * size), rows, jnp.zeros_like(rows))


def attend_kernel(query_ref, key_ref, value_ref, near_ref, out_ref, total_ref, *, block, size, scale):
    length, lanes = query_ref.shape
    heads = lanes // size
    count = length // block
    flipped = value_ref[...].T
    tiles = [near_tiles(near_ref, head, block) for head in range(heads)]
    for i in range(count):
        rows = pl.ds(i * block, block)
        query_rows = query_ref[rows, :] * jnp.bfloat16(scale)
        parts = []
        for head in range(heads):
            query_part = head_part(query_rows, head, size)
            scores = []
            for j in range(i + 1):
                tile = dot_nt(key_ref[pl.ds(j * block, block), :], query_part)
                if j == i:
                    tile = tile + tiles[head][0]
                elif j == i - 1:
                    tile = tile + tiles[head][1]
                scores.append(tile)
            top = reduce(jnp.maximum, scores)
            top = jnp.max(top, axis=0, keepdims=True)
            mixed = None
            total = None
            for j in range(i + 1):
                weights = jnp.exp(scores[j] - top)
                sums = jnp.sum(weights, axis=0, keepdims=True)
                part = dot_nn(flipped[head * size:(head + 1) * size, j * block:(j + 1) * block], weights.astype(jnp.bfloat16))
                mixed = part if mixed is None else mixed + part
                total = sums if total is None else total + sums
            parts.append(mixed / total)
            total_ref[0, head:head + 1, rows] = top + jnp.log(total)
        out_ref[rows, :] = jnp.concatenate(parts, axis=0).T.astype(out_ref.dtype)


def attend(queries, keys, values, near, size, block):
    length, width = queries.shape
    lanes = 128
    heads = lanes // size
    groups = width // lanes
    column = pl.BlockSpec((length, lanes), lambda g: (0, g))
    head_rows = pl.BlockSpec((1, heads, block), lambda g: (g, 0, 0))
    return pl.pallas_call(
        partial(attend_kernel, block=block, size=size, scale=size ** -0.5),
        grid=(groups,),
        in_specs=[column, column, column, head_rows],
        out_specs=[column, pl.BlockSpec((1, heads, length), lambda g: (g, 0, 0))],
        out_shape=[jax.ShapeDtypeStruct((length, width), jnp.bfloat16), jax.ShapeDtypeStruct((groups, heads, length), jnp.float32)],
        compiler_params=pltpu.CompilerParams(vmem_limit_bytes=48 << 20),
        name="attend",
    )(queries, keys, values, near)


def attend_back_kernel(query_ref, key_ref, value_ref, grad_ref, out_ref, total_ref, near_ref, grads_ref, dist_ref, key_acc, value_acc, *, block, size, scale):
    length, lanes = query_ref.shape
    heads = lanes // size
    count = length // block
    flipped = key_ref[...].T
    tiles = [near_tiles(near_ref, head, block) for head in range(heads)]
    near_acc = [None] * heads
    far_acc = [None] * heads
    for i in range(count):
        rows = pl.ds(i * block, block)
        query_rows = query_ref[rows, :] * jnp.bfloat16(scale)
        grad_rows = grad_ref[rows, :]
        products = (grad_rows.astype(jnp.float32) * out_ref[rows, :].astype(jnp.float32)).T
        query_parts = [head_part(query_rows, head, size) for head in range(heads)]
        grad_parts = [head_part(grad_rows, head, size) for head in range(heads)]
        inner = [jnp.sum(products[head * size:(head + 1) * size], axis=0, keepdims=True) for head in range(heads)]
        query_stack = jnp.concatenate(query_parts, axis=0)
        grad_stack = jnp.concatenate(grad_parts, axis=0)
        query_grads = [None] * heads
        for j in range(i + 1):
            cols = pl.ds(j * block, block)
            weight_list = []
            score_list = []
            for head in range(heads):
                tile = dot_nt(key_ref[cols, :], query_parts[head])
                if j == i:
                    tile = tile + tiles[head][0]
                elif j == i - 1:
                    tile = tile + tiles[head][1]
                weights = jnp.exp(tile - total_ref[0, head:head + 1, rows])
                grads = dot_nt(value_ref[cols, :], grad_parts[head])
                score_grads = weights * (grads - inner[head])
                low = score_grads.astype(jnp.bfloat16)
                weight_list.append(weights.astype(jnp.bfloat16))
                score_list.append(low)
                part = dot_nn(flipped[head * size:(head + 1) * size, j * block:(j + 1) * block], low)
                query_grads[head] = part if query_grads[head] is None else query_grads[head] + part
                if j == i:
                    near_acc[head] = score_grads if near_acc[head] is None else near_acc[head] + score_grads
                else:
                    far = score_grads
                    if j == i - 1:
                        close = jnp.where(tiles[head][2], score_grads, 0.0)
                        near_acc[head] = near_acc[head] + close
                        far = score_grads - close
                    far = jnp.sum(far, axis=0, keepdims=True)
                    far_acc[head] = far if far_acc[head] is None else far_acc[head] + far
            value_part = dot_nn(jnp.concatenate(weight_list, axis=1), grad_stack)
            key_part = dot_nn(jnp.concatenate(score_list, axis=1), query_stack)
            if j == i:
                value_acc[cols, :] = value_part
                key_acc[cols, :] = key_part
            else:
                value_acc[cols, :] += value_part
                key_acc[cols, :] += key_part
        grads_ref[0, rows, :] = (jnp.concatenate(query_grads, axis=0) * scale).T.astype(grads_ref.dtype)
    grads_ref[1] = key_acc[...].astype(grads_ref.dtype)
    grads_ref[2] = value_acc[...].astype(grads_ref.dtype)
    for head in range(heads):
        dist_ref[0, head:head + 1, :] = diagonal_sums(near_acc[head])
        dist_ref[0, heads + head:heads + head + 1, :] = far_acc[head]


def attend_back(queries, keys, values, grads, outs, totals, near, size, block):
    length, width = queries.shape
    lanes = 128
    heads = lanes // size
    groups = width // lanes
    column = pl.BlockSpec((length, lanes), lambda g: (0, g))
    head_rows = pl.BlockSpec((1, heads, block), lambda g: (g, 0, 0))
    return pl.pallas_call(
        partial(attend_back_kernel, block=block, size=size, scale=size ** -0.5),
        grid=(groups,),
        in_specs=[column] * 5 + [pl.BlockSpec((1, heads, length), lambda g: (g, 0, 0)), head_rows],
        out_specs=[pl.BlockSpec((3, length, lanes), lambda g: (0, 0, g)), pl.BlockSpec((1, 2 * heads, block), lambda g: (g, 0, 0))],
        out_shape=[jax.ShapeDtypeStruct((3, length, width), jnp.bfloat16), jax.ShapeDtypeStruct((groups, 2 * heads, block), jnp.float32)],
        scratch_shapes=[pltpu.VMEM((length, lanes), jnp.float32)] * 2,
        compiler_params=pltpu.CompilerParams(vmem_limit_bytes=56 << 20),
        name="attend_back",
    )(queries, keys, values, grads, outs, totals, near)


def project_kernel(inputs_ref, gain_ref, query_ref, key_ref, value_ref, low_ref, *out_refs, eps):
    rows = inputs_ref[...].astype(jnp.float32)
    inverse = lax.rsqrt(jnp.mean(rows * rows, axis=1, keepdims=True) + eps)
    low = (rows * inverse * gain_ref[...]).astype(jnp.bfloat16)
    low_ref[...] = low
    for weight_ref, out_ref in zip((query_ref, key_ref, value_ref), out_refs):
        out_ref[...] = dot_nn(low, weight_ref[...]).astype(jnp.bfloat16)


def project(inputs, gain, query, key, value, eps, block=256):
    tokens, width = inputs.shape
    rows = pl.BlockSpec((block, width), lambda i: (i, 0))
    whole = lambda shape: pl.BlockSpec(shape, lambda i: (0, 0))
    return pl.pallas_call(
        partial(project_kernel, eps=eps),
        grid=(tokens // block,),
        in_specs=[rows, whole(gain.shape)] + [whole(query.shape)] * 3,
        out_specs=[rows] * 4,
        out_shape=[jax.ShapeDtypeStruct((tokens, width), jnp.bfloat16)] * 4,
        compiler_params=pltpu.CompilerParams(vmem_limit_bytes=40 << 20),
        name="project",
    )(inputs, gain, query, key, value)


def settle_kernel(mixed_ref, merge_ref, inputs_ref, gain_ref, router_ref, routes_ref, resid_ref, low_ref, gates_ref, *, eps):
    resid = inputs_ref[...].astype(jnp.float32) + dot_nn(mixed_ref[...], merge_ref[...])
    resid_ref[...] = resid
    inverse = lax.rsqrt(jnp.mean(resid * resid, axis=1, keepdims=True) + eps)
    low = (resid * inverse * gain_ref[...]).astype(jnp.bfloat16)
    low_ref[...] = low
    logits = dot_nt(router_ref[...], low)
    expert = lax.broadcasted_iota(jnp.int32, logits.shape, 0)
    chosen = [jnp.sum(jnp.where(routes_ref[c:c + 1, :] == expert, logits, 0.0), axis=0, keepdims=True) for c in range(2)]
    top = jnp.maximum(chosen[0], chosen[1])
    powers = [jnp.exp(value - top) for value in chosen]
    total = powers[0] + powers[1]
    for c in range(2):
        gates_ref[c:c + 1, :] = powers[c] / total


def settle(mixed, merge, inputs, gain, router, routes, eps, block=256):
    tokens, width = inputs.shape
    rows = pl.BlockSpec((block, width), lambda i: (i, 0))
    whole = lambda shape: pl.BlockSpec(shape, lambda i: (0, 0))
    small = pl.BlockSpec((2, block), lambda i: (0, i))
    return pl.pallas_call(
        partial(settle_kernel, eps=eps),
        grid=(tokens // block,),
        in_specs=[rows, whole(merge.shape), rows, whole(gain.shape), whole(router.shape), small],
        out_specs=[rows, rows, small],
        out_shape=[jax.ShapeDtypeStruct((tokens, width), jnp.float32), jax.ShapeDtypeStruct((tokens, width), jnp.bfloat16), jax.ShapeDtypeStruct((2, tokens), jnp.float32)],
        compiler_params=pltpu.CompilerParams(vmem_limit_bytes=40 << 20),
        name="settle",
    )(mixed, merge, inputs, gain, router, routes)


def finish_kernel(heads_ref, query_ref, key_ref, value_ref, gain_ref, inputs_ref, resid_grad_ref, out_ref, gain_grad_ref, *, eps):
    grads = dot_nt(heads_ref[0], query_ref[...]) + dot_nt(heads_ref[1], key_ref[...]) + dot_nt(heads_ref[2], value_ref[...])
    rows = inputs_ref[...].astype(jnp.float32)
    inverse = lax.rsqrt(jnp.mean(rows * rows, axis=1, keepdims=True) + eps)
    unit = rows * inverse
    @pl.when(pl.program_id(0) == 0)
    def _():
        gain_grad_ref[...] = jnp.zeros_like(gain_grad_ref)
    gain_grad_ref[...] += jnp.sum(grads * unit, axis=0, keepdims=True)
    scaled = grads * gain_ref[...]
    inner = jnp.mean(scaled * unit, axis=1, keepdims=True)
    out_ref[...] = resid_grad_ref[...] + inverse * (scaled - unit * inner)


def finish(head_grads, query, key, value, gain, inputs, resid_grad, eps, block=256):
    tokens, width = inputs.shape
    rows = pl.BlockSpec((block, width), lambda i: (i, 0))
    whole = lambda shape: pl.BlockSpec(shape, lambda i: (0, 0))
    return pl.pallas_call(
        partial(finish_kernel, eps=eps),
        grid=(tokens // block,),
        in_specs=[pl.BlockSpec((3, block, width), lambda i: (0, i, 0))] + [whole(query.shape)] * 3 + [whole(gain.shape), rows, rows],
        out_specs=[rows, whole((1, width))],
        out_shape=[jax.ShapeDtypeStruct((tokens, width), jnp.float32), jax.ShapeDtypeStruct((1, width), jnp.float32)],
        compiler_params=pltpu.CompilerParams(vmem_limit_bytes=40 << 20),
        name="finish",
    )(head_grads, query, key, value, gain, inputs, resid_grad)


def weight_kernel(left_ref, right_ref, out_ref, turned):
    shards, part, _ = out_ref.shape
    @pl.when(pl.program_id(0) == 0)
    def _():
        turned[...] = left_ref[...].T
    right = right_ref[...]
    for shard in range(shards):
        grad = dot_nn(turned[shard * part:(shard + 1) * part, :], right)
        out_ref[shard] = grad.astype(jnp.bfloat16)


def weight_grads(left, right, shards):
    count, tokens, width = right.shape
    part = width // shards
    return pl.pallas_call(
        weight_kernel,
        grid=(count,),
        in_specs=[pl.BlockSpec((tokens, width), lambda i: (0, 0)), pl.BlockSpec((None, tokens, width), lambda i: (i, 0, 0))],
        out_specs=pl.BlockSpec((shards, part, width), lambda i: (0, i, 0)),
        out_shape=jax.ShapeDtypeStruct((shards, count * part, width), jnp.bfloat16),
        scratch_shapes=[pltpu.VMEM((width, tokens), jnp.bfloat16)],
        compiler_params=pltpu.CompilerParams(vmem_limit_bytes=40 << 20),
        name="weight_grads",
    )(left, right)


def exchange(rows, bit):
    count = lax.axis_size("expert")
    return lax.ppermute(rows, "expert", [(i, i ^ bit) for i in range(count)])


def shift(rows, step):
    count = lax.axis_size("shard")
    return lax.ppermute(rows, "shard", [(i, (i + step) % count) for i in range(count)])


def gather_line(rows):
    count = lax.axis_size("shard")
    me = lax.axis_index("shard")
    out = jnp.zeros((count,) + rows.shape, rows.dtype)
    out = lax.dynamic_update_index_in_dim(out, rows, me, 0)
    for step in range(1, count):
        out = lax.dynamic_update_index_in_dim(out, shift(rows, step), (me - step) % count, 0)
    return out


def add_low(left, right):
    return (left.astype(jnp.float32) + right.astype(jnp.float32)).astype(jnp.bfloat16)


def reduce_stack(stack, bits):
    me = lax.axis_index("expert")
    for bit in bits:
        half = stack.shape[1] // 2
        side = (me // bit) % 2
        keep = lax.dynamic_slice_in_dim(stack, side * half, half, 1)
        send = lax.dynamic_slice_in_dim(stack, (1 - side) * half, half, 1)
        got = exchange(send, bit)
        stack = add_low(keep, got)
    count = lax.axis_size("shard")
    place = lax.axis_index("shard")
    total = lax.dynamic_index_in_dim(stack, place, 0, False).astype(jnp.float32)
    for step in range(1, count):
        send = lax.dynamic_index_in_dim(stack, (place + step) % count, 0, False)
        total = total + shift(send, step).astype(jnp.float32)
    piece = total.astype(jnp.bfloat16)
    for bit in reversed(bits):
        other = exchange(piece, bit)
        side = (me // bit) % 2
        piece = jnp.where(
            side == 0, jnp.concatenate([piece, other]), jnp.concatenate([other, piece])
        )
    return piece


def scatter_sum(grads):
    shards, rows, width = grads.shape
    grads = grads.reshape(shards * rows, width)
    return lax.psum_scatter(grads, "shard", scatter_dimension=0, tiled=True)


def share_rows(rows):
    return lax.all_to_all(rows, "expert", 0, 0, tiled=True)


def local(
    inputs,
    norm_gain,
    query_weight,
    key_weight,
    value_weight,
    merge_weight,
    bias_table,
    expert_gain,
    router_weight,
    up_weight,
    down_weight,
    routes,
    cotangent,
):
    f32, bf16 = jnp.float32, jnp.bfloat16
    tokens, width = inputs.shape
    owners = lax.axis_size("expert")
    shards = lax.axis_size("shard")
    me = lax.axis_index("expert")
    part = query_weight.shape[0]
    piece = part // owners
    local_heads = bias_table.shape[1]
    heads = local_heads * shards
    size = width // heads
    experts = router_weight.shape[1]
    local_count, _, hidden = up_weight.shape
    capacity = (5 * tokens * routes.shape[1] + 4 * experts - 1) // (4 * experts)
    capacity = -(-capacity // 16) * 16
    rows = owners * capacity
    assert local_count == 2 and hidden // shards == width

    small_rows = 8 * owners
    router_at = 2 + local_heads + (-(2 + local_heads)) % 8

    def widen(block):
        return jnp.pad(block, ((0, 0), (0, width - block.shape[1])))

    def pack(gain_one, gain_two, table, router):
        head = jnp.concatenate([gain_one, gain_two], axis=0)
        gap = jnp.zeros((router_at - 2 - local_heads, width), bf16)
        rest = jnp.zeros((small_rows - router_at - experts, width), bf16)
        return jnp.concatenate([widen(head), widen(table), gap, widen(router), rest], axis=0)

    small = pack(norm_gain[None], expert_gain[None], bias_table.T, router_weight.T)
    slices = [
        lax.dynamic_slice_in_dim(weight, me * piece, piece, 0)
        for weight in (query_weight, key_weight, value_weight)
    ] + [lax.dynamic_slice_in_dim(small, me * 8, 8, 0)]
    lined = gather_line(jnp.concatenate(slices))
    gathered = lax.all_gather(lined, "expert", axis=0, tiled=False)
    merge_full = lax.all_gather(merge_weight, "shard", axis=0, tiled=True)

    def whole_weight(index):
        block = gathered[:, :, index * piece : (index + 1) * piece]
        return block.transpose(1, 0, 2, 3).reshape(width, width)

    query_full, key_full, value_full = (whole_weight(index) for index in range(3))
    small_full = gathered[:, :, 3 * piece :].transpose(1, 0, 2, 3).reshape(shards, small_rows, width)
    gain_one = small_full[:, 0, :part].reshape(1, width).astype(f32)
    gain_two = small_full[:, 1, :part].reshape(1, width).astype(f32)
    table_full = small_full[:, 2 : 2 + local_heads, :BUCKETS].reshape(heads, BUCKETS).astype(f32)
    router_full = small_full[:, router_at : router_at + experts, :part]
    router_full = router_full.transpose(1, 0, 2).reshape(experts, width)

    routes_line = routes.T
    base = (routes_line % local_count * owners + routes_line // local_count) * capacity
    slots = find_slots(routes_line, base, experts)
    cot_rows, other = dispatch_all(
        slots, routes_line.astype(f32), cotangent, owners, capacity, local_count
    )
    other = share_rows(other).reshape(owners, local_count, capacity)

    low_one, queries, keys, values = project(
        inputs, gain_one, query_full, key_full, value_full, epsilon
    )
    cot_in = share_rows(cot_rows).reshape(owners, local_count, capacity, width)
    block = 256
    hot = bucket_hot(tokens)
    assert hot[block:, -1].all()
    near_hot = jnp.asarray((hot[:block] - hot[-1:]).T, dtype=f32)
    group = 128 // size
    near = jnp.dot(table_full, near_hot, precision=lax.Precision.HIGHEST)
    near = near.reshape(heads // group, group, block)
    attended, totals = attend(queries, keys, values, near, size, block)
    resid, low_two, gates = settle(
        attended, merge_full, inputs, gain_two, router_full, routes_line, epsilon
    )

    owner = me.astype(jnp.int32).reshape(1)
    sends, rows_in = [], []
    for index in range(local_count):
        sends.append(dispatch(slots, low_two, index * rows, rows))
        send = share_rows(sends[index].reshape(owners, capacity, width))
        rows_in.append(send.reshape(rows, width))
    others = [other[:, index].reshape(1, rows) for index in range(local_count)]
    act, slope, first_down, grad_in = expert_first(
        owner, rows_in[0], cot_in, others[0], router_full, up_weight, 0, local_count, shards,
        after=(sends[1],),
    )
    first_sum = scatter_sum(first_down)
    first_made, pair = expert_second(
        rows_in[0], grad_in, act, slope, up_weight, down_weight, 0, owners, shards, 2 * width
    )
    act, slope, pair, grad_in = expert_first(
        owner, rows_in[1], cot_in, others[1], router_full, up_weight, 1, local_count, shards,
        into=pair,
    )
    pair_sum = scatter_sum(pair)
    second_made, last_up = expert_second(
        rows_in[1], grad_in, act, slope, up_weight, down_weight, 1, owners, shards, width
    )
    last_sum = scatter_sum(last_up)
    returned = []
    for made in (first_made, second_made):
        returned.append(share_rows(made))
    output, logit_grad = combine_out(slots, routes_line, gates, resid, cotangent, returned)
    router_wide = jnp.pad(router_full, ((0, 128 - experts), (0, 0)))
    resid_grad, branch, mixed_grad, gain_grad = combine_back(
        slots, logit_grad, router_wide, gain_two, resid, cotangent, merge_full, returned, epsilon
    )
    router_grad = jnp.einsum("te,ti->ei", logit_grad, low_two, preferred_element_type=f32)
    merge_grad = weight_grads(attended, branch[None], shards)
    head_grads, distances = attend_back(
        queries, keys, values, mixed_grad, attended, totals, near, size, block
    )
    close_sums = distances[:, :group].reshape(heads, block)
    far_sums = jnp.sum(distances[:, group:].reshape(heads, block), axis=1)
    table_grad = jnp.dot(close_sums, jnp.asarray(hot[:block]), precision=lax.Precision.HIGHEST)
    table_grad = table_grad + far_sums[:, None] * jnp.asarray(hot[-1:])
    head_sums = weight_grads(low_one, head_grads, shards)
    input_gradient, norm_grad = finish(
        head_grads, query_full, key_full, value_full, gain_one, inputs, resid_grad, epsilon
    )
    small_grad = jax.vmap(pack)(
        norm_grad.reshape(shards, 1, part).astype(bf16),
        gain_grad.reshape(shards, 1, part).astype(bf16),
        table_grad.reshape(shards, local_heads, BUCKETS).astype(bf16),
        router_grad[:experts].reshape(experts, shards, part).transpose(1, 0, 2).astype(bf16),
    )
    bits = [1 << level for level in range(owners.bit_length() - 1)]
    head_sums = reduce_stack(head_sums, bits).astype(f32)
    rest_sums = jnp.concatenate([merge_grad, small_grad], axis=1)
    rest_sums = reduce_stack(rest_sums, bits[:1] + bits[:0:-1]).astype(f32)
    small_sum = rest_sums[part:]
    return (
        output,
        input_gradient,
        small_sum[0, :part],
        head_sums[:part],
        head_sums[part : 2 * part],
        head_sums[2 * part :],
        rest_sums[:part],
        small_sum[2 : 2 + local_heads, :BUCKETS].T,
        small_sum[1, :part],
        small_sum[router_at : router_at + experts, :part].T,
        jnp.stack([pair_sum[:width].astype(f32), last_sum.astype(f32)]),
        jnp.stack([first_sum.astype(f32), pair_sum[width:].astype(f32)]),
    )


def solution(mesh):
    in_specs = (
        P(("expert", "shard"), None),
        P("shard"),
        P("shard", None),
        P("shard", None),
        P("shard", None),
        P("shard", None),
        P(None, "shard"),
        P("shard"),
        P("shard", None),
        P("expert", None, None),
        P("expert", None, None),
        P(("expert", "shard"), None),
        P(("expert", "shard"), None),
    )
    out_specs = (
        P(("expert", "shard"), None),
        P(("expert", "shard"), None),
        P("shard"),
        P("shard", None),
        P("shard", None),
        P("shard", None),
        P("shard", None),
        P(None, "shard"),
        P("shard"),
        P("shard", None),
        P("expert", None, "shard"),
        P("expert", "shard", None),
    )
    return jax.shard_map(local, mesh=mesh, in_specs=in_specs, out_specs=out_specs, check_vma=False)
```

```python
from functools import partial, reduce

import jax
import jax.numpy as jnp
import numpy as np
from jax import lax
from jax.experimental import pallas as pl
from jax.experimental.pallas import tpu as pltpu
from jax.sharding import PartitionSpec as P


BUCKETS = 32
MAX_DIST = 128


epsilon = 1e-06
masked_score = -1e30


def bucket_hot(length):
    distance = np.arange(length)
    half_count = BUCKETS // 2
    clipped = np.maximum(distance, half_count)
    spread = np.log(clipped / half_count) / np.log(MAX_DIST / half_count) * (BUCKETS - half_count)
    far_bucket = np.minimum(half_count + np.floor(spread).astype(np.int32), BUCKETS - 1)
    bucket = np.where(distance < half_count, distance, far_bucket)
    return (bucket[:, None] == np.arange(BUCKETS)[None, :]).astype(np.float32)


def dot_nt(a, b):
    return lax.dot_general(a, b, (((1,), (1,)), ((), ())), preferred_element_type=jnp.float32)


def dot_nn(a, b):
    return lax.dot_general(a, b, (((1,), (0,)), ((), ())), preferred_element_type=jnp.float32)


def dot_tn(a, b):
    return lax.dot_general(a, b, (((0,), (0,)), ((), ())), preferred_element_type=jnp.float32)


def slot_kernel(routes_ref, base_ref, slots_ref, *, experts):
    tokens = routes_ref.shape[1]
    expert = lax.broadcasted_iota(jnp.int32, (experts, tokens), 0)
    hits = [routes_ref[c:c + 1, :] == expert for c in range(2)]
    hot = jnp.where(hits[0] | hits[1], 1.0, 0.0).astype(jnp.bfloat16)
    earlier = lax.broadcasted_iota(jnp.int32, (tokens, tokens), 0)
    later = lax.broadcasted_iota(jnp.int32, (tokens, tokens), 1)
    before = jnp.where(earlier < later, 1.0, 0.0).astype(jnp.bfloat16)
    counts = dot_nn(hot, before)
    for c in range(2):
        position = jnp.sum(jnp.where(hits[c], counts, 0.0), axis=0, keepdims=True)
        slots_ref[c:c + 1, :] = base_ref[c:c + 1, :] + position.astype(jnp.int32)


def find_slots(routes, base, experts):
    return pl.pallas_call(
        partial(slot_kernel, experts=experts),
        out_shape=jax.ShapeDtypeStruct(routes.shape, jnp.int32),
        name="find_slots",
    )(routes, base)


def dispatch_kernel(slots_ref, rows_ref, *refs, start):
    out_ref = refs[-1]
    block, tokens = out_ref.shape[0], rows_ref.shape[0]
    slot = lax.broadcasted_iota(jnp.int32, (block, tokens), 0) + (pl.program_id(0) * block + start)
    hot = jnp.where((slot == slots_ref[0:1, :]) | (slot == slots_ref[1:2, :]), 1.0, 0.0)
    out_ref[...] = dot_nn(hot.astype(jnp.bfloat16), rows_ref[...]).astype(out_ref.dtype)


def dispatch(slots, rows, start, count, after=(), block=256):
    _, width = rows.shape
    whole = lambda shape: pl.BlockSpec(shape, lambda i: (0, 0))
    return pl.pallas_call(
        partial(dispatch_kernel, start=start),
        grid=(count // block,),
        in_specs=[whole(slots.shape), whole(rows.shape)] + [pl.BlockSpec(memory_space=pl.ANY)] * len(after),
        out_specs=pl.BlockSpec((block, width), lambda i: (i, 0)),
        out_shape=jax.ShapeDtypeStruct((count, width), rows.dtype),
        name="dispatch",
    )(slots, rows, *after)


def dispatch_all_kernel(slots_ref, routes_ref, rows_ref, *refs, owners, capacity):
    out_refs, other_ref = refs[:-1], refs[-1]
    block, tokens = len(out_refs) * capacity, rows_ref.shape[0]
    row = lax.broadcasted_iota(jnp.int32, (block, tokens), 0)
    slot = row + pl.program_id(0) * capacity
    for index in range(1, block // capacity):
        slot = slot + jnp.where(row >= index * capacity, (owners - 1) * capacity, 0)
    hits = [slot == slots_ref[c:c + 1, :] for c in range(2)]
    hot = jnp.where(hits[0] | hits[1], 1.0, 0.0).astype(jnp.bfloat16)
    picked = dot_nn(hot, rows_ref[...]).astype(rows_ref.dtype)
    for index, out_ref in enumerate(out_refs):
        out_ref[0] = picked[index * capacity:(index + 1) * capacity]
    other = jnp.where(hits[0], routes_ref[1:2, :], jnp.where(hits[1], routes_ref[0:1, :], 0.0))
    column = jnp.sum(other, axis=1, keepdims=True)
    other_ref[0] = jnp.broadcast_to(column, (block, 128)).T[0:1, :]


def dispatch_all(slots, routes, rows, owners, capacity, local_count):
    _, width = rows.shape
    block = local_count * capacity
    whole = lambda shape: pl.BlockSpec(shape, lambda i: (0, 0))
    return pl.pallas_call(
        partial(dispatch_all_kernel, owners=owners, capacity=capacity),
        grid=(owners,),
        in_specs=[whole(slots.shape), whole(routes.shape), whole(rows.shape)],
        out_specs=[pl.BlockSpec((1, capacity, width), lambda i: (i, 0, 0))] * local_count + [pl.BlockSpec((1, 1, block), lambda i: (i, 0, 0))],
        out_shape=[jax.ShapeDtypeStruct((owners, capacity, width), rows.dtype)] * local_count + [jax.ShapeDtypeStruct((owners, 1, block), jnp.float32)],
        name="dispatch_all",
    )(slots, routes, rows)


def gelu_pair(v):
    c = np.float32(np.sqrt(2.0 / np.pi))
    a = np.float32(0.044715)
    square = v * v
    half = 0.5 * jnp.tanh(v * (c * a * square + c)) + 0.5
    value = v * half
    slope = half + value * (1.0 - half) * (6.0 * c * a * square + 2.0 * c)
    return value, slope


def first_kernel(owner_ref, rows_ref, cot_ref, other_ref, router_ref, up_ref, *refs, chunk, index, local_count):
    act_ref, slope_ref, down_grad_ref, grad_ref = refs[-4:]
    rows, width = rows_ref.shape
    @pl.when(pl.program_id(0) == 0)
    def _():
        logits = dot_nt(router_ref[...], rows_ref[...])
        expert = lax.broadcasted_iota(jnp.int32, logits.shape, 0)
        mine = owner_ref[0] * local_count + index
        own = jnp.sum(jnp.where(expert == mine, logits, 0.0), axis=0, keepdims=True)
        other = other_ref[...].astype(jnp.int32)
        other = jnp.sum(jnp.where(expert == other, logits, 0.0), axis=0, keepdims=True)
        top = jnp.maximum(own, other)
        own = jnp.exp(own - top)
        gate = own / (own + jnp.exp(other - top))
        column = jnp.broadcast_to(gate, (128, rows)).T
        for start in range(0, width, 128):
            part = cot_ref[:, start:start + 128].astype(jnp.float32) * column
            grad_ref[:, start:start + 128] = part.astype(jnp.bfloat16)
    up = up_ref[0]
    for start in range(0, rows, chunk):
        pre = dot_nn(rows_ref[start:start + chunk, :], up)
        value, slope = gelu_pair(pre)
        act_ref[start:start + chunk, :] = value.astype(jnp.bfloat16)
        slope_ref[start:start + chunk, :] = slope.astype(jnp.bfloat16)
    down_grad_ref[0] = dot_tn(act_ref[...], grad_ref[...]).astype(jnp.bfloat16)


def expert_first(owner, rows_in, cot, other, router, up, index, local_count, shards, into=None, after=(), chunk=640):
    rows, width = rows_in.shape
    hidden = up.shape[2]
    tile = hidden // shards
    fixed = pl.BlockSpec((rows, width), lambda i: (0, 0))
    column = pl.BlockSpec((rows, tile), lambda i: (0, i))
    chunk = chunk if rows % chunk == 0 else rows // 2
    operands = [owner, rows_in, cot, other, router, up]
    place, aliases = 0, {}
    grad_shape = jax.ShapeDtypeStruct((shards, tile, width), jnp.bfloat16)
    if into is not None:
        aliases = {len(operands): 2}
        operands.append(into)
        place, grad_shape = 1, jax.ShapeDtypeStruct(into.shape, into.dtype)
    operands += list(after)
    return pl.pallas_call(
        partial(first_kernel, chunk=chunk, index=index, local_count=local_count),
        grid=(shards,),
        in_specs=[
            pl.BlockSpec(memory_space=pltpu.SMEM),
            fixed,
            fixed,
            pl.BlockSpec((1, rows), lambda i: (0, 0)),
            pl.BlockSpec(router.shape, lambda i: (0, 0)),
            pl.BlockSpec((1, width, tile), lambda i: (index, 0, i)),
        ]
        + [pl.BlockSpec(memory_space=pl.ANY)] * (len(operands) - 6),
        out_specs=[column, column, pl.BlockSpec((1, tile, width), lambda i: (i, place, 0)), fixed],
        out_shape=[jax.ShapeDtypeStruct((rows, hidden), jnp.bfloat16)] * 2 + [grad_shape, jax.ShapeDtypeStruct((rows, width), jnp.bfloat16)],
        input_output_aliases=aliases,
        compiler_params=pltpu.CompilerParams(vmem_limit_bytes=62 << 20),
        name="expert_first",
    )(*operands)


def second_kernel(rows_ref, grad_ref, act_ref, slope_ref, up_ref, down_ref, *refs):
    made_ref, up_grad_ref, turned, made_acc, back_acc = refs[-5:]
    step = pl.program_id(0)
    owners, _, capacity, width = made_ref.shape
    @pl.when(step == 0)
    def _():
        turned[...] = rows_ref[...].T
    up = up_ref[0]
    down = down_ref[0]
    grads = dot_nt(grad_ref[...], down)
    low = (slope_ref[...].astype(jnp.float32) * grads).astype(jnp.bfloat16)
    up_grad_ref[0] = dot_nn(turned[...], low).astype(jnp.bfloat16)
    back = dot_nt(low, up)
    made = dot_nn(act_ref[...], down)
    last = pl.num_programs(0) - 1
    @pl.when(step == 0)
    def _():
        made_acc[...] = made
        back_acc[...] = back
    @pl.when((step > 0) & (step < last))
    def _():
        made_acc[...] += made
        back_acc[...] += back
    @pl.when(step == last)
    def _():
        made_ref[:, 0] = (made_acc[...] + made).astype(jnp.bfloat16).reshape(owners, capacity, width)
        made_ref[:, 1] = (back_acc[...] + back).astype(jnp.bfloat16).reshape(owners, capacity, width)


def expert_second(rows_in, grad, act, slope, up, down, index, owners, shards, wide, after=()):
    rows, width = rows_in.shape
    hidden = up.shape[2]
    tile = hidden // shards
    fixed = pl.BlockSpec((rows, width), lambda i: (0, 0))
    column = pl.BlockSpec((rows, tile), lambda i: (0, i))
    made_shape = (owners, 2, rows // owners, width)
    return pl.pallas_call(
        second_kernel,
        grid=(shards,),
        in_specs=[fixed, fixed, column, column, pl.BlockSpec((1, width, tile), lambda i: (index, 0, i)), pl.BlockSpec((1, tile, width), lambda i: (index, i, 0))]
        + [pl.BlockSpec(memory_space=pl.ANY)] * len(after),
        out_specs=[pl.BlockSpec(made_shape, lambda i: (0, 0, 0, 0)), pl.BlockSpec((1, width, tile), lambda i: (i, 0, 0))],
        out_shape=[jax.ShapeDtypeStruct(made_shape, jnp.bfloat16), jax.ShapeDtypeStruct((shards, wide, tile), jnp.bfloat16)],
        scratch_shapes=[pltpu.VMEM((width, rows), jnp.bfloat16), pltpu.VMEM((rows, width), jnp.float32), pltpu.VMEM((rows, width), jnp.float32)],
        compiler_params=pltpu.CompilerParams(vmem_limit_bytes=62 << 20),
        name="expert_second",
    )(rows_in, grad, act, slope, up, down, *after)


def spread(row, block):
    return jnp.broadcast_to(row, (128, block)).T


def pick(slots, lane, back_refs):
    picked = None
    for index, back_ref in enumerate(back_refs):
        owners, capacity, width = back_ref.shape
        half = owners * capacity
        hots = []
        for start in range(index * half, (index + 1) * half, 128):
            hit = reduce(jnp.logical_or, [slot == lane + start for slot in slots])
            hots.append(jnp.where(hit, 1.0, 0.0).astype(jnp.bfloat16))
        part = dot_nn(jnp.concatenate(hots, axis=1), back_ref[...].reshape(half, width))
        picked = part if picked is None else picked + part
    return picked


def out_kernel(slots_ref, routes_ref, gates_ref, resid_ref, cot_ref, *refs):
    back_refs, (out_ref, logit_ref) = refs[:-2], refs[-2:]
    block = out_ref.shape[0]
    lane = lax.broadcasted_iota(jnp.int32, (block, 128), 1)
    cot = cot_ref[...].astype(jnp.float32)
    result = resid_ref[...]
    gates, inner = [], []
    for c in range(2):
        slot = spread(slots_ref[c:c + 1, :], block)
        gate = spread(gates_ref[c:c + 1, :], block)[:, 0:1]
        picked = pick([slot], lane, back_refs)
        result = result + gate * picked
        gates.append(gate)
        inner.append(jnp.sum(cot * picked, axis=1, keepdims=True))
    out_ref[...] = result.astype(out_ref.dtype)
    middle = gates[0] * inner[0] + gates[1] * inner[1]
    logit = jnp.zeros((block, 128), jnp.float32)
    for c in range(2):
        route = spread(routes_ref[c:c + 1, :], block)
        logit = logit + jnp.where(route == lane, gates[c] * (inner[c] - middle), 0.0)
    logit_ref[...] = logit.astype(jnp.bfloat16)


def returned_spec(returned, which):
    owners, _, capacity, width = returned.shape
    return pl.BlockSpec((owners, None, capacity, width), lambda i: (0, which, 0, 0))


def combine_out(slots, routes, gates, resid, cot, returned, block=256):
    tokens, width = resid.shape
    small = pl.BlockSpec((2, block), lambda i: (0, i))
    rows = pl.BlockSpec((block, width), lambda i: (i, 0))
    return pl.pallas_call(
        out_kernel,
        grid=(tokens // block,),
        in_specs=[small, small, small, rows, rows] + [returned_spec(part, 0) for part in returned],
        out_specs=[rows, pl.BlockSpec((block, 128), lambda i: (i, 0))],
        out_shape=[jax.ShapeDtypeStruct((tokens, width), jnp.bfloat16), jax.ShapeDtypeStruct((tokens, 128), jnp.bfloat16)],
        compiler_params=pltpu.CompilerParams(vmem_limit_bytes=62 << 20),
        name="combine_out",
    )(slots, routes, gates, resid, cot, *returned)


def back_kernel(slots_ref, logit_ref, router_ref, gain_ref, resid_ref, cot_ref, merge_ref, *refs, eps):
    back_refs, (grad_ref, low_ref, mixed_ref, gain_grad_ref) = refs[:-4], refs[-4:]
    block, _ = grad_ref.shape
    lane = lax.broadcasted_iota(jnp.int32, (block, 128), 1)
    grads = pick([spread(slots_ref[c:c + 1, :], block) for c in range(2)], lane, back_refs)
    grads = grads + dot_nn(logit_ref[...], router_ref[...])
    resid = resid_ref[...]
    inverse = lax.rsqrt(jnp.mean(resid * resid, axis=1, keepdims=True) + eps)
    unit = resid * inverse
    @pl.when(pl.program_id(0) == 0)
    def _():
        gain_grad_ref[...] = jnp.zeros_like(gain_grad_ref)
    gain_grad_ref[...] += jnp.sum(grads * unit, axis=0, keepdims=True)
    scaled = grads * gain_ref[...]
    inner = jnp.mean(scaled * unit, axis=1, keepdims=True)
    total = cot_ref[...].astype(jnp.float32) + inverse * (scaled - unit * inner)
    grad_ref[...] = total
    low = total.astype(jnp.bfloat16)
    low_ref[...] = low
    mixed_ref[...] = dot_nt(low, merge_ref[...]).astype(jnp.bfloat16)


def combine_back(slots, logit, router, gain, resid, cot, merge, returned, eps, block=256):
    tokens, width = resid.shape
    rows = pl.BlockSpec((block, width), lambda i: (i, 0))
    whole = lambda shape: pl.BlockSpec(shape, lambda i: (0, 0))
    low = jax.ShapeDtypeStruct((tokens, width), jnp.bfloat16)
    return pl.pallas_call(
        partial(back_kernel, eps=eps),
        grid=(tokens // block,),
        in_specs=[pl.BlockSpec((2, block), lambda i: (0, i)), pl.BlockSpec((block, 128), lambda i: (i, 0)), whole(router.shape), whole(gain.shape), rows, rows, whole(merge.shape)]
        + [returned_spec(part, 1) for part in returned],
        out_specs=[rows, rows, rows, whole((1, width))],
        out_shape=[jax.ShapeDtypeStruct((tokens, width), jnp.float32), low, low, jax.ShapeDtypeStruct((1, width), jnp.float32)],
        compiler_params=pltpu.CompilerParams(vmem_limit_bytes=62 << 20),
        name="combine_back",
    )(slots, logit, router, gain, resid, cot, merge, *returned)


def near_tiles(near_ref, head, block):
    spread = jnp.broadcast_to(near_ref[0, head:head + 1, :], (block, block))
    spread = pltpu.roll(spread, 0, 1, stride=1, stride_axis=0)
    key_at = lax.broadcasted_iota(jnp.int32, (block, block), 0)
    query_at = lax.broadcasted_iota(jnp.int32, (block, block), 1)
    return (jnp.where(query_at >= key_at, spread, masked_score), jnp.where(query_at < key_at, spread, 0.0), query_at < key_at)


def diagonal_sums(tile):
    block = tile.shape[1]
    total = tile[:8]
    for start in range(8, block, 8):
        total = total + pltpu.roll(tile[start:start + 8], block - start, 1)
    row = lax.broadcasted_iota(jnp.int32, total.shape, 0)
    for step in (1, 2, 4):
        total = jnp.where((row & step) != 0, pltpu.roll(total, block - step, 1), total)
    return jnp.sum(total, axis=0, keepdims=True)


def head_part(rows, head, size):
    lane = lax.broadcasted_iota(jnp.int32, rows.shape, 1)
    return jnp.where((lane >= head * size) & (lane < (head + 1) * size), rows, jnp.zeros_like(rows))


def attend_kernel(query_ref, key_ref, value_ref, near_ref, out_ref, total_ref, *, block, size, scale):
    length, lanes = query_ref.shape
    heads = lanes // size
    count = length // block
    flipped = value_ref[...].T
    tiles = [near_tiles(near_ref, head, block) for head in range(heads)]
    for i in range(count):
        rows = pl.ds(i * block, block)
        query_rows = query_ref[rows, :] * jnp.bfloat16(scale)
        parts = []
        for head in range(heads):
            query_part = head_part(query_rows, head, size)
            scores = []
            for j in range(i + 1):
                tile = dot_nt(key_ref[pl.ds(j * block, block), :], query_part)
                if j == i:
                    tile = tile + tiles[head][0]
                elif j == i - 1:
                    tile = tile + tiles[head][1]
                scores.append(tile)
            top = reduce(jnp.maximum, scores)
            top = jnp.max(top, axis=0, keepdims=True)
            mixed = None
            total = None
            for j in range(i + 1):
                weights = jnp.exp(scores[j] - top)
                sums = jnp.sum(weights, axis=0, keepdims=True)
                part = dot_nn(flipped[head * size:(head + 1) * size, j * block:(j + 1) * block], weights.astype(jnp.bfloat16))
                mixed = part if mixed is None else mixed + part
                total = sums if total is None else total + sums
            parts.append(mixed / total)
            total_ref[0, head:head + 1, rows] = top + jnp.log(total)
        out_ref[rows, :] = jnp.concatenate(parts, axis=0).T.astype(out_ref.dtype)


def attend(queries, keys, values, near, size, block):
    length, width = queries.shape
    lanes = 128
    heads = lanes // size
    groups = width // lanes
    column = pl.BlockSpec((length, lanes), lambda g: (0, g))
    head_rows = pl.BlockSpec((1, heads, block), lambda g: (g, 0, 0))
    return pl.pallas_call(
        partial(attend_kernel, block=block, size=size, scale=size ** -0.5),
        grid=(groups,),
        in_specs=[column, column, column, head_rows],
        out_specs=[column, pl.BlockSpec((1, heads, length), lambda g: (g, 0, 0))],
        out_shape=[jax.ShapeDtypeStruct((length, width), jnp.bfloat16), jax.ShapeDtypeStruct((groups, heads, length), jnp.float32)],
        compiler_params=pltpu.CompilerParams(vmem_limit_bytes=62 << 20),
        name="attend",
    )(queries, keys, values, near)


def attend_back_kernel(query_ref, key_ref, value_ref, grad_ref, out_ref, total_ref, near_ref, grads_ref, dist_ref, key_acc, value_acc, *, block, size, scale):
    length, lanes = query_ref.shape
    heads = lanes // size
    count = length // block
    flipped = key_ref[...].T
    tiles = [near_tiles(near_ref, head, block) for head in range(heads)]
    near_acc = [None] * heads
    far_acc = [None] * heads
    for i in range(count):
        rows = pl.ds(i * block, block)
        query_rows = query_ref[rows, :] * jnp.bfloat16(scale)
        grad_rows = grad_ref[rows, :]
        products = (grad_rows.astype(jnp.float32) * out_ref[rows, :].astype(jnp.float32)).T
        query_parts = [head_part(query_rows, head, size) for head in range(heads)]
        grad_parts = [head_part(grad_rows, head, size) for head in range(heads)]
        inner = [jnp.sum(products[head * size:(head + 1) * size], axis=0, keepdims=True) for head in range(heads)]
        query_stack = jnp.concatenate(query_parts, axis=0)
        grad_stack = jnp.concatenate(grad_parts, axis=0)
        query_grads = [None] * heads
        for j in range(i + 1):
            cols = pl.ds(j * block, block)
            weight_list = []
            score_list = []
            for head in range(heads):
                tile = dot_nt(key_ref[cols, :], query_parts[head])
                if j == i:
                    tile = tile + tiles[head][0]
                elif j == i - 1:
                    tile = tile + tiles[head][1]
                weights = jnp.exp(tile - total_ref[0, head:head + 1, rows])
                grads = dot_nt(value_ref[cols, :], grad_parts[head])
                score_grads = weights * (grads - inner[head])
                low = score_grads.astype(jnp.bfloat16)
                weight_list.append(weights.astype(jnp.bfloat16))
                score_list.append(low)
                part = dot_nn(flipped[head * size:(head + 1) * size, j * block:(j + 1) * block], low)
                query_grads[head] = part if query_grads[head] is None else query_grads[head] + part
                if j == i:
                    near_acc[head] = score_grads if near_acc[head] is None else near_acc[head] + score_grads
                else:
                    far = score_grads
                    if j == i - 1:
                        close = jnp.where(tiles[head][2], score_grads, 0.0)
                        near_acc[head] = near_acc[head] + close
                        far = score_grads - close
                    far = jnp.sum(far, axis=0, keepdims=True)
                    far_acc[head] = far if far_acc[head] is None else far_acc[head] + far
            value_part = dot_nn(jnp.concatenate(weight_list, axis=1), grad_stack)
            key_part = dot_nn(jnp.concatenate(score_list, axis=1), query_stack)
            if j == i:
                value_acc[cols, :] = value_part
                key_acc[cols, :] = key_part
            else:
                value_acc[cols, :] += value_part
                key_acc[cols, :] += key_part
        grads_ref[0, rows, :] = (jnp.concatenate(query_grads, axis=0) * scale).T.astype(grads_ref.dtype)
    grads_ref[1] = key_acc[...].astype(grads_ref.dtype)
    grads_ref[2] = value_acc[...].astype(grads_ref.dtype)
    for head in range(heads):
        dist_ref[0, head:head + 1, :] = diagonal_sums(near_acc[head])
        dist_ref[0, heads + head:heads + head + 1, :] = far_acc[head]


def attend_back(queries, keys, values, grads, outs, totals, near, size, block):
    length, width = queries.shape
    lanes = 128
    heads = lanes // size
    groups = width // lanes
    column = pl.BlockSpec((length, lanes), lambda g: (0, g))
    head_rows = pl.BlockSpec((1, heads, block), lambda g: (g, 0, 0))
    return pl.pallas_call(
        partial(attend_back_kernel, block=block, size=size, scale=size ** -0.5),
        grid=(groups,),
        in_specs=[column] * 5 + [pl.BlockSpec((1, heads, length), lambda g: (g, 0, 0)), head_rows],
        out_specs=[pl.BlockSpec((3, length, lanes), lambda g: (0, 0, g)), pl.BlockSpec((1, 2 * heads, block), lambda g: (g, 0, 0))],
        out_shape=[jax.ShapeDtypeStruct((3, length, width), jnp.bfloat16), jax.ShapeDtypeStruct((groups, 2 * heads, block), jnp.float32)],
        scratch_shapes=[pltpu.VMEM((length, lanes), jnp.float32)] * 2,
        compiler_params=pltpu.CompilerParams(vmem_limit_bytes=62 << 20),
        name="attend_back",
    )(queries, keys, values, grads, outs, totals, near)


def reverse_bits(value, count):
    out = value * 0
    for level in range(count):
        out = out * 2 + (value >> level) % 2
    return out


def project_kernel(owner_ref, inputs_ref, gain_ref, *refs, eps):
    piece_refs, weight_refs, low_ref, out_refs = refs[:4], refs[4:7], refs[7], refs[8:]
    count, half, three, _ = piece_refs[0].shape
    piece = three // 3
    owners = 2 * count
    part = owners * piece
    @pl.when(pl.program_id(0) == 0)
    def _():
        me = owner_ref[0]
        for source in range(owners):
            apart = jnp.bitwise_xor(me, source)
            near = apart % 2 == 0
            place = apart // 2
            places = (place, reverse_bits(place, owners.bit_length() - 2))
            for group in range(2):
                for line in range(half):
                    block = jnp.where(near, piece_refs[2 * group][places[group], line], piece_refs[2 * group + 1][places[group], line])
                    start = (group * half + line) * part + source * piece
                    for index in range(3):
                        weight_refs[index][start:start + piece, :] = block[index * piece:(index + 1) * piece]
    rows = inputs_ref[...].astype(jnp.float32)
    inverse = lax.rsqrt(jnp.mean(rows * rows, axis=1, keepdims=True) + eps)
    low = (rows * inverse * gain_ref[...]).astype(jnp.bfloat16)
    low_ref[...] = low
    for weight_ref, out_ref in zip(weight_refs, out_refs):
        out_ref[...] = dot_nn(low, weight_ref[...]).astype(jnp.bfloat16)


def project(owner, inputs, gain, pieces, eps, block=256):
    tokens, width = inputs.shape
    rows = pl.BlockSpec((block, width), lambda i: (i, 0))
    whole = lambda shape: pl.BlockSpec(shape, lambda i: (0,) * len(shape))
    weight = jax.ShapeDtypeStruct((width, width), jnp.bfloat16)
    return pl.pallas_call(
        partial(project_kernel, eps=eps),
        grid=(tokens // block,),
        in_specs=[pl.BlockSpec(memory_space=pltpu.SMEM), rows, whole(gain.shape)] + [whole(piece.shape) for piece in pieces],
        out_specs=[whole(weight.shape)] * 3 + [rows] * 4,
        out_shape=[weight] * 3 + [jax.ShapeDtypeStruct((tokens, width), jnp.bfloat16)] * 4,
        compiler_params=pltpu.CompilerParams(vmem_limit_bytes=62 << 20),
        name="project",
    )(owner, inputs, gain, *pieces)


def settle_kernel(mixed_ref, merge_ref, inputs_ref, gain_ref, router_ref, routes_ref, resid_ref, low_ref, gates_ref, *, eps):
    resid = inputs_ref[...].astype(jnp.float32) + dot_nn(mixed_ref[...], merge_ref[...])
    resid_ref[...] = resid
    inverse = lax.rsqrt(jnp.mean(resid * resid, axis=1, keepdims=True) + eps)
    low = (resid * inverse * gain_ref[...]).astype(jnp.bfloat16)
    low_ref[...] = low
    logits = dot_nt(router_ref[...], low)
    expert = lax.broadcasted_iota(jnp.int32, logits.shape, 0)
    chosen = [jnp.sum(jnp.where(routes_ref[c:c + 1, :] == expert, logits, 0.0), axis=0, keepdims=True) for c in range(2)]
    top = jnp.maximum(chosen[0], chosen[1])
    powers = [jnp.exp(value - top) for value in chosen]
    total = powers[0] + powers[1]
    for c in range(2):
        gates_ref[c:c + 1, :] = powers[c] / total


def settle(mixed, merge, inputs, gain, router, routes, eps, block=256):
    tokens, width = inputs.shape
    rows = pl.BlockSpec((block, width), lambda i: (i, 0))
    whole = lambda shape: pl.BlockSpec(shape, lambda i: (0, 0))
    small = pl.BlockSpec((2, block), lambda i: (0, i))
    return pl.pallas_call(
        partial(settle_kernel, eps=eps),
        grid=(tokens // block,),
        in_specs=[rows, whole(merge.shape), rows, whole(gain.shape), whole(router.shape), small],
        out_specs=[rows, rows, small],
        out_shape=[jax.ShapeDtypeStruct((tokens, width), jnp.float32), jax.ShapeDtypeStruct((tokens, width), jnp.bfloat16), jax.ShapeDtypeStruct((2, tokens), jnp.float32)],
        compiler_params=pltpu.CompilerParams(vmem_limit_bytes=62 << 20),
        name="settle",
    )(mixed, merge, inputs, gain, router, routes)


def finish_kernel(heads_ref, query_ref, key_ref, value_ref, gain_ref, inputs_ref, resid_grad_ref, out_ref, gain_grad_ref, *, eps):
    grads = dot_nt(heads_ref[0], query_ref[...]) + dot_nt(heads_ref[1], key_ref[...]) + dot_nt(heads_ref[2], value_ref[...])
    rows = inputs_ref[...].astype(jnp.float32)
    inverse = lax.rsqrt(jnp.mean(rows * rows, axis=1, keepdims=True) + eps)
    unit = rows * inverse
    @pl.when(pl.program_id(0) == 0)
    def _():
        gain_grad_ref[...] = jnp.zeros_like(gain_grad_ref)
    gain_grad_ref[...] += jnp.sum(grads * unit, axis=0, keepdims=True)
    scaled = grads * gain_ref[...]
    inner = jnp.mean(scaled * unit, axis=1, keepdims=True)
    out_ref[...] = resid_grad_ref[...] + inverse * (scaled - unit * inner)


def finish(head_grads, query, key, value, gain, inputs, resid_grad, eps, block=256):
    tokens, width = inputs.shape
    rows = pl.BlockSpec((block, width), lambda i: (i, 0))
    whole = lambda shape: pl.BlockSpec(shape, lambda i: (0, 0))
    return pl.pallas_call(
        partial(finish_kernel, eps=eps),
        grid=(tokens // block,),
        in_specs=[pl.BlockSpec((3, block, width), lambda i: (0, i, 0))] + [whole(query.shape)] * 3 + [whole(gain.shape), rows, rows],
        out_specs=[rows, whole((1, width))],
        out_shape=[jax.ShapeDtypeStruct((tokens, width), jnp.float32), jax.ShapeDtypeStruct((1, width), jnp.float32)],
        compiler_params=pltpu.CompilerParams(vmem_limit_bytes=62 << 20),
        name="finish",
    )(head_grads, query, key, value, gain, inputs, resid_grad)


def weight_kernel(left_ref, right_ref, out_ref, turned):
    shards, part, _ = out_ref.shape
    @pl.when(pl.program_id(0) == 0)
    def _():
        turned[...] = left_ref[...].T
    right = right_ref[...]
    for shard in range(shards):
        grad = dot_nn(turned[shard * part:(shard + 1) * part, :], right)
        out_ref[shard] = grad.astype(jnp.bfloat16)


def weight_grads(left, right, shards):
    count, tokens, width = right.shape
    part = width // shards
    return pl.pallas_call(
        weight_kernel,
        grid=(count,),
        in_specs=[pl.BlockSpec((tokens, width), lambda i: (0, 0)), pl.BlockSpec((None, tokens, width), lambda i: (i, 0, 0))],
        out_specs=pl.BlockSpec((shards, part, width), lambda i: (0, i, 0)),
        out_shape=jax.ShapeDtypeStruct((shards, count * part, width), jnp.bfloat16),
        scratch_shapes=[pltpu.VMEM((width, tokens), jnp.bfloat16)],
        compiler_params=pltpu.CompilerParams(vmem_limit_bytes=62 << 20),
        name="weight_grads",
    )(left, right)


def exchange(rows, bit):
    count = lax.axis_size("expert")
    return lax.ppermute(rows, "expert", [(i, i ^ bit) for i in range(count)])


def shift(rows, step):
    count = lax.axis_size("shard")
    return lax.ppermute(rows, "shard", [(i, (i + step) % count) for i in range(count)])


def gather_line(rows):
    count = lax.axis_size("shard")
    me = lax.axis_index("shard")
    out = jnp.zeros((count,) + rows.shape, rows.dtype)
    out = lax.dynamic_update_index_in_dim(out, rows, me, 0)
    for step in range(1, count):
        got = shift(rows, step)
        out = lax.dynamic_update_index_in_dim(out, got, (me - step) % count, 0)
    return out


def add_low(left, right):
    return (left.astype(jnp.float32) + right.astype(jnp.float32)).astype(jnp.bfloat16)


def reduce_stack(stack, bits):
    me = lax.axis_index("expert")
    for bit in bits:
        half = stack.shape[1] // 2
        side = (me // bit) % 2
        keep = lax.dynamic_slice_in_dim(stack, side * half, half, 1)
        send = lax.dynamic_slice_in_dim(stack, (1 - side) * half, half, 1)
        got = exchange(send, bit)
        stack = add_low(keep, got)
    count = lax.axis_size("shard")
    place = lax.axis_index("shard")
    total = lax.dynamic_index_in_dim(stack, place, 0, False).astype(jnp.float32)
    for step in range(1, count):
        send = lax.dynamic_index_in_dim(stack, (place + step) % count, 0, False)
        total = total + shift(send, step).astype(jnp.float32)
    piece = total.astype(jnp.bfloat16)
    for bit in reversed(bits):
        other = exchange(piece, bit)
        side = (me // bit) % 2
        piece = jnp.where(
            side == 0, jnp.concatenate([piece, other]), jnp.concatenate([other, piece])
        )
    return piece


def scatter_sum(grads):
    shards, rows, width = grads.shape
    grads = grads.reshape(shards * rows, width)
    return lax.psum_scatter(grads, "shard", scatter_dimension=0, tiled=True)


def share_rows(rows):
    return lax.all_to_all(rows, "expert", 0, 0, tiled=True)


def local(
    inputs,
    norm_gain,
    query_weight,
    key_weight,
    value_weight,
    merge_weight,
    bias_table,
    expert_gain,
    router_weight,
    up_weight,
    down_weight,
    routes,
    cotangent,
):
    f32, bf16 = jnp.float32, jnp.bfloat16
    tokens, width = inputs.shape
    owners = lax.axis_size("expert")
    shards = lax.axis_size("shard")
    me = lax.axis_index("expert")
    part = query_weight.shape[0]
    piece = part // owners
    local_heads = bias_table.shape[1]
    heads = local_heads * shards
    size = width // heads
    experts = router_weight.shape[1]
    local_count, _, hidden = up_weight.shape
    capacity = (5 * tokens * routes.shape[1] + 4 * experts - 1) // (4 * experts)
    capacity = -(-capacity // 16) * 16
    rows = owners * capacity
    assert local_count == 2 and hidden // shards == width

    router_at = 2 + local_heads + (-(2 + local_heads)) % 8

    def widen(block):
        return jnp.pad(block, ((0, 0), (0, width - block.shape[1])))

    def pack(gain_one, gain_two, table, router):
        head = jnp.concatenate([gain_one, gain_two], axis=0)
        gap = jnp.zeros((router_at - 2 - local_heads, width), bf16)
        return jnp.concatenate([widen(head), widen(table), gap, widen(router)], axis=0)

    small = pack(norm_gain[None], expert_gain[None], bias_table.T, router_weight.T)
    slices = [
        lax.dynamic_slice_in_dim(weight, me * piece, piece, 0)
        for weight in (query_weight, key_weight, value_weight)
    ]
    lined = gather_line(jnp.concatenate(slices + [small]))
    small_full = lined[:, 3 * piece :]
    bits = [1 << level for level in range(owners.bit_length() - 1)]
    pieces = []
    for index, order in enumerate((bits[1:], bits[:0:-1])):
        held = lined[index * shards // 2 : (index + 1) * shards // 2, : 3 * piece][None]
        for bit in order:
            got = exchange(held, bit)
            held = jnp.concatenate([held, got])
        pieces += [held, exchange(held, bits[0])]
    merge_full = lax.all_gather(merge_weight, "shard", axis=0, tiled=True)

    gain_one = small_full[:, 0, :part].reshape(1, width).astype(f32)
    gain_two = small_full[:, 1, :part].reshape(1, width).astype(f32)
    table_full = small_full[:, 2 : 2 + local_heads, :BUCKETS].reshape(heads, BUCKETS).astype(f32)
    router_full = small_full[:, router_at : router_at + experts, :part]
    router_full = router_full.transpose(1, 0, 2).reshape(experts, width)

    routes_line = routes.T
    base = (routes_line % local_count * owners + routes_line // local_count) * capacity
    slots = find_slots(routes_line, base, experts)
    *cot_rows, other = dispatch_all(
        slots, routes_line.astype(f32), cotangent, owners, capacity, local_count
    )
    other = share_rows(other).reshape(owners, local_count, capacity)

    owner = me.astype(jnp.int32).reshape(1)
    query_full, key_full, value_full, low_one, queries, keys, values = project(owner, inputs, gain_one, pieces, epsilon)
    cot_in = []
    for index in range(local_count):
        cot_in.append(share_rows(cot_rows[index]).reshape(rows, width))
    block = 256
    hot = bucket_hot(tokens)
    assert hot[block:, -1].all()
    near_hot = jnp.asarray((hot[:block] - hot[-1:]).T, dtype=f32)
    group = 128 // size
    near = jnp.dot(table_full, near_hot, precision=lax.Precision.HIGHEST)
    near = near.reshape(heads // group, group, block)
    attended, totals = attend(queries, keys, values, near, size, block)
    resid, low_two, gates = settle(
        attended, merge_full, inputs, gain_two, router_full, routes_line, epsilon
    )

    sends, rows_in = [], []
    for index in range(local_count):
        sends.append(dispatch(slots, low_two, index * rows, rows))
        send = share_rows(sends[index].reshape(owners, capacity, width))
        rows_in.append(send.reshape(rows, width))
    others = [other[:, index].reshape(1, rows) for index in range(local_count)]
    act, slope, first_down, grad_in = expert_first(
        owner, rows_in[0], cot_in[0], others[0], router_full, up_weight, 0, local_count, shards,
        after=(sends[1],),
    )
    first_sum = scatter_sum(first_down)
    first_made, pair = expert_second(
        rows_in[0], grad_in, act, slope, up_weight, down_weight, 0, owners, shards, 2 * width
    )
    act, slope, pair, grad_in = expert_first(
        owner, rows_in[1], cot_in[1], others[1], router_full, up_weight, 1, local_count, shards,
        into=pair,
    )
    pair_sum = scatter_sum(pair)
    second_made, last_up = expert_second(
        rows_in[1], grad_in, act, slope, up_weight, down_weight, 1, owners, shards, width
    )
    last_sum = scatter_sum(last_up)
    returned = []
    for made in (first_made, second_made):
        returned.append(share_rows(made))
    output, logit_grad = combine_out(slots, routes_line, gates, resid, cotangent, returned)
    router_wide = jnp.pad(router_full, ((0, 128 - experts), (0, 0)))
    resid_grad, branch, mixed_grad, gain_grad = combine_back(
        slots, logit_grad, router_wide, gain_two, resid, cotangent, merge_full, returned, epsilon
    )
    router_grad = jnp.einsum("te,ti->ei", logit_grad, low_two, preferred_element_type=f32)
    merge_grad = weight_grads(attended, branch[None], shards)
    head_grads, distances = attend_back(
        queries, keys, values, mixed_grad, attended, totals, near, size, block
    )
    close_sums = distances[:, :group].reshape(heads, block)
    far_sums = jnp.sum(distances[:, group:].reshape(heads, block), axis=1)
    table_grad = jnp.dot(close_sums, jnp.asarray(hot[:block]), precision=lax.Precision.HIGHEST)
    table_grad = table_grad + far_sums[:, None] * jnp.asarray(hot[-1:])
    head_sums = weight_grads(low_one, head_grads, shards)
    input_gradient, norm_grad = finish(
        head_grads, query_full, key_full, value_full, gain_one, inputs, resid_grad, epsilon
    )
    small_grad = jax.vmap(pack)(
        norm_grad.reshape(shards, 1, part).astype(bf16),
        gain_grad.reshape(shards, 1, part).astype(bf16),
        table_grad.reshape(shards, local_heads, BUCKETS).astype(bf16),
        router_grad[:experts].reshape(experts, shards, part).transpose(1, 0, 2).astype(bf16),
    )
    head_sums = reduce_stack(head_sums, bits).astype(f32)
    spare = -small_grad.shape[1] % (8 * owners)
    small_grad = jnp.pad(small_grad, ((0, 0), (0, spare), (0, 0)))
    rest_sums = jnp.concatenate([merge_grad, small_grad], axis=1)
    rest_sums = reduce_stack(rest_sums, bits[:1] + bits[:0:-1]).astype(f32)
    small_sum = rest_sums[part:]
    return (
        output,
        input_gradient,
        small_sum[0, :part],
        head_sums[:part],
        head_sums[part : 2 * part],
        head_sums[2 * part :],
        rest_sums[:part],
        small_sum[2 : 2 + local_heads, :BUCKETS].T,
        small_sum[1, :part],
        small_sum[router_at : router_at + experts, :part].T,
        jnp.stack([pair_sum[:width].astype(f32), last_sum.astype(f32)]),
        jnp.stack([first_sum.astype(f32), pair_sum[width:].astype(f32)]),
    )


def solution(mesh):
    in_specs = (
        P(("expert", "shard"), None),
        P("shard"),
        P("shard", None),
        P("shard", None),
        P("shard", None),
        P("shard", None),
        P(None, "shard"),
        P("shard"),
        P("shard", None),
        P("expert", None, None),
        P("expert", None, None),
        P(("expert", "shard"), None),
        P(("expert", "shard"), None),
    )
    out_specs = (
        P(("expert", "shard"), None),
        P(("expert", "shard"), None),
        P("shard"),
        P("shard", None),
        P("shard", None),
        P("shard", None),
        P("shard", None),
        P(None, "shard"),
        P("shard"),
        P("shard", None),
        P("expert", None, "shard"),
        P("expert", "shard", None),
    )
    return jax.shard_map(local, mesh=mesh, in_specs=in_specs, out_specs=out_specs, check_vma=False)
```

```python
from functools import partial, reduce

import jax
import jax.numpy as jnp
import numpy as np
from jax import lax
from jax.experimental import pallas as pl
from jax.experimental.pallas import tpu as pltpu
from jax.sharding import PartitionSpec as P


BUCKETS = 32
MAX_DIST = 128


epsilon = 1e-06
masked_score = -1e30


def bucket_hot(length):
    distance = np.arange(length)
    half_count = BUCKETS // 2
    clipped = np.maximum(distance, half_count)
    spread = np.log(clipped / half_count) / np.log(MAX_DIST / half_count) * (BUCKETS - half_count)
    far_bucket = np.minimum(half_count + np.floor(spread).astype(np.int32), BUCKETS - 1)
    bucket = np.where(distance < half_count, distance, far_bucket)
    return (bucket[:, None] == np.arange(BUCKETS)[None, :]).astype(np.float32)


def dot_nt(a, b):
    return lax.dot_general(a, b, (((1,), (1,)), ((), ())), preferred_element_type=jnp.float32)


def dot_nn(a, b):
    return lax.dot_general(a, b, (((1,), (0,)), ((), ())), preferred_element_type=jnp.float32)


def dot_tn(a, b):
    return lax.dot_general(a, b, (((0,), (0,)), ((), ())), preferred_element_type=jnp.float32)


def slot_kernel(routes_ref, base_ref, slots_ref, *, experts):
    tokens = routes_ref.shape[1]
    expert = lax.broadcasted_iota(jnp.int32, (experts, tokens), 0)
    hits = [routes_ref[c:c + 1, :] == expert for c in range(2)]
    hot = jnp.where(hits[0] | hits[1], 1.0, 0.0).astype(jnp.bfloat16)
    earlier = lax.broadcasted_iota(jnp.int32, (tokens, tokens), 0)
    later = lax.broadcasted_iota(jnp.int32, (tokens, tokens), 1)
    before = jnp.where(earlier < later, 1.0, 0.0).astype(jnp.bfloat16)
    counts = dot_nn(hot, before)
    for c in range(2):
        position = jnp.sum(jnp.where(hits[c], counts, 0.0), axis=0, keepdims=True)
        slots_ref[c:c + 1, :] = base_ref[c:c + 1, :] + position.astype(jnp.int32)


def find_slots(routes, base, experts):
    return pl.pallas_call(
        partial(slot_kernel, experts=experts),
        out_shape=jax.ShapeDtypeStruct(routes.shape, jnp.int32),
    )(routes, base)


def dispatch_kernel(slots_ref, rows_ref, *refs, start):
    out_ref = refs[-1]
    block, tokens = out_ref.shape[0], rows_ref.shape[0]
    slot = lax.broadcasted_iota(jnp.int32, (block, tokens), 0) + (pl.program_id(0) * block + start)
    hot = jnp.where((slot == slots_ref[0:1, :]) | (slot == slots_ref[1:2, :]), 1.0, 0.0)
    out_ref[...] = dot_nn(hot.astype(jnp.bfloat16), rows_ref[...]).astype(out_ref.dtype)


def dispatch(slots, rows, start, count, after=(), block=256):
    _, width = rows.shape
    whole = lambda shape: pl.BlockSpec(shape, lambda i: (0, 0))
    return pl.pallas_call(
        partial(dispatch_kernel, start=start),
        grid=(count // block,),
        in_specs=[whole(slots.shape), whole(rows.shape)] + [pl.BlockSpec(memory_space=pl.ANY)] * len(after),
        out_specs=pl.BlockSpec((block, width), lambda i: (i, 0)),
        out_shape=jax.ShapeDtypeStruct((count, width), rows.dtype),
    )(slots, rows, *after)


def dispatch_into_kernel(slots_ref, rows_ref, into_ref, out_ref, *, start):
    del into_ref
    _, _, block, _ = out_ref.shape
    tokens = rows_ref.shape[0]
    slot = lax.broadcasted_iota(jnp.int32, (block, tokens), 0) + (pl.program_id(0) * block + start)
    hot = jnp.where((slot == slots_ref[0:1, :]) | (slot == slots_ref[1:2, :]), 1.0, 0.0)
    out_ref[0, 0] = dot_nn(hot.astype(jnp.bfloat16), rows_ref[...]).astype(out_ref.dtype)


def dispatch_into(slots, rows, start, into):
    owners, _, capacity, width = into.shape
    whole = lambda shape: pl.BlockSpec(shape, lambda i: (0, 0))
    return pl.pallas_call(
        partial(dispatch_into_kernel, start=start),
        grid=(owners,),
        in_specs=[whole(slots.shape), whole(rows.shape), pl.BlockSpec(memory_space=pl.ANY)],
        out_specs=pl.BlockSpec((1, 1, capacity, width), lambda i: (i, 0, 0, 0)),
        out_shape=jax.ShapeDtypeStruct(into.shape, into.dtype),
        input_output_aliases={2: 0},
    )(slots, rows, into)


def dispatch_all_kernel(slots_ref, routes_ref, rows_ref, *refs, owners, capacity):
    out_refs, other_ref = refs[:-1], refs[-1]
    block, tokens = len(out_refs) * capacity, rows_ref.shape[0]
    row = lax.broadcasted_iota(jnp.int32, (block, tokens), 0)
    slot = row + pl.program_id(0) * capacity
    for index in range(1, block // capacity):
        slot = slot + jnp.where(row >= index * capacity, (owners - 1) * capacity, 0)
    hits = [slot == slots_ref[c:c + 1, :] for c in range(2)]
    hot = jnp.where(hits[0] | hits[1], 1.0, 0.0).astype(jnp.bfloat16)
    picked = dot_nn(hot, rows_ref[...]).astype(rows_ref.dtype)
    out_refs[0][0] = picked[:capacity]
    out_refs[1][0, 0] = picked[capacity:]
    other = jnp.where(hits[0], routes_ref[1:2, :], jnp.where(hits[1], routes_ref[0:1, :], 0.0))
    column = jnp.sum(other, axis=1, keepdims=True)
    other_ref[0] = jnp.broadcast_to(column, (block, 128)).T[0:1, :]


def dispatch_all(slots, routes, rows, owners, capacity, local_count):
    _, width = rows.shape
    block = local_count * capacity
    whole = lambda shape: pl.BlockSpec(shape, lambda i: (0, 0))
    return pl.pallas_call(
        partial(dispatch_all_kernel, owners=owners, capacity=capacity),
        grid=(owners,),
        in_specs=[whole(slots.shape), whole(routes.shape), whole(rows.shape)],
        out_specs=[pl.BlockSpec((1, capacity, width), lambda i: (i, 0, 0)), pl.BlockSpec((1, 1, capacity, width), lambda i: (i, 1, 0, 0)), pl.BlockSpec((1, 1, block), lambda i: (i, 0, 0))],
        out_shape=[jax.ShapeDtypeStruct((owners, capacity, width), rows.dtype), jax.ShapeDtypeStruct((owners, 2, capacity, width), rows.dtype), jax.ShapeDtypeStruct((owners, 1, block), jnp.float32)],
    )(slots, routes, rows)


def gelu_pair(v):
    c = np.float32(np.sqrt(2.0 / np.pi))
    a = np.float32(0.044715)
    square = v * v
    half = 0.5 * jnp.tanh(v * (c * a * square + c)) + 0.5
    value = v * half
    slope = half + value * (1.0 - half) * (6.0 * c * a * square + 2.0 * c)
    return value, slope


def first_kernel(owner_ref, rows_ref, cot_ref, other_ref, router_ref, up_ref, *refs, chunk, index, local_count):
    act_ref, slope_ref, down_grad_ref, grad_ref = refs[-4:]
    owners, capacity, width = rows_ref.shape
    rows = owners * capacity
    @pl.when(pl.program_id(0) == 0)
    def _():
        logits = dot_nt(router_ref[...], rows_ref[...].reshape(rows, width))
        expert = lax.broadcasted_iota(jnp.int32, logits.shape, 0)
        mine = owner_ref[0] * local_count + index
        own = jnp.sum(jnp.where(expert == mine, logits, 0.0), axis=0, keepdims=True)
        other = other_ref[...].astype(jnp.int32)
        other = jnp.sum(jnp.where(expert == other, logits, 0.0), axis=0, keepdims=True)
        top = jnp.maximum(own, other)
        own = jnp.exp(own - top)
        gate = own / (own + jnp.exp(other - top))
        column = jnp.broadcast_to(gate, (128, rows)).T
        for start in range(0, width, 128):
            part = cot_ref[:, :, start:start + 128].reshape(rows, 128).astype(jnp.float32) * column
            grad_ref[:, start:start + 128] = part.astype(jnp.bfloat16)
    up = up_ref[0]
    for start in range(0, rows, chunk):
        part = rows_ref[start // capacity:(start + chunk) // capacity].reshape(chunk, width)
        pre = dot_nn(part, up)
        value, slope = gelu_pair(pre)
        act_ref[start:start + chunk, :] = value.astype(jnp.bfloat16)
        slope_ref[start:start + chunk, :] = slope.astype(jnp.bfloat16)
    down_grad_ref[0] = dot_tn(act_ref[...], grad_ref[...]).astype(jnp.bfloat16)


def arrived_spec(arrived, which):
    if arrived.ndim == 3:
        return pl.BlockSpec(arrived.shape, lambda i: (0, 0, 0))
    owners, _, capacity, width = arrived.shape
    return pl.BlockSpec((owners, None, capacity, width), lambda i: (0, which, 0, 0))


def expert_first(owner, rows_in, cot, other, router, up, index, local_count, shards, into=None, after=()):
    owners, capacity, width = rows_in.shape[0], *rows_in.shape[-2:]
    rows = owners * capacity
    hidden = up.shape[2]
    tile = hidden // shards
    chunk = rows // 2
    fixed = pl.BlockSpec((rows, width), lambda i: (0, 0))
    column = pl.BlockSpec((rows, tile), lambda i: (0, i))
    operands = [owner, rows_in, cot, other, router, up]
    place, aliases = 0, {}
    grad_shape = jax.ShapeDtypeStruct((shards, tile, width), jnp.bfloat16)
    if into is not None:
        aliases = {len(operands): 2}
        operands.append(into)
        place, grad_shape = 1, jax.ShapeDtypeStruct(into.shape, into.dtype)
    operands += list(after)
    return pl.pallas_call(
        partial(first_kernel, chunk=chunk, index=index, local_count=local_count),
        grid=(shards,),
        in_specs=[
            pl.BlockSpec(memory_space=pltpu.SMEM),
            arrived_spec(rows_in, 0),
            arrived_spec(cot, 1),
            pl.BlockSpec((1, rows), lambda i: (0, 0)),
            pl.BlockSpec(router.shape, lambda i: (0, 0)),
            pl.BlockSpec((1, width, tile), lambda i: (index, 0, i)),
        ]
        + [pl.BlockSpec(memory_space=pl.ANY)] * (len(operands) - 6),
        out_specs=[column, column, pl.BlockSpec((1, tile, width), lambda i: (i, place, 0)), fixed],
        out_shape=[jax.ShapeDtypeStruct((rows, hidden), jnp.bfloat16)] * 2 + [grad_shape, jax.ShapeDtypeStruct((rows, width), jnp.bfloat16)],
        input_output_aliases=aliases,
        compiler_params=pltpu.CompilerParams(vmem_limit_bytes=62 << 20),
    )(*operands)


def second_kernel(rows_ref, grad_ref, act_ref, slope_ref, up_ref, down_ref, *refs):
    made_ref, up_grad_ref, turned, made_acc, back_acc = refs[-5:]
    step = pl.program_id(0)
    owners, _, capacity, width = made_ref.shape
    @pl.when(step == 0)
    def _():
        turned[...] = rows_ref[...].reshape(grad_ref.shape).T
    up = up_ref[0]
    down = down_ref[0]
    grads = dot_nt(grad_ref[...], down)
    low = (slope_ref[...].astype(jnp.float32) * grads).astype(jnp.bfloat16)
    up_grad_ref[0] = dot_nn(turned[...], low).astype(jnp.bfloat16)
    back = dot_nt(low, up)
    made = dot_nn(act_ref[...], down)
    last = pl.num_programs(0) - 1
    @pl.when(step == 0)
    def _():
        made_acc[...] = made
        back_acc[...] = back
    @pl.when((step > 0) & (step < last))
    def _():
        made_acc[...] += made
        back_acc[...] += back
    @pl.when(step == last)
    def _():
        made_ref[:, 0] = (made_acc[...] + made).astype(jnp.bfloat16).reshape(owners, capacity, width)
        made_ref[:, 1] = (back_acc[...] + back).astype(jnp.bfloat16).reshape(owners, capacity, width)


def expert_second(rows_in, grad, act, slope, up, down, index, owners, shards, wide, after=()):
    rows, width = grad.shape
    hidden = up.shape[2]
    tile = hidden // shards
    fixed = pl.BlockSpec((rows, width), lambda i: (0, 0))
    column = pl.BlockSpec((rows, tile), lambda i: (0, i))
    made_shape = (owners, 2, rows // owners, width)
    return pl.pallas_call(
        second_kernel,
        grid=(shards,),
        in_specs=[arrived_spec(rows_in, 0), fixed, column, column, pl.BlockSpec((1, width, tile), lambda i: (index, 0, i)), pl.BlockSpec((1, tile, width), lambda i: (index, i, 0))]
        + [pl.BlockSpec(memory_space=pl.ANY)] * len(after),
        out_specs=[pl.BlockSpec(made_shape, lambda i: (0, 0, 0, 0)), pl.BlockSpec((1, width, tile), lambda i: (i, 0, 0))],
        out_shape=[jax.ShapeDtypeStruct(made_shape, jnp.bfloat16), jax.ShapeDtypeStruct((shards, wide, tile), jnp.bfloat16)],
        scratch_shapes=[pltpu.VMEM((width, rows), jnp.bfloat16), pltpu.VMEM((rows, width), jnp.float32), pltpu.VMEM((rows, width), jnp.float32)],
        compiler_params=pltpu.CompilerParams(vmem_limit_bytes=62 << 20),
    )(rows_in, grad, act, slope, up, down, *after)


def spread(row, block):
    return jnp.broadcast_to(row, (128, block)).T


def pick(slots, lane, back_refs, first=0):
    picked = None
    for index, back_ref in enumerate(back_refs, first):
        owners, capacity, width = back_ref.shape
        half = owners * capacity
        hots = []
        for start in range(index * half, (index + 1) * half, 128):
            hit = reduce(jnp.logical_or, [slot == lane + start for slot in slots])
            hots.append(jnp.where(hit, 1.0, 0.0).astype(jnp.bfloat16))
        part = dot_nn(jnp.concatenate(hots, axis=1), back_ref[...].reshape(half, width))
        picked = part if picked is None else picked + part
    return picked


def part_kernel(slots_ref, gates_ref, resid_ref, cot_ref, made_ref, back_ref, result_ref, inner_ref, grads_ref):
    block = result_ref.shape[0]
    lane = lax.broadcasted_iota(jnp.int32, (block, 128), 1)
    cot = cot_ref[...].astype(jnp.float32)
    result = resid_ref[...]
    inner = jnp.zeros((block, 128), jnp.float32)
    slots = [spread(slots_ref[c:c + 1, :], block) for c in range(2)]
    for c in range(2):
        picked = pick([slots[c]], lane, [made_ref])
        result = result + spread(gates_ref[c:c + 1, :], block)[:, 0:1] * picked
        inner = inner + jnp.where(lane == c, jnp.sum(cot * picked, axis=1, keepdims=True), 0.0)
    result_ref[...] = result
    inner_ref[...] = inner
    grads_ref[...] = pick(slots, lane, [back_ref])


def combine_part(slots, gates, resid, cot, returned, block=256):
    tokens, width = resid.shape
    small = pl.BlockSpec((2, block), lambda i: (0, i))
    rows = pl.BlockSpec((block, width), lambda i: (i, 0))
    wide = jax.ShapeDtypeStruct((tokens, width), jnp.float32)
    return pl.pallas_call(
        part_kernel,
        grid=(tokens // block,),
        in_specs=[small, small, rows, rows, returned_spec(returned, 0), returned_spec(returned, 1)],
        out_specs=[rows, pl.BlockSpec((block, 128), lambda i: (i, 0)), rows],
        out_shape=[wide, jax.ShapeDtypeStruct((tokens, 128), jnp.float32), wide],
        compiler_params=pltpu.CompilerParams(vmem_limit_bytes=62 << 20),
    )(slots, gates, resid, cot, returned, returned)


def out_kernel(slots_ref, routes_ref, gates_ref, result_ref, inner_ref, cot_ref, made_ref, out_ref, logit_ref):
    block = out_ref.shape[0]
    lane = lax.broadcasted_iota(jnp.int32, (block, 128), 1)
    cot = cot_ref[...].astype(jnp.float32)
    result = result_ref[...]
    gates, inner = [], []
    for c in range(2):
        slot = spread(slots_ref[c:c + 1, :], block)
        gate = spread(gates_ref[c:c + 1, :], block)[:, 0:1]
        picked = pick([slot], lane, [made_ref], 1)
        result = result + gate * picked
        gates.append(gate)
        inner.append(inner_ref[:, c:c + 1] + jnp.sum(cot * picked, axis=1, keepdims=True))
    out_ref[...] = result.astype(out_ref.dtype)
    middle = gates[0] * inner[0] + gates[1] * inner[1]
    logit = jnp.zeros((block, 128), jnp.float32)
    for c in range(2):
        route = spread(routes_ref[c:c + 1, :], block)
        logit = logit + jnp.where(route == lane, gates[c] * (inner[c] - middle), 0.0)
    logit_ref[...] = logit.astype(jnp.bfloat16)


def returned_spec(returned, which):
    owners, _, capacity, width = returned.shape
    return pl.BlockSpec((owners, None, capacity, width), lambda i: (0, which, 0, 0))


def combine_out(slots, routes, gates, result, inner, cot, returned, block=256):
    tokens, width = result.shape
    small = pl.BlockSpec((2, block), lambda i: (0, i))
    rows = pl.BlockSpec((block, width), lambda i: (i, 0))
    return pl.pallas_call(
        out_kernel,
        grid=(tokens // block,),
        in_specs=[small, small, small, rows, pl.BlockSpec((block, 128), lambda i: (i, 0)), rows, returned_spec(returned, 0)],
        out_specs=[rows, pl.BlockSpec((block, 128), lambda i: (i, 0))],
        out_shape=[jax.ShapeDtypeStruct((tokens, width), jnp.bfloat16), jax.ShapeDtypeStruct((tokens, 128), jnp.bfloat16)],
        compiler_params=pltpu.CompilerParams(vmem_limit_bytes=62 << 20),
    )(slots, routes, gates, result, inner, cot, returned)


def back_kernel(slots_ref, logit_ref, router_ref, gain_ref, resid_ref, cot_ref, merge_ref, part_ref, back_ref, grad_ref, low_ref, mixed_ref, gain_grad_ref, *, eps):
    block, _ = grad_ref.shape
    lane = lax.broadcasted_iota(jnp.int32, (block, 128), 1)
    grads = part_ref[...] + pick([spread(slots_ref[c:c + 1, :], block) for c in range(2)], lane, [back_ref], 1)
    grads = grads + dot_nn(logit_ref[...], router_ref[...])
    resid = resid_ref[...]
    inverse = lax.rsqrt(jnp.mean(resid * resid, axis=1, keepdims=True) + eps)
    unit = resid * inverse
    @pl.when(pl.program_id(0) == 0)
    def _():
        gain_grad_ref[...] = jnp.zeros_like(gain_grad_ref)
    gain_grad_ref[...] += jnp.sum(grads * unit, axis=0, keepdims=True)
    scaled = grads * gain_ref[...]
    inner = jnp.mean(scaled * unit, axis=1, keepdims=True)
    total = cot_ref[...].astype(jnp.float32) + inverse * (scaled - unit * inner)
    grad_ref[...] = total
    low = total.astype(jnp.bfloat16)
    low_ref[...] = low
    mixed_ref[...] = dot_nt(low, merge_ref[...]).astype(jnp.bfloat16)


def combine_back(slots, logit, router, gain, resid, cot, merge, part, returned, eps, block=256):
    tokens, width = resid.shape
    rows = pl.BlockSpec((block, width), lambda i: (i, 0))
    whole = lambda shape: pl.BlockSpec(shape, lambda i: (0, 0))
    low = jax.ShapeDtypeStruct((tokens, width), jnp.bfloat16)
    return pl.pallas_call(
        partial(back_kernel, eps=eps),
        grid=(tokens // block,),
        in_specs=[pl.BlockSpec((2, block), lambda i: (0, i)), pl.BlockSpec((block, 128), lambda i: (i, 0)), whole(router.shape), whole(gain.shape), rows, rows, whole(merge.shape), rows, returned_spec(returned, 1)],
        out_specs=[rows, rows, rows, whole((1, width))],
        out_shape=[jax.ShapeDtypeStruct((tokens, width), jnp.float32), low, low, jax.ShapeDtypeStruct((1, width), jnp.float32)],
        compiler_params=pltpu.CompilerParams(vmem_limit_bytes=62 << 20),
    )(slots, logit, router, gain, resid, cot, merge, part, returned)


def near_tiles(near_ref, head, block):
    spread = jnp.broadcast_to(near_ref[0, head:head + 1, :], (block, block))
    spread = pltpu.roll(spread, 0, 1, stride=1, stride_axis=0)
    key_at = lax.broadcasted_iota(jnp.int32, (block, block), 0)
    query_at = lax.broadcasted_iota(jnp.int32, (block, block), 1)
    return (jnp.where(query_at >= key_at, spread, masked_score), jnp.where(query_at < key_at, spread, 0.0), query_at < key_at)


def diagonal_sums(tile):
    block = tile.shape[1]
    total = tile[:8]
    for start in range(8, block, 8):
        total = total + pltpu.roll(tile[start:start + 8], block - start, 1)
    row = lax.broadcasted_iota(jnp.int32, total.shape, 0)
    for step in (1, 2, 4):
        total = jnp.where((row & step) != 0, pltpu.roll(total, block - step, 1), total)
    return jnp.sum(total, axis=0, keepdims=True)


def head_part(rows, head, size):
    lane = lax.broadcasted_iota(jnp.int32, rows.shape, 1)
    return jnp.where((lane >= head * size) & (lane < (head + 1) * size), rows, jnp.zeros_like(rows))


def attend_kernel(query_ref, key_ref, value_ref, near_ref, out_ref, total_ref, *, block, size, scale):
    length, lanes = query_ref.shape
    heads = lanes // size
    count = length // block
    flipped = value_ref[...].T
    tiles = [near_tiles(near_ref, head, block) for head in range(heads)]
    for i in range(count):
        rows = pl.ds(i * block, block)
        query_rows = query_ref[rows, :] * jnp.bfloat16(scale)
        parts = []
        for head in range(heads):
            query_part = head_part(query_rows, head, size)
            scores = []
            for j in range(i + 1):
                tile = dot_nt(key_ref[pl.ds(j * block, block), :], query_part)
                if j == i:
                    tile = tile + tiles[head][0]
                elif j == i - 1:
                    tile = tile + tiles[head][1]
                scores.append(tile)
            top = reduce(jnp.maximum, scores)
            top = jnp.max(top, axis=0, keepdims=True)
            mixed = None
            total = None
            for j in range(i + 1):
                weights = jnp.exp(scores[j] - top)
                sums = jnp.sum(weights, axis=0, keepdims=True)
                part = dot_nn(flipped[head * size:(head + 1) * size, j * block:(j + 1) * block], weights.astype(jnp.bfloat16))
                mixed = part if mixed is None else mixed + part
                total = sums if total is None else total + sums
            parts.append(mixed / total)
            total_ref[0, head:head + 1, rows] = top + jnp.log(total)
        out_ref[rows, :] = jnp.concatenate(parts, axis=0).T.astype(out_ref.dtype)


def attend(queries, keys, values, near, size, block):
    length, width = queries.shape
    lanes = 128
    heads = lanes // size
    groups = width // lanes
    column = pl.BlockSpec((length, lanes), lambda g: (0, g))
    head_rows = pl.BlockSpec((1, heads, block), lambda g: (g, 0, 0))
    return pl.pallas_call(
        partial(attend_kernel, block=block, size=size, scale=size ** -0.5),
        grid=(groups,),
        in_specs=[column, column, column, head_rows],
        out_specs=[column, pl.BlockSpec((1, heads, length), lambda g: (g, 0, 0))],
        out_shape=[jax.ShapeDtypeStruct((length, width), jnp.bfloat16), jax.ShapeDtypeStruct((groups, heads, length), jnp.float32)],
        compiler_params=pltpu.CompilerParams(vmem_limit_bytes=62 << 20),
    )(queries, keys, values, near)


def attend_back_kernel(query_ref, key_ref, value_ref, grad_ref, out_ref, total_ref, near_ref, grads_ref, dist_ref, key_acc, value_acc, *, block, size, scale):
    length, lanes = query_ref.shape
    heads = lanes // size
    count = length // block
    flipped = key_ref[...].T
    tiles = [near_tiles(near_ref, head, block) for head in range(heads)]
    near_acc = [None] * heads
    far_acc = [None] * heads
    for i in range(count):
        rows = pl.ds(i * block, block)
        query_rows = query_ref[rows, :] * jnp.bfloat16(scale)
        grad_rows = grad_ref[rows, :]
        products = (grad_rows.astype(jnp.float32) * out_ref[rows, :].astype(jnp.float32)).T
        query_parts = [head_part(query_rows, head, size) for head in range(heads)]
        grad_parts = [head_part(grad_rows, head, size) for head in range(heads)]
        inner = [jnp.sum(products[head * size:(head + 1) * size], axis=0, keepdims=True) for head in range(heads)]
        query_stack = jnp.concatenate(query_parts, axis=0)
        grad_stack = jnp.concatenate(grad_parts, axis=0)
        query_grads = [None] * heads
        for j in range(i + 1):
            cols = pl.ds(j * block, block)
            weight_list = []
            score_list = []
            for head in range(heads):
                tile = dot_nt(key_ref[cols, :], query_parts[head])
                if j == i:
                    tile = tile + tiles[head][0]
                elif j == i - 1:
                    tile = tile + tiles[head][1]
                weights = jnp.exp(tile - total_ref[0, head:head + 1, rows])
                grads = dot_nt(value_ref[cols, :], grad_parts[head])
                score_grads = weights * (grads - inner[head])
                low = score_grads.astype(jnp.bfloat16)
                weight_list.append(weights.astype(jnp.bfloat16))
                score_list.append(low)
                part = dot_nn(flipped[head * size:(head + 1) * size, j * block:(j + 1) * block], low)
                query_grads[head] = part if query_grads[head] is None else query_grads[head] + part
                if j == i:
                    near_acc[head] = score_grads if near_acc[head] is None else near_acc[head] + score_grads
                else:
                    far = score_grads
                    if j == i - 1:
                        close = jnp.where(tiles[head][2], score_grads, 0.0)
                        near_acc[head] = near_acc[head] + close
                        far = score_grads - close
                    far = jnp.sum(far, axis=0, keepdims=True)
                    far_acc[head] = far if far_acc[head] is None else far_acc[head] + far
            value_part = dot_nn(jnp.concatenate(weight_list, axis=1), grad_stack)
            key_part = dot_nn(jnp.concatenate(score_list, axis=1), query_stack)
            if j == i:
                value_acc[cols, :] = value_part
                key_acc[cols, :] = key_part
            else:
                value_acc[cols, :] += value_part
                key_acc[cols, :] += key_part
        grads_ref[0, rows, :] = (jnp.concatenate(query_grads, axis=0) * scale).T.astype(grads_ref.dtype)
    grads_ref[1] = key_acc[...].astype(grads_ref.dtype)
    grads_ref[2] = value_acc[...].astype(grads_ref.dtype)
    for head in range(heads):
        dist_ref[0, head:head + 1, :] = diagonal_sums(near_acc[head])
        dist_ref[0, heads + head:heads + head + 1, :] = far_acc[head]


def attend_back(queries, keys, values, grads, outs, totals, near, size, block):
    length, width = queries.shape
    lanes = 128
    heads = lanes // size
    groups = width // lanes
    column = pl.BlockSpec((length, lanes), lambda g: (0, g))
    head_rows = pl.BlockSpec((1, heads, block), lambda g: (g, 0, 0))
    return pl.pallas_call(
        partial(attend_back_kernel, block=block, size=size, scale=size ** -0.5),
        grid=(groups,),
        in_specs=[column] * 5 + [pl.BlockSpec((1, heads, length), lambda g: (g, 0, 0)), head_rows],
        out_specs=[pl.BlockSpec((3, length, lanes), lambda g: (0, 0, g)), pl.BlockSpec((1, 2 * heads, block), lambda g: (g, 0, 0))],
        out_shape=[jax.ShapeDtypeStruct((3, length, width), jnp.bfloat16), jax.ShapeDtypeStruct((groups, 2 * heads, block), jnp.float32)],
        scratch_shapes=[pltpu.VMEM((length, lanes), jnp.float32)] * 2,
        compiler_params=pltpu.CompilerParams(vmem_limit_bytes=62 << 20),
    )(queries, keys, values, grads, outs, totals, near)


def reverse_bits(value, count):
    out = value * 0
    for level in range(count):
        out = out * 2 + (value >> level) % 2
    return out


def project_kernel(owner_ref, inputs_ref, gain_ref, *refs, eps):
    piece_refs, weight_refs, low_ref, out_refs = refs[:4], refs[-7:-4], refs[-4], refs[-3:]
    count, half, three, _ = piece_refs[0].shape
    piece = three // 3
    owners = 2 * count
    part = owners * piece
    @pl.when(pl.program_id(0) == 0)
    def _():
        me = owner_ref[0]
        for source in range(owners):
            apart = jnp.bitwise_xor(me, source)
            near = apart % 2 == 0
            place = apart // 2
            places = (place, reverse_bits(place, owners.bit_length() - 2))
            for group in range(2):
                for line in range(half):
                    block = jnp.where(near, piece_refs[2 * group][places[group], line], piece_refs[2 * group + 1][places[group], line])
                    start = (group * half + line) * part + source * piece
                    for index in range(3):
                        weight_refs[index][start:start + piece, :] = block[index * piece:(index + 1) * piece]
    rows = inputs_ref[...].astype(jnp.float32)
    inverse = lax.rsqrt(jnp.mean(rows * rows, axis=1, keepdims=True) + eps)
    low = (rows * inverse * gain_ref[...]).astype(jnp.bfloat16)
    low_ref[...] = low
    for weight_ref, out_ref in zip(weight_refs, out_refs):
        out_ref[...] = dot_nn(low, weight_ref[...]).astype(jnp.bfloat16)


def project(owner, inputs, gain, pieces, eps, after=(), block=256):
    tokens, width = inputs.shape
    rows = pl.BlockSpec((block, width), lambda i: (i, 0))
    whole = lambda shape: pl.BlockSpec(shape, lambda i: (0,) * len(shape))
    weight = jax.ShapeDtypeStruct((width, width), jnp.bfloat16)
    return pl.pallas_call(
        partial(project_kernel, eps=eps),
        grid=(tokens // block,),
        in_specs=[pl.BlockSpec(memory_space=pltpu.SMEM), rows, whole(gain.shape)] + [whole(piece.shape) for piece in pieces] + [pl.BlockSpec(memory_space=pl.ANY)] * len(after),
        out_specs=[whole(weight.shape)] * 3 + [rows] * 4,
        out_shape=[weight] * 3 + [jax.ShapeDtypeStruct((tokens, width), jnp.bfloat16)] * 4,
        compiler_params=pltpu.CompilerParams(vmem_limit_bytes=62 << 20),
    )(owner, inputs, gain, *pieces, *after)


def settle_kernel(mixed_ref, merge_ref, inputs_ref, gain_ref, router_ref, routes_ref, resid_ref, low_ref, gates_ref, *, eps):
    resid = inputs_ref[...].astype(jnp.float32) + dot_nn(mixed_ref[...], merge_ref[...])
    resid_ref[...] = resid
    inverse = lax.rsqrt(jnp.mean(resid * resid, axis=1, keepdims=True) + eps)
    low = (resid * inverse * gain_ref[...]).astype(jnp.bfloat16)
    low_ref[...] = low
    logits = dot_nt(router_ref[...], low)
    expert = lax.broadcasted_iota(jnp.int32, logits.shape, 0)
    chosen = [jnp.sum(jnp.where(routes_ref[c:c + 1, :] == expert, logits, 0.0), axis=0, keepdims=True) for c in range(2)]
    top = jnp.maximum(chosen[0], chosen[1])
    powers = [jnp.exp(value - top) for value in chosen]
    total = powers[0] + powers[1]
    for c in range(2):
        gates_ref[c:c + 1, :] = powers[c] / total


def settle(mixed, merge, inputs, gain, router, routes, eps, block=256):
    tokens, width = inputs.shape
    rows = pl.BlockSpec((block, width), lambda i: (i, 0))
    whole = lambda shape: pl.BlockSpec(shape, lambda i: (0, 0))
    small = pl.BlockSpec((2, block), lambda i: (0, i))
    return pl.pallas_call(
        partial(settle_kernel, eps=eps),
        grid=(tokens // block,),
        in_specs=[rows, whole(merge.shape), rows, whole(gain.shape), whole(router.shape), small],
        out_specs=[rows, rows, small],
        out_shape=[jax.ShapeDtypeStruct((tokens, width), jnp.float32), jax.ShapeDtypeStruct((tokens, width), jnp.bfloat16), jax.ShapeDtypeStruct((2, tokens), jnp.float32)],
        compiler_params=pltpu.CompilerParams(vmem_limit_bytes=62 << 20),
    )(mixed, merge, inputs, gain, router, routes)


def finish_kernel(heads_ref, query_ref, key_ref, value_ref, gain_ref, inputs_ref, resid_grad_ref, out_ref, gain_grad_ref, *, eps):
    grads = dot_nt(heads_ref[0], query_ref[...]) + dot_nt(heads_ref[1], key_ref[...]) + dot_nt(heads_ref[2], value_ref[...])
    rows = inputs_ref[...].astype(jnp.float32)
    inverse = lax.rsqrt(jnp.mean(rows * rows, axis=1, keepdims=True) + eps)
    unit = rows * inverse
    @pl.when(pl.program_id(0) == 0)
    def _():
        gain_grad_ref[...] = jnp.zeros_like(gain_grad_ref)
    gain_grad_ref[...] += jnp.sum(grads * unit, axis=0, keepdims=True)
    scaled = grads * gain_ref[...]
    inner = jnp.mean(scaled * unit, axis=1, keepdims=True)
    out_ref[...] = resid_grad_ref[...] + inverse * (scaled - unit * inner)


def finish(head_grads, query, key, value, gain, inputs, resid_grad, eps, block=256):
    tokens, width = inputs.shape
    rows = pl.BlockSpec((block, width), lambda i: (i, 0))
    whole = lambda shape: pl.BlockSpec(shape, lambda i: (0, 0))
    return pl.pallas_call(
        partial(finish_kernel, eps=eps),
        grid=(tokens // block,),
        in_specs=[pl.BlockSpec((3, block, width), lambda i: (0, i, 0))] + [whole(query.shape)] * 3 + [whole(gain.shape), rows, rows],
        out_specs=[rows, whole((1, width))],
        out_shape=[jax.ShapeDtypeStruct((tokens, width), jnp.float32), jax.ShapeDtypeStruct((1, width), jnp.float32)],
        compiler_params=pltpu.CompilerParams(vmem_limit_bytes=62 << 20),
    )(head_grads, query, key, value, gain, inputs, resid_grad)


def weight_kernel(left_ref, right_ref, out_ref, turned):
    shards, part, _ = out_ref.shape
    @pl.when(pl.program_id(0) == 0)
    def _():
        turned[...] = left_ref[...].T
    right = right_ref[...]
    for shard in range(shards):
        grad = dot_nn(turned[shard * part:(shard + 1) * part, :], right)
        out_ref[shard] = grad.astype(jnp.bfloat16)


def weight_grads(left, right, shards):
    count, tokens, width = right.shape
    part = width // shards
    return pl.pallas_call(
        weight_kernel,
        grid=(count,),
        in_specs=[pl.BlockSpec((tokens, width), lambda i: (0, 0)), pl.BlockSpec((None, tokens, width), lambda i: (i, 0, 0))],
        out_specs=pl.BlockSpec((shards, part, width), lambda i: (0, i, 0)),
        out_shape=jax.ShapeDtypeStruct((shards, count * part, width), jnp.bfloat16),
        scratch_shapes=[pltpu.VMEM((width, tokens), jnp.bfloat16)],
        compiler_params=pltpu.CompilerParams(vmem_limit_bytes=62 << 20),
    )(left, right)


OWNER = "expert"
LINE = "shard"


def exchange(rows, bit):
    count = lax.axis_size(OWNER)
    return lax.ppermute(rows, OWNER, [(i, i ^ bit) for i in range(count)])


def shift(rows, step):
    count = lax.axis_size(LINE)
    return lax.ppermute(rows, LINE, [(i, (i + step) % count) for i in range(count)])


def gather_line(rows):
    count = lax.axis_size(LINE)
    me = lax.axis_index(LINE)
    out = jnp.zeros((count,) + rows.shape, rows.dtype)
    out = lax.dynamic_update_index_in_dim(out, rows, me, 0)
    for step in range(1, count):
        got = shift(rows, step)
        out = lax.dynamic_update_index_in_dim(out, got, (me - step) % count, 0)
    return out


def add_low(left, right):
    return (left.astype(jnp.float32) + right.astype(jnp.float32)).astype(jnp.bfloat16)


def side(bit):
    return (lax.axis_index(OWNER) // bit) % 2


def halve(stack, bit):
    half = stack.shape[1] // 2
    keep = lax.dynamic_slice_in_dim(stack, side(bit) * half, half, 1)
    send = lax.dynamic_slice_in_dim(stack, (1 - side(bit)) * half, half, 1)
    got = exchange(send, bit)
    return add_low(keep, got)


def line_sum(stack):
    count = lax.axis_size(LINE)
    place = lax.axis_index(LINE)
    total = lax.dynamic_index_in_dim(stack, place, 0, False).astype(jnp.float32)
    for step in range(1, count):
        send = lax.dynamic_index_in_dim(stack, (place + step) % count, 0, False)
        total = total + shift(send, step).astype(jnp.float32)
    return total.astype(jnp.bfloat16)


def grow(piece, bit):
    other = exchange(piece, bit)
    return jnp.where(
        side(bit) == 0, jnp.concatenate([piece, other]), jnp.concatenate([other, piece])
    )


def reduce_stack(stack, bits, cuts):
    stack = halve(stack, bits[0])
    cuts = [0] + cuts + [stack.shape[1]]
    parts = [stack[:, low:high] for low, high in zip(cuts, cuts[1:])]
    orders = [bits[1:], bits[:0:-1]]
    for level in range(len(bits) - 1):
        parts = [halve(part, order[level]) for part, order in zip(parts, orders)]
    sizes = [part.shape[1] for part in parts]
    piece = line_sum(jnp.concatenate(parts, axis=1))
    parts = [piece[: sizes[0]], piece[sizes[0] :]][: len(parts)]
    for level in reversed(range(len(bits) - 1)):
        parts = [grow(part, order[level]) for part, order in zip(parts, orders)]
    return grow(jnp.concatenate(parts), bits[0])


def scatter_sum(grads):
    shards, rows, width = grads.shape
    grads = grads.reshape(shards * rows, width)
    return lax.psum_scatter(grads, LINE, scatter_dimension=0, tiled=True)


def share_rows(rows):
    return lax.all_to_all(rows, OWNER, 0, 0, tiled=True)


def share_large(rows):
    return pltpu.with_memory_space_constraint(share_rows(rows), pltpu.HBM)


def local(
    inputs,
    norm_gain,
    query_weight,
    key_weight,
    value_weight,
    merge_weight,
    bias_table,
    expert_gain,
    router_weight,
    up_weight,
    down_weight,
    routes,
    cotangent,
):
    f32, bf16 = jnp.float32, jnp.bfloat16
    tokens, width = inputs.shape
    owners = lax.axis_size(OWNER)
    shards = lax.axis_size(LINE)
    me = lax.axis_index(OWNER)
    part = query_weight.shape[0]
    piece = part // owners
    local_heads = bias_table.shape[1]
    heads = local_heads * shards
    size = width // heads
    experts = router_weight.shape[1]
    local_count, _, hidden = up_weight.shape
    capacity = (5 * tokens * routes.shape[1] + 4 * experts - 1) // (4 * experts)
    capacity = -(-capacity // 16) * 16
    rows = owners * capacity
    assert local_count == 2 and hidden // shards == width

    router_at = 2 + local_heads + (-(2 + local_heads)) % 8

    def widen(block):
        return jnp.pad(block, ((0, 0), (0, width - block.shape[1])))

    def pack(gain_one, gain_two, table, router):
        head = jnp.concatenate([gain_one, gain_two], axis=0)
        gap = jnp.zeros((router_at - 2 - local_heads, width), bf16)
        return jnp.concatenate([widen(head), widen(table), gap, widen(router)], axis=0)

    small = pack(norm_gain[None], expert_gain[None], bias_table.T, router_weight.T)
    slices = [
        lax.dynamic_slice_in_dim(weight, me * piece, piece, 0)
        for weight in (query_weight, key_weight, value_weight)
    ]
    lined = gather_line(jnp.concatenate(slices + [small]))
    small_full = lined[:, 3 * piece :]
    bits = [1 << level for level in range(owners.bit_length() - 1)]
    pieces = []
    for index, order in enumerate((bits[1:], bits[:0:-1])):
        held = lined[index * shards // 2 : (index + 1) * shards // 2, : 3 * piece][None]
        for bit in order:
            got = exchange(held, bit)
            held = jnp.concatenate([held, got])
        pieces += [held, exchange(held, bits[0])]
    merge_full = lax.all_gather(merge_weight, LINE, axis=0, tiled=True)

    gain_one = small_full[:, 0, :part].reshape(1, width).astype(f32)
    gain_two = small_full[:, 1, :part].reshape(1, width).astype(f32)
    table_full = small_full[:, 2 : 2 + local_heads, :BUCKETS].reshape(heads, BUCKETS).astype(f32)
    router_full = small_full[:, router_at : router_at + experts, :part]
    router_full = router_full.transpose(1, 0, 2).reshape(experts, width)

    routes_line = routes.T
    base = (routes_line % local_count * owners + routes_line // local_count) * capacity
    slots = find_slots(routes_line, base, experts)
    cot_rows, joint, other = dispatch_all(
        slots, routes_line.astype(f32), cotangent, owners, capacity, local_count
    )
    other = share_rows(other).reshape(owners, local_count, capacity)

    owner = me.astype(jnp.int32).reshape(1)
    block = 256
    hot = bucket_hot(tokens)
    assert hot[block:, -1].all()
    near_hot = jnp.asarray((hot[:block] - hot[-1:]).T, dtype=f32)
    group = 128 // size
    near = jnp.dot(table_full, near_hot, precision=lax.Precision.HIGHEST)
    near = near.reshape(heads // group, group, block)
    query_full, key_full, value_full, low_one, queries, keys, values = project(
        owner, inputs, gain_one, pieces, epsilon, after=(near, router_full)
    )
    cot_in = share_large(cot_rows)
    attended, totals = attend(queries, keys, values, near, size, block)
    resid, low_two, gates = settle(
        attended, merge_full, inputs, gain_two, router_full, routes_line, epsilon
    )

    send = dispatch(slots, low_two, 0, rows).reshape(owners, capacity, width)
    rows_in = share_large(send)
    joint = dispatch_into(slots, low_two, rows, joint)
    joint_in = share_large(joint)
    others = [other[:, index].reshape(1, rows) for index in range(local_count)]
    act, slope, first_down, grad_in = expert_first(
    owner, rows_in, cot_in, others[0], router_full, up_weight, 0, local_count, shards,
    )
    first_sum = scatter_sum(first_down)
    first_made, pair = expert_second(rows_in, grad_in, act, slope, up_weight, down_weight, 0, owners, shards, 2 * width)
    act, slope, pair, grad_in = expert_first(
        owner, joint_in, joint_in, others[1], router_full, up_weight, 1, local_count, shards,
        into=pair,
    )
    pair_sum = scatter_sum(pair)
    second_made, last_up = expert_second(
        joint_in, grad_in, act, slope, up_weight, down_weight, 1, owners, shards, width
    )
    last_sum = scatter_sum(last_up)
    returned = share_rows(first_made)
    result, inner, part_grads = combine_part(slots, gates, resid, cotangent, returned)
    returned = share_rows(second_made)
    output, logit_grad = combine_out(
        slots, routes_line, gates, result, inner, cotangent, returned
    )
    router_wide = jnp.pad(router_full, ((0, 128 - experts), (0, 0)))
    resid_grad, branch, mixed_grad, gain_grad = combine_back(
        slots, logit_grad, router_wide, gain_two, resid, cotangent, merge_full,
        part_grads, returned, epsilon
    )
    router_grad = jnp.einsum("te,ti->ei", logit_grad, low_two, preferred_element_type=f32)
    merge_grad = weight_grads(attended, branch[None], shards)
    head_grads, distances = attend_back(
        queries, keys, values, mixed_grad, attended, totals, near, size, block
    )
    close_sums = distances[:, :group].reshape(heads, block)
    far_sums = jnp.sum(distances[:, group:].reshape(heads, block), axis=1)
    table_grad = jnp.dot(close_sums, jnp.asarray(hot[:block]), precision=lax.Precision.HIGHEST)
    table_grad = table_grad + far_sums[:, None] * jnp.asarray(hot[-1:])
    head_sums = weight_grads(low_one, head_grads, shards)
    input_gradient, norm_grad = finish(
        head_grads, query_full, key_full, value_full, gain_one, inputs, resid_grad, epsilon
    )
    small_grad = jax.vmap(pack)(
        norm_grad.reshape(shards, 1, part).astype(bf16),
        gain_grad.reshape(shards, 1, part).astype(bf16),
        table_grad.reshape(shards, local_heads, BUCKETS).astype(bf16),
        router_grad[:experts].reshape(experts, shards, part).transpose(1, 0, 2).astype(bf16),
    )
    head_sums = reduce_stack(head_sums, bits, [5 * part // 6]).astype(f32)
    spare = -small_grad.shape[1] % (8 * owners)
    small_grad = jnp.pad(small_grad, ((0, 0), (0, spare), (0, 0)))
    rest_sums = jnp.concatenate([merge_grad, small_grad], axis=1)
    rest_sums = reduce_stack(rest_sums, bits[:1] + bits[:0:-1], []).astype(f32)
    small_sum = rest_sums[part:]
    return (
        output,
        input_gradient,
        small_sum[0, :part],
        head_sums[:part],
        head_sums[part : 2 * part],
        head_sums[2 * part :],
        rest_sums[:part],
        small_sum[2 : 2 + local_heads, :BUCKETS].T,
        small_sum[1, :part],
        small_sum[router_at : router_at + experts, :part].T,
        jnp.stack([pair_sum[:width].astype(f32), last_sum.astype(f32)]),
        jnp.stack([first_sum.astype(f32), pair_sum[width:].astype(f32)]),
    )


def solution(mesh):
    in_specs = (
        P((OWNER, LINE), None),
        P(LINE),
        P(LINE, None),
        P(LINE, None),
        P(LINE, None),
        P(LINE, None),
        P(None, LINE),
        P(LINE),
        P(LINE, None),
        P(OWNER, None, None),
        P(OWNER, None, None),
        P((OWNER, LINE), None),
        P((OWNER, LINE), None),
    )
    out_specs = (
        P((OWNER, LINE), None),
        P((OWNER, LINE), None),
        P(LINE),
        P(LINE, None),
        P(LINE, None),
        P(LINE, None),
        P(LINE, None),
        P(None, LINE),
        P(LINE),
        P(LINE, None),
        P(OWNER, None, LINE),
        P(OWNER, LINE, None),
    )

    return jax.shard_map(local, mesh=mesh, in_specs=in_specs, out_specs=out_specs, check_vma=False)
```

```python
from functools import partial, reduce

import jax
import jax.numpy as jnp
import numpy as np
from jax import lax
from jax.experimental import pallas as pl
from jax.experimental.pallas import tpu as pltpu
from jax.sharding import PartitionSpec as P


BUCKETS = 32
MAX_DIST = 128


epsilon = 1e-06
masked_score = -1e30


def bucket_hot(length):
    distance = np.arange(length)
    half_count = BUCKETS // 2
    clipped = np.maximum(distance, half_count)
    spread = np.log(clipped / half_count) / np.log(MAX_DIST / half_count) * (BUCKETS - half_count)
    far_bucket = np.minimum(half_count + np.floor(spread).astype(np.int32), BUCKETS - 1)
    bucket = np.where(distance < half_count, distance, far_bucket)
    return (bucket[:, None] == np.arange(BUCKETS)[None, :]).astype(np.float32)


def dot_nt(a, b):
    return lax.dot_general(a, b, (((1,), (1,)), ((), ())), preferred_element_type=jnp.float32)


def dot_nn(a, b):
    return lax.dot_general(a, b, (((1,), (0,)), ((), ())), preferred_element_type=jnp.float32)


def dot_tn(a, b):
    return lax.dot_general(a, b, (((0,), (0,)), ((), ())), preferred_element_type=jnp.float32)


def slot_kernel(routes_ref, base_ref, slots_ref, *, experts):
    tokens = routes_ref.shape[1]
    expert = lax.broadcasted_iota(jnp.int32, (experts, tokens), 0)
    hits = [routes_ref[c:c + 1, :] == expert for c in range(2)]
    hot = jnp.where(hits[0] | hits[1], 1.0, 0.0).astype(jnp.bfloat16)
    earlier = lax.broadcasted_iota(jnp.int32, (tokens, tokens), 0)
    later = lax.broadcasted_iota(jnp.int32, (tokens, tokens), 1)
    before = jnp.where(earlier < later, 1.0, 0.0).astype(jnp.bfloat16)
    counts = dot_nn(hot, before)
    for c in range(2):
        position = jnp.sum(jnp.where(hits[c], counts, 0.0), axis=0, keepdims=True)
        slots_ref[c:c + 1, :] = base_ref[c:c + 1, :] + position.astype(jnp.int32)


def find_slots(routes, base, experts):
    return pl.pallas_call(
        partial(slot_kernel, experts=experts),
        out_shape=jax.ShapeDtypeStruct(routes.shape, jnp.int32),
    )(routes, base)


def dispatch_kernel(slots_ref, rows_ref, *refs, start):
    out_ref = refs[-1]
    block, tokens = out_ref.shape[0], rows_ref.shape[0]
    slot = lax.broadcasted_iota(jnp.int32, (block, tokens), 0) + (pl.program_id(0) * block + start)
    hot = jnp.where((slot == slots_ref[0:1, :]) | (slot == slots_ref[1:2, :]), 1.0, 0.0)
    out_ref[...] = dot_nn(hot.astype(jnp.bfloat16), rows_ref[...]).astype(out_ref.dtype)


def dispatch(slots, rows, start, count, after=(), block=256):
    _, width = rows.shape
    whole = lambda shape: pl.BlockSpec(shape, lambda i: (0, 0))
    return pl.pallas_call(
        partial(dispatch_kernel, start=start),
        grid=(count // block,),
        in_specs=[whole(slots.shape), whole(rows.shape)] + [pl.BlockSpec(memory_space=pl.ANY)] * len(after),
        out_specs=pl.BlockSpec((block, width), lambda i: (i, 0)),
        out_shape=jax.ShapeDtypeStruct((count, width), rows.dtype),
    )(slots, rows, *after)


def dispatch_both_kernel(slots_ref, rows_ref, cot_ref, out_ref, *, start):
    block, tokens = out_ref.shape[2], rows_ref.shape[0]
    slot = lax.broadcasted_iota(jnp.int32, (block, tokens), 0) + (pl.program_id(0) * block + start)
    hot = jnp.where((slot == slots_ref[0:1, :]) | (slot == slots_ref[1:2, :]), 1.0, 0.0)
    hot = hot.astype(jnp.bfloat16)
    out_ref[0, 0] = dot_nn(hot, rows_ref[...]).astype(out_ref.dtype)
    out_ref[0, 1] = dot_nn(hot, cot_ref[...]).astype(out_ref.dtype)


def dispatch_both(slots, rows, cot, start, owners, capacity):
    width = rows.shape[1]
    whole = lambda shape: pl.BlockSpec(shape, lambda i: (0, 0))
    return pl.pallas_call(
        partial(dispatch_both_kernel, start=start),
        grid=(owners,),
        in_specs=[whole(slots.shape), whole(rows.shape), whole(cot.shape)],
        out_specs=pl.BlockSpec((1, 2, capacity, width), lambda i: (i, 0, 0, 0)),
        out_shape=jax.ShapeDtypeStruct((owners, 2, capacity, width), rows.dtype),
    )(slots, rows, cot)


def dispatch_first_kernel(slots_ref, routes_ref, rows_ref, out_ref, other_ref, *, owners, capacity):
    block, tokens = other_ref.shape[2], rows_ref.shape[0]
    row = lax.broadcasted_iota(jnp.int32, (block, tokens), 0)
    slot = row + pl.program_id(0) * capacity
    slot = slot + jnp.where(row >= capacity, (owners - 1) * capacity, 0)
    hits = [slot == slots_ref[c:c + 1, :] for c in range(2)]
    hot = jnp.where(hits[0] | hits[1], 1.0, 0.0)[:capacity]
    out_ref[0] = dot_nn(hot.astype(jnp.bfloat16), rows_ref[...]).astype(out_ref.dtype)
    other = jnp.where(hits[0], routes_ref[1:2, :], jnp.where(hits[1], routes_ref[0:1, :], 0.0))
    column = jnp.sum(other, axis=1, keepdims=True)
    other_ref[0] = jnp.broadcast_to(column, (block, 128)).T[0:1, :]


def dispatch_first(slots, routes, rows, owners, capacity):
    width = rows.shape[1]
    whole = lambda shape: pl.BlockSpec(shape, lambda i: (0, 0))
    return pl.pallas_call(
        partial(dispatch_first_kernel, owners=owners, capacity=capacity),
        grid=(owners,),
        in_specs=[whole(slots.shape), whole(routes.shape), whole(rows.shape)],
        out_specs=[pl.BlockSpec((1, capacity, width), lambda i: (i, 0, 0)), pl.BlockSpec((1, 1, 2 * capacity), lambda i: (i, 0, 0))],
        out_shape=[jax.ShapeDtypeStruct((owners, capacity, width), rows.dtype), jax.ShapeDtypeStruct((owners, 1, 2 * capacity), jnp.float32)],
    )(slots, routes, rows)


def gelu_pair(v):
    c = np.float32(np.sqrt(2.0 / np.pi))
    a = np.float32(0.044715)
    square = v * v
    half = 0.5 * jnp.tanh(v * (c * a * square + c)) + 0.5
    value = v * half
    slope = half + value * (1.0 - half) * (6.0 * c * a * square + 2.0 * c)
    return value, slope


def first_kernel(owner_ref, rows_ref, cot_ref, other_ref, router_ref, up_ref, *refs, chunk, index, local_count):
    act_ref, slope_ref, down_grad_ref, grad_ref = refs[-4:]
    owners, capacity, width = rows_ref.shape
    rows = owners * capacity
    @pl.when(pl.program_id(0) == 0)
    def _():
        logits = dot_nt(router_ref[...], rows_ref[...].reshape(rows, width))
        expert = lax.broadcasted_iota(jnp.int32, logits.shape, 0)
        mine = owner_ref[0] * local_count + index
        own = jnp.sum(jnp.where(expert == mine, logits, 0.0), axis=0, keepdims=True)
        other = other_ref[...].astype(jnp.int32)
        other = jnp.sum(jnp.where(expert == other, logits, 0.0), axis=0, keepdims=True)
        top = jnp.maximum(own, other)
        own = jnp.exp(own - top)
        gate = own / (own + jnp.exp(other - top))
        column = jnp.broadcast_to(gate, (128, rows)).T
        for start in range(0, width, 128):
            part = cot_ref[:, :, start:start + 128].reshape(rows, 128).astype(jnp.float32) * column
            grad_ref[:, start:start + 128] = part.astype(jnp.bfloat16)
    up = up_ref[0]
    for start in range(0, rows, chunk):
        part = rows_ref[start // capacity:(start + chunk) // capacity].reshape(chunk, width)
        pre = dot_nn(part, up)
        value, slope = gelu_pair(pre)
        act_ref[start:start + chunk, :] = value.astype(jnp.bfloat16)
        slope_ref[start:start + chunk, :] = slope.astype(jnp.bfloat16)
    down_grad_ref[0] = dot_tn(act_ref[...], grad_ref[...]).astype(jnp.bfloat16)


def arrived_spec(arrived, which):
    if arrived.ndim == 3:
        return pl.BlockSpec(arrived.shape, lambda i: (0, 0, 0))
    owners, _, capacity, width = arrived.shape
    return pl.BlockSpec((owners, None, capacity, width), lambda i: (0, which, 0, 0))


def expert_first(owner, rows_in, cot, other, router, up, index, local_count, shards, into=None, after=()):
    owners, capacity, width = rows_in.shape[0], *rows_in.shape[-2:]
    rows = owners * capacity
    hidden = up.shape[2]
    tile = hidden // shards
    chunk = rows // 2
    fixed = pl.BlockSpec((rows, width), lambda i: (0, 0))
    column = pl.BlockSpec((rows, tile), lambda i: (0, i))
    operands = [owner, rows_in, cot, other, router, up]
    place, aliases = 0, {}
    grad_shape = jax.ShapeDtypeStruct((shards, tile, width), jnp.bfloat16)
    if into is not None:
        aliases = {len(operands): 2}
        operands.append(into)
        place, grad_shape = 2, jax.ShapeDtypeStruct(into.shape, into.dtype)
    operands += list(after)
    return pl.pallas_call(
        partial(first_kernel, chunk=chunk, index=index, local_count=local_count),
        grid=(shards,),
        in_specs=[
            pl.BlockSpec(memory_space=pltpu.SMEM),
            arrived_spec(rows_in, 0),
            arrived_spec(cot, 1),
            pl.BlockSpec((1, rows), lambda i: (0, 0)),
            pl.BlockSpec(router.shape, lambda i: (0, 0)),
            pl.BlockSpec((1, width, tile), lambda i: (index, 0, i)),
        ]
        + [pl.BlockSpec(memory_space=pl.ANY)] * (len(operands) - 6),
        out_specs=[column, column, pl.BlockSpec((1, tile, width), lambda i: (i, place, 0)), fixed],
        out_shape=[jax.ShapeDtypeStruct((rows, hidden), jnp.bfloat16)] * 2 + [grad_shape, jax.ShapeDtypeStruct((rows, width), jnp.bfloat16)],
        input_output_aliases=aliases,
        compiler_params=pltpu.CompilerParams(vmem_limit_bytes=62 << 20),
    )(*operands)


def second_kernel(rows_ref, grad_ref, act_ref, slope_ref, up_ref, down_ref, *refs):
    made_ref, up_grad_ref, turned, made_acc, back_acc = refs[-5:]
    step = pl.program_id(0)
    owners, _, capacity, width = made_ref.shape
    @pl.when(step == 0)
    def _():
        turned[...] = rows_ref[...].reshape(grad_ref.shape).T
    up = up_ref[0]
    down = down_ref[0]
    grads = dot_nt(grad_ref[...], down)
    low = (slope_ref[...].astype(jnp.float32) * grads).astype(jnp.bfloat16)
    up_grad_ref[0] = dot_nn(turned[...], low).astype(jnp.bfloat16)
    back = dot_nt(low, up)
    made = dot_nn(act_ref[...], down)
    last = pl.num_programs(0) - 1
    @pl.when(step == 0)
    def _():
        made_acc[...] = made
        back_acc[...] = back
    @pl.when((step > 0) & (step < last))
    def _():
        made_acc[...] += made
        back_acc[...] += back
    @pl.when(step == last)
    def _():
        made_ref[:, 0] = (made_acc[...] + made).astype(jnp.bfloat16).reshape(owners, capacity, width)
        made_ref[:, 1] = (back_acc[...] + back).astype(jnp.bfloat16).reshape(owners, capacity, width)


def expert_second(rows_in, grad, act, slope, up, down, index, owners, shards, wide, after=()):
    rows, width = grad.shape
    hidden = up.shape[2]
    tile = hidden // shards
    fixed = pl.BlockSpec((rows, width), lambda i: (0, 0))
    column = pl.BlockSpec((rows, tile), lambda i: (0, i))
    made_shape = (owners, 2, rows // owners, width)
    return pl.pallas_call(
        second_kernel,
        grid=(shards,),
        in_specs=[arrived_spec(rows_in, 0), fixed, column, column, pl.BlockSpec((1, width, tile), lambda i: (index, 0, i)), pl.BlockSpec((1, tile, width), lambda i: (index, i, 0))]
        + [pl.BlockSpec(memory_space=pl.ANY)] * len(after),
        out_specs=[pl.BlockSpec(made_shape, lambda i: (0, 0, 0, 0)), pl.BlockSpec((1, width, tile), lambda i: (i, 0, 0))],
        out_shape=[jax.ShapeDtypeStruct(made_shape, jnp.bfloat16), jax.ShapeDtypeStruct((shards, wide, tile), jnp.bfloat16)],
        scratch_shapes=[pltpu.VMEM((width, rows), jnp.bfloat16), pltpu.VMEM((rows, width), jnp.float32), pltpu.VMEM((rows, width), jnp.float32)],
        compiler_params=pltpu.CompilerParams(vmem_limit_bytes=62 << 20),
    )(rows_in, grad, act, slope, up, down, *after)


def slope_kernel(rows_ref, grad_ref, slope_ref, down_ref, into_ref, low_ref, up_grad_ref, turned):
    del into_ref
    @pl.when(pl.program_id(0) == 0)
    def _():
        turned[...] = rows_ref[...].reshape(grad_ref.shape).T
    grads = dot_nt(grad_ref[...], down_ref[0])
    low = (slope_ref[...].astype(jnp.float32) * grads).astype(jnp.bfloat16)
    low_ref[...] = low
    up_grad_ref[0] = dot_nn(turned[...], low).astype(jnp.bfloat16)


def expert_slope(rows_in, grad, slope, down, index, shards, into, place):
    rows, width = grad.shape
    hidden = slope.shape[1]
    tile = hidden // shards
    fixed = pl.BlockSpec((rows, width), lambda i: (0, 0))
    column = pl.BlockSpec((rows, tile), lambda i: (0, i))
    return pl.pallas_call(
        slope_kernel,
        grid=(shards,),
        in_specs=[arrived_spec(rows_in, 0), fixed, column, pl.BlockSpec((1, tile, width), lambda i: (index, i, 0)), pl.BlockSpec(memory_space=pl.ANY)],
        out_specs=[column, pl.BlockSpec((1, width, tile), lambda i: (i, place, 0))],
        out_shape=[jax.ShapeDtypeStruct((rows, hidden), jnp.bfloat16), jax.ShapeDtypeStruct(into.shape, into.dtype)],
        input_output_aliases={4: 1},
        scratch_shapes=[pltpu.VMEM((width, rows), jnp.bfloat16)],
        compiler_params=pltpu.CompilerParams(vmem_limit_bytes=62 << 20),
    )(rows_in, grad, slope, down, into)


def last_kernel(act_ref, low_ref, up_ref, down_ref, made_ref, made_acc, back_acc):
    step = pl.program_id(0)
    owners, _, capacity, width = made_ref.shape
    back = dot_nt(low_ref[...], up_ref[0])
    made = dot_nn(act_ref[...], down_ref[0])
    last = pl.num_programs(0) - 1
    @pl.when(step == 0)
    def _():
        made_acc[...] = made
        back_acc[...] = back
    @pl.when((step > 0) & (step < last))
    def _():
        made_acc[...] += made
        back_acc[...] += back
    @pl.when(step == last)
    def _():
        made_ref[:, 0] = (made_acc[...] + made).astype(jnp.bfloat16).reshape(owners, capacity, width)
        made_ref[:, 1] = (back_acc[...] + back).astype(jnp.bfloat16).reshape(owners, capacity, width)


def expert_last(act, low, up, down, index, owners, shards):
    rows, hidden = act.shape
    width = up.shape[1]
    tile = hidden // shards
    column = pl.BlockSpec((rows, tile), lambda i: (0, i))
    made_shape = (owners, 2, rows // owners, width)
    return pl.pallas_call(
        last_kernel,
        grid=(shards,),
        in_specs=[column, column, pl.BlockSpec((1, width, tile), lambda i: (index, 0, i)), pl.BlockSpec((1, tile, width), lambda i: (index, i, 0))],
        out_specs=pl.BlockSpec(made_shape, lambda i: (0, 0, 0, 0)),
        out_shape=jax.ShapeDtypeStruct(made_shape, jnp.bfloat16),
        scratch_shapes=[pltpu.VMEM((rows, width), jnp.float32), pltpu.VMEM((rows, width), jnp.float32)],
        compiler_params=pltpu.CompilerParams(vmem_limit_bytes=62 << 20),
    )(act, low, up, down)


def spread(row, block):
    return jnp.broadcast_to(row, (128, block)).T


def pick(slots, lane, back_refs, first=0):
    picked = None
    for index, back_ref in enumerate(back_refs, first):
        owners, capacity, width = back_ref.shape
        half = owners * capacity
        hots = []
        for start in range(index * half, (index + 1) * half, 128):
            hit = reduce(jnp.logical_or, [slot == lane + start for slot in slots])
            hots.append(jnp.where(hit, 1.0, 0.0).astype(jnp.bfloat16))
        part = dot_nn(jnp.concatenate(hots, axis=1), back_ref[...].reshape(half, width))
        picked = part if picked is None else picked + part
    return picked


def part_kernel(slots_ref, gates_ref, resid_ref, cot_ref, made_ref, back_ref, result_ref, inner_ref, grads_ref):
    block = result_ref.shape[0]
    lane = lax.broadcasted_iota(jnp.int32, (block, 128), 1)
    cot = cot_ref[...].astype(jnp.float32)
    result = resid_ref[...]
    inner = jnp.zeros((block, 128), jnp.float32)
    slots = [spread(slots_ref[c:c + 1, :], block) for c in range(2)]
    for c in range(2):
        picked = pick([slots[c]], lane, [made_ref])
        result = result + spread(gates_ref[c:c + 1, :], block)[:, 0:1] * picked
        inner = inner + jnp.where(lane == c, jnp.sum(cot * picked, axis=1, keepdims=True), 0.0)
    result_ref[...] = result
    inner_ref[...] = inner
    grads_ref[...] = pick(slots, lane, [back_ref])


def combine_part(slots, gates, resid, cot, returned, block=256):
    tokens, width = resid.shape
    small = pl.BlockSpec((2, block), lambda i: (0, i))
    rows = pl.BlockSpec((block, width), lambda i: (i, 0))
    wide = jax.ShapeDtypeStruct((tokens, width), jnp.float32)
    return pl.pallas_call(
        part_kernel,
        grid=(tokens // block,),
        in_specs=[small, small, rows, rows, returned_spec(returned, 0), returned_spec(returned, 1)],
        out_specs=[rows, pl.BlockSpec((block, 128), lambda i: (i, 0)), rows],
        out_shape=[wide, jax.ShapeDtypeStruct((tokens, 128), jnp.float32), wide],
        compiler_params=pltpu.CompilerParams(vmem_limit_bytes=62 << 20),
    )(slots, gates, resid, cot, returned, returned)


def out_kernel(slots_ref, routes_ref, gates_ref, result_ref, inner_ref, cot_ref, made_ref, out_ref, logit_ref):
    block = out_ref.shape[0]
    lane = lax.broadcasted_iota(jnp.int32, (block, 128), 1)
    cot = cot_ref[...].astype(jnp.float32)
    result = result_ref[...]
    gates, inner = [], []
    for c in range(2):
        slot = spread(slots_ref[c:c + 1, :], block)
        gate = spread(gates_ref[c:c + 1, :], block)[:, 0:1]
        picked = pick([slot], lane, [made_ref], 1)
        result = result + gate * picked
        gates.append(gate)
        inner.append(inner_ref[:, c:c + 1] + jnp.sum(cot * picked, axis=1, keepdims=True))
    out_ref[...] = result.astype(out_ref.dtype)
    middle = gates[0] * inner[0] + gates[1] * inner[1]
    logit = jnp.zeros((block, 128), jnp.float32)
    for c in range(2):
        route = spread(routes_ref[c:c + 1, :], block)
        logit = logit + jnp.where(route == lane, gates[c] * (inner[c] - middle), 0.0)
    logit_ref[...] = logit.astype(jnp.bfloat16)


def returned_spec(returned, which):
    owners, _, capacity, width = returned.shape
    return pl.BlockSpec((owners, None, capacity, width), lambda i: (0, which, 0, 0))


def combine_out(slots, routes, gates, result, inner, cot, returned, block=256):
    tokens, width = result.shape
    small = pl.BlockSpec((2, block), lambda i: (0, i))
    rows = pl.BlockSpec((block, width), lambda i: (i, 0))
    return pl.pallas_call(
        out_kernel,
        grid=(tokens // block,),
        in_specs=[small, small, small, rows, pl.BlockSpec((block, 128), lambda i: (i, 0)), rows, returned_spec(returned, 0)],
        out_specs=[rows, pl.BlockSpec((block, 128), lambda i: (i, 0))],
        out_shape=[jax.ShapeDtypeStruct((tokens, width), jnp.bfloat16), jax.ShapeDtypeStruct((tokens, 128), jnp.bfloat16)],
        compiler_params=pltpu.CompilerParams(vmem_limit_bytes=62 << 20),
    )(slots, routes, gates, result, inner, cot, returned)


def back_kernel(slots_ref, logit_ref, router_ref, gain_ref, resid_ref, cot_ref, merge_ref, part_ref, back_ref, grad_ref, low_ref, mixed_ref, gain_grad_ref, *, eps):
    block, _ = grad_ref.shape
    lane = lax.broadcasted_iota(jnp.int32, (block, 128), 1)
    grads = part_ref[...] + pick([spread(slots_ref[c:c + 1, :], block) for c in range(2)], lane, [back_ref], 1)
    grads = grads + dot_nn(logit_ref[...], router_ref[...])
    resid = resid_ref[...]
    inverse = lax.rsqrt(jnp.mean(resid * resid, axis=1, keepdims=True) + eps)
    unit = resid * inverse
    @pl.when(pl.program_id(0) == 0)
    def _():
        gain_grad_ref[...] = jnp.zeros_like(gain_grad_ref)
    gain_grad_ref[...] += jnp.sum(grads * unit, axis=0, keepdims=True)
    scaled = grads * gain_ref[...]
    inner = jnp.mean(scaled * unit, axis=1, keepdims=True)
    total = cot_ref[...].astype(jnp.float32) + inverse * (scaled - unit * inner)
    grad_ref[...] = total
    low = total.astype(jnp.bfloat16)
    low_ref[...] = low
    mixed_ref[...] = dot_nt(low, merge_ref[...]).astype(jnp.bfloat16)


def combine_back(slots, logit, router, gain, resid, cot, merge, part, returned, eps, block=256):
    tokens, width = resid.shape
    rows = pl.BlockSpec((block, width), lambda i: (i, 0))
    whole = lambda shape: pl.BlockSpec(shape, lambda i: (0, 0))
    low = jax.ShapeDtypeStruct((tokens, width), jnp.bfloat16)
    return pl.pallas_call(
        partial(back_kernel, eps=eps),
        grid=(tokens // block,),
        in_specs=[pl.BlockSpec((2, block), lambda i: (0, i)), pl.BlockSpec((block, 128), lambda i: (i, 0)), whole(router.shape), whole(gain.shape), rows, rows, whole(merge.shape), rows, returned_spec(returned, 1)],
        out_specs=[rows, rows, rows, whole((1, width))],
        out_shape=[jax.ShapeDtypeStruct((tokens, width), jnp.float32), low, low, jax.ShapeDtypeStruct((1, width), jnp.float32)],
        compiler_params=pltpu.CompilerParams(vmem_limit_bytes=62 << 20),
    )(slots, logit, router, gain, resid, cot, merge, part, returned)


def near_tiles(near_ref, head, block):
    spread = jnp.broadcast_to(near_ref[0, head:head + 1, :], (block, block))
    spread = pltpu.roll(spread, 0, 1, stride=1, stride_axis=0)
    key_at = lax.broadcasted_iota(jnp.int32, (block, block), 0)
    query_at = lax.broadcasted_iota(jnp.int32, (block, block), 1)
    return (jnp.where(query_at >= key_at, spread, masked_score), jnp.where(query_at < key_at, spread, 0.0), query_at < key_at)


def diagonal_sums(tile):
    block = tile.shape[1]
    total = tile[:8]
    for start in range(8, block, 8):
        total = total + pltpu.roll(tile[start:start + 8], block - start, 1)
    row = lax.broadcasted_iota(jnp.int32, total.shape, 0)
    for step in (1, 2, 4):
        total = jnp.where((row & step) != 0, pltpu.roll(total, block - step, 1), total)
    return jnp.sum(total, axis=0, keepdims=True)


def head_part(rows, head, size):
    lane = lax.broadcasted_iota(jnp.int32, rows.shape, 1)
    return jnp.where((lane >= head * size) & (lane < (head + 1) * size), rows, jnp.zeros_like(rows))


def attend_kernel(query_ref, key_ref, value_ref, near_ref, out_ref, total_ref, *, block, size, scale):
    length, lanes = query_ref.shape
    heads = lanes // size
    count = length // block
    flipped = value_ref[...].T
    tiles = [near_tiles(near_ref, head, block) for head in range(heads)]
    for i in range(count):
        rows = pl.ds(i * block, block)
        query_rows = query_ref[rows, :] * jnp.bfloat16(scale)
        parts = []
        for head in range(heads):
            query_part = head_part(query_rows, head, size)
            scores = []
            for j in range(i + 1):
                tile = dot_nt(key_ref[pl.ds(j * block, block), :], query_part)
                if j == i:
                    tile = tile + tiles[head][0]
                elif j == i - 1:
                    tile = tile + tiles[head][1]
                scores.append(tile)
            top = reduce(jnp.maximum, scores)
            top = jnp.max(top, axis=0, keepdims=True)
            mixed = None
            total = None
            for j in range(i + 1):
                weights = jnp.exp(scores[j] - top)
                sums = jnp.sum(weights, axis=0, keepdims=True)
                part = dot_nn(flipped[head * size:(head + 1) * size, j * block:(j + 1) * block], weights.astype(jnp.bfloat16))
                mixed = part if mixed is None else mixed + part
                total = sums if total is None else total + sums
            parts.append(mixed / total)
            total_ref[0, head:head + 1, rows] = top + jnp.log(total)
        out_ref[rows, :] = jnp.concatenate(parts, axis=0).T.astype(out_ref.dtype)


def attend(queries, keys, values, near, size, block):
    length, width = queries.shape
    lanes = 128
    heads = lanes // size
    groups = width // lanes
    column = pl.BlockSpec((length, lanes), lambda g: (0, g))
    head_rows = pl.BlockSpec((1, heads, block), lambda g: (g, 0, 0))
    return pl.pallas_call(
        partial(attend_kernel, block=block, size=size, scale=size ** -0.5),
        grid=(groups,),
        in_specs=[column, column, column, head_rows],
        out_specs=[column, pl.BlockSpec((1, heads, length), lambda g: (g, 0, 0))],
        out_shape=[jax.ShapeDtypeStruct((length, width), jnp.bfloat16), jax.ShapeDtypeStruct((groups, heads, length), jnp.float32)],
        compiler_params=pltpu.CompilerParams(vmem_limit_bytes=62 << 20),
    )(queries, keys, values, near)


def attend_back_kernel(query_ref, key_ref, value_ref, grad_ref, out_ref, total_ref, near_ref, grads_ref, dist_ref, key_acc, value_acc, *, block, size, scale):
    length, lanes = query_ref.shape
    heads = lanes // size
    count = length // block
    flipped = key_ref[...].T
    tiles = [near_tiles(near_ref, head, block) for head in range(heads)]
    near_acc = [None] * heads
    far_acc = [None] * heads
    for i in range(count):
        rows = pl.ds(i * block, block)
        query_rows = query_ref[rows, :] * jnp.bfloat16(scale)
        grad_rows = grad_ref[rows, :]
        products = (grad_rows.astype(jnp.float32) * out_ref[rows, :].astype(jnp.float32)).T
        query_parts = [head_part(query_rows, head, size) for head in range(heads)]
        grad_parts = [head_part(grad_rows, head, size) for head in range(heads)]
        inner = [jnp.sum(products[head * size:(head + 1) * size], axis=0, keepdims=True) for head in range(heads)]
        query_stack = jnp.concatenate(query_parts, axis=0)
        grad_stack = jnp.concatenate(grad_parts, axis=0)
        query_grads = [None] * heads
        for j in range(i + 1):
            cols = pl.ds(j * block, block)
            weight_list = []
            score_list = []
            for head in range(heads):
                tile = dot_nt(key_ref[cols, :], query_parts[head])
                if j == i:
                    tile = tile + tiles[head][0]
                elif j == i - 1:
                    tile = tile + tiles[head][1]
                weights = jnp.exp(tile - total_ref[0, head:head + 1, rows])
                grads = dot_nt(value_ref[cols, :], grad_parts[head])
                score_grads = weights * (grads - inner[head])
                low = score_grads.astype(jnp.bfloat16)
                weight_list.append(weights.astype(jnp.bfloat16))
                score_list.append(low)
                part = dot_nn(flipped[head * size:(head + 1) * size, j * block:(j + 1) * block], low)
                query_grads[head] = part if query_grads[head] is None else query_grads[head] + part
                if j == i:
                    near_acc[head] = score_grads if near_acc[head] is None else near_acc[head] + score_grads
                else:
                    far = score_grads
                    if j == i - 1:
                        close = jnp.where(tiles[head][2], score_grads, 0.0)
                        near_acc[head] = near_acc[head] + close
                        far = score_grads - close
                    far = jnp.sum(far, axis=0, keepdims=True)
                    far_acc[head] = far if far_acc[head] is None else far_acc[head] + far
            value_part = dot_nn(jnp.concatenate(weight_list, axis=1), grad_stack)
            key_part = dot_nn(jnp.concatenate(score_list, axis=1), query_stack)
            if j == i:
                value_acc[cols, :] = value_part
                key_acc[cols, :] = key_part
            else:
                value_acc[cols, :] += value_part
                key_acc[cols, :] += key_part
        grads_ref[0, rows, :] = (jnp.concatenate(query_grads, axis=0) * scale).T.astype(grads_ref.dtype)
    grads_ref[1] = key_acc[...].astype(grads_ref.dtype)
    grads_ref[2] = value_acc[...].astype(grads_ref.dtype)
    for head in range(heads):
        dist_ref[0, head:head + 1, :] = diagonal_sums(near_acc[head])
        dist_ref[0, heads + head:heads + head + 1, :] = far_acc[head]


def attend_back(queries, keys, values, grads, outs, totals, near, size, block):
    length, width = queries.shape
    lanes = 128
    heads = lanes // size
    groups = width // lanes
    column = pl.BlockSpec((length, lanes), lambda g: (0, g))
    head_rows = pl.BlockSpec((1, heads, block), lambda g: (g, 0, 0))
    return pl.pallas_call(
        partial(attend_back_kernel, block=block, size=size, scale=size ** -0.5),
        grid=(groups,),
        in_specs=[column] * 5 + [pl.BlockSpec((1, heads, length), lambda g: (g, 0, 0)), head_rows],
        out_specs=[pl.BlockSpec((3, length, lanes), lambda g: (0, 0, g)), pl.BlockSpec((1, 2 * heads, block), lambda g: (g, 0, 0))],
        out_shape=[jax.ShapeDtypeStruct((3, length, width), jnp.bfloat16), jax.ShapeDtypeStruct((groups, 2 * heads, block), jnp.float32)],
        scratch_shapes=[pltpu.VMEM((length, lanes), jnp.float32)] * 2,
        compiler_params=pltpu.CompilerParams(vmem_limit_bytes=62 << 20),
    )(queries, keys, values, grads, outs, totals, near)


def reverse_bits(value, count):
    out = value * 0
    for level in range(count):
        out = out * 2 + (value >> level) % 2
    return out


def project_kernel(owner_ref, inputs_ref, gain_ref, *refs, eps):
    piece_refs, weight_refs, low_ref, out_refs = refs[:4], refs[-7:-4], refs[-4], refs[-3:]
    count, half, three, _ = piece_refs[0].shape
    piece = three // 3
    owners = 2 * count
    part = owners * piece
    @pl.when(pl.program_id(0) == 0)
    def _():
        me = owner_ref[0]
        for source in range(owners):
            apart = jnp.bitwise_xor(me, source)
            near = apart % 2 == 0
            place = apart // 2
            places = (place, reverse_bits(place, owners.bit_length() - 2))
            for group in range(2):
                for line in range(half):
                    block = jnp.where(near, piece_refs[2 * group][places[group], line], piece_refs[2 * group + 1][places[group], line])
                    start = (group * half + line) * part + source * piece
                    for index in range(3):
                        weight_refs[index][start:start + piece, :] = block[index * piece:(index + 1) * piece]
    rows = inputs_ref[...].astype(jnp.float32)
    inverse = lax.rsqrt(jnp.mean(rows * rows, axis=1, keepdims=True) + eps)
    low = (rows * inverse * gain_ref[...]).astype(jnp.bfloat16)
    low_ref[...] = low
    for weight_ref, out_ref in zip(weight_refs, out_refs):
        out_ref[...] = dot_nn(low, weight_ref[...]).astype(jnp.bfloat16)


def project(owner, inputs, gain, pieces, eps, after=(), block=256):
    tokens, width = inputs.shape
    rows = pl.BlockSpec((block, width), lambda i: (i, 0))
    whole = lambda shape: pl.BlockSpec(shape, lambda i: (0,) * len(shape))
    weight = jax.ShapeDtypeStruct((width, width), jnp.bfloat16)
    return pl.pallas_call(
        partial(project_kernel, eps=eps),
        grid=(tokens // block,),
        in_specs=[pl.BlockSpec(memory_space=pltpu.SMEM), rows, whole(gain.shape)] + [whole(piece.shape) for piece in pieces] + [pl.BlockSpec(memory_space=pl.ANY)] * len(after),
        out_specs=[whole(weight.shape)] * 3 + [rows] * 4,
        out_shape=[weight] * 3 + [jax.ShapeDtypeStruct((tokens, width), jnp.bfloat16)] * 4,
        compiler_params=pltpu.CompilerParams(vmem_limit_bytes=62 << 20),
    )(owner, inputs, gain, *pieces, *after)


def settle_kernel(mixed_ref, merge_ref, inputs_ref, gain_ref, router_ref, routes_ref, resid_ref, low_ref, gates_ref, *, eps):
    resid = inputs_ref[...].astype(jnp.float32) + dot_nn(mixed_ref[...], merge_ref[...])
    resid_ref[...] = resid
    inverse = lax.rsqrt(jnp.mean(resid * resid, axis=1, keepdims=True) + eps)
    low = (resid * inverse * gain_ref[...]).astype(jnp.bfloat16)
    low_ref[...] = low
    logits = dot_nt(router_ref[...], low)
    expert = lax.broadcasted_iota(jnp.int32, logits.shape, 0)
    chosen = [jnp.sum(jnp.where(routes_ref[c:c + 1, :] == expert, logits, 0.0), axis=0, keepdims=True) for c in range(2)]
    top = jnp.maximum(chosen[0], chosen[1])
    powers = [jnp.exp(value - top) for value in chosen]
    total = powers[0] + powers[1]
    for c in range(2):
        gates_ref[c:c + 1, :] = powers[c] / total


def settle(mixed, merge, inputs, gain, router, routes, eps, block=256):
    tokens, width = inputs.shape
    rows = pl.BlockSpec((block, width), lambda i: (i, 0))
    whole = lambda shape: pl.BlockSpec(shape, lambda i: (0, 0))
    small = pl.BlockSpec((2, block), lambda i: (0, i))
    return pl.pallas_call(
        partial(settle_kernel, eps=eps),
        grid=(tokens // block,),
        in_specs=[rows, whole(merge.shape), rows, whole(gain.shape), whole(router.shape), small],
        out_specs=[rows, rows, small],
        out_shape=[jax.ShapeDtypeStruct((tokens, width), jnp.float32), jax.ShapeDtypeStruct((tokens, width), jnp.bfloat16), jax.ShapeDtypeStruct((2, tokens), jnp.float32)],
        compiler_params=pltpu.CompilerParams(vmem_limit_bytes=62 << 20),
    )(mixed, merge, inputs, gain, router, routes)


def finish_kernel(heads_ref, query_ref, key_ref, value_ref, gain_ref, inputs_ref, resid_grad_ref, out_ref, gain_grad_ref, *, eps):
    grads = dot_nt(heads_ref[0], query_ref[...]) + dot_nt(heads_ref[1], key_ref[...]) + dot_nt(heads_ref[2], value_ref[...])
    rows = inputs_ref[...].astype(jnp.float32)
    inverse = lax.rsqrt(jnp.mean(rows * rows, axis=1, keepdims=True) + eps)
    unit = rows * inverse
    @pl.when(pl.program_id(0) == 0)
    def _():
        gain_grad_ref[...] = jnp.zeros_like(gain_grad_ref)
    gain_grad_ref[...] += jnp.sum(grads * unit, axis=0, keepdims=True)
    scaled = grads * gain_ref[...]
    inner = jnp.mean(scaled * unit, axis=1, keepdims=True)
    out_ref[...] = resid_grad_ref[...] + inverse * (scaled - unit * inner)


def finish(head_grads, query, key, value, gain, inputs, resid_grad, eps, block=256):
    tokens, width = inputs.shape
    rows = pl.BlockSpec((block, width), lambda i: (i, 0))
    whole = lambda shape: pl.BlockSpec(shape, lambda i: (0, 0))
    return pl.pallas_call(
        partial(finish_kernel, eps=eps),
        grid=(tokens // block,),
        in_specs=[pl.BlockSpec((3, block, width), lambda i: (0, i, 0))] + [whole(query.shape)] * 3 + [whole(gain.shape), rows, rows],
        out_specs=[rows, whole((1, width))],
        out_shape=[jax.ShapeDtypeStruct((tokens, width), jnp.float32), jax.ShapeDtypeStruct((1, width), jnp.float32)],
        compiler_params=pltpu.CompilerParams(vmem_limit_bytes=62 << 20),
    )(head_grads, query, key, value, gain, inputs, resid_grad)


def weight_kernel(left_ref, mixed_ref, heads_ref, branch_ref, out_ref, turned, right):
    shards, part, _ = out_ref.shape
    step = pl.program_id(0)
    last = pl.num_programs(0) - 1
    @pl.when(step == 0)
    def _():
        turned[...] = left_ref[...].T
    @pl.when(step < last)
    def _():
        right[...] = heads_ref[...]
    @pl.when(step == last)
    def _():
        turned[...] = mixed_ref[...].T
        right[...] = branch_ref[...]
    for shard in range(shards):
        grad = dot_nn(turned[shard * part:(shard + 1) * part, :], right[...])
        out_ref[shard] = grad.astype(jnp.bfloat16)


def weight_grads(left, mixed, head_grads, branch, shards):
    count, tokens, width = head_grads.shape
    part = width // shards
    fixed = pl.BlockSpec((tokens, width), lambda i: (0, 0))
    return pl.pallas_call(
        weight_kernel,
        grid=(count + 1,),
        in_specs=[fixed, fixed, pl.BlockSpec((None, tokens, width), lambda i: (jnp.minimum(i, count - 1), 0, 0)), fixed],
        out_specs=pl.BlockSpec((shards, part, width), lambda i: (0, i, 0)),
        out_shape=jax.ShapeDtypeStruct((shards, (count + 1) * part, width), jnp.bfloat16),
        scratch_shapes=[pltpu.VMEM((width, tokens), jnp.bfloat16), pltpu.VMEM((tokens, width), jnp.bfloat16)],
        compiler_params=pltpu.CompilerParams(vmem_limit_bytes=62 << 20),
    )(left, mixed, head_grads, branch)


def widen_first_kernel(rows_ref, out_ref):
    out_ref[...] = rows_ref[...].astype(jnp.float32)


def widen_first(rows):
    count, width = rows.shape
    half = pl.BlockSpec((count // 2, width), lambda i: (i, 0))
    return pl.pallas_call(
        widen_first_kernel,
        grid=(2,),
        in_specs=[half],
        out_specs=half,
        out_shape=jax.ShapeDtypeStruct((2 * count, width), jnp.float32),
        compiler_params=pltpu.CompilerParams(vmem_limit_bytes=62 << 20),
    )(rows)


def widen_rest_kernel(rows_ref, into_ref, up_ref, down_ref):
    del into_ref
    wide = rows_ref[...].astype(jnp.float32)
    step = pl.program_id(0)
    @pl.when(step < 4)
    def _():
        up_ref[...] = wide
    @pl.when(step >= 4)
    def _():
        down_ref[...] = wide


def widen_rest(rows, into):
    count, width = rows.shape[0] // 3, rows.shape[1]
    half = lambda place: pl.BlockSpec((count // 2, width), lambda i: (place(i), 0))
    wide = jax.ShapeDtypeStruct((2 * count, width), jnp.float32)
    return pl.pallas_call(
        widen_rest_kernel,
        grid=(6,),
        in_specs=[half(lambda i: i), pl.BlockSpec(memory_space=pl.ANY)],
        out_specs=[half(lambda i: jnp.minimum(i, 3)), half(lambda i: jnp.maximum(i - 4, 0) + 2)],
        out_shape=[wide, wide],
        input_output_aliases={1: 1},
        compiler_params=pltpu.CompilerParams(vmem_limit_bytes=62 << 20),
    )(rows, into)


OWNER = "expert"
LINE = "shard"


def exchange(rows, bit):
    count = lax.axis_size(OWNER)
    return lax.ppermute(rows, OWNER, [(i, i ^ bit) for i in range(count)])


def shift(rows, step):
    count = lax.axis_size(LINE)
    return lax.ppermute(rows, LINE, [(i, (i + step) % count) for i in range(count)])


def gather_line(rows):
    count = lax.axis_size(LINE)
    me = lax.axis_index(LINE)
    out = jnp.zeros((count,) + rows.shape, rows.dtype)
    out = lax.dynamic_update_index_in_dim(out, rows, me, 0)
    for step in range(1, count):
        got = shift(rows, step)
        out = lax.dynamic_update_index_in_dim(out, got, (me - step) % count, 0)
    return out


def add_low(left, right):
    return (left.astype(jnp.float32) + right.astype(jnp.float32)).astype(jnp.bfloat16)


def side(bit):
    return (lax.axis_index(OWNER) // bit) % 2


def halve(stack, bit):
    half = stack.shape[1] // 2
    keep = lax.dynamic_slice_in_dim(stack, side(bit) * half, half, 1)
    send = lax.dynamic_slice_in_dim(stack, (1 - side(bit)) * half, half, 1)
    got = exchange(send, bit)
    return add_low(keep, got)


def line_sum(stack):
    count = lax.axis_size(LINE)
    place = lax.axis_index(LINE)
    total = lax.dynamic_index_in_dim(stack, place, 0, False).astype(jnp.float32)
    for step in range(1, count):
        send = lax.dynamic_index_in_dim(stack, (place + step) % count, 0, False)
        total = total + shift(send, step).astype(jnp.float32)
    return total.astype(jnp.bfloat16)


def grow(piece, bit):
    other = exchange(piece, bit)
    return jnp.where(
        side(bit) == 0, jnp.concatenate([piece, other]), jnp.concatenate([other, piece])
    )


def reduce_rows(stack, bits):
    unit = 8 << (len(bits) - 1)
    cut = -(-stack.shape[1] // (2 * unit)) * unit
    parts = [stack[:, :cut], stack[:, cut:]]
    orders = [bits[1:], bits[:0:-1]]
    for level in range(len(bits) - 1):
        parts = [halve(part, order[level]) for part, order in zip(parts, orders)]
    low = parts[0].shape[1]
    piece = line_sum(jnp.concatenate(parts, axis=1))
    parts = [piece[:low], piece[low:]]
    for level in reversed(range(len(bits) - 1)):
        parts = [grow(part, order[level]) for part, order in zip(parts, orders)]
    return grow(jnp.concatenate(parts), bits[0])


def scatter_sum(grads):
    shards, rows, width = grads.shape
    grads = grads.reshape(shards * rows, width)
    return lax.psum_scatter(grads, LINE, scatter_dimension=0, tiled=True)


def share_rows(rows):
    return lax.all_to_all(rows, OWNER, 0, 0, tiled=True)


def share_large(rows):
    return pltpu.with_memory_space_constraint(share_rows(rows), pltpu.HBM)


def local(
    inputs,
    norm_gain,
    query_weight,
    key_weight,
    value_weight,
    merge_weight,
    bias_table,
    expert_gain,
    router_weight,
    up_weight,
    down_weight,
    routes,
    cotangent,
):
    f32, bf16 = jnp.float32, jnp.bfloat16
    tokens, width = inputs.shape
    owners = lax.axis_size(OWNER)
    shards = lax.axis_size(LINE)
    me = lax.axis_index(OWNER)
    part = query_weight.shape[0]
    piece = part // owners
    local_heads = bias_table.shape[1]
    heads = local_heads * shards
    size = width // heads
    experts = router_weight.shape[1]
    local_count, _, hidden = up_weight.shape
    capacity = (5 * tokens * routes.shape[1] + 4 * experts - 1) // (4 * experts)
    capacity = -(-capacity // 16) * 16
    rows = owners * capacity
    assert local_count == 2 and hidden // shards == width

    router_at = 2 + local_heads + (-(2 + local_heads)) % 8

    def widen(block):
        return jnp.pad(block, ((0, 0), (0, width - block.shape[1])))

    def pack(gain_one, gain_two, table, router):
        head = jnp.concatenate([gain_one, gain_two], axis=0)
        gap = jnp.zeros((router_at - 2 - local_heads, width), bf16)
        return jnp.concatenate([widen(head), widen(table), gap, widen(router)], axis=0)

    small = pack(norm_gain[None], expert_gain[None], bias_table.T, router_weight.T)
    slices = [
        lax.dynamic_slice_in_dim(weight, me * piece, piece, 0)
        for weight in (query_weight, key_weight, value_weight)
    ]
    lined = gather_line(jnp.concatenate(slices + [small]))
    small_full = lined[:, 3 * piece :]
    bits = [1 << level for level in range(owners.bit_length() - 1)]
    pieces = []
    for index, order in enumerate((bits[1:], bits[:0:-1])):
        held = lined[index * shards // 2 : (index + 1) * shards // 2, : 3 * piece][None]
        for bit in order:
            got = exchange(held, bit)
            held = jnp.concatenate([held, got])
        pieces += [held, exchange(held, bits[0])]
    merge_full = lax.all_gather(merge_weight, LINE, axis=0, tiled=True)

    gain_one = small_full[:, 0, :part].reshape(1, width).astype(f32)
    gain_two = small_full[:, 1, :part].reshape(1, width).astype(f32)
    table_full = small_full[:, 2 : 2 + local_heads, :BUCKETS].reshape(heads, BUCKETS).astype(f32)
    router_full = small_full[:, router_at : router_at + experts, :part]
    router_full = router_full.transpose(1, 0, 2).reshape(experts, width)

    routes_line = routes.T
    base = (routes_line % local_count * owners + routes_line // local_count) * capacity
    slots = find_slots(routes_line, base, experts)
    cot_rows, other = dispatch_first(
        slots, routes_line.astype(f32), cotangent, owners, capacity
    )
    other = share_rows(other).reshape(owners, local_count, capacity)

    owner = me.astype(jnp.int32).reshape(1)
    block = 256
    hot = bucket_hot(tokens)
    assert hot[block:, -1].all()
    near_hot = jnp.asarray((hot[:block] - hot[-1:]).T, dtype=f32)
    group = 128 // size
    near = jnp.dot(table_full, near_hot, precision=lax.Precision.HIGHEST)
    near = near.reshape(heads // group, group, block)
    query_full, key_full, value_full, low_one, queries, keys, values = project(
        owner, inputs, gain_one, pieces, epsilon, after=(near, router_full)
    )
    cot_in = share_large(cot_rows)
    attended, totals = attend(queries, keys, values, near, size, block)
    resid, low_two, gates = settle(
        attended, merge_full, inputs, gain_two, router_full, routes_line, epsilon
    )

    send = dispatch(slots, low_two, 0, rows).reshape(owners, capacity, width)
    rows_in = share_large(send)
    joint = dispatch_both(slots, low_two, cotangent, rows, owners, capacity)
    joint_in = share_large(joint)
    others = [other[:, index].reshape(1, rows) for index in range(local_count)]
    act, slope, first_down, grad_in = expert_first(
    owner, rows_in, cot_in, others[0], router_full, up_weight, 0, local_count, shards,
    )
    first_sum = scatter_sum(first_down)
    first_made, pair = expert_second(rows_in, grad_in, act, slope, up_weight, down_weight, 0, owners, shards, 3 * width)
    act, slope, pair, grad_in = expert_first(
        owner, joint_in, joint_in, others[1], router_full, up_weight, 1, local_count, shards,
        into=pair,
    )
    low, pair = expert_slope(joint_in, grad_in, slope, down_weight, 1, shards, pair, 1)
    pair_sum = scatter_sum(pair)
    second_made = expert_last(act, low, up_weight, down_weight, 1, owners, shards)
    returned = share_rows(first_made)
    result, inner, part_grads = combine_part(slots, gates, resid, cotangent, returned)
    returned = share_rows(second_made)
    output, logit_grad = combine_out(
        slots, routes_line, gates, result, inner, cotangent, returned
    )
    router_wide = jnp.pad(router_full, ((0, 128 - experts), (0, 0)))
    resid_grad, branch, mixed_grad, gain_grad = combine_back(
        slots, logit_grad, router_wide, gain_two, resid, cotangent, merge_full,
        part_grads, returned, epsilon
    )
    router_grad = jnp.einsum("te,ti->ei", logit_grad, low_two, preferred_element_type=f32)
    head_grads, distances = attend_back(
        queries, keys, values, mixed_grad, attended, totals, near, size, block
    )
    close_sums = distances[:, :group].reshape(heads, block)
    far_sums = jnp.sum(distances[:, group:].reshape(heads, block), axis=1)
    table_grad = jnp.dot(close_sums, jnp.asarray(hot[:block]), precision=lax.Precision.HIGHEST)
    table_grad = table_grad + far_sums[:, None] * jnp.asarray(hot[-1:])
    sums = weight_grads(low_one, attended, head_grads, branch, shards)
    sums = halve(sums, bits[0])
    input_gradient, norm_grad = finish(
        head_grads, query_full, key_full, value_full, gain_one, inputs, resid_grad, epsilon
    )
    small_grad = jax.vmap(pack)(
        norm_grad.reshape(shards, 1, part).astype(bf16),
        gain_grad.reshape(shards, 1, part).astype(bf16),
        table_grad.reshape(shards, local_heads, BUCKETS).astype(bf16),
        router_grad[:experts].reshape(experts, shards, part).transpose(1, 0, 2).astype(bf16),
    )
    spare = -small_grad.shape[1] % (8 * owners)
    small_grad = halve(jnp.pad(small_grad, ((0, 0), (0, spare), (0, 0))), bits[0])
    kept = sums.shape[1]
    sums = reduce_rows(jnp.concatenate([sums, small_grad], axis=1), bits)
    half = sums.shape[0] // 2
    weights = jnp.concatenate([sums[:kept], sums[half : half + kept]]).astype(f32)
    small_sum = jnp.concatenate([sums[kept:half], sums[half + kept :]]).astype(f32)
    up_sum, down_sum = widen_rest(pair_sum, widen_first(first_sum))
    return (
        output,
        input_gradient,
        small_sum[0, :part],
        weights[:part],
        weights[part : 2 * part],
        weights[2 * part : 3 * part],
        weights[3 * part :],
        small_sum[2 : 2 + local_heads, :BUCKETS].T,
        small_sum[1, :part],
        small_sum[router_at : router_at + experts, :part].T,
        up_sum.reshape(local_count, width, width),
        down_sum.reshape(local_count, width, width),
    )


def solution(mesh):
    in_specs = (
        P((OWNER, LINE), None),
        P(LINE),
        P(LINE, None),
        P(LINE, None),
        P(LINE, None),
        P(LINE, None),
        P(None, LINE),
        P(LINE),
        P(LINE, None),
        P(OWNER, None, None),
        P(OWNER, None, None),
        P((OWNER, LINE), None),
        P((OWNER, LINE), None),
    )
    out_specs = (
        P((OWNER, LINE), None),
        P((OWNER, LINE), None),
        P(LINE),
        P(LINE, None),
        P(LINE, None),
        P(LINE, None),
        P(LINE, None),
        P(None, LINE),
        P(LINE),
        P(LINE, None),
        P(OWNER, None, LINE),
        P(OWNER, LINE, None),
    )

    return jax.shard_map(local, mesh=mesh, in_specs=in_specs, out_specs=out_specs, check_vma=False)
```

```python
from functools import partial, reduce

import jax
import jax.numpy as jnp
import numpy as np
from jax import lax
from jax.experimental import pallas as pl
from jax.experimental.pallas import tpu as pltpu
from jax.sharding import PartitionSpec as P


BUCKETS = 32
MAX_DIST = 128


epsilon = 1e-06
masked_score = -1e30


def bucket_hot(length):
    distance = np.arange(length)
    half_count = BUCKETS // 2
    clipped = np.maximum(distance, half_count)
    spread = np.log(clipped / half_count) / np.log(MAX_DIST / half_count) * (BUCKETS - half_count)
    far_bucket = np.minimum(half_count + np.floor(spread).astype(np.int32), BUCKETS - 1)
    bucket = np.where(distance < half_count, distance, far_bucket)
    return (bucket[:, None] == np.arange(BUCKETS)[None, :]).astype(np.float32)


def dot_nt(a, b):
    return lax.dot_general(a, b, (((1,), (1,)), ((), ())), preferred_element_type=jnp.float32)


def dot_nn(a, b):
    return lax.dot_general(a, b, (((1,), (0,)), ((), ())), preferred_element_type=jnp.float32)


def dot_tn(a, b):
    return lax.dot_general(a, b, (((0,), (0,)), ((), ())), preferred_element_type=jnp.float32)


def slot_kernel(routes_ref, base_ref, slots_ref, *, experts):
    tokens = routes_ref.shape[1]
    expert = lax.broadcasted_iota(jnp.int32, (experts, tokens), 0)
    hits = [routes_ref[c:c + 1, :] == expert for c in range(2)]
    hot = jnp.where(hits[0] | hits[1], 1.0, 0.0).astype(jnp.bfloat16)
    earlier = lax.broadcasted_iota(jnp.int32, (tokens, tokens), 0)
    later = lax.broadcasted_iota(jnp.int32, (tokens, tokens), 1)
    before = jnp.where(earlier < later, 1.0, 0.0).astype(jnp.bfloat16)
    counts = dot_nn(hot, before)
    for c in range(2):
        position = jnp.sum(jnp.where(hits[c], counts, 0.0), axis=0, keepdims=True)
        slots_ref[c:c + 1, :] = base_ref[c:c + 1, :] + position.astype(jnp.int32)


def find_slots(routes, base, experts):
    return pl.pallas_call(
        partial(slot_kernel, experts=experts),
        out_shape=jax.ShapeDtypeStruct(routes.shape, jnp.int32),
    )(routes, base)


def dispatch_both_kernel(slots_ref, rows_ref, cot_ref, *refs, start):
    out_ref = refs[-1]
    block, tokens = out_ref.shape[2], rows_ref.shape[0]
    slot = lax.broadcasted_iota(jnp.int32, (block, tokens), 0) + (pl.program_id(0) * block + start)
    hot = jnp.where((slot == slots_ref[0:1, :]) | (slot == slots_ref[1:2, :]), 1.0, 0.0)
    hot = hot.astype(jnp.bfloat16)
    out_ref[0, 0] = dot_nn(hot, rows_ref[...]).astype(out_ref.dtype)
    out_ref[0, 1] = dot_nn(hot, cot_ref[...]).astype(out_ref.dtype)


def dispatch_both(slots, rows, cot, start, owners, capacity, after=()):
    width = rows.shape[1]
    whole = lambda shape: pl.BlockSpec(shape, lambda i: (0, 0))
    return pl.pallas_call(
        partial(dispatch_both_kernel, start=start),
        grid=(owners,),
        in_specs=[whole(slots.shape), whole(rows.shape), whole(cot.shape)] + [pl.BlockSpec(memory_space=pl.ANY)] * len(after),
        out_specs=pl.BlockSpec((1, 2, capacity, width), lambda i: (i, 0, 0, 0)),
        out_shape=jax.ShapeDtypeStruct((owners, 2, capacity, width), rows.dtype),
        compiler_params=pltpu.CompilerParams(vmem_limit_bytes=62 << 20),
    )(slots, rows, cot, *after)


def dispatch_first_kernel(slots_ref, routes_ref, rows_ref, out_ref, other_ref, *, owners, capacity):
    block, tokens = other_ref.shape[2], rows_ref.shape[0]
    row = lax.broadcasted_iota(jnp.int32, (block, tokens), 0)
    slot = row + pl.program_id(0) * capacity
    slot = slot + jnp.where(row >= capacity, (owners - 1) * capacity, 0)
    hits = [slot == slots_ref[c:c + 1, :] for c in range(2)]
    hot = jnp.where(hits[0] | hits[1], 1.0, 0.0)[:capacity]
    out_ref[0] = dot_nn(hot.astype(jnp.bfloat16), rows_ref[...]).astype(out_ref.dtype)
    other = jnp.where(hits[0], routes_ref[1:2, :], jnp.where(hits[1], routes_ref[0:1, :], 0.0))
    column = jnp.sum(other, axis=1, keepdims=True)
    other_ref[0] = jnp.broadcast_to(column, (block, 128)).T[0:1, :]


def dispatch_first(slots, routes, rows, owners, capacity):
    width = rows.shape[1]
    whole = lambda shape: pl.BlockSpec(shape, lambda i: (0, 0))
    return pl.pallas_call(
        partial(dispatch_first_kernel, owners=owners, capacity=capacity),
        grid=(owners,),
        in_specs=[whole(slots.shape), whole(routes.shape), whole(rows.shape)],
        out_specs=[pl.BlockSpec((1, capacity, width), lambda i: (i, 0, 0)), pl.BlockSpec((1, 1, 2 * capacity), lambda i: (i, 0, 0))],
        out_shape=[jax.ShapeDtypeStruct((owners, capacity, width), rows.dtype), jax.ShapeDtypeStruct((owners, 1, 2 * capacity), jnp.float32)],
    )(slots, routes, rows)


def gelu_pair(v):
    c = np.float32(np.sqrt(2.0 / np.pi))
    a = np.float32(0.044715)
    square = v * v
    half = 0.5 * jnp.tanh(v * (c * a * square + c)) + 0.5
    value = v * half
    slope = half + value * (1.0 - half) * (6.0 * c * a * square + 2.0 * c)
    return value, slope


def first_kernel(owner_ref, rows_ref, cot_ref, other_ref, router_ref, up_ref, *refs, chunk, index, local_count):
    act_ref, slope_ref, down_grad_ref, grad_ref = refs[-4:]
    owners, capacity, width = rows_ref.shape
    rows = owners * capacity
    @pl.when(pl.program_id(0) == 0)
    def _():
        logits = dot_nt(router_ref[...], rows_ref[...].reshape(rows, width))
        expert = lax.broadcasted_iota(jnp.int32, logits.shape, 0)
        mine = owner_ref[0] * local_count + index
        own = jnp.sum(jnp.where(expert == mine, logits, 0.0), axis=0, keepdims=True)
        other = other_ref[...].astype(jnp.int32)
        other = jnp.sum(jnp.where(expert == other, logits, 0.0), axis=0, keepdims=True)
        top = jnp.maximum(own, other)
        own = jnp.exp(own - top)
        gate = own / (own + jnp.exp(other - top))
        column = jnp.broadcast_to(gate, (128, rows)).T
        for start in range(0, width, 128):
            part = cot_ref[:, :, start:start + 128].reshape(rows, 128).astype(jnp.float32) * column
            grad_ref[:, start:start + 128] = part.astype(jnp.bfloat16)
    up = up_ref[0]
    for start in range(0, rows, chunk):
        part = rows_ref[start // capacity:(start + chunk) // capacity].reshape(chunk, width)
        pre = dot_nn(part, up)
        value, slope = gelu_pair(pre)
        act_ref[start:start + chunk, :] = value.astype(jnp.bfloat16)
        slope_ref[start:start + chunk, :] = slope.astype(jnp.bfloat16)
    down_grad_ref[0] = dot_tn(act_ref[...], grad_ref[...]).astype(jnp.bfloat16)


def arrived_spec(arrived, which):
    if arrived.ndim == 3:
        return pl.BlockSpec(arrived.shape, lambda i: (0, 0, 0))
    owners, _, capacity, width = arrived.shape
    return pl.BlockSpec((owners, None, capacity, width), lambda i: (0, which, 0, 0))


def expert_first(owner, rows_in, cot, other, router, up, index, local_count, shards, into=None, after=()):
    owners, capacity, width = rows_in.shape[0], *rows_in.shape[-2:]
    rows = owners * capacity
    hidden = up.shape[2]
    tile = hidden // shards
    chunk = rows // 2
    fixed = pl.BlockSpec((rows, width), lambda i: (0, 0))
    column = pl.BlockSpec((rows, tile), lambda i: (0, i))
    operands = [owner, rows_in, cot, other, router, up]
    place, aliases = 0, {}
    grad_shape = jax.ShapeDtypeStruct((shards, tile, width), jnp.bfloat16)
    if into is not None:
        aliases = {len(operands): 2}
        operands.append(into)
        place, grad_shape = 2, jax.ShapeDtypeStruct(into.shape, into.dtype)
    operands += list(after)
    return pl.pallas_call(
        partial(first_kernel, chunk=chunk, index=index, local_count=local_count),
        grid=(shards,),
        in_specs=[
            pl.BlockSpec(memory_space=pltpu.SMEM),
            arrived_spec(rows_in, 0),
            arrived_spec(cot, 1),
            pl.BlockSpec((1, rows), lambda i: (0, 0)),
            pl.BlockSpec(router.shape, lambda i: (0, 0)),
            pl.BlockSpec((1, width, tile), lambda i: (index, 0, i)),
        ]
        + [pl.BlockSpec(memory_space=pl.ANY)] * (len(operands) - 6),
        out_specs=[column, column, pl.BlockSpec((1, tile, width), lambda i: (i, place, 0)), fixed],
        out_shape=[jax.ShapeDtypeStruct((rows, hidden), jnp.bfloat16)] * 2 + [grad_shape, jax.ShapeDtypeStruct((rows, width), jnp.bfloat16)],
        input_output_aliases=aliases,
        compiler_params=pltpu.CompilerParams(vmem_limit_bytes=62 << 20),
    )(*operands)


def second_kernel(rows_ref, grad_ref, act_ref, slope_ref, up_ref, down_ref, *refs):
    made_ref, up_grad_ref, turned, made_acc, back_acc = refs[-5:]
    step = pl.program_id(0)
    owners, _, capacity, width = made_ref.shape
    @pl.when(step == 0)
    def _():
        turned[...] = rows_ref[...].reshape(grad_ref.shape).T
    up = up_ref[0]
    down = down_ref[0]
    grads = dot_nt(grad_ref[...], down)
    low = (slope_ref[...].astype(jnp.float32) * grads).astype(jnp.bfloat16)
    up_grad_ref[0] = dot_nn(turned[...], low).astype(jnp.bfloat16)
    back = dot_nt(low, up)
    made = dot_nn(act_ref[...], down)
    last = pl.num_programs(0) - 1
    @pl.when(step == 0)
    def _():
        made_acc[...] = made
        back_acc[...] = back
    @pl.when((step > 0) & (step < last))
    def _():
        made_acc[...] += made
        back_acc[...] += back
    @pl.when(step == last)
    def _():
        made_ref[:, 0] = (made_acc[...] + made).astype(jnp.bfloat16).reshape(owners, capacity, width)
        made_ref[:, 1] = (back_acc[...] + back).astype(jnp.bfloat16).reshape(owners, capacity, width)


def expert_second(rows_in, grad, act, slope, up, down, index, owners, shards, wide, after=()):
    rows, width = grad.shape
    hidden = up.shape[2]
    tile = hidden // shards
    fixed = pl.BlockSpec((rows, width), lambda i: (0, 0))
    column = pl.BlockSpec((rows, tile), lambda i: (0, i))
    made_shape = (owners, 2, rows // owners, width)
    return pl.pallas_call(
        second_kernel,
        grid=(shards,),
        in_specs=[arrived_spec(rows_in, 0), fixed, column, column, pl.BlockSpec((1, width, tile), lambda i: (index, 0, i)), pl.BlockSpec((1, tile, width), lambda i: (index, i, 0))]
        + [pl.BlockSpec(memory_space=pl.ANY)] * len(after),
        out_specs=[pl.BlockSpec(made_shape, lambda i: (0, 0, 0, 0)), pl.BlockSpec((1, width, tile), lambda i: (i, 0, 0))],
        out_shape=[jax.ShapeDtypeStruct(made_shape, jnp.bfloat16), jax.ShapeDtypeStruct((shards, wide, tile), jnp.bfloat16)],
        scratch_shapes=[pltpu.VMEM((width, rows), jnp.bfloat16), pltpu.VMEM((rows, width), jnp.float32), pltpu.VMEM((rows, width), jnp.float32)],
        compiler_params=pltpu.CompilerParams(vmem_limit_bytes=62 << 20),
    )(rows_in, grad, act, slope, up, down, *after)


def slope_kernel(rows_ref, grad_ref, slope_ref, down_ref, into_ref, low_ref, up_grad_ref, turned):
    del into_ref
    @pl.when(pl.program_id(0) == 0)
    def _():
        turned[...] = rows_ref[...].reshape(grad_ref.shape).T
    grads = dot_nt(grad_ref[...], down_ref[0])
    low = (slope_ref[...].astype(jnp.float32) * grads).astype(jnp.bfloat16)
    low_ref[...] = low
    up_grad_ref[0] = dot_nn(turned[...], low).astype(jnp.bfloat16)


def expert_slope(rows_in, grad, slope, down, index, shards, into, place):
    rows, width = grad.shape
    hidden = slope.shape[1]
    tile = hidden // shards
    fixed = pl.BlockSpec((rows, width), lambda i: (0, 0))
    column = pl.BlockSpec((rows, tile), lambda i: (0, i))
    return pl.pallas_call(
        slope_kernel,
        grid=(shards,),
        in_specs=[arrived_spec(rows_in, 0), fixed, column, pl.BlockSpec((1, tile, width), lambda i: (index, i, 0)), pl.BlockSpec(memory_space=pl.ANY)],
        out_specs=[column, pl.BlockSpec((1, width, tile), lambda i: (i, place, 0))],
        out_shape=[jax.ShapeDtypeStruct((rows, hidden), jnp.bfloat16), jax.ShapeDtypeStruct(into.shape, into.dtype)],
        input_output_aliases={4: 1},
        scratch_shapes=[pltpu.VMEM((width, rows), jnp.bfloat16)],
        compiler_params=pltpu.CompilerParams(vmem_limit_bytes=62 << 20),
    )(rows_in, grad, slope, down, into)


def last_kernel(act_ref, low_ref, up_ref, down_ref, made_ref, made_acc, back_acc):
    step = pl.program_id(0)
    owners, _, capacity, width = made_ref.shape
    back = dot_nt(low_ref[...], up_ref[0])
    made = dot_nn(act_ref[...], down_ref[0])
    last = pl.num_programs(0) - 1
    @pl.when(step == 0)
    def _():
        made_acc[...] = made
        back_acc[...] = back
    @pl.when((step > 0) & (step < last))
    def _():
        made_acc[...] += made
        back_acc[...] += back
    @pl.when(step == last)
    def _():
        made_ref[:, 0] = (made_acc[...] + made).astype(jnp.bfloat16).reshape(owners, capacity, width)
        made_ref[:, 1] = (back_acc[...] + back).astype(jnp.bfloat16).reshape(owners, capacity, width)


def expert_last(act, low, up, down, index, owners, shards):
    rows, hidden = act.shape
    width = up.shape[1]
    tile = hidden // shards
    column = pl.BlockSpec((rows, tile), lambda i: (0, i))
    made_shape = (owners, 2, rows // owners, width)
    return pl.pallas_call(
        last_kernel,
        grid=(shards,),
        in_specs=[column, column, pl.BlockSpec((1, width, tile), lambda i: (index, 0, i)), pl.BlockSpec((1, tile, width), lambda i: (index, i, 0))],
        out_specs=pl.BlockSpec(made_shape, lambda i: (0, 0, 0, 0)),
        out_shape=jax.ShapeDtypeStruct(made_shape, jnp.bfloat16),
        scratch_shapes=[pltpu.VMEM((rows, width), jnp.float32), pltpu.VMEM((rows, width), jnp.float32)],
        compiler_params=pltpu.CompilerParams(vmem_limit_bytes=62 << 20),
    )(act, low, up, down)


def spread(row, block):
    return jnp.broadcast_to(row, (128, block)).T


def pick(slots, lane, back_refs, first=0):
    picked = None
    for index, back_ref in enumerate(back_refs, first):
        owners, capacity, width = back_ref.shape
        half = owners * capacity
        hots = []
        for start in range(index * half, (index + 1) * half, 128):
            hit = reduce(jnp.logical_or, [slot == lane + start for slot in slots])
            hots.append(jnp.where(hit, 1.0, 0.0).astype(jnp.bfloat16))
        part = dot_nn(jnp.concatenate(hots, axis=1), back_ref[...].reshape(half, width))
        picked = part if picked is None else picked + part
    return picked


def part_kernel(slots_ref, gates_ref, resid_ref, cot_ref, made_ref, back_ref, result_ref, inner_ref, grads_ref):
    block = result_ref.shape[0]
    lane = lax.broadcasted_iota(jnp.int32, (block, 128), 1)
    cot = cot_ref[...].astype(jnp.float32)
    result = resid_ref[...]
    inner = jnp.zeros((block, 128), jnp.float32)
    slots = [spread(slots_ref[c:c + 1, :], block) for c in range(2)]
    for c in range(2):
        picked = pick([slots[c]], lane, [made_ref])
        result = result + spread(gates_ref[c:c + 1, :], block)[:, 0:1] * picked
        inner = inner + jnp.where(lane == c, jnp.sum(cot * picked, axis=1, keepdims=True), 0.0)
    result_ref[...] = result
    inner_ref[...] = inner
    grads_ref[...] = pick(slots, lane, [back_ref])


def combine_part(slots, gates, resid, cot, returned, block=256):
    tokens, width = resid.shape
    small = pl.BlockSpec((2, block), lambda i: (0, i))
    rows = pl.BlockSpec((block, width), lambda i: (i, 0))
    wide = jax.ShapeDtypeStruct((tokens, width), jnp.float32)
    return pl.pallas_call(
        part_kernel,
        grid=(tokens // block,),
        in_specs=[small, small, rows, rows, returned_spec(returned, 0), returned_spec(returned, 1)],
        out_specs=[rows, pl.BlockSpec((block, 128), lambda i: (i, 0)), rows],
        out_shape=[wide, jax.ShapeDtypeStruct((tokens, 128), jnp.float32), wide],
        compiler_params=pltpu.CompilerParams(vmem_limit_bytes=62 << 20),
    )(slots, gates, resid, cot, returned, returned)


def out_kernel(slots_ref, routes_ref, gates_ref, result_ref, inner_ref, cot_ref, made_ref, out_ref, logit_ref):
    block = out_ref.shape[0]
    lane = lax.broadcasted_iota(jnp.int32, (block, 128), 1)
    cot = cot_ref[...].astype(jnp.float32)
    result = result_ref[...]
    gates, inner = [], []
    for c in range(2):
        slot = spread(slots_ref[c:c + 1, :], block)
        gate = spread(gates_ref[c:c + 1, :], block)[:, 0:1]
        picked = pick([slot], lane, [made_ref], 1)
        result = result + gate * picked
        gates.append(gate)
        inner.append(inner_ref[:, c:c + 1] + jnp.sum(cot * picked, axis=1, keepdims=True))
    out_ref[...] = result.astype(out_ref.dtype)
    middle = gates[0] * inner[0] + gates[1] * inner[1]
    logit = jnp.zeros((block, 128), jnp.float32)
    for c in range(2):
        route = spread(routes_ref[c:c + 1, :], block)
        logit = logit + jnp.where(route == lane, gates[c] * (inner[c] - middle), 0.0)
    logit_ref[...] = logit.astype(jnp.bfloat16)


def returned_spec(returned, which):
    owners, _, capacity, width = returned.shape
    return pl.BlockSpec((owners, None, capacity, width), lambda i: (0, which, 0, 0))


def combine_out(slots, routes, gates, result, inner, cot, returned, block=256):
    tokens, width = result.shape
    small = pl.BlockSpec((2, block), lambda i: (0, i))
    rows = pl.BlockSpec((block, width), lambda i: (i, 0))
    return pl.pallas_call(
        out_kernel,
        grid=(tokens // block,),
        in_specs=[small, small, small, rows, pl.BlockSpec((block, 128), lambda i: (i, 0)), rows, returned_spec(returned, 0)],
        out_specs=[rows, pl.BlockSpec((block, 128), lambda i: (i, 0))],
        out_shape=[jax.ShapeDtypeStruct((tokens, width), jnp.bfloat16), jax.ShapeDtypeStruct((tokens, 128), jnp.bfloat16)],
        compiler_params=pltpu.CompilerParams(vmem_limit_bytes=62 << 20),
    )(slots, routes, gates, result, inner, cot, returned)


def back_kernel(slots_ref, logit_ref, router_ref, gain_ref, resid_ref, cot_ref, merge_ref, part_ref, back_ref, grad_ref, low_ref, mixed_ref, gain_grad_ref, *, eps):
    block, _ = grad_ref.shape
    lane = lax.broadcasted_iota(jnp.int32, (block, 128), 1)
    grads = part_ref[...] + pick([spread(slots_ref[c:c + 1, :], block) for c in range(2)], lane, [back_ref], 1)
    grads = grads + dot_nn(logit_ref[...], router_ref[...])
    resid = resid_ref[...]
    inverse = lax.rsqrt(jnp.mean(resid * resid, axis=1, keepdims=True) + eps)
    unit = resid * inverse
    @pl.when(pl.program_id(0) == 0)
    def _():
        gain_grad_ref[...] = jnp.zeros_like(gain_grad_ref)
    gain_grad_ref[...] += jnp.sum(grads * unit, axis=0, keepdims=True)
    scaled = grads * gain_ref[...]
    inner = jnp.mean(scaled * unit, axis=1, keepdims=True)
    total = cot_ref[...].astype(jnp.float32) + inverse * (scaled - unit * inner)
    grad_ref[...] = total
    low = total.astype(jnp.bfloat16)
    low_ref[...] = low
    mixed_ref[...] = dot_nt(low, merge_ref[...]).astype(jnp.bfloat16)


def combine_back(slots, logit, router, gain, resid, cot, merge, part, returned, eps, block=256):
    tokens, width = resid.shape
    rows = pl.BlockSpec((block, width), lambda i: (i, 0))
    whole = lambda shape: pl.BlockSpec(shape, lambda i: (0, 0))
    low = jax.ShapeDtypeStruct((tokens, width), jnp.bfloat16)
    return pl.pallas_call(
        partial(back_kernel, eps=eps),
        grid=(tokens // block,),
        in_specs=[pl.BlockSpec((2, block), lambda i: (0, i)), pl.BlockSpec((block, 128), lambda i: (i, 0)), whole(router.shape), whole(gain.shape), rows, rows, whole(merge.shape), rows, returned_spec(returned, 1)],
        out_specs=[rows, rows, rows, whole((1, width))],
        out_shape=[jax.ShapeDtypeStruct((tokens, width), jnp.float32), low, low, jax.ShapeDtypeStruct((1, width), jnp.float32)],
        compiler_params=pltpu.CompilerParams(vmem_limit_bytes=62 << 20),
    )(slots, logit, router, gain, resid, cot, merge, part, returned)


def near_tiles(near_ref, head, block):
    spread = jnp.broadcast_to(near_ref[0, head:head + 1, :], (block, block))
    spread = pltpu.roll(spread, 0, 1, stride=1, stride_axis=0)
    key_at = lax.broadcasted_iota(jnp.int32, (block, block), 0)
    query_at = lax.broadcasted_iota(jnp.int32, (block, block), 1)
    return (jnp.where(query_at >= key_at, spread, masked_score), jnp.where(query_at < key_at, spread, 0.0), query_at < key_at)


def diagonal_sums(tile):
    block = tile.shape[1]
    total = tile[:8]
    for start in range(8, block, 8):
        total = total + pltpu.roll(tile[start:start + 8], block - start, 1)
    row = lax.broadcasted_iota(jnp.int32, total.shape, 0)
    for step in (1, 2, 4):
        total = jnp.where((row & step) != 0, pltpu.roll(total, block - step, 1), total)
    return jnp.sum(total, axis=0, keepdims=True)


def head_part(rows, head, size):
    lane = lax.broadcasted_iota(jnp.int32, rows.shape, 1)
    return jnp.where((lane >= head * size) & (lane < (head + 1) * size), rows, jnp.zeros_like(rows))


def attend_kernel(query_ref, key_ref, value_ref, near_ref, out_ref, total_ref, held, *, block, size, scale):
    length, lanes = query_ref.shape
    heads = lanes // size
    count = length // block
    turned = value_ref[...].T
    ones = jnp.ones((16, length), jnp.bfloat16)
    flipped = [jnp.concatenate([turned[head * size:(head + 1) * size], ones], axis=0) for head in range(heads)]
    tiles = [near_tiles(near_ref, head, block) for head in range(heads)]
    units = [(i, head) for i in range(count) for head in range(heads)]
    def fold(tile, op):
        parts = [tile[k:k + 8] for k in range(0, tile.shape[0], 8)]
        while len(parts) > 1:
            parts = [op(parts[k], parts[k + 1]) for k in range(0, len(parts), 2)]
        return parts[0]
    def score_tile(unit, query_part, j, slot):
        i, head = unit
        tile = dot_nt(key_ref[pl.ds(j * block, block), :], query_part)
        if j == i:
            tile = tile + tiles[head][0]
        elif j == i - 1:
            tile = tile + tiles[head][1]
        held[slot, pl.ds(j * block, block), :] = tile
        return fold(tile, jnp.maximum)
    def part_of(unit):
        i, head = unit
        return head_part(query_ref[pl.ds(i * block, block), :] * jnp.bfloat16(scale), head, size)
    tops = {0: [score_tile(units[0], part_of(units[0]), 0, 0)]}
    outs = []
    for n, (i, head) in enumerate(units):
        top = jnp.max(reduce(jnp.maximum, tops[n]), axis=0, keepdims=True)
        following = units[n + 1] if n + 1 < len(units) else None
        if following is not None:
            query_part = part_of(following)
            tops[n + 1] = []
        mixed = None
        total = None
        steps = max(i + 1, following[0] + 1 if following else 0)
        for j in range(steps):
            if following is not None and j <= following[0]:
                tops[n + 1].append(score_tile(following, query_part, j, (n + 1) % 2))
            if j <= i:
                weights = jnp.exp(held[n % 2, pl.ds(j * block, block), :] - top)
                part = dot_nn(flipped[head][:, j * block:(j + 1) * block], weights.astype(jnp.bfloat16))
                mixed = part if mixed is None else mixed + part
        total = mixed[size:size + 1]
        outs.append(mixed[:size] / total)
        rows = pl.ds(i * block, block)
        total_ref[0, head:head + 1, rows] = top + jnp.log(total)
        if head == heads - 1:
            out_ref[rows, :] = jnp.concatenate(outs[-heads:], axis=0).T.astype(out_ref.dtype)


def attend(queries, keys, values, near, size, block):
    length, width = queries.shape
    lanes = 128
    heads = lanes // size
    groups = width // lanes
    column = pl.BlockSpec((length, lanes), lambda g: (0, g))
    head_rows = pl.BlockSpec((1, heads, block), lambda g: (g, 0, 0))
    return pl.pallas_call(
        partial(attend_kernel, block=block, size=size, scale=size ** -0.5),
        grid=(groups,),
        in_specs=[column, column, column, head_rows],
        out_specs=[column, pl.BlockSpec((1, heads, length), lambda g: (g, 0, 0))],
        out_shape=[jax.ShapeDtypeStruct((length, width), jnp.bfloat16), jax.ShapeDtypeStruct((groups, heads, length), jnp.float32)],
        scratch_shapes=[pltpu.VMEM((2, length, block), jnp.float32)],
        compiler_params=pltpu.CompilerParams(vmem_limit_bytes=62 << 20),
    )(queries, keys, values, near)


def attend_back_kernel(query_ref, key_ref, value_ref, grad_ref, out_ref, total_ref, near_ref, grads_ref, dist_ref, key_acc, value_acc, *, block, size, scale):
    length, lanes = query_ref.shape
    heads = lanes // size
    count = length // block
    flipped = key_ref[...].T
    tiles = [near_tiles(near_ref, head, block) for head in range(heads)]
    near_acc = [None] * heads
    far_acc = [None] * heads
    for i in range(count):
        rows = pl.ds(i * block, block)
        query_rows = query_ref[rows, :] * jnp.bfloat16(scale)
        grad_rows = grad_ref[rows, :]
        products = (grad_rows.astype(jnp.float32) * out_ref[rows, :].astype(jnp.float32)).T
        query_parts = [head_part(query_rows, head, size) for head in range(heads)]
        grad_parts = [head_part(grad_rows, head, size) for head in range(heads)]
        inner = [jnp.sum(products[head * size:(head + 1) * size], axis=0, keepdims=True) for head in range(heads)]
        query_stack = jnp.concatenate(query_parts, axis=0)
        grad_stack = jnp.concatenate(grad_parts, axis=0)
        query_grads = [None] * heads
        for j in range(i + 1):
            cols = pl.ds(j * block, block)
            weight_list = []
            score_list = []
            for head in range(heads):
                tile = dot_nt(key_ref[cols, :], query_parts[head])
                if j == i:
                    tile = tile + tiles[head][0]
                elif j == i - 1:
                    tile = tile + tiles[head][1]
                weights = jnp.exp(tile - total_ref[0, head:head + 1, rows])
                grads = dot_nt(value_ref[cols, :], grad_parts[head])
                score_grads = weights * (grads - inner[head])
                low = score_grads.astype(jnp.bfloat16)
                weight_list.append(weights.astype(jnp.bfloat16))
                score_list.append(low)
                part = dot_nn(flipped[head * size:(head + 1) * size, j * block:(j + 1) * block], low)
                query_grads[head] = part if query_grads[head] is None else query_grads[head] + part
                if j == i:
                    near_acc[head] = score_grads if near_acc[head] is None else near_acc[head] + score_grads
                else:
                    far = score_grads
                    if j == i - 1:
                        close = jnp.where(tiles[head][2], score_grads, 0.0)
                        near_acc[head] = near_acc[head] + close
                        far = score_grads - close
                    far = jnp.sum(far, axis=0, keepdims=True)
                    far_acc[head] = far if far_acc[head] is None else far_acc[head] + far
            value_part = dot_nn(jnp.concatenate(weight_list, axis=1), grad_stack)
            key_part = dot_nn(jnp.concatenate(score_list, axis=1), query_stack)
            if j == i:
                value_acc[cols, :] = value_part
                key_acc[cols, :] = key_part
            else:
                value_acc[cols, :] += value_part
                key_acc[cols, :] += key_part
        grads_ref[0, rows, :] = (jnp.concatenate(query_grads, axis=0) * scale).T.astype(grads_ref.dtype)
    grads_ref[1] = key_acc[...].astype(grads_ref.dtype)
    grads_ref[2] = value_acc[...].astype(grads_ref.dtype)
    for head in range(heads):
        dist_ref[0, head:head + 1, :] = diagonal_sums(near_acc[head])
        dist_ref[0, heads + head:heads + head + 1, :] = far_acc[head]


def attend_back(queries, keys, values, grads, outs, totals, near, size, block):
    length, width = queries.shape
    lanes = 128
    heads = lanes // size
    groups = width // lanes
    column = pl.BlockSpec((length, lanes), lambda g: (0, g))
    head_rows = pl.BlockSpec((1, heads, block), lambda g: (g, 0, 0))
    return pl.pallas_call(
        partial(attend_back_kernel, block=block, size=size, scale=size ** -0.5),
        grid=(groups,),
        in_specs=[column] * 5 + [pl.BlockSpec((1, heads, length), lambda g: (g, 0, 0)), head_rows],
        out_specs=[pl.BlockSpec((3, length, lanes), lambda g: (0, 0, g)), pl.BlockSpec((1, 2 * heads, block), lambda g: (g, 0, 0))],
        out_shape=[jax.ShapeDtypeStruct((3, length, width), jnp.bfloat16), jax.ShapeDtypeStruct((groups, 2 * heads, block), jnp.float32)],
        scratch_shapes=[pltpu.VMEM((length, lanes), jnp.float32)] * 2,
        compiler_params=pltpu.CompilerParams(vmem_limit_bytes=62 << 20),
    )(queries, keys, values, grads, outs, totals, near)


def reverse_bits(value, count):
    out = value * 0
    for level in range(count):
        out = out * 2 + (value >> level) % 2
    return out


def project_kernel(owner_ref, inputs_ref, gain_ref, *refs, eps):
    piece_refs, weight_refs, low_ref, out_refs = refs[:4], refs[-7:-4], refs[-4], refs[-3:]
    count, half, three, _ = piece_refs[0].shape
    piece = three // 3
    owners = 2 * count
    part = owners * piece
    @pl.when(pl.program_id(0) == 0)
    def _():
        me = owner_ref[0]
        for source in range(owners):
            apart = jnp.bitwise_xor(me, source)
            near = apart % 2 == 0
            place = apart // 2
            places = (place, reverse_bits(place, owners.bit_length() - 2))
            for group in range(2):
                for line in range(half):
                    block = jnp.where(near, piece_refs[2 * group][places[group], line], piece_refs[2 * group + 1][places[group], line])
                    start = (group * half + line) * part + source * piece
                    for index in range(3):
                        weight_refs[index][start:start + piece, :] = block[index * piece:(index + 1) * piece]
    rows = inputs_ref[...].astype(jnp.float32)
    inverse = lax.rsqrt(jnp.mean(rows * rows, axis=1, keepdims=True) + eps)
    low = (rows * inverse * gain_ref[...]).astype(jnp.bfloat16)
    low_ref[...] = low
    for weight_ref, out_ref in zip(weight_refs, out_refs):
        out_ref[...] = dot_nn(low, weight_ref[...]).astype(jnp.bfloat16)


def project(owner, inputs, gain, pieces, eps, after=(), block=256):
    tokens, width = inputs.shape
    rows = pl.BlockSpec((block, width), lambda i: (i, 0))
    whole = lambda shape: pl.BlockSpec(shape, lambda i: (0,) * len(shape))
    weight = jax.ShapeDtypeStruct((width, width), jnp.bfloat16)
    return pl.pallas_call(
        partial(project_kernel, eps=eps),
        grid=(tokens // block,),
        in_specs=[pl.BlockSpec(memory_space=pltpu.SMEM), rows, whole(gain.shape)] + [whole(piece.shape) for piece in pieces] + [pl.BlockSpec(memory_space=pl.ANY)] * len(after),
        out_specs=[whole(weight.shape)] * 3 + [rows] * 4,
        out_shape=[weight] * 3 + [jax.ShapeDtypeStruct((tokens, width), jnp.bfloat16)] * 4,
        compiler_params=pltpu.CompilerParams(vmem_limit_bytes=62 << 20),
    )(owner, inputs, gain, *pieces, *after)


def settle_kernel(mixed_ref, merge_ref, inputs_ref, gain_ref, router_ref, routes_ref, slots_ref, resid_ref, low_ref, gates_ref, out_ref, held, *, eps, settling):
    step = pl.program_id(0)
    block = mixed_ref.shape[0]
    @pl.when(step < settling)
    def _():
        resid = inputs_ref[...].astype(jnp.float32) + dot_nn(mixed_ref[...], merge_ref[...])
        resid_ref[...] = resid
        inverse = lax.rsqrt(jnp.mean(resid * resid, axis=1, keepdims=True) + eps)
        low = (resid * inverse * gain_ref[...]).astype(jnp.bfloat16)
        low_ref[...] = low
        held[pl.ds(pl.multiple_of(step * block, block), block), :] = low
        logits = dot_nt(router_ref[...], low)
        expert = lax.broadcasted_iota(jnp.int32, logits.shape, 0)
        chosen = [jnp.sum(jnp.where(routes_ref[c:c + 1, :] == expert, logits, 0.0), axis=0, keepdims=True) for c in range(2)]
        top = jnp.maximum(chosen[0], chosen[1])
        powers = [jnp.exp(value - top) for value in chosen]
        total = powers[0] + powers[1]
        for c in range(2):
            gates_ref[c:c + 1, :] = powers[c] / total
    @pl.when(step >= settling)
    def _():
        tokens = held.shape[0]
        slot = lax.broadcasted_iota(jnp.int32, (block, tokens), 0) + (step - settling) * block
        hot = jnp.where((slot == slots_ref[0:1, :]) | (slot == slots_ref[1:2, :]), 1.0, 0.0)
        out_ref[...] = dot_nn(hot.astype(jnp.bfloat16), held[...]).astype(out_ref.dtype)


def settle(mixed, merge, inputs, gain, router, routes, slots, count, eps, block=256):
    tokens, width = inputs.shape
    settling = tokens // block
    early = lambda i: jnp.minimum(i, settling - 1)
    rows = pl.BlockSpec((block, width), lambda i: (early(i), 0))
    whole = lambda shape: pl.BlockSpec(shape, lambda i: (0, 0))
    small = pl.BlockSpec((2, block), lambda i: (0, early(i)))
    return pl.pallas_call(
        partial(settle_kernel, eps=eps, settling=settling),
        grid=(settling + count // block,),
        in_specs=[rows, whole(merge.shape), rows, whole(gain.shape), whole(router.shape), small, whole(slots.shape)],
        out_specs=[rows, rows, small, pl.BlockSpec((block, width), lambda i: (jnp.maximum(i - settling, 0), 0))],
        out_shape=[jax.ShapeDtypeStruct((tokens, width), jnp.float32), jax.ShapeDtypeStruct((tokens, width), jnp.bfloat16), jax.ShapeDtypeStruct((2, tokens), jnp.float32), jax.ShapeDtypeStruct((count, width), jnp.bfloat16)],
        scratch_shapes=[pltpu.VMEM((tokens, width), jnp.bfloat16)],
        compiler_params=pltpu.CompilerParams(vmem_limit_bytes=62 << 20),
    )(mixed, merge, inputs, gain, router, routes, slots)


def finish_kernel(heads_ref, query_ref, key_ref, value_ref, gain_ref, inputs_ref, resid_grad_ref, out_ref, gain_grad_ref, *, eps):
    grads = dot_nt(heads_ref[0], query_ref[...]) + dot_nt(heads_ref[1], key_ref[...]) + dot_nt(heads_ref[2], value_ref[...])
    rows = inputs_ref[...].astype(jnp.float32)
    inverse = lax.rsqrt(jnp.mean(rows * rows, axis=1, keepdims=True) + eps)
    unit = rows * inverse
    @pl.when(pl.program_id(0) == 0)
    def _():
        gain_grad_ref[...] = jnp.zeros_like(gain_grad_ref)
    gain_grad_ref[...] += jnp.sum(grads * unit, axis=0, keepdims=True)
    scaled = grads * gain_ref[...]
    inner = jnp.mean(scaled * unit, axis=1, keepdims=True)
    out_ref[...] = resid_grad_ref[...] + inverse * (scaled - unit * inner)


def finish(head_grads, query, key, value, gain, inputs, resid_grad, eps, block=256):
    tokens, width = inputs.shape
    rows = pl.BlockSpec((block, width), lambda i: (i, 0))
    whole = lambda shape: pl.BlockSpec(shape, lambda i: (0, 0))
    return pl.pallas_call(
        partial(finish_kernel, eps=eps),
        grid=(tokens // block,),
        in_specs=[pl.BlockSpec((3, block, width), lambda i: (0, i, 0))] + [whole(query.shape)] * 3 + [whole(gain.shape), rows, rows],
        out_specs=[rows, whole((1, width))],
        out_shape=[jax.ShapeDtypeStruct((tokens, width), jnp.float32), jax.ShapeDtypeStruct((1, width), jnp.float32)],
        compiler_params=pltpu.CompilerParams(vmem_limit_bytes=62 << 20),
    )(head_grads, query, key, value, gain, inputs, resid_grad)


def weight_kernel(left_ref, mixed_ref, heads_ref, branch_ref, out_ref, turned, right):
    shards, part, _ = out_ref.shape
    step = pl.program_id(0)
    last = pl.num_programs(0) - 1
    @pl.when(step == 0)
    def _():
        turned[...] = left_ref[...].T
    @pl.when(step < last)
    def _():
        right[...] = heads_ref[...]
    @pl.when(step == last)
    def _():
        turned[...] = mixed_ref[...].T
        right[...] = branch_ref[...]
    for shard in range(shards):
        grad = dot_nn(turned[shard * part:(shard + 1) * part, :], right[...])
        out_ref[shard] = grad.astype(jnp.bfloat16)


def weight_grads(left, mixed, head_grads, branch, shards):
    count, tokens, width = head_grads.shape
    part = width // shards
    fixed = pl.BlockSpec((tokens, width), lambda i: (0, 0))
    return pl.pallas_call(
        weight_kernel,
        grid=(count + 1,),
        in_specs=[fixed, fixed, pl.BlockSpec((None, tokens, width), lambda i: (jnp.minimum(i, count - 1), 0, 0)), fixed],
        out_specs=pl.BlockSpec((shards, part, width), lambda i: (0, i, 0)),
        out_shape=jax.ShapeDtypeStruct((shards, (count + 1) * part, width), jnp.bfloat16),
        scratch_shapes=[pltpu.VMEM((width, tokens), jnp.bfloat16), pltpu.VMEM((tokens, width), jnp.bfloat16)],
        compiler_params=pltpu.CompilerParams(vmem_limit_bytes=62 << 20),
    )(left, mixed, head_grads, branch)


def widen_first_kernel(rows_ref, out_ref):
    out_ref[...] = rows_ref[...].astype(jnp.float32)


def widen_first(rows):
    count, width = rows.shape
    half = pl.BlockSpec((count // 2, width), lambda i: (i, 0))
    return pl.pallas_call(
        widen_first_kernel,
        grid=(2,),
        in_specs=[half],
        out_specs=half,
        out_shape=jax.ShapeDtypeStruct((2 * count, width), jnp.float32),
        compiler_params=pltpu.CompilerParams(vmem_limit_bytes=62 << 20),
    )(rows)


def widen_rest_kernel(rows_ref, into_ref, up_ref, down_ref):
    del into_ref
    wide = rows_ref[...].astype(jnp.float32)
    step = pl.program_id(0)
    @pl.when(step < 2)
    def _():
        up_ref[...] = wide
    @pl.when(step >= 2)
    def _():
        down_ref[...] = wide


def widen_rest(rows, into):
    count, width = rows.shape[0] // 3, rows.shape[1]
    half = lambda place: pl.BlockSpec((count, width), lambda i: (place(i), 0))
    wide = jax.ShapeDtypeStruct((2 * count, width), jnp.float32)
    return pl.pallas_call(
        widen_rest_kernel,
        grid=(3,),
        in_specs=[half(lambda i: i), pl.BlockSpec(memory_space=pl.ANY)],
        out_specs=[half(lambda i: jnp.minimum(i, 1)), half(lambda i: 1)],
        out_shape=[wide, wide],
        input_output_aliases={1: 1},
        compiler_params=pltpu.CompilerParams(vmem_limit_bytes=62 << 20),
    )(rows, into)


OWNER = "expert"
LINE = "shard"


def exchange(rows, bit):
    count = lax.axis_size(OWNER)
    return lax.ppermute(rows, OWNER, [(i, i ^ bit) for i in range(count)])


def shift(rows, step):
    count = lax.axis_size(LINE)
    return lax.ppermute(rows, LINE, [(i, (i + step) % count) for i in range(count)])


def gather_line(rows):
    count = lax.axis_size(LINE)
    me = lax.axis_index(LINE)
    out = jnp.zeros((count,) + rows.shape, rows.dtype)
    out = lax.dynamic_update_index_in_dim(out, rows, me, 0)
    for step in range(1, count):
        got = shift(rows, step)
        out = lax.dynamic_update_index_in_dim(out, got, (me - step) % count, 0)
    return out


def add_low(left, right):
    return (left.astype(jnp.float32) + right.astype(jnp.float32)).astype(jnp.bfloat16)


def side(bit):
    return (lax.axis_index(OWNER) // bit) % 2


def halve(stack, bit):
    half = stack.shape[1] // 2
    keep = lax.dynamic_slice_in_dim(stack, side(bit) * half, half, 1)
    send = lax.dynamic_slice_in_dim(stack, (1 - side(bit)) * half, half, 1)
    got = exchange(send, bit)
    return add_low(keep, got)


def line_sum(stack):
    count = lax.axis_size(LINE)
    place = lax.axis_index(LINE)
    total = lax.dynamic_index_in_dim(stack, place, 0, False).astype(jnp.float32)
    for step in range(1, count):
        send = lax.dynamic_index_in_dim(stack, (place + step) % count, 0, False)
        total = total + shift(send, step).astype(jnp.float32)
    return total.astype(jnp.bfloat16)


def grow(piece, bit):
    other = exchange(piece, bit)
    return jnp.where(
        side(bit) == 0, jnp.concatenate([piece, other]), jnp.concatenate([other, piece])
    )


def reduce_rows(stack, bits):
    unit = 8 << (len(bits) - 1)
    cut = -(-stack.shape[1] // (2 * unit)) * unit
    parts = [stack[:, :cut], stack[:, cut:]]
    orders = [bits[1:], bits[:0:-1]]
    for level in range(len(bits) - 1):
        parts = [halve(part, order[level]) for part, order in zip(parts, orders)]
    low = parts[0].shape[1]
    piece = line_sum(jnp.concatenate(parts, axis=1))
    parts = [piece[:low], piece[low:]]
    for level in reversed(range(len(bits) - 1)):
        parts = [grow(part, order[level]) for part, order in zip(parts, orders)]
    return grow(jnp.concatenate(parts), bits[0])


def scatter_sum(grads):
    shards, rows, width = grads.shape
    grads = grads.reshape(shards * rows, width)
    return lax.psum_scatter(grads, LINE, scatter_dimension=0, tiled=True)


def share_rows(rows):
    return lax.all_to_all(rows, OWNER, 0, 0, tiled=True)


def share_large(rows):
    return pltpu.with_memory_space_constraint(share_rows(rows), pltpu.HBM)


def local(
    inputs,
    norm_gain,
    query_weight,
    key_weight,
    value_weight,
    merge_weight,
    bias_table,
    expert_gain,
    router_weight,
    up_weight,
    down_weight,
    routes,
    cotangent,
):
    f32, bf16 = jnp.float32, jnp.bfloat16
    tokens, width = inputs.shape
    owners = lax.axis_size(OWNER)
    shards = lax.axis_size(LINE)
    me = lax.axis_index(OWNER)
    part = query_weight.shape[0]
    piece = part // owners
    local_heads = bias_table.shape[1]
    heads = local_heads * shards
    size = width // heads
    experts = router_weight.shape[1]
    local_count, _, hidden = up_weight.shape
    capacity = (5 * tokens * routes.shape[1] + 4 * experts - 1) // (4 * experts)
    capacity = -(-capacity // 16) * 16
    rows = owners * capacity
    assert local_count == 2 and hidden // shards == width

    router_at = 2 + local_heads + (-(2 + local_heads)) % 8

    def widen(block):
        return jnp.pad(block, ((0, 0), (0, width - block.shape[1])))

    def pack(gain_one, gain_two, table, router):
        head = jnp.concatenate([gain_one, gain_two], axis=0)
        gap = jnp.zeros((router_at - 2 - local_heads, width), bf16)
        return jnp.concatenate([widen(head), widen(table), gap, widen(router)], axis=0)

    small = pack(norm_gain[None], expert_gain[None], bias_table.T, router_weight.T)
    slices = [
        lax.dynamic_slice_in_dim(weight, me * piece, piece, 0)
        for weight in (query_weight, key_weight, value_weight)
    ]
    lined = gather_line(jnp.concatenate(slices + [small]))
    small_full = lined[:, 3 * piece :]
    bits = [1 << level for level in range(owners.bit_length() - 1)]
    pieces = []
    for index, order in enumerate((bits[1:], bits[:0:-1])):
        held = lined[index * shards // 2 : (index + 1) * shards // 2, : 3 * piece][None]
        for bit in order:
            got = exchange(held, bit)
            held = jnp.concatenate([held, got])
        pieces += [held, exchange(held, bits[0])]
    merge_full = lax.all_gather(merge_weight, LINE, axis=0, tiled=True)

    gain_one = small_full[:, 0, :part].reshape(1, width).astype(f32)
    gain_two = small_full[:, 1, :part].reshape(1, width).astype(f32)
    table_full = small_full[:, 2 : 2 + local_heads, :BUCKETS].reshape(heads, BUCKETS).astype(f32)
    router_full = small_full[:, router_at : router_at + experts, :part]
    router_full = router_full.transpose(1, 0, 2).reshape(experts, width)

    routes_line = routes.T
    base = (routes_line % local_count * owners + routes_line // local_count) * capacity
    slots = find_slots(routes_line, base, experts)
    cot_rows, other = dispatch_first(
        slots, routes_line.astype(f32), cotangent, owners, capacity
    )
    other = share_rows(other).reshape(owners, local_count, capacity)

    owner = me.astype(jnp.int32).reshape(1)
    block = 256
    hot = bucket_hot(tokens)
    assert hot[block:, -1].all()
    near_hot = jnp.asarray((hot[:block] - hot[-1:]).T, dtype=f32)
    group = 128 // size
    near = jnp.dot(table_full, near_hot, precision=lax.Precision.HIGHEST)
    near = near.reshape(heads // group, group, block)
    query_full, key_full, value_full, low_one, queries, keys, values = project(
        owner, inputs, gain_one, pieces, epsilon, after=(near, router_full)
    )
    cot_in = share_large(cot_rows)
    attended, totals = attend(queries, keys, values, near, size, block)
    resid, low_two, gates, send = settle(
        attended, merge_full, inputs, gain_two, router_full, routes_line, slots, rows, epsilon
    )

    others = [other[:, index].reshape(1, rows) for index in range(local_count)]
    rows_in = share_large(send.reshape(owners, capacity, width))
    joint = dispatch_both(
        slots, low_two, cotangent, rows, owners, capacity, after=others
    )
    joint_in = share_large(joint)
    act, slope, first_down, grad_in = expert_first(
    owner, rows_in, cot_in, others[0], router_full, up_weight, 0, local_count, shards,
    )
    first_sum = scatter_sum(first_down)
    first_made, pair = expert_second(rows_in, grad_in, act, slope, up_weight, down_weight, 0, owners, shards, 3 * width)
    act, slope, pair, grad_in = expert_first(
        owner, joint_in, joint_in, others[1], router_full, up_weight, 1, local_count, shards,
        into=pair,
    )
    low, pair = expert_slope(joint_in, grad_in, slope, down_weight, 1, shards, pair, 1)
    pair_sum = scatter_sum(pair)
    second_made = expert_last(act, low, up_weight, down_weight, 1, owners, shards)
    returned = share_rows(first_made)
    result, inner, part_grads = combine_part(slots, gates, resid, cotangent, returned)
    returned = share_rows(second_made)
    output, logit_grad = combine_out(
        slots, routes_line, gates, result, inner, cotangent, returned
    )
    router_wide = jnp.pad(router_full, ((0, 128 - experts), (0, 0)))
    resid_grad, branch, mixed_grad, gain_grad = combine_back(
        slots, logit_grad, router_wide, gain_two, resid, cotangent, merge_full,
        part_grads, returned, epsilon
    )
    router_grad = jnp.einsum("te,ti->ei", logit_grad, low_two, preferred_element_type=f32)
    head_grads, distances = attend_back(
        queries, keys, values, mixed_grad, attended, totals, near, size, block
    )
    close_sums = distances[:, :group].reshape(heads, block)
    far_sums = jnp.sum(distances[:, group:].reshape(heads, block), axis=1)
    table_grad = jnp.dot(close_sums, jnp.asarray(hot[:block]), precision=lax.Precision.HIGHEST)
    table_grad = table_grad + far_sums[:, None] * jnp.asarray(hot[-1:])
    sums = weight_grads(low_one, attended, head_grads, branch, shards)
    sums = halve(sums, bits[0])
    input_gradient, norm_grad = finish(
        head_grads, query_full, key_full, value_full, gain_one, inputs, resid_grad, epsilon
    )
    small_grad = jax.vmap(pack)(
        norm_grad.reshape(shards, 1, part).astype(bf16),
        gain_grad.reshape(shards, 1, part).astype(bf16),
        table_grad.reshape(shards, local_heads, BUCKETS).astype(bf16),
        router_grad[:experts].reshape(experts, shards, part).transpose(1, 0, 2).astype(bf16),
    )
    spare = -small_grad.shape[1] % (8 * owners)
    small_grad = halve(jnp.pad(small_grad, ((0, 0), (0, spare), (0, 0))), bits[0])
    kept = sums.shape[1]
    sums = reduce_rows(jnp.concatenate([sums, small_grad], axis=1), bits)
    half = sums.shape[0] // 2
    weights = jnp.concatenate([sums[:kept], sums[half : half + kept]]).astype(f32)
    small_sum = jnp.concatenate([sums[kept:half], sums[half + kept :]]).astype(f32)
    up_sum, down_sum = widen_rest(pair_sum, widen_first(first_sum))
    return (
        output,
        input_gradient,
        small_sum[0, :part],
        weights[:part],
        weights[part : 2 * part],
        weights[2 * part : 3 * part],
        weights[3 * part :],
        small_sum[2 : 2 + local_heads, :BUCKETS].T,
        small_sum[1, :part],
        small_sum[router_at : router_at + experts, :part].T,
        up_sum.reshape(local_count, width, width),
        down_sum.reshape(local_count, width, width),
    )


def solution(mesh):
    in_specs = (
        P((OWNER, LINE), None),
        P(LINE),
        P(LINE, None),
        P(LINE, None),
        P(LINE, None),
        P(LINE, None),
        P(None, LINE),
        P(LINE),
        P(LINE, None),
        P(OWNER, None, None),
        P(OWNER, None, None),
        P((OWNER, LINE), None),
        P((OWNER, LINE), None),
    )
    out_specs = (
        P((OWNER, LINE), None),
        P((OWNER, LINE), None),
        P(LINE),
        P(LINE, None),
        P(LINE, None),
        P(LINE, None),
        P(LINE, None),
        P(None, LINE),
        P(LINE),
        P(LINE, None),
        P(OWNER, None, LINE),
        P(OWNER, LINE, None),
    )

    return jax.shard_map(local, mesh=mesh, in_specs=in_specs, out_specs=out_specs, check_vma=False)
```

```python
from functools import partial, reduce

import jax
import jax.numpy as jnp
import numpy as np
from jax import lax
from jax.experimental import pallas as pl
from jax.experimental.pallas import tpu as pltpu
from jax.sharding import PartitionSpec as P


BUCKETS = 32
MAX_DIST = 128


epsilon = 1e-06
masked_score = -1e30


def bucket_hot(length):
    distance = np.arange(length)
    half_count = BUCKETS // 2
    clipped = np.maximum(distance, half_count)
    spread = np.log(clipped / half_count) / np.log(MAX_DIST / half_count) * (BUCKETS - half_count)
    far_bucket = np.minimum(half_count + np.floor(spread).astype(np.int32), BUCKETS - 1)
    bucket = np.where(distance < half_count, distance, far_bucket)
    return (bucket[:, None] == np.arange(BUCKETS)[None, :]).astype(np.float32)


def dot_nt(a, b):
    return lax.dot_general(a, b, (((1,), (1,)), ((), ())), preferred_element_type=jnp.float32)


def dot_nn(a, b):
    return lax.dot_general(a, b, (((1,), (0,)), ((), ())), preferred_element_type=jnp.float32)


def dot_tn(a, b):
    return lax.dot_general(a, b, (((0,), (0,)), ((), ())), preferred_element_type=jnp.float32)


def slot_kernel(routes_ref, slots_ref, float_ref, *, experts, local_count, owners, capacity):
    tokens = routes_ref.shape[1]
    expert = lax.broadcasted_iota(jnp.int32, (experts, tokens), 0)
    hits = [routes_ref[c:c + 1, :] == expert for c in range(2)]
    hot = jnp.where(hits[0] | hits[1], 1.0, 0.0).astype(jnp.bfloat16)
    earlier = lax.broadcasted_iota(jnp.int32, (tokens, tokens), 0)
    later = lax.broadcasted_iota(jnp.int32, (tokens, tokens), 1)
    before = jnp.where(earlier < later, 1.0, 0.0).astype(jnp.bfloat16)
    counts = dot_nn(hot, before)
    column = lax.broadcasted_iota(jnp.int32, (experts, 1), 0)
    base = (column % local_count * owners + column // local_count) * capacity
    counts = counts + base.astype(jnp.float32)
    for c in range(2):
        slot = jnp.sum(jnp.where(hits[c], counts, 0.0), axis=0, keepdims=True)
        slots_ref[c:c + 1, :] = slot.astype(jnp.int32)
    float_ref[...] = routes_ref[...].astype(jnp.float32)


def find_slots(routes, experts, local_count, owners, capacity):
    return pl.pallas_call(
        partial(slot_kernel, experts=experts, local_count=local_count, owners=owners, capacity=capacity),
        out_shape=[jax.ShapeDtypeStruct(routes.shape, jnp.int32), jax.ShapeDtypeStruct(routes.shape, jnp.float32)],
    )(routes)


def dispatch_both_kernel(slots_ref, rows_ref, cot_ref, *refs, start, capacity, early):
    out_ref = refs[-1]
    block, tokens = capacity, rows_ref.shape[0]
    slot = lax.broadcasted_iota(jnp.int32, (block, tokens), 0) + (pl.program_id(0) * block + start)
    hot = jnp.where((slot == slots_ref[0:1, :]) | (slot == slots_ref[1:2, :]), 1.0, 0.0)
    hot = hot.astype(jnp.bfloat16)
    out_ref[0, :capacity] = dot_nn(hot, rows_ref[...]).astype(out_ref.dtype)
    out_ref[0, capacity:] = dot_nn(hot[early:], cot_ref[...]).astype(out_ref.dtype)


def dispatch_both(slots, rows, cot, start, owners, capacity, early, after=()):
    width = rows.shape[1]
    total = 2 * capacity - early
    whole = lambda shape: pl.BlockSpec(shape, lambda i: (0, 0))
    return pl.pallas_call(
        partial(dispatch_both_kernel, start=start, capacity=capacity, early=early),
        grid=(owners,),
        in_specs=[whole(slots.shape), whole(rows.shape), whole(cot.shape)] + [pl.BlockSpec(memory_space=pl.ANY)] * len(after),
        out_specs=pl.BlockSpec((1, total, width), lambda i: (i, 0, 0)),
        out_shape=jax.ShapeDtypeStruct((owners, total, width), rows.dtype),
        compiler_params=pltpu.CompilerParams(vmem_limit_bytes=62 << 20),
    )(slots, rows, cot, *after)


def dispatch_first_kernel(slots_ref, routes_ref, rows_ref, out_ref, other_ref, *, owners, capacity):
    block, tokens = other_ref.shape[2], rows_ref.shape[0]
    row = lax.broadcasted_iota(jnp.int32, (block, tokens), 0)
    slot = row + pl.program_id(0) * capacity
    slot = slot + jnp.where(row >= capacity, (owners - 1) * capacity, 0)
    hits = [slot == slots_ref[c:c + 1, :] for c in range(2)]
    hot = jnp.where(hits[0] | hits[1], 1.0, 0.0)[:out_ref.shape[1]]
    out_ref[0] = dot_nn(hot.astype(jnp.bfloat16), rows_ref[...]).astype(out_ref.dtype)
    other = jnp.where(hits[0], routes_ref[1:2, :], jnp.where(hits[1], routes_ref[0:1, :], 0.0))
    column = jnp.sum(other, axis=1, keepdims=True)
    other_ref[0] = jnp.broadcast_to(column, (block, 128)).T[0:1, :]


def dispatch_first(slots, routes, rows, owners, capacity, early):
    width = rows.shape[1]
    total = capacity + early
    whole = lambda shape: pl.BlockSpec(shape, lambda i: (0, 0))
    return pl.pallas_call(
        partial(dispatch_first_kernel, owners=owners, capacity=capacity),
        grid=(owners,),
        in_specs=[whole(slots.shape), whole(routes.shape), whole(rows.shape)],
        out_specs=[pl.BlockSpec((1, total, width), lambda i: (i, 0, 0)), pl.BlockSpec((1, 1, 2 * capacity), lambda i: (i, 0, 0))],
        out_shape=[jax.ShapeDtypeStruct((owners, total, width), rows.dtype), jax.ShapeDtypeStruct((owners, 1, 2 * capacity), jnp.float32)],
    )(slots, routes, rows)


def gelu_half(v):
    c = np.float32(np.sqrt(2.0 / np.pi))
    square = v * v
    half = 0.5 * jnp.tanh(v * (np.float32(0.044715) * c * square + c)) + 0.5
    return half, square


def gelu_slope(v):
    c = np.float32(np.sqrt(2.0 / np.pi))
    half, square = gelu_half(v)
    return half + v * half * (1.0 - half) * (np.float32(6.0 * 0.044715) * c * square + 2.0 * c)


def arrived_spec(arrived):
    return pl.BlockSpec(arrived.shape, lambda i: (0, 0, 0))


def first_kernel(owner_ref, rows_ref, other_ref, router_ref, up_ref, *refs, index, local_count, capacity, pieces):
    act_ref, pre_ref, down_grad_ref, grad_ref = refs[-4:]
    owners, _, width = rows_ref.shape
    rows = owners * capacity
    chunk = rows // 2
    @pl.when(pl.program_id(0) == 0)
    def _():
        logits = dot_nt(router_ref[...], rows_ref[:, :capacity].reshape(rows, width))
        expert = lax.broadcasted_iota(jnp.int32, logits.shape, 0)
        mine = owner_ref[0] * local_count + index
        own = jnp.sum(jnp.where(expert == mine, logits, 0.0), axis=0, keepdims=True)
        other = other_ref[...].astype(jnp.int32)
        other = jnp.sum(jnp.where(expert == other, logits, 0.0), axis=0, keepdims=True)
        top = jnp.maximum(own, other)
        own = jnp.exp(own - top)
        gate = own / (own + jnp.exp(other - top))
        column = jnp.broadcast_to(gate, (128, rows)).T
        for start in range(0, width, 128):
            parts = [refs[place][:, low:low + size, start:start + 128] for place, low, size in pieces]
            part = parts[0] if len(parts) == 1 else jnp.concatenate(parts, axis=1)
            part = part.reshape(rows, 128).astype(jnp.float32) * column
            grad_ref[:, start:start + 128] = part.astype(jnp.bfloat16)
    up = up_ref[0]
    for start in range(0, rows, chunk):
        part = rows_ref[start // capacity:(start + chunk) // capacity, :capacity].reshape(chunk, width)
        pre = dot_nn(part, up)
        half, _ = gelu_half(pre)
        act_ref[start:start + chunk, :] = (pre * half).astype(jnp.bfloat16)
        pre_ref[start:start + chunk, :] = pre.astype(jnp.bfloat16)
    down_grad_ref[0] = dot_tn(act_ref[...], grad_ref[...]).astype(jnp.bfloat16)


def expert_first(owner, rows_in, cots, pieces, other, router, up, index, local_count, capacity, shards, into=None):
    owners, _, width = rows_in.shape
    rows = owners * capacity
    hidden = up.shape[2]
    tile = hidden // shards
    fixed = pl.BlockSpec((rows, width), lambda i: (0, 0))
    column = pl.BlockSpec((rows, tile), lambda i: (0, i))
    operands = [owner, rows_in, other, router, up, *cots]
    place, aliases = 0, {}
    grad_shape = jax.ShapeDtypeStruct((shards, tile, width), jnp.bfloat16)
    if into is not None:
        aliases = {len(operands): 2}
        operands.append(into)
        place, grad_shape = 2, jax.ShapeDtypeStruct(into.shape, into.dtype)
    return pl.pallas_call(
        partial(first_kernel, index=index, local_count=local_count, capacity=capacity, pieces=pieces),
        grid=(shards,),
        in_specs=[
            pl.BlockSpec(memory_space=pltpu.SMEM),
            arrived_spec(rows_in),
            pl.BlockSpec((1, rows), lambda i: (0, 0)),
            pl.BlockSpec(router.shape, lambda i: (0, 0)),
            pl.BlockSpec((1, width, tile), lambda i: (index, 0, i)),
        ]
        + [arrived_spec(cot) for cot in cots]
        + [pl.BlockSpec(memory_space=pl.ANY)] * (into is not None),
        out_specs=[column, column, pl.BlockSpec((1, tile, width), lambda i: (i, place, 0)), fixed],
        out_shape=[jax.ShapeDtypeStruct((rows, hidden), jnp.bfloat16)] * 2 + [grad_shape, jax.ShapeDtypeStruct((rows, width), jnp.bfloat16)],
        input_output_aliases=aliases,
        compiler_params=pltpu.CompilerParams(vmem_limit_bytes=62 << 20),
    )(*operands)


def second_kernel(rows_ref, grad_ref, act_ref, pre_ref, up_ref, down_ref, *refs):
    made_ref, up_grad_ref, turned, made_acc, back_acc = refs[-5:]
    step = pl.program_id(0)
    owners, _, capacity, width = made_ref.shape
    @pl.when(step == 0)
    def _():
        rows, width = grad_ref.shape
        owners = rows_ref.shape[0]
        turned[...] = rows_ref[:, :rows // owners].reshape(rows, width).T
    up = up_ref[0]
    down = down_ref[0]
    grads = dot_nt(grad_ref[...], down)
    low = (gelu_slope(pre_ref[...].astype(jnp.float32)) * grads).astype(jnp.bfloat16)
    up_grad_ref[0] = dot_nn(turned[...], low).astype(jnp.bfloat16)
    back = dot_nt(low, up)
    made = dot_nn(act_ref[...], down)
    last = pl.num_programs(0) - 1
    @pl.when(step == 0)
    def _():
        made_acc[...] = made
        back_acc[...] = back
    @pl.when((step > 0) & (step < last))
    def _():
        made_acc[...] += made
        back_acc[...] += back
    @pl.when(step == last)
    def _():
        made_ref[:, 0] = (made_acc[...] + made).astype(jnp.bfloat16).reshape(owners, capacity, width)
        made_ref[:, 1] = (back_acc[...] + back).astype(jnp.bfloat16).reshape(owners, capacity, width)


def expert_second(rows_in, grad, act, pre, up, down, index, owners, shards, wide, after=()):
    rows, width = grad.shape
    hidden = up.shape[2]
    tile = hidden // shards
    fixed = pl.BlockSpec((rows, width), lambda i: (0, 0))
    column = pl.BlockSpec((rows, tile), lambda i: (0, i))
    made_shape = (owners, 2, rows // owners, width)
    return pl.pallas_call(
        second_kernel,
        grid=(shards,),
        in_specs=[arrived_spec(rows_in), fixed, column, column, pl.BlockSpec((1, width, tile), lambda i: (index, 0, i)), pl.BlockSpec((1, tile, width), lambda i: (index, i, 0))]
        + [pl.BlockSpec(memory_space=pl.ANY)] * len(after),
        out_specs=[pl.BlockSpec(made_shape, lambda i: (0, 0, 0, 0)), pl.BlockSpec((1, width, tile), lambda i: (i, 0, 0))],
        out_shape=[jax.ShapeDtypeStruct(made_shape, jnp.bfloat16), jax.ShapeDtypeStruct((shards, wide, tile), jnp.bfloat16)],
        scratch_shapes=[pltpu.VMEM((width, rows), jnp.bfloat16), pltpu.VMEM((rows, width), jnp.float32), pltpu.VMEM((rows, width), jnp.float32)],
        compiler_params=pltpu.CompilerParams(vmem_limit_bytes=62 << 20),
    )(rows_in, grad, act, pre, up, down, *after)


def slope_kernel(rows_ref, grad_ref, pre_ref, down_ref, into_ref, low_ref, up_grad_ref, turned):
    del into_ref
    @pl.when(pl.program_id(0) == 0)
    def _():
        rows, width = grad_ref.shape
        owners = rows_ref.shape[0]
        turned[...] = rows_ref[:, :rows // owners].reshape(rows, width).T
    grads = dot_nt(grad_ref[...], down_ref[0])
    low = (gelu_slope(pre_ref[...].astype(jnp.float32)) * grads).astype(jnp.bfloat16)
    low_ref[...] = low
    up_grad_ref[0] = dot_nn(turned[...], low).astype(jnp.bfloat16)


def expert_slope(rows_in, grad, pre, down, index, shards, into, place):
    rows, width = grad.shape
    hidden = pre.shape[1]
    tile = hidden // shards
    fixed = pl.BlockSpec((rows, width), lambda i: (0, 0))
    column = pl.BlockSpec((rows, tile), lambda i: (0, i))
    return pl.pallas_call(
        slope_kernel,
        grid=(shards,),
        in_specs=[arrived_spec(rows_in), fixed, column, pl.BlockSpec((1, tile, width), lambda i: (index, i, 0)), pl.BlockSpec(memory_space=pl.ANY)],
        out_specs=[column, pl.BlockSpec((1, width, tile), lambda i: (i, place, 0))],
        out_shape=[jax.ShapeDtypeStruct((rows, hidden), jnp.bfloat16), jax.ShapeDtypeStruct(into.shape, into.dtype)],
        input_output_aliases={4: 1},
        scratch_shapes=[pltpu.VMEM((width, rows), jnp.bfloat16)],
        compiler_params=pltpu.CompilerParams(vmem_limit_bytes=62 << 20),
    )(rows_in, grad, pre, down, into)


def last_kernel(act_ref, low_ref, up_ref, down_ref, made_ref, made_acc, back_acc):
    step = pl.program_id(0)
    owners, _, capacity, width = made_ref.shape
    back = dot_nt(low_ref[...], up_ref[0])
    made = dot_nn(act_ref[...], down_ref[0])
    last = pl.num_programs(0) - 1
    @pl.when(step == 0)
    def _():
        made_acc[...] = made
        back_acc[...] = back
    @pl.when((step > 0) & (step < last))
    def _():
        made_acc[...] += made
        back_acc[...] += back
    @pl.when(step == last)
    def _():
        made_ref[:, 0] = (made_acc[...] + made).astype(jnp.bfloat16).reshape(owners, capacity, width)
        made_ref[:, 1] = (back_acc[...] + back).astype(jnp.bfloat16).reshape(owners, capacity, width)


def expert_last(act, low, up, down, index, owners, shards):
    rows, hidden = act.shape
    width = up.shape[1]
    tile = hidden // shards
    column = pl.BlockSpec((rows, tile), lambda i: (0, i))
    made_shape = (owners, 2, rows // owners, width)
    return pl.pallas_call(
        last_kernel,
        grid=(shards,),
        in_specs=[column, column, pl.BlockSpec((1, width, tile), lambda i: (index, 0, i)), pl.BlockSpec((1, tile, width), lambda i: (index, i, 0))],
        out_specs=pl.BlockSpec(made_shape, lambda i: (0, 0, 0, 0)),
        out_shape=jax.ShapeDtypeStruct(made_shape, jnp.bfloat16),
        scratch_shapes=[pltpu.VMEM((rows, width), jnp.float32), pltpu.VMEM((rows, width), jnp.float32)],
        compiler_params=pltpu.CompilerParams(vmem_limit_bytes=62 << 20),
    )(act, low, up, down)


def spread(row, block):
    return jnp.broadcast_to(row, (128, block)).T


def pick(slots, lane, back_refs, first=0):
    picked = None
    for index, back_ref in enumerate(back_refs, first):
        owners, capacity, width = back_ref.shape
        half = owners * capacity
        hots = []
        for start in range(index * half, (index + 1) * half, 128):
            hit = reduce(jnp.logical_or, [slot == lane + start for slot in slots])
            hots.append(jnp.where(hit, 1.0, 0.0).astype(jnp.bfloat16))
        part = dot_nn(jnp.concatenate(hots, axis=1), back_ref[...].reshape(half, width))
        picked = part if picked is None else picked + part
    return picked


def part_kernel(slots_ref, gates_ref, resid_ref, cot_ref, made_ref, back_ref, result_ref, inner_ref, grads_ref):
    block = result_ref.shape[0]
    lane = lax.broadcasted_iota(jnp.int32, (block, 128), 1)
    cot = cot_ref[...].astype(jnp.float32)
    result = resid_ref[...]
    inner = jnp.zeros((block, 128), jnp.float32)
    slots = [spread(slots_ref[c:c + 1, :], block) for c in range(2)]
    for c in range(2):
        picked = pick([slots[c]], lane, [made_ref])
        result = result + spread(gates_ref[c:c + 1, :], block)[:, 0:1] * picked
        inner = inner + jnp.where(lane == c, jnp.sum(cot * picked, axis=1, keepdims=True), 0.0)
    result_ref[...] = result
    inner_ref[...] = inner
    grads_ref[...] = pick(slots, lane, [back_ref])


def combine_part(slots, gates, resid, cot, returned, block=256):
    tokens, width = resid.shape
    small = pl.BlockSpec((2, block), lambda i: (0, i))
    rows = pl.BlockSpec((block, width), lambda i: (i, 0))
    wide = jax.ShapeDtypeStruct((tokens, width), jnp.float32)
    return pl.pallas_call(
        part_kernel,
        grid=(tokens // block,),
        in_specs=[small, small, rows, rows, returned_spec(returned, 0), returned_spec(returned, 1)],
        out_specs=[rows, pl.BlockSpec((block, 128), lambda i: (i, 0)), rows],
        out_shape=[wide, jax.ShapeDtypeStruct((tokens, 128), jnp.float32), wide],
        compiler_params=pltpu.CompilerParams(vmem_limit_bytes=62 << 20),
    )(slots, gates, resid, cot, returned, returned)


def out_kernel(slots_ref, routes_ref, gates_ref, result_ref, inner_ref, cot_ref, made_ref, out_ref, logit_ref):
    block = out_ref.shape[0]
    lane = lax.broadcasted_iota(jnp.int32, (block, 128), 1)
    cot = cot_ref[...].astype(jnp.float32)
    result = result_ref[...]
    gates, inner = [], []
    for c in range(2):
        slot = spread(slots_ref[c:c + 1, :], block)
        gate = spread(gates_ref[c:c + 1, :], block)[:, 0:1]
        picked = pick([slot], lane, [made_ref], 1)
        result = result + gate * picked
        gates.append(gate)
        inner.append(inner_ref[:, c:c + 1] + jnp.sum(cot * picked, axis=1, keepdims=True))
    out_ref[...] = result.astype(out_ref.dtype)
    middle = gates[0] * inner[0] + gates[1] * inner[1]
    logit = jnp.zeros((block, 128), jnp.float32)
    for c in range(2):
        route = spread(routes_ref[c:c + 1, :], block)
        logit = logit + jnp.where(route == lane, gates[c] * (inner[c] - middle), 0.0)
    logit_ref[...] = logit.astype(jnp.bfloat16)


def returned_spec(returned, which):
    owners, _, capacity, width = returned.shape
    return pl.BlockSpec((owners, None, capacity, width), lambda i: (0, which, 0, 0))


def combine_out(slots, routes, gates, result, inner, cot, returned, block=256):
    tokens, width = result.shape
    small = pl.BlockSpec((2, block), lambda i: (0, i))
    rows = pl.BlockSpec((block, width), lambda i: (i, 0))
    return pl.pallas_call(
        out_kernel,
        grid=(tokens // block,),
        in_specs=[small, small, small, rows, pl.BlockSpec((block, 128), lambda i: (i, 0)), rows, returned_spec(returned, 0)],
        out_specs=[rows, pl.BlockSpec((block, 128), lambda i: (i, 0))],
        out_shape=[jax.ShapeDtypeStruct((tokens, width), jnp.bfloat16), jax.ShapeDtypeStruct((tokens, 128), jnp.bfloat16)],
        compiler_params=pltpu.CompilerParams(vmem_limit_bytes=62 << 20),
    )(slots, routes, gates, result, inner, cot, returned)


def back_kernel(slots_ref, logit_ref, router_ref, gain_ref, resid_ref, cot_ref, merge_ref, part_ref, back_ref, grad_ref, low_ref, mixed_ref, gain_grad_ref, *, eps):
    block, _ = grad_ref.shape
    lane = lax.broadcasted_iota(jnp.int32, (block, 128), 1)
    grads = part_ref[...] + pick([spread(slots_ref[c:c + 1, :], block) for c in range(2)], lane, [back_ref], 1)
    grads = grads + dot_nn(logit_ref[...], router_ref[...])
    resid = resid_ref[...]
    inverse = lax.rsqrt(jnp.mean(resid * resid, axis=1, keepdims=True) + eps)
    unit = resid * inverse
    @pl.when(pl.program_id(0) == 0)
    def _():
        gain_grad_ref[...] = jnp.zeros_like(gain_grad_ref)
    gain_grad_ref[...] += jnp.sum(grads * unit, axis=0, keepdims=True)
    scaled = grads * gain_ref[...]
    inner = jnp.mean(scaled * unit, axis=1, keepdims=True)
    total = cot_ref[...].astype(jnp.float32) + inverse * (scaled - unit * inner)
    grad_ref[...] = total
    low = total.astype(jnp.bfloat16)
    low_ref[...] = low
    mixed_ref[...] = dot_nt(low, merge_ref[...]).astype(jnp.bfloat16)


def combine_back(slots, logit, router, gain, resid, cot, merge, part, returned, eps, block=256):
    tokens, width = resid.shape
    rows = pl.BlockSpec((block, width), lambda i: (i, 0))
    whole = lambda shape: pl.BlockSpec(shape, lambda i: (0, 0))
    low = jax.ShapeDtypeStruct((tokens, width), jnp.bfloat16)
    return pl.pallas_call(
        partial(back_kernel, eps=eps),
        grid=(tokens // block,),
        in_specs=[pl.BlockSpec((2, block), lambda i: (0, i)), pl.BlockSpec((block, 128), lambda i: (i, 0)), whole(router.shape), whole(gain.shape), rows, rows, whole(merge.shape), rows, returned_spec(returned, 1)],
        out_specs=[rows, rows, rows, whole((1, width))],
        out_shape=[jax.ShapeDtypeStruct((tokens, width), jnp.float32), low, low, jax.ShapeDtypeStruct((1, width), jnp.float32)],
        compiler_params=pltpu.CompilerParams(vmem_limit_bytes=62 << 20),
    )(slots, logit, router, gain, resid, cot, merge, part, returned)


def near_tiles(near_ref, head, block):
    spread = jnp.broadcast_to(near_ref[0, head:head + 1, :], (block, block))
    spread = pltpu.roll(spread, 0, 1, stride=1, stride_axis=0)
    key_at = lax.broadcasted_iota(jnp.int32, (block, block), 0)
    query_at = lax.broadcasted_iota(jnp.int32, (block, block), 1)
    return (jnp.where(query_at >= key_at, spread, masked_score), jnp.where(query_at < key_at, spread, 0.0), query_at < key_at)


def diagonal_sums(tile):
    block = tile.shape[1]
    total = tile[:8]
    for start in range(8, block, 8):
        total = total + pltpu.roll(tile[start:start + 8], block - start, 1)
    row = lax.broadcasted_iota(jnp.int32, total.shape, 0)
    for step in (1, 2, 4):
        total = jnp.where((row & step) != 0, pltpu.roll(total, block - step, 1), total)
    return jnp.sum(total, axis=0, keepdims=True)


def head_part(rows, head, size):
    lane = lax.broadcasted_iota(jnp.int32, rows.shape, 1)
    return jnp.where((lane >= head * size) & (lane < (head + 1) * size), rows, jnp.zeros_like(rows))


def attend_kernel(query_ref, key_ref, value_ref, near_ref, out_ref, total_ref, held, *, block, size, scale):
    length, lanes = query_ref.shape
    heads = lanes // size
    count = length // block
    turned = value_ref[...].T
    ones = jnp.ones((16, length), jnp.bfloat16)
    flipped = [jnp.concatenate([turned[head * size:(head + 1) * size], ones], axis=0) for head in range(heads)]
    tiles = [near_tiles(near_ref, head, block) for head in range(heads)]
    units = [(i, head) for i in range(count) for head in range(heads)]
    def fold(tile, op):
        parts = [tile[k:k + 8] for k in range(0, tile.shape[0], 8)]
        while len(parts) > 1:
            parts = [op(parts[k], parts[k + 1]) for k in range(0, len(parts), 2)]
        return parts[0]
    def score_tile(unit, query_part, j, slot):
        i, head = unit
        tile = dot_nt(key_ref[pl.ds(j * block, block), :], query_part)
        if j == i:
            tile = tile + tiles[head][0]
        elif j == i - 1:
            tile = tile + tiles[head][1]
        held[slot, pl.ds(j * block, block), :] = tile
        return fold(tile, jnp.maximum)
    def part_of(unit):
        i, head = unit
        return head_part(query_ref[pl.ds(i * block, block), :] * jnp.bfloat16(scale), head, size)
    tops = {0: [score_tile(units[0], part_of(units[0]), 0, 0)]}
    outs = []
    for n, (i, head) in enumerate(units):
        top = jnp.max(reduce(jnp.maximum, tops[n]), axis=0, keepdims=True)
        following = units[n + 1] if n + 1 < len(units) else None
        if following is not None:
            query_part = part_of(following)
            tops[n + 1] = []
        mixed = None
        total = None
        steps = max(i + 1, following[0] + 1 if following else 0)
        for j in range(steps):
            if following is not None and j <= following[0]:
                tops[n + 1].append(score_tile(following, query_part, j, (n + 1) % 2))
            if j <= i:
                weights = jnp.exp(held[n % 2, pl.ds(j * block, block), :] - top)
                part = dot_nn(flipped[head][:, j * block:(j + 1) * block], weights.astype(jnp.bfloat16))
                mixed = part if mixed is None else mixed + part
        total = mixed[size:size + 1]
        outs.append(mixed[:size] / total)
        rows = pl.ds(i * block, block)
        total_ref[0, head:head + 1, rows] = top + jnp.log(total)
        if head == heads - 1:
            out_ref[rows, :] = jnp.concatenate(outs[-heads:], axis=0).T.astype(out_ref.dtype)


def attend(queries, keys, values, near, size, block):
    length, width = queries.shape
    lanes = 128
    heads = lanes // size
    groups = width // lanes
    column = pl.BlockSpec((length, lanes), lambda g: (0, g))
    head_rows = pl.BlockSpec((1, heads, block), lambda g: (g, 0, 0))
    return pl.pallas_call(
        partial(attend_kernel, block=block, size=size, scale=size ** -0.5),
        grid=(groups,),
        in_specs=[column, column, column, head_rows],
        out_specs=[column, pl.BlockSpec((1, heads, length), lambda g: (g, 0, 0))],
        out_shape=[jax.ShapeDtypeStruct((length, width), jnp.bfloat16), jax.ShapeDtypeStruct((groups, heads, length), jnp.float32)],
        scratch_shapes=[pltpu.VMEM((2, length, block), jnp.float32)],
        compiler_params=pltpu.CompilerParams(vmem_limit_bytes=62 << 20),
    )(queries, keys, values, near)


def attend_back_kernel(query_ref, key_ref, value_ref, grad_ref, out_ref, total_ref, near_ref, grads_ref, dist_ref, key_acc, value_acc, *, block, size, scale):
    length, lanes = query_ref.shape
    heads = lanes // size
    count = length // block
    flipped = key_ref[...].T
    tiles = [near_tiles(near_ref, head, block) for head in range(heads)]
    near_acc = [None] * heads
    far_acc = [None] * heads
    for i in range(count):
        rows = pl.ds(i * block, block)
        query_rows = query_ref[rows, :] * jnp.bfloat16(scale)
        grad_rows = grad_ref[rows, :]
        products = (grad_rows.astype(jnp.float32) * out_ref[rows, :].astype(jnp.float32)).T
        query_parts = [head_part(query_rows, head, size) for head in range(heads)]
        grad_parts = [head_part(grad_rows, head, size) for head in range(heads)]
        inner = [jnp.sum(products[head * size:(head + 1) * size], axis=0, keepdims=True) for head in range(heads)]
        query_stack = jnp.concatenate(query_parts, axis=0)
        grad_stack = jnp.concatenate(grad_parts, axis=0)
        query_grads = [None] * heads
        for j in range(i + 1):
            cols = pl.ds(j * block, block)
            weight_list = []
            score_list = []
            for head in range(heads):
                tile = dot_nt(key_ref[cols, :], query_parts[head])
                if j == i:
                    tile = tile + tiles[head][0]
                elif j == i - 1:
                    tile = tile + tiles[head][1]
                weights = jnp.exp(tile - total_ref[0, head:head + 1, rows])
                grads = dot_nt(value_ref[cols, :], grad_parts[head])
                score_grads = weights * (grads - inner[head])
                low = score_grads.astype(jnp.bfloat16)
                weight_list.append(weights.astype(jnp.bfloat16))
                score_list.append(low)
                part = dot_nn(flipped[head * size:(head + 1) * size, j * block:(j + 1) * block], low)
                query_grads[head] = part if query_grads[head] is None else query_grads[head] + part
                if j == i:
                    near_acc[head] = score_grads if near_acc[head] is None else near_acc[head] + score_grads
                else:
                    far = score_grads
                    if j == i - 1:
                        close = jnp.where(tiles[head][2], score_grads, 0.0)
                        near_acc[head] = near_acc[head] + close
                        far = score_grads - close
                    far = jnp.sum(far, axis=0, keepdims=True)
                    far_acc[head] = far if far_acc[head] is None else far_acc[head] + far
            value_part = dot_nn(jnp.concatenate(weight_list, axis=1), grad_stack)
            key_part = dot_nn(jnp.concatenate(score_list, axis=1), query_stack)
            if j == i:
                value_acc[cols, :] = value_part
                key_acc[cols, :] = key_part
            else:
                value_acc[cols, :] += value_part
                key_acc[cols, :] += key_part
        grads_ref[0, rows, :] = (jnp.concatenate(query_grads, axis=0) * scale).T.astype(grads_ref.dtype)
    grads_ref[1] = key_acc[...].astype(grads_ref.dtype)
    grads_ref[2] = value_acc[...].astype(grads_ref.dtype)
    for head in range(heads):
        dist_ref[0, head:head + 1, :] = diagonal_sums(near_acc[head])
        dist_ref[0, heads + head:heads + head + 1, :] = far_acc[head]


def attend_back(queries, keys, values, grads, outs, totals, near, size, block):
    length, width = queries.shape
    lanes = 128
    heads = lanes // size
    groups = width // lanes
    column = pl.BlockSpec((length, lanes), lambda g: (0, g))
    head_rows = pl.BlockSpec((1, heads, block), lambda g: (g, 0, 0))
    return pl.pallas_call(
        partial(attend_back_kernel, block=block, size=size, scale=size ** -0.5),
        grid=(groups,),
        in_specs=[column] * 5 + [pl.BlockSpec((1, heads, length), lambda g: (g, 0, 0)), head_rows],
        out_specs=[pl.BlockSpec((3, length, lanes), lambda g: (0, 0, g)), pl.BlockSpec((1, 2 * heads, block), lambda g: (g, 0, 0))],
        out_shape=[jax.ShapeDtypeStruct((3, length, width), jnp.bfloat16), jax.ShapeDtypeStruct((groups, 2 * heads, block), jnp.float32)],
        scratch_shapes=[pltpu.VMEM((length, lanes), jnp.float32)] * 2,
        compiler_params=pltpu.CompilerParams(vmem_limit_bytes=62 << 20),
    )(queries, keys, values, grads, outs, totals, near)


def reverse_bits(value, count):
    out = value * 0
    for level in range(count):
        out = out * 2 + (value >> level) % 2
    return out


def project_kernel(owner_ref, inputs_ref, gain_ref, *refs, eps):
    piece_refs, weight_refs, low_ref, out_refs = refs[:4], refs[-7:-4], refs[-4], refs[-3:]
    count, half, three, _ = piece_refs[0].shape
    piece = three // 3
    owners = 2 * count
    part = owners * piece
    @pl.when(pl.program_id(0) == 0)
    def _():
        me = owner_ref[0]
        for source in range(owners):
            apart = jnp.bitwise_xor(me, source)
            near = apart % 2 == 0
            place = apart // 2
            places = (place, reverse_bits(place, owners.bit_length() - 2))
            for group in range(2):
                for line in range(half):
                    block = jnp.where(near, piece_refs[2 * group][places[group], line], piece_refs[2 * group + 1][places[group], line])
                    start = (group * half + line) * part + source * piece
                    for index in range(3):
                        weight_refs[index][start:start + piece, :] = block[index * piece:(index + 1) * piece]
    rows = inputs_ref[...].astype(jnp.float32)
    inverse = lax.rsqrt(jnp.mean(rows * rows, axis=1, keepdims=True) + eps)
    low = (rows * inverse * gain_ref[...]).astype(jnp.bfloat16)
    low_ref[...] = low
    for weight_ref, out_ref in zip(weight_refs, out_refs):
        out_ref[...] = dot_nn(low, weight_ref[...]).astype(jnp.bfloat16)


def project(owner, inputs, gain, pieces, eps, after=(), block=256):
    tokens, width = inputs.shape
    rows = pl.BlockSpec((block, width), lambda i: (i, 0))
    whole = lambda shape: pl.BlockSpec(shape, lambda i: (0,) * len(shape))
    weight = jax.ShapeDtypeStruct((width, width), jnp.bfloat16)
    return pl.pallas_call(
        partial(project_kernel, eps=eps),
        grid=(tokens // block,),
        in_specs=[pl.BlockSpec(memory_space=pltpu.SMEM), rows, whole(gain.shape)] + [whole(piece.shape) for piece in pieces] + [pl.BlockSpec(memory_space=pl.ANY)] * len(after),
        out_specs=[whole(weight.shape)] * 3 + [rows] * 4,
        out_shape=[weight] * 3 + [jax.ShapeDtypeStruct((tokens, width), jnp.bfloat16)] * 4,
        compiler_params=pltpu.CompilerParams(vmem_limit_bytes=62 << 20),
    )(owner, inputs, gain, *pieces, *after)


def settle_kernel(mixed_ref, merge_ref, inputs_ref, gain_ref, router_ref, routes_ref, slots_ref, resid_ref, low_ref, gates_ref, out_ref, held, *, eps, settling):
    step = pl.program_id(0)
    block = mixed_ref.shape[0]
    @pl.when(step < settling)
    def _():
        resid = inputs_ref[...].astype(jnp.float32) + dot_nn(mixed_ref[...], merge_ref[...])
        resid_ref[...] = resid
        inverse = lax.rsqrt(jnp.mean(resid * resid, axis=1, keepdims=True) + eps)
        low = (resid * inverse * gain_ref[...]).astype(jnp.bfloat16)
        low_ref[...] = low
        held[pl.ds(pl.multiple_of(step * block, block), block), :] = low
        logits = dot_nt(router_ref[...], low)
        expert = lax.broadcasted_iota(jnp.int32, logits.shape, 0)
        chosen = [jnp.sum(jnp.where(routes_ref[c:c + 1, :] == expert, logits, 0.0), axis=0, keepdims=True) for c in range(2)]
        top = jnp.maximum(chosen[0], chosen[1])
        powers = [jnp.exp(value - top) for value in chosen]
        total = powers[0] + powers[1]
        for c in range(2):
            gates_ref[c:c + 1, :] = powers[c] / total
    @pl.when(step >= settling)
    def _():
        tokens = held.shape[0]
        slot = lax.broadcasted_iota(jnp.int32, (block, tokens), 0) + (step - settling) * block
        hot = jnp.where((slot == slots_ref[0:1, :]) | (slot == slots_ref[1:2, :]), 1.0, 0.0)
        out_ref[...] = dot_nn(hot.astype(jnp.bfloat16), held[...]).astype(out_ref.dtype)


def settle(mixed, merge, inputs, gain, router, routes, slots, count, eps, block=256):
    tokens, width = inputs.shape
    settling = tokens // block
    early = lambda i: jnp.minimum(i, settling - 1)
    rows = pl.BlockSpec((block, width), lambda i: (early(i), 0))
    whole = lambda shape: pl.BlockSpec(shape, lambda i: (0, 0))
    small = pl.BlockSpec((2, block), lambda i: (0, early(i)))
    return pl.pallas_call(
        partial(settle_kernel, eps=eps, settling=settling),
        grid=(settling + count // block,),
        in_specs=[rows, whole(merge.shape), rows, whole(gain.shape), whole(router.shape), small, whole(slots.shape)],
        out_specs=[rows, rows, small, pl.BlockSpec((block, width), lambda i: (jnp.maximum(i - settling, 0), 0))],
        out_shape=[jax.ShapeDtypeStruct((tokens, width), jnp.float32), jax.ShapeDtypeStruct((tokens, width), jnp.bfloat16), jax.ShapeDtypeStruct((2, tokens), jnp.float32), jax.ShapeDtypeStruct((count, width), jnp.bfloat16)],
        scratch_shapes=[pltpu.VMEM((tokens, width), jnp.bfloat16)],
        compiler_params=pltpu.CompilerParams(vmem_limit_bytes=62 << 20),
    )(mixed, merge, inputs, gain, router, routes, slots)


def finish_kernel(heads_ref, query_ref, key_ref, value_ref, gain_ref, inputs_ref, resid_grad_ref, out_ref, gain_grad_ref, *, eps):
    grads = dot_nt(heads_ref[0], query_ref[...]) + dot_nt(heads_ref[1], key_ref[...]) + dot_nt(heads_ref[2], value_ref[...])
    rows = inputs_ref[...].astype(jnp.float32)
    inverse = lax.rsqrt(jnp.mean(rows * rows, axis=1, keepdims=True) + eps)
    unit = rows * inverse
    @pl.when(pl.program_id(0) == 0)
    def _():
        gain_grad_ref[...] = jnp.zeros_like(gain_grad_ref)
    gain_grad_ref[...] += jnp.sum(grads * unit, axis=0, keepdims=True)
    scaled = grads * gain_ref[...]
    inner = jnp.mean(scaled * unit, axis=1, keepdims=True)
    out_ref[...] = resid_grad_ref[...] + inverse * (scaled - unit * inner)


def finish(head_grads, query, key, value, gain, inputs, resid_grad, eps, block=256):
    tokens, width = inputs.shape
    rows = pl.BlockSpec((block, width), lambda i: (i, 0))
    whole = lambda shape: pl.BlockSpec(shape, lambda i: (0, 0))
    return pl.pallas_call(
        partial(finish_kernel, eps=eps),
        grid=(tokens // block,),
        in_specs=[pl.BlockSpec((3, block, width), lambda i: (0, i, 0))] + [whole(query.shape)] * 3 + [whole(gain.shape), rows, rows],
        out_specs=[rows, whole((1, width))],
        out_shape=[jax.ShapeDtypeStruct((tokens, width), jnp.float32), jax.ShapeDtypeStruct((1, width), jnp.float32)],
        compiler_params=pltpu.CompilerParams(vmem_limit_bytes=62 << 20),
    )(head_grads, query, key, value, gain, inputs, resid_grad)


def weight_kernel(left_ref, mixed_ref, heads_ref, branch_ref, out_ref, turned, right):
    shards, part, _ = out_ref.shape
    step = pl.program_id(0)
    last = pl.num_programs(0) - 1
    @pl.when(step == 0)
    def _():
        turned[...] = left_ref[...].T
    @pl.when(step < last)
    def _():
        right[...] = heads_ref[...]
    @pl.when(step == last)
    def _():
        turned[...] = mixed_ref[...].T
        right[...] = branch_ref[...]
    for shard in range(shards):
        grad = dot_nn(turned[shard * part:(shard + 1) * part, :], right[...])
        out_ref[shard] = grad.astype(jnp.bfloat16)


def weight_grads(left, mixed, head_grads, branch, shards):
    count, tokens, width = head_grads.shape
    part = width // shards
    fixed = pl.BlockSpec((tokens, width), lambda i: (0, 0))
    return pl.pallas_call(
        weight_kernel,
        grid=(count + 1,),
        in_specs=[fixed, fixed, pl.BlockSpec((None, tokens, width), lambda i: (jnp.minimum(i, count - 1), 0, 0)), fixed],
        out_specs=pl.BlockSpec((shards, part, width), lambda i: (0, i, 0)),
        out_shape=jax.ShapeDtypeStruct((shards, (count + 1) * part, width), jnp.bfloat16),
        scratch_shapes=[pltpu.VMEM((width, tokens), jnp.bfloat16), pltpu.VMEM((tokens, width), jnp.bfloat16)],
        compiler_params=pltpu.CompilerParams(vmem_limit_bytes=62 << 20),
    )(left, mixed, head_grads, branch)


def widen_first_kernel(rows_ref, out_ref):
    out_ref[...] = rows_ref[...].astype(jnp.float32)


def widen_first(rows):
    count, width = rows.shape
    half = pl.BlockSpec((count // 2, width), lambda i: (i, 0))
    return pl.pallas_call(
        widen_first_kernel,
        grid=(2,),
        in_specs=[half],
        out_specs=half,
        out_shape=jax.ShapeDtypeStruct((2 * count, width), jnp.float32),
        compiler_params=pltpu.CompilerParams(vmem_limit_bytes=62 << 20),
    )(rows)


def widen_rest_kernel(rows_ref, into_ref, up_ref, down_ref):
    del into_ref
    wide = rows_ref[...].astype(jnp.float32)
    step = pl.program_id(0)
    @pl.when(step < 2)
    def _():
        up_ref[...] = wide
    @pl.when(step >= 2)
    def _():
        down_ref[...] = wide


def widen_rest(rows, into):
    count, width = rows.shape[0] // 3, rows.shape[1]
    half = lambda place: pl.BlockSpec((count, width), lambda i: (place(i), 0))
    wide = jax.ShapeDtypeStruct((2 * count, width), jnp.float32)
    return pl.pallas_call(
        widen_rest_kernel,
        grid=(3,),
        in_specs=[half(lambda i: i), pl.BlockSpec(memory_space=pl.ANY)],
        out_specs=[half(lambda i: jnp.minimum(i, 1)), half(lambda i: 1)],
        out_shape=[wide, wide],
        input_output_aliases={1: 1},
        compiler_params=pltpu.CompilerParams(vmem_limit_bytes=62 << 20),
    )(rows, into)


OWNER = "expert"
LINE = "shard"


def exchange(rows, bit):
    count = lax.axis_size(OWNER)
    return lax.ppermute(rows, OWNER, [(i, i ^ bit) for i in range(count)])


def shift(rows, step):
    count = lax.axis_size(LINE)
    return lax.ppermute(rows, LINE, [(i, (i + step) % count) for i in range(count)])


def gather_line(rows):
    count = lax.axis_size(LINE)
    me = lax.axis_index(LINE)
    out = jnp.zeros((count,) + rows.shape, rows.dtype)
    out = lax.dynamic_update_index_in_dim(out, rows, me, 0)
    for step in range(1, count):
        got = shift(rows, step)
        out = lax.dynamic_update_index_in_dim(out, got, (me - step) % count, 0)
    return out


def add_low(left, right):
    return (left.astype(jnp.float32) + right.astype(jnp.float32)).astype(jnp.bfloat16)


def side(bit):
    return (lax.axis_index(OWNER) // bit) % 2


def halve(stack, bit):
    half = stack.shape[1] // 2
    keep = lax.dynamic_slice_in_dim(stack, side(bit) * half, half, 1)
    send = lax.dynamic_slice_in_dim(stack, (1 - side(bit)) * half, half, 1)
    got = exchange(send, bit)
    return add_low(keep, got)


def line_sum(stack):
    count = lax.axis_size(LINE)
    place = lax.axis_index(LINE)
    total = lax.dynamic_index_in_dim(stack, place, 0, False).astype(jnp.float32)
    for step in range(1, count):
        send = lax.dynamic_index_in_dim(stack, (place + step) % count, 0, False)
        total = total + shift(send, step).astype(jnp.float32)
    return total.astype(jnp.bfloat16)


def grow(piece, bit):
    other = exchange(piece, bit)
    return jnp.where(
        side(bit) == 0, jnp.concatenate([piece, other]), jnp.concatenate([other, piece])
    )


def reduce_rows(stack, bits):
    unit = 8 << (len(bits) - 1)
    cut = -(-stack.shape[1] // (2 * unit)) * unit
    parts = [stack[:, :cut], stack[:, cut:]]
    orders = [bits[1:], bits[:0:-1]]
    for level in range(len(bits) - 1):
        parts = [halve(part, order[level]) for part, order in zip(parts, orders)]
    low = parts[0].shape[1]
    piece = line_sum(jnp.concatenate(parts, axis=1))
    parts = [piece[:low], piece[low:]]
    for level in reversed(range(len(bits) - 1)):
        parts = [grow(part, order[level]) for part, order in zip(parts, orders)]
    return grow(jnp.concatenate(parts), bits[0])


def scatter_sum(grads):
    shards, rows, width = grads.shape
    grads = grads.reshape(shards * rows, width)
    return lax.psum_scatter(grads, LINE, scatter_dimension=0, tiled=True)


def share_rows(rows):
    return lax.all_to_all(rows, OWNER, 0, 0, tiled=True)


def share_large(rows):
    return pltpu.with_memory_space_constraint(share_rows(rows), pltpu.HBM)


def local(
    inputs,
    norm_gain,
    query_weight,
    key_weight,
    value_weight,
    merge_weight,
    bias_table,
    expert_gain,
    router_weight,
    up_weight,
    down_weight,
    routes,
    cotangent,
):
    f32, bf16 = jnp.float32, jnp.bfloat16
    tokens, width = inputs.shape
    owners = lax.axis_size(OWNER)
    shards = lax.axis_size(LINE)
    me = lax.axis_index(OWNER)
    part = query_weight.shape[0]
    piece = part // owners
    local_heads = bias_table.shape[1]
    heads = local_heads * shards
    size = width // heads
    experts = router_weight.shape[1]
    local_count, _, hidden = up_weight.shape
    capacity = (5 * tokens * routes.shape[1] + 4 * experts - 1) // (4 * experts)
    capacity = -(-capacity // 16) * 16
    rows = owners * capacity
    assert local_count == 2 and hidden // shards == width
    early = -(-capacity // 32) * 16

    router_at = 2 + local_heads + (-(2 + local_heads)) % 8

    def widen(block):
        return jnp.pad(block, ((0, 0), (0, width - block.shape[1])))

    def pack(gain_one, gain_two, table, router):
        head = jnp.concatenate([gain_one, gain_two], axis=0)
        gap = jnp.zeros((router_at - 2 - local_heads, width), bf16)
        return jnp.concatenate([widen(head), widen(table), gap, widen(router)], axis=0)

    small = pack(norm_gain[None], expert_gain[None], bias_table.T, router_weight.T)
    slices = [
        lax.dynamic_slice_in_dim(weight, me * piece, piece, 0)
        for weight in (query_weight, key_weight, value_weight)
    ]
    lined = gather_line(jnp.concatenate(slices + [small]))
    small_full = lined[:, 3 * piece :]
    bits = [1 << level for level in range(owners.bit_length() - 1)]
    pieces = []
    for index, order in enumerate((bits[1:], bits[:0:-1])):
        held = lined[index * shards // 2 : (index + 1) * shards // 2, : 3 * piece][None]
        for bit in order:
            got = exchange(held, bit)
            held = jnp.concatenate([held, got])
        pieces += [held, exchange(held, bits[0])]
    merge_full = lax.all_gather(merge_weight, LINE, axis=0, tiled=True)

    gain_one = small_full[:, 0, :part].reshape(1, width).astype(f32)
    gain_two = small_full[:, 1, :part].reshape(1, width).astype(f32)
    table_full = small_full[:, 2 : 2 + local_heads, :BUCKETS].reshape(heads, BUCKETS).astype(f32)
    router_full = small_full[:, router_at : router_at + experts, :part]
    router_full = router_full.transpose(1, 0, 2).reshape(experts, width)

    routes_line = routes.T
    slots, routes_float = find_slots(routes_line, experts, local_count, owners, capacity)
    cot_rows, other = dispatch_first(
        slots, routes_float, cotangent, owners, capacity, early
    )
    other = share_rows(other).reshape(owners, local_count, capacity)

    owner = me.astype(jnp.int32).reshape(1)
    block = 256
    hot = bucket_hot(tokens)
    assert hot[block:, -1].all()
    near_hot = jnp.asarray((hot[:block] - hot[-1:]).T, dtype=f32)
    group = 128 // size
    near = jnp.dot(table_full, near_hot, precision=lax.Precision.HIGHEST)
    near = near.reshape(heads // group, group, block)
    query_full, key_full, value_full, low_one, queries, keys, values = project(
        owner, inputs, gain_one, pieces, epsilon, after=(near, router_full)
    )
    cot_in = share_large(cot_rows)
    attended, totals = attend(queries, keys, values, near, size, block)
    resid, low_two, gates, send = settle(
        attended, merge_full, inputs, gain_two, router_full, routes_line, slots, rows, epsilon
    )

    others = [other[:, index].reshape(1, rows) for index in range(local_count)]
    rows_in = share_large(send.reshape(owners, capacity, width))
    joint = dispatch_both(
        slots, low_two, cotangent, rows, owners, capacity, early, after=others
    )
    joint_in = share_large(joint)
    act, pre, first_down, grad_in = expert_first(
        owner, rows_in, [cot_in], [(0, 0, capacity)], others[0], router_full, up_weight,
        0, local_count, capacity, shards,
    )
    first_sum = scatter_sum(first_down)
    first_made, pair = expert_second(rows_in, grad_in, act, pre, up_weight, down_weight, 0, owners, shards, 3 * width)
    late = capacity - early
    act, pre, pair, grad_in = expert_first(
        owner, joint_in, [cot_in, joint_in], [(0, capacity, early), (1, capacity, late)],
        others[1], router_full, up_weight, 1, local_count, capacity, shards, into=pair,
    )
    low, pair = expert_slope(joint_in, grad_in, pre, down_weight, 1, shards, pair, 1)
    pair_sum = scatter_sum(pair)
    second_made = expert_last(act, low, up_weight, down_weight, 1, owners, shards)
    returned = share_rows(first_made)
    result, inner, part_grads = combine_part(slots, gates, resid, cotangent, returned)
    returned = share_rows(second_made)
    output, logit_grad = combine_out(
        slots, routes_line, gates, result, inner, cotangent, returned
    )
    router_wide = jnp.pad(router_full, ((0, 128 - experts), (0, 0)))
    resid_grad, branch, mixed_grad, gain_grad = combine_back(
        slots, logit_grad, router_wide, gain_two, resid, cotangent, merge_full,
        part_grads, returned, epsilon
    )
    router_grad = jnp.einsum("te,ti->ei", logit_grad, low_two, preferred_element_type=f32)
    head_grads, distances = attend_back(
        queries, keys, values, mixed_grad, attended, totals, near, size, block
    )
    close_sums = distances[:, :group].reshape(heads, block)
    far_sums = jnp.sum(distances[:, group:].reshape(heads, block), axis=1)
    table_grad = jnp.dot(close_sums, jnp.asarray(hot[:block]), precision=lax.Precision.HIGHEST)
    table_grad = table_grad + far_sums[:, None] * jnp.asarray(hot[-1:])
    sums = weight_grads(low_one, attended, head_grads, branch, shards)
    sums = halve(sums, bits[0])
    input_gradient, norm_grad = finish(
        head_grads, query_full, key_full, value_full, gain_one, inputs, resid_grad, epsilon
    )
    small_grad = jax.vmap(pack)(
        norm_grad.reshape(shards, 1, part).astype(bf16),
        gain_grad.reshape(shards, 1, part).astype(bf16),
        table_grad.reshape(shards, local_heads, BUCKETS).astype(bf16),
        router_grad[:experts].reshape(experts, shards, part).transpose(1, 0, 2).astype(bf16),
    )
    spare = -small_grad.shape[1] % (8 * owners)
    small_grad = halve(jnp.pad(small_grad, ((0, 0), (0, spare), (0, 0))), bits[0])
    kept = sums.shape[1]
    sums = reduce_rows(jnp.concatenate([sums, small_grad], axis=1), bits)
    half = sums.shape[0] // 2
    weights = jnp.concatenate([sums[:kept], sums[half : half + kept]]).astype(f32)
    small_sum = jnp.concatenate([sums[kept:half], sums[half + kept :]]).astype(f32)
    up_sum, down_sum = widen_rest(pair_sum, widen_first(first_sum))
    return (
        output,
        input_gradient,
        small_sum[0, :part],
        weights[:part],
        weights[part : 2 * part],
        weights[2 * part : 3 * part],
        weights[3 * part :],
        small_sum[2 : 2 + local_heads, :BUCKETS].T,
        small_sum[1, :part],
        small_sum[router_at : router_at + experts, :part].T,
        up_sum.reshape(local_count, width, width),
        down_sum.reshape(local_count, width, width),
    )


def solution(mesh):
    in_specs = (
        P((OWNER, LINE), None),
        P(LINE),
        P(LINE, None),
        P(LINE, None),
        P(LINE, None),
        P(LINE, None),
        P(None, LINE),
        P(LINE),
        P(LINE, None),
        P(OWNER, None, None),
        P(OWNER, None, None),
        P((OWNER, LINE), None),
        P((OWNER, LINE), None),
    )
    out_specs = (
        P((OWNER, LINE), None),
        P((OWNER, LINE), None),
        P(LINE),
        P(LINE, None),
        P(LINE, None),
        P(LINE, None),
        P(LINE, None),
        P(None, LINE),
        P(LINE),
        P(LINE, None),
        P(OWNER, None, LINE),
        P(OWNER, LINE, None),
    )

    return jax.shard_map(local, mesh=mesh, in_specs=in_specs, out_specs=out_specs, check_vma=False)
```

```python
from functools import partial, reduce

import jax
import jax.numpy as jnp
import numpy as np
from jax import lax
from jax.experimental import pallas as pl
from jax.experimental.pallas import tpu as pltpu
from jax.sharding import PartitionSpec as P


BUCKETS = 32
MAX_DIST = 128


epsilon = 1e-06
masked_score = -1e30


def bucket_hot(length):
    distance = np.arange(length)
    half_count = BUCKETS // 2
    clipped = np.maximum(distance, half_count)
    spread = np.log(clipped / half_count) / np.log(MAX_DIST / half_count) * (BUCKETS - half_count)
    far_bucket = np.minimum(half_count + np.floor(spread).astype(np.int32), BUCKETS - 1)
    bucket = np.where(distance < half_count, distance, far_bucket)
    return (bucket[:, None] == np.arange(BUCKETS)[None, :]).astype(np.float32)


def dot_nt(a, b):
    return lax.dot_general(a, b, (((1,), (1,)), ((), ())), preferred_element_type=jnp.float32)


def dot_nn(a, b):
    return lax.dot_general(a, b, (((1,), (0,)), ((), ())), preferred_element_type=jnp.float32)


def dot_tn(a, b):
    return lax.dot_general(a, b, (((0,), (0,)), ((), ())), preferred_element_type=jnp.float32)


def slot_kernel(routes_ref, slots_ref, float_ref, *, experts, local_count, owners, capacity):
    tokens = routes_ref.shape[1]
    expert = lax.broadcasted_iota(jnp.int32, (experts, tokens), 0)
    hits = [routes_ref[c:c + 1, :] == expert for c in range(2)]
    hot = jnp.where(hits[0] | hits[1], 1.0, 0.0).astype(jnp.bfloat16)
    earlier = lax.broadcasted_iota(jnp.int32, (tokens, tokens), 0)
    later = lax.broadcasted_iota(jnp.int32, (tokens, tokens), 1)
    before = jnp.where(earlier < later, 1.0, 0.0).astype(jnp.bfloat16)
    counts = dot_nn(hot, before)
    column = lax.broadcasted_iota(jnp.int32, (experts, 1), 0)
    base = (column % local_count * owners + column // local_count) * capacity
    counts = counts + base.astype(jnp.float32)
    for c in range(2):
        slot = jnp.sum(jnp.where(hits[c], counts, 0.0), axis=0, keepdims=True)
        slots_ref[c:c + 1, :] = slot.astype(jnp.int32)
    float_ref[...] = routes_ref[...].astype(jnp.float32)


def find_slots(routes, experts, local_count, owners, capacity):
    return pl.pallas_call(
        partial(slot_kernel, experts=experts, local_count=local_count, owners=owners, capacity=capacity),
        out_shape=[jax.ShapeDtypeStruct(routes.shape, jnp.int32), jax.ShapeDtypeStruct(routes.shape, jnp.float32)],
    )(routes)


def dispatch_both_kernel(slots_ref, rows_ref, cot_ref, *refs, start, capacity, early):
    out_ref = refs[-1]
    block, tokens = capacity, rows_ref.shape[0]
    slot = lax.broadcasted_iota(jnp.int32, (block, tokens), 0) + (pl.program_id(0) * block + start)
    hot = jnp.where((slot == slots_ref[0:1, :]) | (slot == slots_ref[1:2, :]), 1.0, 0.0)
    hot = hot.astype(jnp.bfloat16)
    out_ref[0, :capacity] = dot_nn(hot, rows_ref[...]).astype(out_ref.dtype)
    out_ref[0, capacity:] = dot_nn(hot[early:], cot_ref[...]).astype(out_ref.dtype)


def dispatch_both(slots, rows, cot, start, owners, capacity, early, after=()):
    width = rows.shape[1]
    total = 2 * capacity - early
    whole = lambda shape: pl.BlockSpec(shape, lambda i: (0, 0))
    return pl.pallas_call(
        partial(dispatch_both_kernel, start=start, capacity=capacity, early=early),
        grid=(owners,),
        in_specs=[whole(slots.shape), whole(rows.shape), whole(cot.shape)] + [pl.BlockSpec(memory_space=pl.ANY)] * len(after),
        out_specs=pl.BlockSpec((1, total, width), lambda i: (i, 0, 0)),
        out_shape=jax.ShapeDtypeStruct((owners, total, width), rows.dtype),
        compiler_params=pltpu.CompilerParams(vmem_limit_bytes=62 << 20),
    )(slots, rows, cot, *after)


def dispatch_first_kernel(slots_ref, routes_ref, rows_ref, out_ref, other_ref, *, owners, capacity):
    block, tokens = other_ref.shape[2], rows_ref.shape[0]
    row = lax.broadcasted_iota(jnp.int32, (block, tokens), 0)
    slot = row + pl.program_id(0) * capacity
    slot = slot + jnp.where(row >= capacity, (owners - 1) * capacity, 0)
    hits = [slot == slots_ref[c:c + 1, :] for c in range(2)]
    hot = jnp.where(hits[0] | hits[1], 1.0, 0.0)[:out_ref.shape[1]]
    out_ref[0] = dot_nn(hot.astype(jnp.bfloat16), rows_ref[...]).astype(out_ref.dtype)
    other = jnp.where(hits[0], routes_ref[1:2, :], jnp.where(hits[1], routes_ref[0:1, :], 0.0))
    column = jnp.sum(other, axis=1, keepdims=True)
    other_ref[0] = jnp.broadcast_to(column, (block, 128)).T[0:1, :]


def dispatch_first(slots, routes, rows, owners, capacity, early):
    width = rows.shape[1]
    total = capacity + early
    whole = lambda shape: pl.BlockSpec(shape, lambda i: (0, 0))
    return pl.pallas_call(
        partial(dispatch_first_kernel, owners=owners, capacity=capacity),
        grid=(owners,),
        in_specs=[whole(slots.shape), whole(routes.shape), whole(rows.shape)],
        out_specs=[pl.BlockSpec((1, total, width), lambda i: (i, 0, 0)), pl.BlockSpec((1, 1, 2 * capacity), lambda i: (i, 0, 0))],
        out_shape=[jax.ShapeDtypeStruct((owners, total, width), rows.dtype), jax.ShapeDtypeStruct((owners, 1, 2 * capacity), jnp.float32)],
    )(slots, routes, rows)


def gelu_half(v):
    c = np.float32(np.sqrt(2.0 / np.pi))
    square = v * v
    half = 0.5 * jnp.tanh(v * (np.float32(0.044715) * c * square + c)) + 0.5
    return half, square


def gelu_slope(v):
    c = np.float32(np.sqrt(2.0 / np.pi))
    half, square = gelu_half(v)
    return half + v * half * (1.0 - half) * (np.float32(6.0 * 0.044715) * c * square + 2.0 * c)


def arrived_spec(arrived, used=None):
    owners, count, width = arrived.shape
    return pl.BlockSpec((owners, used or count, width), lambda i: (0, 0, 0))


def first_kernel(owner_ref, rows_ref, other_ref, router_ref, up_ref, *refs, index, local_count, capacity, pieces):
    act_ref, pre_ref, down_grad_ref, grad_ref = refs[-4:]
    owners, _, width = rows_ref.shape
    rows = owners * capacity
    chunk = rows // 2
    @pl.when(pl.program_id(0) == 0)
    def _():
        logits = dot_nt(router_ref[...], rows_ref[:, :capacity].reshape(rows, width))
        expert = lax.broadcasted_iota(jnp.int32, logits.shape, 0)
        mine = owner_ref[0] * local_count + index
        own = jnp.sum(jnp.where(expert == mine, logits, 0.0), axis=0, keepdims=True)
        other = other_ref[...].astype(jnp.int32)
        other = jnp.sum(jnp.where(expert == other, logits, 0.0), axis=0, keepdims=True)
        top = jnp.maximum(own, other)
        own = jnp.exp(own - top)
        gate = own / (own + jnp.exp(other - top))
        column = jnp.broadcast_to(gate, (128, rows)).T
        for start in range(0, width, 128):
            parts = [refs[place][:, low:low + size, start:start + 128] for place, low, size in pieces]
            part = parts[0] if len(parts) == 1 else jnp.concatenate(parts, axis=1)
            part = part.reshape(rows, 128).astype(jnp.float32) * column
            grad_ref[:, start:start + 128] = part.astype(jnp.bfloat16)
    up = up_ref[0]
    for start in range(0, rows, chunk):
        part = rows_ref[start // capacity:(start + chunk) // capacity, :capacity].reshape(chunk, width)
        pre = dot_nn(part, up)
        half, _ = gelu_half(pre)
        act_ref[start:start + chunk, :] = (pre * half).astype(jnp.bfloat16)
        pre_ref[start:start + chunk, :] = pre.astype(jnp.bfloat16)
    down_grad_ref[0] = dot_tn(act_ref[...], grad_ref[...]).astype(jnp.bfloat16)


def expert_first(owner, rows_in, cots, pieces, other, router, up, index, local_count, capacity, shards, into=None):
    owners, _, width = rows_in.shape
    rows = owners * capacity
    hidden = up.shape[2]
    tile = hidden // shards
    fixed = pl.BlockSpec((rows, width), lambda i: (0, 0))
    column = pl.BlockSpec((rows, tile), lambda i: (0, i))
    operands = [owner, rows_in, other, router, up, *cots]
    place, aliases = 0, {}
    grad_shape = jax.ShapeDtypeStruct((shards, tile, width), jnp.bfloat16)
    if into is not None:
        aliases = {len(operands): 2}
        operands.append(into)
        place, grad_shape = 2, jax.ShapeDtypeStruct(into.shape, into.dtype)
    return pl.pallas_call(
        partial(first_kernel, index=index, local_count=local_count, capacity=capacity, pieces=pieces),
        grid=(shards,),
        in_specs=[
            pl.BlockSpec(memory_space=pltpu.SMEM),
            arrived_spec(rows_in, capacity),
            pl.BlockSpec((1, rows), lambda i: (0, 0)),
            pl.BlockSpec(router.shape, lambda i: (0, 0)),
            pl.BlockSpec((1, width, tile), lambda i: (index, 0, i)),
        ]
        + [arrived_spec(cot, low + size) for cot, (_, low, size) in zip(cots, pieces)]
        + [pl.BlockSpec(memory_space=pl.ANY)] * (into is not None),
        out_specs=[column, column, pl.BlockSpec((1, tile, width), lambda i: (i, place, 0)), fixed],
        out_shape=[jax.ShapeDtypeStruct((rows, hidden), jnp.bfloat16)] * 2 + [grad_shape, jax.ShapeDtypeStruct((rows, width), jnp.bfloat16)],
        input_output_aliases=aliases,
        compiler_params=pltpu.CompilerParams(vmem_limit_bytes=62 << 20),
    )(*operands)


def second_kernel(rows_ref, grad_ref, act_ref, pre_ref, up_ref, down_ref, *refs):
    made_ref, up_grad_ref, turned, made_acc, back_acc = refs[-5:]
    step = pl.program_id(0)
    owners, _, capacity, width = made_ref.shape
    @pl.when(step == 0)
    def _():
        rows, width = grad_ref.shape
        owners = rows_ref.shape[0]
        turned[...] = rows_ref[:, :rows // owners].reshape(rows, width).T
    up = up_ref[0]
    down = down_ref[0]
    grads = dot_nt(grad_ref[...], down)
    low = (gelu_slope(pre_ref[...].astype(jnp.float32)) * grads).astype(jnp.bfloat16)
    up_grad_ref[0] = dot_nn(turned[...], low).astype(jnp.bfloat16)
    back = dot_nt(low, up)
    made = dot_nn(act_ref[...], down)
    last = pl.num_programs(0) - 1
    @pl.when(step == 0)
    def _():
        made_acc[...] = made
        back_acc[...] = back
    @pl.when((step > 0) & (step < last))
    def _():
        made_acc[...] += made
        back_acc[...] += back
    @pl.when(step == last)
    def _():
        made_ref[:, 0] = (made_acc[...] + made).astype(jnp.bfloat16).reshape(owners, capacity, width)
        made_ref[:, 1] = (back_acc[...] + back).astype(jnp.bfloat16).reshape(owners, capacity, width)


def expert_second(rows_in, grad, act, pre, up, down, index, owners, shards, wide, after=()):
    rows, width = grad.shape
    hidden = up.shape[2]
    tile = hidden // shards
    fixed = pl.BlockSpec((rows, width), lambda i: (0, 0))
    column = pl.BlockSpec((rows, tile), lambda i: (0, i))
    made_shape = (owners, 2, rows // owners, width)
    return pl.pallas_call(
        second_kernel,
        grid=(shards,),
        in_specs=[arrived_spec(rows_in, rows // rows_in.shape[0]), fixed, column, column, pl.BlockSpec((1, width, tile), lambda i: (index, 0, i)), pl.BlockSpec((1, tile, width), lambda i: (index, i, 0))]
        + [pl.BlockSpec(memory_space=pl.ANY)] * len(after),
        out_specs=[pl.BlockSpec(made_shape, lambda i: (0, 0, 0, 0)), pl.BlockSpec((1, width, tile), lambda i: (i, 0, 0))],
        out_shape=[jax.ShapeDtypeStruct(made_shape, jnp.bfloat16), jax.ShapeDtypeStruct((shards, wide, tile), jnp.bfloat16)],
        scratch_shapes=[pltpu.VMEM((width, rows), jnp.bfloat16), pltpu.VMEM((rows, width), jnp.float32), pltpu.VMEM((rows, width), jnp.float32)],
        compiler_params=pltpu.CompilerParams(vmem_limit_bytes=62 << 20),
    )(rows_in, grad, act, pre, up, down, *after)


def slope_kernel(rows_ref, grad_ref, pre_ref, down_ref, into_ref, low_ref, up_grad_ref, turned):
    del into_ref
    @pl.when(pl.program_id(0) == 0)
    def _():
        rows, width = grad_ref.shape
        owners = rows_ref.shape[0]
        turned[...] = rows_ref[:, :rows // owners].reshape(rows, width).T
    grads = dot_nt(grad_ref[...], down_ref[0])
    low = (gelu_slope(pre_ref[...].astype(jnp.float32)) * grads).astype(jnp.bfloat16)
    low_ref[...] = low
    up_grad_ref[0] = dot_nn(turned[...], low).astype(jnp.bfloat16)


def expert_slope(rows_in, grad, pre, down, index, shards, into, place):
    rows, width = grad.shape
    hidden = pre.shape[1]
    tile = hidden // shards
    fixed = pl.BlockSpec((rows, width), lambda i: (0, 0))
    column = pl.BlockSpec((rows, tile), lambda i: (0, i))
    return pl.pallas_call(
        slope_kernel,
        grid=(shards,),
        in_specs=[arrived_spec(rows_in, rows // rows_in.shape[0]), fixed, column, pl.BlockSpec((1, tile, width), lambda i: (index, i, 0)), pl.BlockSpec(memory_space=pl.ANY)],
        out_specs=[column, pl.BlockSpec((1, width, tile), lambda i: (i, place, 0))],
        out_shape=[jax.ShapeDtypeStruct((rows, hidden), jnp.bfloat16), jax.ShapeDtypeStruct(into.shape, into.dtype)],
        input_output_aliases={4: 1},
        scratch_shapes=[pltpu.VMEM((width, rows), jnp.bfloat16)],
        compiler_params=pltpu.CompilerParams(vmem_limit_bytes=62 << 20),
    )(rows_in, grad, pre, down, into)


def last_kernel(act_ref, low_ref, up_ref, down_ref, made_ref, made_acc, back_acc):
    step = pl.program_id(0)
    owners, _, capacity, width = made_ref.shape
    back = dot_nt(low_ref[...], up_ref[0])
    made = dot_nn(act_ref[...], down_ref[0])
    last = pl.num_programs(0) - 1
    @pl.when(step == 0)
    def _():
        made_acc[...] = made
        back_acc[...] = back
    @pl.when((step > 0) & (step < last))
    def _():
        made_acc[...] += made
        back_acc[...] += back
    @pl.when(step == last)
    def _():
        made_ref[:, 0] = (made_acc[...] + made).astype(jnp.bfloat16).reshape(owners, capacity, width)
        made_ref[:, 1] = (back_acc[...] + back).astype(jnp.bfloat16).reshape(owners, capacity, width)


def expert_last(act, low, up, down, index, owners, shards):
    rows, hidden = act.shape
    width = up.shape[1]
    tile = hidden // shards
    column = pl.BlockSpec((rows, tile), lambda i: (0, i))
    made_shape = (owners, 2, rows // owners, width)
    return pl.pallas_call(
        last_kernel,
        grid=(shards,),
        in_specs=[column, column, pl.BlockSpec((1, width, tile), lambda i: (index, 0, i)), pl.BlockSpec((1, tile, width), lambda i: (index, i, 0))],
        out_specs=pl.BlockSpec(made_shape, lambda i: (0, 0, 0, 0)),
        out_shape=jax.ShapeDtypeStruct(made_shape, jnp.bfloat16),
        scratch_shapes=[pltpu.VMEM((rows, width), jnp.float32), pltpu.VMEM((rows, width), jnp.float32)],
        compiler_params=pltpu.CompilerParams(vmem_limit_bytes=62 << 20),
    )(act, low, up, down)


def spread(row, block):
    return jnp.broadcast_to(row, (128, block)).T


def pick(slots, lane, back_refs, first=0):
    picked = None
    for index, back_ref in enumerate(back_refs, first):
        owners, capacity, width = back_ref.shape
        half = owners * capacity
        hots = []
        for start in range(index * half, (index + 1) * half, 128):
            hit = reduce(jnp.logical_or, [slot == lane + start for slot in slots])
            hots.append(jnp.where(hit, 1.0, 0.0).astype(jnp.bfloat16))
        part = dot_nn(jnp.concatenate(hots, axis=1), back_ref[...].reshape(half, width))
        picked = part if picked is None else picked + part
    return picked


def part_kernel(slots_ref, gates_ref, resid_ref, cot_ref, made_ref, back_ref, result_ref, inner_ref, grads_ref):
    block = result_ref.shape[0]
    lane = lax.broadcasted_iota(jnp.int32, (block, 128), 1)
    cot = cot_ref[...].astype(jnp.float32)
    result = resid_ref[...]
    inner = jnp.zeros((block, 128), jnp.float32)
    slots = [spread(slots_ref[c:c + 1, :], block) for c in range(2)]
    for c in range(2):
        picked = pick([slots[c]], lane, [made_ref])
        result = result + spread(gates_ref[c:c + 1, :], block)[:, 0:1] * picked
        inner = inner + jnp.where(lane == c, jnp.sum(cot * picked, axis=1, keepdims=True), 0.0)
    result_ref[...] = result
    inner_ref[...] = inner
    grads_ref[...] = pick(slots, lane, [back_ref])


def combine_part(slots, gates, resid, cot, returned, block=256):
    tokens, width = resid.shape
    small = pl.BlockSpec((2, block), lambda i: (0, i))
    rows = pl.BlockSpec((block, width), lambda i: (i, 0))
    wide = jax.ShapeDtypeStruct((tokens, width), jnp.float32)
    return pl.pallas_call(
        part_kernel,
        grid=(tokens // block,),
        in_specs=[small, small, rows, rows, returned_spec(returned, 0), returned_spec(returned, 1)],
        out_specs=[rows, pl.BlockSpec((block, 128), lambda i: (i, 0)), rows],
        out_shape=[wide, jax.ShapeDtypeStruct((tokens, 128), jnp.float32), wide],
        compiler_params=pltpu.CompilerParams(vmem_limit_bytes=62 << 20),
    )(slots, gates, resid, cot, returned, returned)


def out_kernel(slots_ref, routes_ref, gates_ref, result_ref, inner_ref, cot_ref, made_ref, out_ref, logit_ref):
    block = out_ref.shape[0]
    lane = lax.broadcasted_iota(jnp.int32, (block, 128), 1)
    cot = cot_ref[...].astype(jnp.float32)
    result = result_ref[...]
    gates, inner = [], []
    for c in range(2):
        slot = spread(slots_ref[c:c + 1, :], block)
        gate = spread(gates_ref[c:c + 1, :], block)[:, 0:1]
        picked = pick([slot], lane, [made_ref], 1)
        result = result + gate * picked
        gates.append(gate)
        inner.append(inner_ref[:, c:c + 1] + jnp.sum(cot * picked, axis=1, keepdims=True))
    out_ref[...] = result.astype(out_ref.dtype)
    middle = gates[0] * inner[0] + gates[1] * inner[1]
    logit = jnp.zeros((block, 128), jnp.float32)
    for c in range(2):
        route = spread(routes_ref[c:c + 1, :], block)
        logit = logit + jnp.where(route == lane, gates[c] * (inner[c] - middle), 0.0)
    logit_ref[...] = logit.astype(jnp.bfloat16)


def returned_spec(returned, which):
    owners, _, capacity, width = returned.shape
    return pl.BlockSpec((owners, None, capacity, width), lambda i: (0, which, 0, 0))


def combine_out(slots, routes, gates, result, inner, cot, returned, block=256):
    tokens, width = result.shape
    small = pl.BlockSpec((2, block), lambda i: (0, i))
    rows = pl.BlockSpec((block, width), lambda i: (i, 0))
    return pl.pallas_call(
        out_kernel,
        grid=(tokens // block,),
        in_specs=[small, small, small, rows, pl.BlockSpec((block, 128), lambda i: (i, 0)), rows, returned_spec(returned, 0)],
        out_specs=[rows, pl.BlockSpec((block, 128), lambda i: (i, 0))],
        out_shape=[jax.ShapeDtypeStruct((tokens, width), jnp.bfloat16), jax.ShapeDtypeStruct((tokens, 128), jnp.bfloat16)],
        compiler_params=pltpu.CompilerParams(vmem_limit_bytes=62 << 20),
    )(slots, routes, gates, result, inner, cot, returned)


def back_kernel(slots_ref, logit_ref, router_ref, gain_ref, resid_ref, cot_ref, merge_ref, part_ref, back_ref, grad_ref, low_ref, mixed_ref, gain_grad_ref, *, eps):
    block, _ = grad_ref.shape
    lane = lax.broadcasted_iota(jnp.int32, (block, 128), 1)
    grads = part_ref[...] + pick([spread(slots_ref[c:c + 1, :], block) for c in range(2)], lane, [back_ref], 1)
    grads = grads + dot_nn(logit_ref[...], router_ref[...])
    resid = resid_ref[...]
    inverse = lax.rsqrt(jnp.mean(resid * resid, axis=1, keepdims=True) + eps)
    unit = resid * inverse
    @pl.when(pl.program_id(0) == 0)
    def _():
        gain_grad_ref[...] = jnp.zeros_like(gain_grad_ref)
    gain_grad_ref[...] += jnp.sum(grads * unit, axis=0, keepdims=True)
    scaled = grads * gain_ref[...]
    inner = jnp.mean(scaled * unit, axis=1, keepdims=True)
    total = cot_ref[...].astype(jnp.float32) + inverse * (scaled - unit * inner)
    grad_ref[...] = total
    low = total.astype(jnp.bfloat16)
    low_ref[...] = low
    mixed_ref[...] = dot_nt(low, merge_ref[...]).astype(jnp.bfloat16)


def combine_back(slots, logit, router, gain, resid, cot, merge, part, returned, eps, block=256):
    tokens, width = resid.shape
    rows = pl.BlockSpec((block, width), lambda i: (i, 0))
    whole = lambda shape: pl.BlockSpec(shape, lambda i: (0, 0))
    low = jax.ShapeDtypeStruct((tokens, width), jnp.bfloat16)
    return pl.pallas_call(
        partial(back_kernel, eps=eps),
        grid=(tokens // block,),
        in_specs=[pl.BlockSpec((2, block), lambda i: (0, i)), pl.BlockSpec((block, 128), lambda i: (i, 0)), whole(router.shape), whole(gain.shape), rows, rows, whole(merge.shape), rows, returned_spec(returned, 1)],
        out_specs=[rows, rows, rows, whole((1, width))],
        out_shape=[jax.ShapeDtypeStruct((tokens, width), jnp.float32), low, low, jax.ShapeDtypeStruct((1, width), jnp.float32)],
        compiler_params=pltpu.CompilerParams(vmem_limit_bytes=62 << 20),
    )(slots, logit, router, gain, resid, cot, merge, part, returned)


def near_tiles(near_ref, head, block):
    spread = jnp.broadcast_to(near_ref[0, head:head + 1, :], (block, block))
    spread = pltpu.roll(spread, 0, 1, stride=1, stride_axis=0)
    key_at = lax.broadcasted_iota(jnp.int32, (block, block), 0)
    query_at = lax.broadcasted_iota(jnp.int32, (block, block), 1)
    return (jnp.where(query_at >= key_at, spread, masked_score), jnp.where(query_at < key_at, spread, 0.0), query_at < key_at)


def diagonal_sums(tile):
    block = tile.shape[1]
    total = tile[:8]
    for start in range(8, block, 8):
        total = total + pltpu.roll(tile[start:start + 8], block - start, 1)
    row = lax.broadcasted_iota(jnp.int32, total.shape, 0)
    for step in (1, 2, 4):
        total = jnp.where((row & step) != 0, pltpu.roll(total, block - step, 1), total)
    return jnp.sum(total, axis=0, keepdims=True)


def head_part(rows, head, size):
    lane = lax.broadcasted_iota(jnp.int32, rows.shape, 1)
    return jnp.where((lane >= head * size) & (lane < (head + 1) * size), rows, jnp.zeros_like(rows))


def attend_kernel(query_ref, key_ref, value_ref, near_ref, out_ref, total_ref, held, *, block, size, scale):
    length, lanes = query_ref.shape
    heads = lanes // size
    count = length // block
    turned = value_ref[...].T
    ones = jnp.ones((16, length), jnp.bfloat16)
    flipped = [jnp.concatenate([turned[head * size:(head + 1) * size], ones], axis=0) for head in range(heads)]
    tiles = [near_tiles(near_ref, head, block) for head in range(heads)]
    units = [(i, head) for i in range(count) for head in range(heads)]
    def fold(tile, op):
        parts = [tile[k:k + 8] for k in range(0, tile.shape[0], 8)]
        while len(parts) > 1:
            parts = [op(parts[k], parts[k + 1]) for k in range(0, len(parts), 2)]
        return parts[0]
    def score_tile(unit, query_part, j, slot):
        i, head = unit
        tile = dot_nt(key_ref[pl.ds(j * block, block), :], query_part)
        if j == i:
            tile = tile + tiles[head][0]
        elif j == i - 1:
            tile = tile + tiles[head][1]
        held[slot, pl.ds(j * block, block), :] = tile
        return fold(tile, jnp.maximum)
    def part_of(unit):
        i, head = unit
        return head_part(query_ref[pl.ds(i * block, block), :] * jnp.bfloat16(scale), head, size)
    tops = {0: [score_tile(units[0], part_of(units[0]), 0, 0)]}
    outs = []
    for n, (i, head) in enumerate(units):
        top = jnp.max(reduce(jnp.maximum, tops[n]), axis=0, keepdims=True)
        following = units[n + 1] if n + 1 < len(units) else None
        if following is not None:
            query_part = part_of(following)
            tops[n + 1] = []
        mixed = None
        total = None
        steps = max(i + 1, following[0] + 1 if following else 0)
        for j in range(steps):
            if following is not None and j <= following[0]:
                tops[n + 1].append(score_tile(following, query_part, j, (n + 1) % 2))
            if j <= i:
                weights = jnp.exp(held[n % 2, pl.ds(j * block, block), :] - top)
                part = dot_nn(flipped[head][:, j * block:(j + 1) * block], weights.astype(jnp.bfloat16))
                mixed = part if mixed is None else mixed + part
        total = mixed[size:size + 1]
        outs.append(mixed[:size] / total)
        rows = pl.ds(i * block, block)
        total_ref[0, head:head + 1, rows] = top + jnp.log(total)
        if head == heads - 1:
            out_ref[rows, :] = jnp.concatenate(outs[-heads:], axis=0).T.astype(out_ref.dtype)


def attend(queries, keys, values, near, size, block):
    length, width = queries.shape
    lanes = 128
    heads = lanes // size
    groups = width // lanes
    column = pl.BlockSpec((length, lanes), lambda g: (0, g))
    head_rows = pl.BlockSpec((1, heads, block), lambda g: (g, 0, 0))
    return pl.pallas_call(
        partial(attend_kernel, block=block, size=size, scale=size ** -0.5),
        grid=(groups,),
        in_specs=[column, column, column, head_rows],
        out_specs=[column, pl.BlockSpec((1, heads, length), lambda g: (g, 0, 0))],
        out_shape=[jax.ShapeDtypeStruct((length, width), jnp.bfloat16), jax.ShapeDtypeStruct((groups, heads, length), jnp.float32)],
        scratch_shapes=[pltpu.VMEM((2, length, block), jnp.float32)],
        compiler_params=pltpu.CompilerParams(vmem_limit_bytes=62 << 20),
    )(queries, keys, values, near)


def attend_back_kernel(query_ref, key_ref, value_ref, grad_ref, out_ref, total_ref, near_ref, grads_ref, dist_ref, key_acc, value_acc, *, block, size, scale):
    length, lanes = query_ref.shape
    heads = lanes // size
    count = length // block
    flipped = key_ref[...].T
    tiles = [near_tiles(near_ref, head, block) for head in range(heads)]
    near_acc = [None] * heads
    far_acc = [None] * heads
    for i in range(count):
        rows = pl.ds(i * block, block)
        query_rows = query_ref[rows, :] * jnp.bfloat16(scale)
        grad_rows = grad_ref[rows, :]
        products = (grad_rows.astype(jnp.float32) * out_ref[rows, :].astype(jnp.float32)).T
        query_parts = [head_part(query_rows, head, size) for head in range(heads)]
        grad_parts = [head_part(grad_rows, head, size) for head in range(heads)]
        inner = [jnp.sum(products[head * size:(head + 1) * size], axis=0, keepdims=True) for head in range(heads)]
        query_stack = jnp.concatenate(query_parts, axis=0)
        grad_stack = jnp.concatenate(grad_parts, axis=0)
        query_grads = [None] * heads
        for j in range(i + 1):
            cols = pl.ds(j * block, block)
            weight_list = []
            score_list = []
            for head in range(heads):
                tile = dot_nt(key_ref[cols, :], query_parts[head])
                if j == i:
                    tile = tile + tiles[head][0]
                elif j == i - 1:
                    tile = tile + tiles[head][1]
                weights = jnp.exp(tile - total_ref[0, head:head + 1, rows])
                grads = dot_nt(value_ref[cols, :], grad_parts[head])
                score_grads = weights * (grads - inner[head])
                low = score_grads.astype(jnp.bfloat16)
                weight_list.append(weights.astype(jnp.bfloat16))
                score_list.append(low)
                part = dot_nn(flipped[head * size:(head + 1) * size, j * block:(j + 1) * block], low)
                query_grads[head] = part if query_grads[head] is None else query_grads[head] + part
                if j == i:
                    near_acc[head] = score_grads if near_acc[head] is None else near_acc[head] + score_grads
                else:
                    far = score_grads
                    if j == i - 1:
                        close = jnp.where(tiles[head][2], score_grads, 0.0)
                        near_acc[head] = near_acc[head] + close
                        far = score_grads - close
                    far = jnp.sum(far, axis=0, keepdims=True)
                    far_acc[head] = far if far_acc[head] is None else far_acc[head] + far
            value_part = dot_nn(jnp.concatenate(weight_list, axis=1), grad_stack)
            key_part = dot_nn(jnp.concatenate(score_list, axis=1), query_stack)
            if j == i:
                value_acc[cols, :] = value_part
                key_acc[cols, :] = key_part
            else:
                value_acc[cols, :] += value_part
                key_acc[cols, :] += key_part
        grads_ref[0, rows, :] = (jnp.concatenate(query_grads, axis=0) * scale).T.astype(grads_ref.dtype)
    grads_ref[1] = key_acc[...].astype(grads_ref.dtype)
    grads_ref[2] = value_acc[...].astype(grads_ref.dtype)
    for head in range(heads):
        dist_ref[0, head:head + 1, :] = diagonal_sums(near_acc[head])
        dist_ref[0, heads + head:heads + head + 1, :] = far_acc[head]


def attend_back(queries, keys, values, grads, outs, totals, near, size, block):
    length, width = queries.shape
    lanes = 128
    heads = lanes // size
    groups = width // lanes
    column = pl.BlockSpec((length, lanes), lambda g: (0, g))
    head_rows = pl.BlockSpec((1, heads, block), lambda g: (g, 0, 0))
    return pl.pallas_call(
        partial(attend_back_kernel, block=block, size=size, scale=size ** -0.5),
        grid=(groups,),
        in_specs=[column] * 5 + [pl.BlockSpec((1, heads, length), lambda g: (g, 0, 0)), head_rows],
        out_specs=[pl.BlockSpec((3, length, lanes), lambda g: (0, 0, g)), pl.BlockSpec((1, 2 * heads, block), lambda g: (g, 0, 0))],
        out_shape=[jax.ShapeDtypeStruct((3, length, width), jnp.bfloat16), jax.ShapeDtypeStruct((groups, 2 * heads, block), jnp.float32)],
        scratch_shapes=[pltpu.VMEM((length, lanes), jnp.float32)] * 2,
        compiler_params=pltpu.CompilerParams(vmem_limit_bytes=62 << 20),
    )(queries, keys, values, grads, outs, totals, near)


def reverse_bits(value, count):
    out = value * 0
    for level in range(count):
        out = out * 2 + (value >> level) % 2
    return out


def project_kernel(owner_ref, inputs_ref, gain_ref, *refs, eps):
    piece_refs, weight_refs, low_ref, out_refs = refs[:4], refs[-7:-4], refs[-4], refs[-3:]
    count, half, three, _ = piece_refs[0].shape
    piece = three // 3
    owners = 2 * count
    part = owners * piece
    @pl.when(pl.program_id(0) == 0)
    def _():
        me = owner_ref[0]
        for source in range(owners):
            apart = jnp.bitwise_xor(me, source)
            near = apart % 2 == 0
            place = apart // 2
            places = (place, reverse_bits(place, owners.bit_length() - 2))
            for group in range(2):
                for line in range(half):
                    block = jnp.where(near, piece_refs[2 * group][places[group], line], piece_refs[2 * group + 1][places[group], line])
                    start = (group * half + line) * part + source * piece
                    for index in range(3):
                        weight_refs[index][start:start + piece, :] = block[index * piece:(index + 1) * piece]
    rows = inputs_ref[...].astype(jnp.float32)
    inverse = lax.rsqrt(jnp.mean(rows * rows, axis=1, keepdims=True) + eps)
    low = (rows * inverse * gain_ref[...]).astype(jnp.bfloat16)
    low_ref[...] = low
    for weight_ref, out_ref in zip(weight_refs, out_refs):
        out_ref[...] = dot_nn(low, weight_ref[...]).astype(jnp.bfloat16)


def project(owner, inputs, gain, pieces, eps, after=(), block=512):
    tokens, width = inputs.shape
    rows = pl.BlockSpec((block, width), lambda i: (i, 0))
    whole = lambda shape: pl.BlockSpec(shape, lambda i: (0,) * len(shape))
    weight = jax.ShapeDtypeStruct((width, width), jnp.bfloat16)
    return pl.pallas_call(
        partial(project_kernel, eps=eps),
        grid=(tokens // block,),
        in_specs=[pl.BlockSpec(memory_space=pltpu.SMEM), rows, whole(gain.shape)] + [whole(piece.shape) for piece in pieces] + [pl.BlockSpec(memory_space=pl.ANY)] * len(after),
        out_specs=[whole(weight.shape)] * 3 + [rows] * 4,
        out_shape=[weight] * 3 + [jax.ShapeDtypeStruct((tokens, width), jnp.bfloat16)] * 4,
        compiler_params=pltpu.CompilerParams(vmem_limit_bytes=62 << 20),
    )(owner, inputs, gain, *pieces, *after)


def settle_kernel(mixed_ref, merge_ref, inputs_ref, gain_ref, router_ref, routes_ref, slots_ref, resid_ref, low_ref, gates_ref, out_ref, held, *, eps, settling):
    step = pl.program_id(0)
    block, picking = mixed_ref.shape[0], out_ref.shape[0]
    @pl.when(step < settling)
    def _():
        resid = inputs_ref[...].astype(jnp.float32) + dot_nn(mixed_ref[...], merge_ref[...])
        resid_ref[...] = resid
        inverse = lax.rsqrt(jnp.mean(resid * resid, axis=1, keepdims=True) + eps)
        low = (resid * inverse * gain_ref[...]).astype(jnp.bfloat16)
        low_ref[...] = low
        held[pl.ds(pl.multiple_of(step * block, block), block), :] = low
        logits = dot_nt(router_ref[...], low)
        expert = lax.broadcasted_iota(jnp.int32, logits.shape, 0)
        chosen = [jnp.sum(jnp.where(routes_ref[c:c + 1, :] == expert, logits, 0.0), axis=0, keepdims=True) for c in range(2)]
        top = jnp.maximum(chosen[0], chosen[1])
        powers = [jnp.exp(value - top) for value in chosen]
        total = powers[0] + powers[1]
        for c in range(2):
            gates_ref[c:c + 1, :] = powers[c] / total
    @pl.when(step >= settling)
    def _():
        tokens = held.shape[0]
        slot = lax.broadcasted_iota(jnp.int32, (picking, tokens), 0) + (step - settling) * picking
        hot = jnp.where((slot == slots_ref[0:1, :]) | (slot == slots_ref[1:2, :]), 1.0, 0.0)
        out_ref[...] = dot_nn(hot.astype(jnp.bfloat16), held[...]).astype(out_ref.dtype)


def settle(mixed, merge, inputs, gain, router, routes, slots, count, eps, block=512):
    tokens, width = inputs.shape
    picking = count // 4
    settling = tokens // block
    early = lambda i: jnp.minimum(i, settling - 1)
    rows = pl.BlockSpec((block, width), lambda i: (early(i), 0))
    whole = lambda shape: pl.BlockSpec(shape, lambda i: (0, 0))
    small = pl.BlockSpec((2, block), lambda i: (0, early(i)))
    return pl.pallas_call(
        partial(settle_kernel, eps=eps, settling=settling),
        grid=(settling + 4,),
        in_specs=[rows, whole(merge.shape), rows, whole(gain.shape), whole(router.shape), small, whole(slots.shape)],
        out_specs=[rows, rows, small, pl.BlockSpec((picking, width), lambda i: (jnp.maximum(i - settling, 0), 0))],
        out_shape=[jax.ShapeDtypeStruct((tokens, width), jnp.float32), jax.ShapeDtypeStruct((tokens, width), jnp.bfloat16), jax.ShapeDtypeStruct((2, tokens), jnp.float32), jax.ShapeDtypeStruct((count, width), jnp.bfloat16)],
        scratch_shapes=[pltpu.VMEM((tokens, width), jnp.bfloat16)],
        compiler_params=pltpu.CompilerParams(vmem_limit_bytes=62 << 20),
    )(mixed, merge, inputs, gain, router, routes, slots)


def finish_kernel(heads_ref, query_ref, key_ref, value_ref, gain_ref, inputs_ref, resid_grad_ref, out_ref, gain_grad_ref, *, eps):
    grads = dot_nt(heads_ref[0], query_ref[...]) + dot_nt(heads_ref[1], key_ref[...]) + dot_nt(heads_ref[2], value_ref[...])
    rows = inputs_ref[...].astype(jnp.float32)
    inverse = lax.rsqrt(jnp.mean(rows * rows, axis=1, keepdims=True) + eps)
    unit = rows * inverse
    @pl.when(pl.program_id(0) == 0)
    def _():
        gain_grad_ref[...] = jnp.zeros_like(gain_grad_ref)
    gain_grad_ref[...] += jnp.sum(grads * unit, axis=0, keepdims=True)
    scaled = grads * gain_ref[...]
    inner = jnp.mean(scaled * unit, axis=1, keepdims=True)
    out_ref[...] = resid_grad_ref[...] + inverse * (scaled - unit * inner)


def finish(head_grads, query, key, value, gain, inputs, resid_grad, eps, block=256):
    tokens, width = inputs.shape
    rows = pl.BlockSpec((block, width), lambda i: (i, 0))
    whole = lambda shape: pl.BlockSpec(shape, lambda i: (0, 0))
    return pl.pallas_call(
        partial(finish_kernel, eps=eps),
        grid=(tokens // block,),
        in_specs=[pl.BlockSpec((3, block, width), lambda i: (0, i, 0))] + [whole(query.shape)] * 3 + [whole(gain.shape), rows, rows],
        out_specs=[rows, whole((1, width))],
        out_shape=[jax.ShapeDtypeStruct((tokens, width), jnp.float32), jax.ShapeDtypeStruct((1, width), jnp.float32)],
        compiler_params=pltpu.CompilerParams(vmem_limit_bytes=62 << 20),
    )(head_grads, query, key, value, gain, inputs, resid_grad)


def weight_kernel(left_ref, mixed_ref, heads_ref, branch_ref, out_ref, turned, right):
    shards, part, _ = out_ref.shape
    step = pl.program_id(0)
    last = pl.num_programs(0) - 1
    @pl.when(step == 0)
    def _():
        turned[...] = left_ref[...].T
    @pl.when(step < last)
    def _():
        right[...] = heads_ref[...]
    @pl.when(step == last)
    def _():
        turned[...] = mixed_ref[...].T
        right[...] = branch_ref[...]
    for shard in range(shards):
        grad = dot_nn(turned[shard * part:(shard + 1) * part, :], right[...])
        out_ref[shard] = grad.astype(jnp.bfloat16)


def weight_grads(left, mixed, head_grads, branch, shards):
    count, tokens, width = head_grads.shape
    part = width // shards
    fixed = pl.BlockSpec((tokens, width), lambda i: (0, 0))
    return pl.pallas_call(
        weight_kernel,
        grid=(count + 1,),
        in_specs=[fixed, fixed, pl.BlockSpec((None, tokens, width), lambda i: (jnp.minimum(i, count - 1), 0, 0)), fixed],
        out_specs=pl.BlockSpec((shards, part, width), lambda i: (0, i, 0)),
        out_shape=jax.ShapeDtypeStruct((shards, (count + 1) * part, width), jnp.bfloat16),
        scratch_shapes=[pltpu.VMEM((width, tokens), jnp.bfloat16), pltpu.VMEM((tokens, width), jnp.bfloat16)],
        compiler_params=pltpu.CompilerParams(vmem_limit_bytes=62 << 20),
    )(left, mixed, head_grads, branch)


def widen_first_kernel(rows_ref, out_ref):
    out_ref[...] = rows_ref[...].astype(jnp.float32)


def widen_first(rows):
    count, width = rows.shape
    half = pl.BlockSpec((count // 2, width), lambda i: (i, 0))
    return pl.pallas_call(
        widen_first_kernel,
        grid=(2,),
        in_specs=[half],
        out_specs=half,
        out_shape=jax.ShapeDtypeStruct((2 * count, width), jnp.float32),
        compiler_params=pltpu.CompilerParams(vmem_limit_bytes=62 << 20),
    )(rows)


def widen_rest_kernel(rows_ref, into_ref, up_ref, down_ref):
    del into_ref
    wide = rows_ref[...].astype(jnp.float32)
    step = pl.program_id(0)
    @pl.when(step < 2)
    def _():
        up_ref[...] = wide
    @pl.when(step >= 2)
    def _():
        down_ref[...] = wide


def widen_rest(rows, into):
    count, width = rows.shape[0] // 3, rows.shape[1]
    half = lambda place: pl.BlockSpec((count, width), lambda i: (place(i), 0))
    wide = jax.ShapeDtypeStruct((2 * count, width), jnp.float32)
    return pl.pallas_call(
        widen_rest_kernel,
        grid=(3,),
        in_specs=[half(lambda i: i), pl.BlockSpec(memory_space=pl.ANY)],
        out_specs=[half(lambda i: jnp.minimum(i, 1)), half(lambda i: 1)],
        out_shape=[wide, wide],
        input_output_aliases={1: 1},
        compiler_params=pltpu.CompilerParams(vmem_limit_bytes=62 << 20),
    )(rows, into)


def smalls_kernel(small_ref, near_ref, gain_one_ref, gain_two_ref, router_ref, table_ref, *, part, heads, router_at):
    shards, _, width = small_ref.shape
    group = table_ref.shape[1]
    lanes = -(-part // 128) * 128
    row = lax.broadcasted_iota(jnp.int32, (lanes, width), 0)
    column = lax.broadcasted_iota(jnp.int32, (lanes, width), 1)
    wide = None
    for shard in range(shards):
        place = jnp.where((column == row + shard * part) & (row < part), 1.0, 0.0).astype(jnp.bfloat16)
        rows = dot_nn(small_ref[shard][:, :lanes], place)
        wide = rows if wide is None else wide + rows
        near = dot_nn(small_ref[shard][:8, :128], near_ref[...])
        for head in range(heads):
            at = shard * heads + head
            table_ref[at // group, at % group:at % group + 1, :] = near[2 + head:3 + head, :]
    gain_one_ref[...] = wide[0:1]
    gain_two_ref[...] = wide[1:2]
    router_ref[...] = wide[router_at:router_at + router_ref.shape[0]].astype(jnp.bfloat16)


def spread_smalls(small, near, part, heads, group, experts, router_at):
    shards, _, width = small.shape
    f32 = jnp.float32
    return pl.pallas_call(
        partial(smalls_kernel, part=part, heads=heads, router_at=router_at),
        out_shape=[
            jax.ShapeDtypeStruct((1, width), f32),
            jax.ShapeDtypeStruct((1, width), f32),
            jax.ShapeDtypeStruct((experts, width), jnp.bfloat16),
            jax.ShapeDtypeStruct((shards * heads // group, group, near.shape[1]), f32),
        ],
    )(small, near)


OWNER = "expert"
LINE = "shard"


def exchange(rows, bit):
    count = lax.axis_size(OWNER)
    return lax.ppermute(rows, OWNER, [(i, i ^ bit) for i in range(count)])


def shift(rows, step):
    count = lax.axis_size(LINE)
    return lax.ppermute(rows, LINE, [(i, (i + step) % count) for i in range(count)])


def gather_line(rows):
    count = lax.axis_size(LINE)
    me = lax.axis_index(LINE)
    out = jnp.zeros((count,) + rows.shape, rows.dtype)
    out = lax.dynamic_update_index_in_dim(out, rows, me, 0)
    for step in range(1, count):
        got = shift(rows, step)
        out = lax.dynamic_update_index_in_dim(out, got, (me - step) % count, 0)
    return out


def add_low(left, right):
    return (left.astype(jnp.float32) + right.astype(jnp.float32)).astype(jnp.bfloat16)


def side(bit):
    return (lax.axis_index(OWNER) // bit) % 2


def halve(stack, bit):
    half = stack.shape[1] // 2
    keep = lax.dynamic_slice_in_dim(stack, side(bit) * half, half, 1)
    send = lax.dynamic_slice_in_dim(stack, (1 - side(bit)) * half, half, 1)
    got = exchange(send, bit)
    return add_low(keep, got)


def line_sum(stack):
    count = lax.axis_size(LINE)
    place = lax.axis_index(LINE)
    total = lax.dynamic_index_in_dim(stack, place, 0, False).astype(jnp.float32)
    for step in range(1, count):
        send = lax.dynamic_index_in_dim(stack, (place + step) % count, 0, False)
        total = total + shift(send, step).astype(jnp.float32)
    return total.astype(jnp.bfloat16)


def grow(piece, bit):
    other = exchange(piece, bit)
    return jnp.where(
        side(bit) == 0, jnp.concatenate([piece, other]), jnp.concatenate([other, piece])
    )


def reduce_rows(stack, bits):
    unit = 8 << (len(bits) - 1)
    cut = -(-stack.shape[1] // (2 * unit)) * unit
    parts = [stack[:, :cut], stack[:, cut:]]
    orders = [bits[1:], bits[:0:-1]]
    for level in range(len(bits) - 1):
        parts = [halve(part, order[level]) for part, order in zip(parts, orders)]
    low = parts[0].shape[1]
    piece = line_sum(jnp.concatenate(parts, axis=1))
    parts = [piece[:low], piece[low:]]
    for level in reversed(range(len(bits) - 1)):
        parts = [grow(part, order[level]) for part, order in zip(parts, orders)]
    return grow(jnp.concatenate(parts), bits[0])


def scatter_sum(grads):
    shards, rows, width = grads.shape
    grads = grads.reshape(shards * rows, width)
    return lax.psum_scatter(grads, LINE, scatter_dimension=0, tiled=True)


def share_rows(rows):
    return lax.all_to_all(rows, OWNER, 0, 0, tiled=True)


def share_large(rows):
    return pltpu.with_memory_space_constraint(share_rows(rows), pltpu.HBM)


def local(
    inputs,
    norm_gain,
    query_weight,
    key_weight,
    value_weight,
    merge_weight,
    bias_table,
    expert_gain,
    router_weight,
    up_weight,
    down_weight,
    routes,
    cotangent,
):
    f32, bf16 = jnp.float32, jnp.bfloat16
    tokens, width = inputs.shape
    owners = lax.axis_size(OWNER)
    shards = lax.axis_size(LINE)
    me = lax.axis_index(OWNER)
    part = query_weight.shape[0]
    piece = part // owners
    local_heads = bias_table.shape[1]
    heads = local_heads * shards
    size = width // heads
    experts = router_weight.shape[1]
    local_count, _, hidden = up_weight.shape
    capacity = (5 * tokens * routes.shape[1] + 4 * experts - 1) // (4 * experts)
    capacity = -(-capacity // 16) * 16
    rows = owners * capacity
    assert local_count == 2 and hidden // shards == width
    early = -(-capacity // 32) * 16

    router_at = 2 + local_heads + (-(2 + local_heads)) % 8

    def widen(block):
        return jnp.pad(block, ((0, 0), (0, width - block.shape[1])))

    def pack(gain_one, gain_two, table, router):
        head = jnp.concatenate([gain_one, gain_two], axis=0)
        gap = jnp.zeros((router_at - 2 - local_heads, width), bf16)
        return jnp.concatenate([widen(head), widen(table), gap, widen(router)], axis=0)

    small = pack(norm_gain[None], expert_gain[None], bias_table.T, router_weight.T)
    slices = [
        lax.dynamic_slice_in_dim(weight, me * piece, piece, 0)
        for weight in (query_weight, key_weight, value_weight)
    ]
    lined = gather_line(jnp.concatenate(slices + [small]))
    small_full = lined[:, 3 * piece :]
    bits = [1 << level for level in range(owners.bit_length() - 1)]
    pieces = []
    for index, order in enumerate((bits[1:], bits[:0:-1])):
        held = lined[index * shards // 2 : (index + 1) * shards // 2, : 3 * piece][None]
        for bit in order:
            got = exchange(held, bit)
            held = jnp.concatenate([held, got])
        pieces += [held, exchange(held, bits[0])]
    merge_full = lax.all_gather(merge_weight, LINE, axis=0, tiled=True)

    block = 256
    hot = bucket_hot(tokens)
    assert hot[block:, -1].all()
    near_hot = np.zeros((128, block), np.float32)
    near_hot[:BUCKETS] = (hot[:block] - hot[-1:]).T
    group = 128 // size
    gain_one, gain_two, router_full, near = spread_smalls(
        small_full, jnp.asarray(near_hot, bf16), part, local_heads, group, experts, router_at
    )

    routes_line = routes.T
    slots, routes_float = find_slots(routes_line, experts, local_count, owners, capacity)
    cot_rows, other = dispatch_first(
        slots, routes_float, cotangent, owners, capacity, early
    )
    other = share_rows(other).reshape(owners, local_count, capacity)

    owner = me.astype(jnp.int32).reshape(1)
    query_full, key_full, value_full, low_one, queries, keys, values = project(
        owner, inputs, gain_one, pieces, epsilon, after=(near, router_full)
    )
    cot_in = share_large(cot_rows)
    attended, totals = attend(queries, keys, values, near, size, block)
    resid, low_two, gates, send = settle(
        attended, merge_full, inputs, gain_two, router_full, routes_line, slots, rows, epsilon
    )

    others = [other[:, index].reshape(1, rows) for index in range(local_count)]
    rows_in = share_large(send.reshape(owners, capacity, width))
    joint = dispatch_both(
        slots, low_two, cotangent, rows, owners, capacity, early, after=others
    )
    joint_in = share_large(joint)
    act, pre, first_down, grad_in = expert_first(
        owner, rows_in, [cot_in], [(0, 0, capacity)], others[0], router_full, up_weight,
        0, local_count, capacity, shards,
    )
    first_sum = scatter_sum(first_down)
    first_made, pair = expert_second(rows_in, grad_in, act, pre, up_weight, down_weight, 0, owners, shards, 3 * width)
    late = capacity - early
    act, pre, pair, grad_in = expert_first(
        owner, joint_in, [cot_in, joint_in], [(0, capacity, early), (1, capacity, late)],
        others[1], router_full, up_weight, 1, local_count, capacity, shards, into=pair,
    )
    low, pair = expert_slope(joint_in, grad_in, pre, down_weight, 1, shards, pair, 1)
    pair_sum = scatter_sum(pair)
    second_made = expert_last(act, low, up_weight, down_weight, 1, owners, shards)
    returned = share_rows(first_made)
    result, inner, part_grads = combine_part(slots, gates, resid, cotangent, returned)
    returned = share_rows(second_made)
    output, logit_grad = combine_out(
        slots, routes_line, gates, result, inner, cotangent, returned
    )
    router_wide = jnp.pad(router_full, ((0, 128 - experts), (0, 0)))
    resid_grad, branch, mixed_grad, gain_grad = combine_back(
        slots, logit_grad, router_wide, gain_two, resid, cotangent, merge_full,
        part_grads, returned, epsilon
    )
    router_grad = jnp.einsum("te,ti->ei", logit_grad, low_two, preferred_element_type=f32)
    head_grads, distances = attend_back(
        queries, keys, values, mixed_grad, attended, totals, near, size, block
    )
    close_sums = distances[:, :group].reshape(heads, block)
    far_sums = jnp.sum(distances[:, group:].reshape(heads, block), axis=1)
    table_grad = jnp.dot(close_sums, jnp.asarray(hot[:block]), precision=lax.Precision.HIGHEST)
    table_grad = table_grad + far_sums[:, None] * jnp.asarray(hot[-1:])
    sums = weight_grads(low_one, attended, head_grads, branch, shards)
    sums = halve(sums, bits[0])
    input_gradient, norm_grad = finish(
        head_grads, query_full, key_full, value_full, gain_one, inputs, resid_grad, epsilon
    )
    small_grad = jax.vmap(pack)(
        norm_grad.reshape(shards, 1, part).astype(bf16),
        gain_grad.reshape(shards, 1, part).astype(bf16),
        table_grad.reshape(shards, local_heads, BUCKETS).astype(bf16),
        router_grad[:experts].reshape(experts, shards, part).transpose(1, 0, 2).astype(bf16),
    )
    spare = -small_grad.shape[1] % (8 * owners)
    small_grad = halve(jnp.pad(small_grad, ((0, 0), (0, spare), (0, 0))), bits[0])
    kept = sums.shape[1]
    sums = reduce_rows(jnp.concatenate([sums, small_grad], axis=1), bits)
    half = sums.shape[0] // 2
    weights = jnp.concatenate([sums[:kept], sums[half : half + kept]]).astype(f32)
    small_sum = jnp.concatenate([sums[kept:half], sums[half + kept :]]).astype(f32)
    up_sum, down_sum = widen_rest(pair_sum, widen_first(first_sum))
    return (
        output,
        input_gradient,
        small_sum[0, :part],
        weights[:part],
        weights[part : 2 * part],
        weights[2 * part : 3 * part],
        weights[3 * part :],
        small_sum[2 : 2 + local_heads, :BUCKETS].T,
        small_sum[1, :part],
        small_sum[router_at : router_at + experts, :part].T,
        up_sum.reshape(local_count, width, width),
        down_sum.reshape(local_count, width, width),
    )


def solution(mesh):
    in_specs = (
        P((OWNER, LINE), None),
        P(LINE),
        P(LINE, None),
        P(LINE, None),
        P(LINE, None),
        P(LINE, None),
        P(None, LINE),
        P(LINE),
        P(LINE, None),
        P(OWNER, None, None),
        P(OWNER, None, None),
        P((OWNER, LINE), None),
        P((OWNER, LINE), None),
    )
    out_specs = (
        P((OWNER, LINE), None),
        P((OWNER, LINE), None),
        P(LINE),
        P(LINE, None),
        P(LINE, None),
        P(LINE, None),
        P(LINE, None),
        P(None, LINE),
        P(LINE),
        P(LINE, None),
        P(OWNER, None, LINE),
        P(OWNER, LINE, None),
    )

    return jax.shard_map(local, mesh=mesh, in_specs=in_specs, out_specs=out_specs, check_vma=False)
```

```python
from functools import partial, reduce

import jax
import jax.numpy as jnp
import numpy as np
from jax import lax
from jax.experimental import pallas as pl
from jax.experimental.pallas import tpu as pltpu
from jax.sharding import PartitionSpec as P


BUCKETS = 32
MAX_DIST = 128


epsilon = 1e-06
masked_score = -1e30


def bucket_hot(length):
    distance = np.arange(length)
    half_count = BUCKETS // 2
    clipped = np.maximum(distance, half_count)
    spread = np.log(clipped / half_count) / np.log(MAX_DIST / half_count) * (BUCKETS - half_count)
    far_bucket = np.minimum(half_count + np.floor(spread).astype(np.int32), BUCKETS - 1)
    bucket = np.where(distance < half_count, distance, far_bucket)
    return (bucket[:, None] == np.arange(BUCKETS)[None, :]).astype(np.float32)


def dot_nt(a, b):
    return lax.dot_general(a, b, (((1,), (1,)), ((), ())), preferred_element_type=jnp.float32)


def dot_nn(a, b):
    return lax.dot_general(a, b, (((1,), (0,)), ((), ())), preferred_element_type=jnp.float32)


def dot_tn(a, b):
    return lax.dot_general(a, b, (((0,), (0,)), ((), ())), preferred_element_type=jnp.float32)


def slot_kernel(routes_ref, slots_ref, float_ref, *, experts, local_count, owners, capacity):
    tokens = routes_ref.shape[1]
    expert = lax.broadcasted_iota(jnp.int32, (experts, tokens), 0)
    hits = [routes_ref[c:c + 1, :] == expert for c in range(2)]
    hot = jnp.where(hits[0] | hits[1], 1.0, 0.0).astype(jnp.bfloat16)
    earlier = lax.broadcasted_iota(jnp.int32, (tokens, tokens), 0)
    later = lax.broadcasted_iota(jnp.int32, (tokens, tokens), 1)
    before = jnp.where(earlier < later, 1.0, 0.0).astype(jnp.bfloat16)
    counts = dot_nn(hot, before)
    column = lax.broadcasted_iota(jnp.int32, (experts, 1), 0)
    base = (column % local_count * owners + column // local_count) * capacity
    counts = counts + base.astype(jnp.float32)
    for c in range(2):
        slot = jnp.sum(jnp.where(hits[c], counts, 0.0), axis=0, keepdims=True)
        slots_ref[c:c + 1, :] = slot.astype(jnp.int32)
    float_ref[...] = routes_ref[...].astype(jnp.float32)


def find_slots(routes, experts, local_count, owners, capacity):
    return pl.pallas_call(
        partial(slot_kernel, experts=experts, local_count=local_count, owners=owners, capacity=capacity),
        out_shape=[jax.ShapeDtypeStruct(routes.shape, jnp.int32), jax.ShapeDtypeStruct(routes.shape, jnp.float32)],
    )(routes)


def dispatch_both_kernel(slots_ref, rows_ref, cot_ref, out_ref, *, start, capacity, early):
    block, tokens = capacity, rows_ref.shape[0]
    slot = lax.broadcasted_iota(jnp.int32, (block, tokens), 0) + (pl.program_id(0) * block + start)
    hot = jnp.where((slot == slots_ref[0:1, :]) | (slot == slots_ref[1:2, :]), 1.0, 0.0)
    hot = hot.astype(jnp.bfloat16)
    out_ref[0, :capacity] = dot_nn(hot, rows_ref[...]).astype(out_ref.dtype)
    out_ref[0, capacity:] = dot_nn(hot[early:], cot_ref[...]).astype(out_ref.dtype)


def dispatch_both(slots, rows, cot, start, owners, capacity, early):
    width = rows.shape[1]
    total = 2 * capacity - early
    whole = lambda shape: pl.BlockSpec(shape, lambda i: (0, 0))
    return pl.pallas_call(
        partial(dispatch_both_kernel, start=start, capacity=capacity, early=early),
        grid=(owners,),
        in_specs=[whole(slots.shape), whole(rows.shape), whole(cot.shape)],
        out_specs=pl.BlockSpec((1, total, width), lambda i: (i, 0, 0)),
        out_shape=jax.ShapeDtypeStruct((owners, total, width), rows.dtype),
        compiler_params=pltpu.CompilerParams(vmem_limit_bytes=62 << 20),
    )(slots, rows, cot)


def padded(count):
    return -(-count // 128) * 128


def dispatch_first_kernel(slots_ref, routes_ref, rows_ref, out_ref, *, owners, capacity, early):
    per, _, width = out_ref.shape
    block, tokens, total = 2 * capacity, rows_ref.shape[0], capacity + early
    wide = padded(capacity)
    row = lax.broadcasted_iota(jnp.int32, (block, tokens), 0)
    row = row + jnp.where(row >= capacity, (owners - 1) * capacity, 0)
    hots = []
    for index in range(per):
        slot = row + (pl.program_id(0) * per + index) * capacity
        hits = [slot == slots_ref[c:c + 1, :] for c in range(2)]
        hots.append(jnp.where(hits[0] | hits[1], 1.0, 0.0)[:total].astype(jnp.bfloat16))
        other = jnp.where(hits[0], routes_ref[1:2, :], jnp.where(hits[1], routes_ref[0:1, :], 0.0))
        column = jnp.broadcast_to(jnp.sum(other, axis=1, keepdims=True), (block, 128))
        gap = jnp.zeros((wide - capacity, 128), jnp.float32)
        for local in range(2):
            part = jnp.concatenate([column[local * capacity:(local + 1) * capacity], gap], axis=0)
            out_ref[index, total:, local * wide:(local + 1) * wide] = part.T[:16].astype(out_ref.dtype)
        out_ref[index, total:, 2 * wide:] = jnp.zeros((16, width - 2 * wide), out_ref.dtype)
    picked = dot_nn(jnp.concatenate(hots, axis=0), rows_ref[...]).astype(out_ref.dtype)
    for index in range(per):
        out_ref[index, :total] = picked[index * total:(index + 1) * total]


def dispatch_first(slots, routes, rows, owners, capacity, early, per=4):
    width = rows.shape[1]
    total = capacity + early + 16
    whole = lambda shape: pl.BlockSpec(shape, lambda i: (0, 0))
    return pl.pallas_call(
        partial(dispatch_first_kernel, owners=owners, capacity=capacity, early=early),
        grid=(owners // per,),
        in_specs=[whole(slots.shape), whole(routes.shape), whole(rows.shape)],
        out_specs=pl.BlockSpec((per, total, width), lambda i: (i, 0, 0)),
        out_shape=jax.ShapeDtypeStruct((owners, total, width), rows.dtype),
        compiler_params=pltpu.CompilerParams(vmem_limit_bytes=62 << 20),
    )(slots, routes, rows)


def gelu_half(v):
    c = np.float32(np.sqrt(2.0 / np.pi))
    square = v * v
    half = 0.5 * jnp.tanh(v * (np.float32(0.044715) * c * square + c)) + 0.5
    return half, square


def gelu_slope(v):
    c = np.float32(np.sqrt(2.0 / np.pi))
    half, square = gelu_half(v)
    return half + v * half * (1.0 - half) * (np.float32(6.0 * 0.044715) * c * square + 2.0 * c)


def arrived_spec(arrived, used=None):
    owners, count, width = arrived.shape
    return pl.BlockSpec((owners, used or count, width), lambda i: (0, 0, 0))


def first_kernel(owner_ref, rows_ref, router_ref, up_ref, *refs, index, local_count, capacity, pieces):
    act_ref, pre_ref, down_grad_ref, grad_ref = refs[-4:]
    owners, _, width = rows_ref.shape
    rows = owners * capacity
    chunk = rows // 2
    @pl.when(pl.program_id(0) == 0)
    def _():
        wide = padded(capacity)
        expert = lax.broadcasted_iota(jnp.int32, (router_ref.shape[0], capacity), 0)
        mine = owner_ref[0] * local_count + index
        for owner in range(owners):
            logits = dot_nt(router_ref[...], rows_ref[owner, :capacity])
            other = refs[0][owner, -16:, index * wide:(index + 1) * wide].astype(jnp.float32)
            other = other[0:1, :capacity].astype(jnp.int32)
            own = jnp.sum(jnp.where(expert == mine, logits, 0.0), axis=0, keepdims=True)
            other = jnp.sum(jnp.where(expert == other, logits, 0.0), axis=0, keepdims=True)
            top = jnp.maximum(own, other)
            own = jnp.exp(own - top)
            gate = own / (own + jnp.exp(other - top))
            column = jnp.broadcast_to(gate, (128, capacity)).T
            at = owner * capacity
            for start in range(0, width, 128):
                parts = [refs[place][owner, low:low + size, start:start + 128] for place, low, size in pieces]
                part = parts[0] if len(parts) == 1 else jnp.concatenate(parts, axis=0)
                part = part.astype(jnp.float32) * column
                grad_ref[at:at + capacity, start:start + 128] = part.astype(jnp.bfloat16)
    up = up_ref[0]
    for start in range(0, rows, chunk):
        part = rows_ref[start // capacity:(start + chunk) // capacity, :capacity].reshape(chunk, width)
        pre = dot_nn(part, up)
        half, _ = gelu_half(pre)
        act_ref[start:start + chunk, :] = (pre * half).astype(jnp.bfloat16)
        pre_ref[start:start + chunk, :] = pre.astype(jnp.bfloat16)
    down_grad_ref[0] = dot_tn(act_ref[...], grad_ref[...]).astype(jnp.bfloat16)


def expert_first(owner, rows_in, cots, pieces, router, up, index, local_count, capacity, shards, into=None):
    owners, _, width = rows_in.shape
    rows = owners * capacity
    hidden = up.shape[2]
    tile = hidden // shards
    fixed = pl.BlockSpec((rows, width), lambda i: (0, 0))
    column = pl.BlockSpec((rows, tile), lambda i: (0, i))
    operands = [owner, rows_in, router, up, *cots]
    place, aliases = 0, {}
    grad_shape = jax.ShapeDtypeStruct((shards, tile, width), jnp.bfloat16)
    if into is not None:
        aliases = {len(operands): 2}
        operands.append(into)
        place, grad_shape = 2, jax.ShapeDtypeStruct(into.shape, into.dtype)
    return pl.pallas_call(
        partial(first_kernel, index=index, local_count=local_count, capacity=capacity, pieces=pieces),
        grid=(shards,),
        in_specs=[
            pl.BlockSpec(memory_space=pltpu.SMEM),
            arrived_spec(rows_in, capacity),
            pl.BlockSpec(router.shape, lambda i: (0, 0)),
            pl.BlockSpec((1, width, tile), lambda i: (index, 0, i)),
        ]
        + [arrived_spec(cot) for cot in cots]
        + [pl.BlockSpec(memory_space=pl.ANY)] * (into is not None),
        out_specs=[column, column, pl.BlockSpec((1, tile, width), lambda i: (i, place, 0)), fixed],
        out_shape=[jax.ShapeDtypeStruct((rows, hidden), jnp.bfloat16)] * 2 + [grad_shape, jax.ShapeDtypeStruct((rows, width), jnp.bfloat16)],
        input_output_aliases=aliases,
        compiler_params=pltpu.CompilerParams(vmem_limit_bytes=62 << 20),
    )(*operands)


def second_kernel(rows_ref, grad_ref, act_ref, pre_ref, up_ref, down_ref, *refs):
    made_ref, up_grad_ref, turned, made_acc, back_acc = refs[-5:]
    step = pl.program_id(0)
    owners, _, capacity, width = made_ref.shape
    @pl.when(step == 0)
    def _():
        rows, width = grad_ref.shape
        owners = rows_ref.shape[0]
        turned[...] = rows_ref[:, :rows // owners].reshape(rows, width).T
    up = up_ref[0]
    down = down_ref[0]
    grads = dot_nt(grad_ref[...], down)
    low = (gelu_slope(pre_ref[...].astype(jnp.float32)) * grads).astype(jnp.bfloat16)
    up_grad_ref[0] = dot_nn(turned[...], low).astype(jnp.bfloat16)
    back = dot_nt(low, up)
    made = dot_nn(act_ref[...], down)
    last = pl.num_programs(0) - 1
    @pl.when(step == 0)
    def _():
        made_acc[...] = made
        back_acc[...] = back
    @pl.when((step > 0) & (step < last))
    def _():
        made_acc[...] += made
        back_acc[...] += back
    @pl.when(step == last)
    def _():
        made_ref[:, 0] = (made_acc[...] + made).astype(jnp.bfloat16).reshape(owners, capacity, width)
        made_ref[:, 1] = (back_acc[...] + back).astype(jnp.bfloat16).reshape(owners, capacity, width)


def expert_second(rows_in, grad, act, pre, up, down, index, owners, shards, wide, after=()):
    rows, width = grad.shape
    hidden = up.shape[2]
    tile = hidden // shards
    fixed = pl.BlockSpec((rows, width), lambda i: (0, 0))
    column = pl.BlockSpec((rows, tile), lambda i: (0, i))
    made_shape = (owners, 2, rows // owners, width)
    return pl.pallas_call(
        second_kernel,
        grid=(shards,),
        in_specs=[arrived_spec(rows_in, rows // rows_in.shape[0]), fixed, column, column, pl.BlockSpec((1, width, tile), lambda i: (index, 0, i)), pl.BlockSpec((1, tile, width), lambda i: (index, i, 0))]
        + [pl.BlockSpec(memory_space=pl.ANY)] * len(after),
        out_specs=[pl.BlockSpec(made_shape, lambda i: (0, 0, 0, 0)), pl.BlockSpec((1, width, tile), lambda i: (i, 0, 0))],
        out_shape=[jax.ShapeDtypeStruct(made_shape, jnp.bfloat16), jax.ShapeDtypeStruct((shards, wide, tile), jnp.bfloat16)],
        scratch_shapes=[pltpu.VMEM((width, rows), jnp.bfloat16), pltpu.VMEM((rows, width), jnp.float32), pltpu.VMEM((rows, width), jnp.float32)],
        compiler_params=pltpu.CompilerParams(vmem_limit_bytes=62 << 20),
    )(rows_in, grad, act, pre, up, down, *after)


def slope_kernel(rows_ref, grad_ref, pre_ref, down_ref, into_ref, low_ref, up_grad_ref, turned):
    del into_ref
    @pl.when(pl.program_id(0) == 0)
    def _():
        rows, width = grad_ref.shape
        owners = rows_ref.shape[0]
        turned[...] = rows_ref[:, :rows // owners].reshape(rows, width).T
    grads = dot_nt(grad_ref[...], down_ref[0])
    low = (gelu_slope(pre_ref[...].astype(jnp.float32)) * grads).astype(jnp.bfloat16)
    low_ref[...] = low
    up_grad_ref[0] = dot_nn(turned[...], low).astype(jnp.bfloat16)


def expert_slope(rows_in, grad, pre, down, index, shards, into, place):
    rows, width = grad.shape
    hidden = pre.shape[1]
    tile = hidden // shards
    fixed = pl.BlockSpec((rows, width), lambda i: (0, 0))
    column = pl.BlockSpec((rows, tile), lambda i: (0, i))
    return pl.pallas_call(
        slope_kernel,
        grid=(shards,),
        in_specs=[arrived_spec(rows_in, rows // rows_in.shape[0]), fixed, column, pl.BlockSpec((1, tile, width), lambda i: (index, i, 0)), pl.BlockSpec(memory_space=pl.ANY)],
        out_specs=[column, pl.BlockSpec((1, width, tile), lambda i: (i, place, 0))],
        out_shape=[jax.ShapeDtypeStruct((rows, hidden), jnp.bfloat16), jax.ShapeDtypeStruct(into.shape, into.dtype)],
        input_output_aliases={4: 1},
        scratch_shapes=[pltpu.VMEM((width, rows), jnp.bfloat16)],
        compiler_params=pltpu.CompilerParams(vmem_limit_bytes=62 << 20),
    )(rows_in, grad, pre, down, into)


def last_kernel(act_ref, low_ref, up_ref, down_ref, made_ref, made_acc, back_acc):
    step = pl.program_id(0)
    owners, _, capacity, width = made_ref.shape
    back = dot_nt(low_ref[...], up_ref[0])
    made = dot_nn(act_ref[...], down_ref[0])
    last = pl.num_programs(0) - 1
    @pl.when(step == 0)
    def _():
        made_acc[...] = made
        back_acc[...] = back
    @pl.when((step > 0) & (step < last))
    def _():
        made_acc[...] += made
        back_acc[...] += back
    @pl.when(step == last)
    def _():
        made_ref[:, 0] = (made_acc[...] + made).astype(jnp.bfloat16).reshape(owners, capacity, width)
        made_ref[:, 1] = (back_acc[...] + back).astype(jnp.bfloat16).reshape(owners, capacity, width)


def expert_last(act, low, up, down, index, owners, shards):
    rows, hidden = act.shape
    width = up.shape[1]
    tile = hidden // shards
    column = pl.BlockSpec((rows, tile), lambda i: (0, i))
    made_shape = (owners, 2, rows // owners, width)
    return pl.pallas_call(
        last_kernel,
        grid=(shards,),
        in_specs=[column, column, pl.BlockSpec((1, width, tile), lambda i: (index, 0, i)), pl.BlockSpec((1, tile, width), lambda i: (index, i, 0))],
        out_specs=pl.BlockSpec(made_shape, lambda i: (0, 0, 0, 0)),
        out_shape=jax.ShapeDtypeStruct(made_shape, jnp.bfloat16),
        scratch_shapes=[pltpu.VMEM((rows, width), jnp.float32), pltpu.VMEM((rows, width), jnp.float32)],
        compiler_params=pltpu.CompilerParams(vmem_limit_bytes=62 << 20),
    )(act, low, up, down)


def spread(row, block):
    return jnp.broadcast_to(row, (128, block)).T


def pick(slots, lane, back_refs, first=0):
    picked = None
    for index, back_ref in enumerate(back_refs, first):
        owners, capacity, width = back_ref.shape
        half = owners * capacity
        hots = []
        for start in range(index * half, (index + 1) * half, 128):
            hit = reduce(jnp.logical_or, [slot == lane + start for slot in slots])
            hots.append(jnp.where(hit, 1.0, 0.0).astype(jnp.bfloat16))
        part = dot_nn(jnp.concatenate(hots, axis=1), back_ref[...].reshape(half, width))
        picked = part if picked is None else picked + part
    return picked


def part_kernel(slots_ref, gates_ref, resid_ref, cot_ref, made_ref, back_ref, result_ref, inner_ref, grads_ref):
    block = result_ref.shape[0]
    lane = lax.broadcasted_iota(jnp.int32, (block, 128), 1)
    cot = cot_ref[...].astype(jnp.float32)
    result = resid_ref[...]
    inner = jnp.zeros((block, 128), jnp.float32)
    slots = [spread(slots_ref[c:c + 1, :], block) for c in range(2)]
    for c in range(2):
        picked = pick([slots[c]], lane, [made_ref])
        result = result + spread(gates_ref[c:c + 1, :], block)[:, 0:1] * picked
        inner = inner + jnp.where(lane == c, jnp.sum(cot * picked, axis=1, keepdims=True), 0.0)
    result_ref[...] = result
    inner_ref[...] = inner
    grads_ref[...] = pick(slots, lane, [back_ref])


def combine_part(slots, gates, resid, cot, returned, block=256):
    tokens, width = resid.shape
    small = pl.BlockSpec((2, block), lambda i: (0, i))
    rows = pl.BlockSpec((block, width), lambda i: (i, 0))
    wide = jax.ShapeDtypeStruct((tokens, width), jnp.float32)
    return pl.pallas_call(
        part_kernel,
        grid=(tokens // block,),
        in_specs=[small, small, rows, rows, returned_spec(returned, 0), returned_spec(returned, 1)],
        out_specs=[rows, pl.BlockSpec((block, 128), lambda i: (i, 0)), rows],
        out_shape=[wide, jax.ShapeDtypeStruct((tokens, 128), jnp.float32), wide],
        compiler_params=pltpu.CompilerParams(vmem_limit_bytes=62 << 20),
    )(slots, gates, resid, cot, returned, returned)


def out_kernel(slots_ref, routes_ref, gates_ref, result_ref, inner_ref, cot_ref, made_ref, out_ref, logit_ref):
    block = out_ref.shape[0]
    lane = lax.broadcasted_iota(jnp.int32, (block, 128), 1)
    cot = cot_ref[...].astype(jnp.float32)
    result = result_ref[...]
    gates, inner = [], []
    for c in range(2):
        slot = spread(slots_ref[c:c + 1, :], block)
        gate = spread(gates_ref[c:c + 1, :], block)[:, 0:1]
        picked = pick([slot], lane, [made_ref], 1)
        result = result + gate * picked
        gates.append(gate)
        inner.append(inner_ref[:, c:c + 1] + jnp.sum(cot * picked, axis=1, keepdims=True))
    out_ref[...] = result.astype(out_ref.dtype)
    middle = gates[0] * inner[0] + gates[1] * inner[1]
    logit = jnp.zeros((block, 128), jnp.float32)
    for c in range(2):
        route = spread(routes_ref[c:c + 1, :], block)
        logit = logit + jnp.where(route == lane, gates[c] * (inner[c] - middle), 0.0)
    logit_ref[...] = logit.astype(jnp.bfloat16)


def returned_spec(returned, which):
    owners, _, capacity, width = returned.shape
    return pl.BlockSpec((owners, None, capacity, width), lambda i: (0, which, 0, 0))


def combine_out(slots, routes, gates, result, inner, cot, returned, block=256):
    tokens, width = result.shape
    small = pl.BlockSpec((2, block), lambda i: (0, i))
    rows = pl.BlockSpec((block, width), lambda i: (i, 0))
    return pl.pallas_call(
        out_kernel,
        grid=(tokens // block,),
        in_specs=[small, small, small, rows, pl.BlockSpec((block, 128), lambda i: (i, 0)), rows, returned_spec(returned, 0)],
        out_specs=[rows, pl.BlockSpec((block, 128), lambda i: (i, 0))],
        out_shape=[jax.ShapeDtypeStruct((tokens, width), jnp.bfloat16), jax.ShapeDtypeStruct((tokens, 128), jnp.bfloat16)],
        compiler_params=pltpu.CompilerParams(vmem_limit_bytes=62 << 20),
    )(slots, routes, gates, result, inner, cot, returned)


def back_kernel(slots_ref, logit_ref, router_ref, gain_ref, resid_ref, cot_ref, merge_ref, part_ref, back_ref, grad_ref, low_ref, mixed_ref, gain_grad_ref, *, eps):
    block, _ = grad_ref.shape
    lane = lax.broadcasted_iota(jnp.int32, (block, 128), 1)
    grads = part_ref[...] + pick([spread(slots_ref[c:c + 1, :], block) for c in range(2)], lane, [back_ref], 1)
    grads = grads + dot_nn(logit_ref[...], router_ref[...])
    resid = resid_ref[...]
    inverse = lax.rsqrt(jnp.mean(resid * resid, axis=1, keepdims=True) + eps)
    unit = resid * inverse
    @pl.when(pl.program_id(0) == 0)
    def _():
        gain_grad_ref[...] = jnp.zeros_like(gain_grad_ref)
    gain_grad_ref[...] += jnp.sum(grads * unit, axis=0, keepdims=True)
    scaled = grads * gain_ref[...]
    inner = jnp.mean(scaled * unit, axis=1, keepdims=True)
    total = cot_ref[...].astype(jnp.float32) + inverse * (scaled - unit * inner)
    grad_ref[...] = total
    low = total.astype(jnp.bfloat16)
    low_ref[...] = low
    mixed_ref[...] = dot_nt(low, merge_ref[...]).astype(jnp.bfloat16)


def combine_back(slots, logit, router, gain, resid, cot, merge, part, returned, eps, block=256):
    tokens, width = resid.shape
    rows = pl.BlockSpec((block, width), lambda i: (i, 0))
    whole = lambda shape: pl.BlockSpec(shape, lambda i: (0, 0))
    low = jax.ShapeDtypeStruct((tokens, width), jnp.bfloat16)
    return pl.pallas_call(
        partial(back_kernel, eps=eps),
        grid=(tokens // block,),
        in_specs=[pl.BlockSpec((2, block), lambda i: (0, i)), pl.BlockSpec((block, 128), lambda i: (i, 0)), whole(router.shape), whole(gain.shape), rows, rows, whole(merge.shape), rows, returned_spec(returned, 1)],
        out_specs=[rows, rows, rows, whole((1, width))],
        out_shape=[jax.ShapeDtypeStruct((tokens, width), jnp.float32), low, low, jax.ShapeDtypeStruct((1, width), jnp.float32)],
        compiler_params=pltpu.CompilerParams(vmem_limit_bytes=62 << 20),
    )(slots, logit, router, gain, resid, cot, merge, part, returned)


def near_tiles(near_ref, head, block):
    spread = jnp.broadcast_to(near_ref[0, head:head + 1, :], (block, block))
    spread = pltpu.roll(spread, 0, 1, stride=1, stride_axis=0)
    key_at = lax.broadcasted_iota(jnp.int32, (block, block), 0)
    query_at = lax.broadcasted_iota(jnp.int32, (block, block), 1)
    return (jnp.where(query_at >= key_at, spread, masked_score), jnp.where(query_at < key_at, spread, 0.0), query_at < key_at)


def diagonal_sums(tile):
    block = tile.shape[1]
    total = tile[:8]
    for start in range(8, block, 8):
        total = total + pltpu.roll(tile[start:start + 8], block - start, 1)
    row = lax.broadcasted_iota(jnp.int32, total.shape, 0)
    for step in (1, 2, 4):
        total = jnp.where((row & step) != 0, pltpu.roll(total, block - step, 1), total)
    return jnp.sum(total, axis=0, keepdims=True)


def head_part(rows, head, size):
    lane = lax.broadcasted_iota(jnp.int32, rows.shape, 1)
    return jnp.where((lane >= head * size) & (lane < (head + 1) * size), rows, jnp.zeros_like(rows))


def attend_kernel(query_ref, key_ref, value_ref, near_ref, out_ref, total_ref, held, *, block, size, scale):
    length, lanes = query_ref.shape
    heads = lanes // size
    count = length // block
    turned = value_ref[...].T
    ones = jnp.ones((16, length), jnp.bfloat16)
    flipped = [jnp.concatenate([turned[head * size:(head + 1) * size], ones], axis=0) for head in range(heads)]
    tiles = [near_tiles(near_ref, head, block) for head in range(heads)]
    units = [(i, head) for i in range(count) for head in range(heads)]
    def fold(tile, op):
        parts = [tile[k:k + 8] for k in range(0, tile.shape[0], 8)]
        while len(parts) > 1:
            parts = [op(parts[k], parts[k + 1]) for k in range(0, len(parts), 2)]
        return parts[0]
    def score_tile(unit, query_part, j, slot):
        i, head = unit
        tile = dot_nt(key_ref[pl.ds(j * block, block), :], query_part)
        if j == i:
            tile = tile + tiles[head][0]
        elif j == i - 1:
            tile = tile + tiles[head][1]
        held[slot, pl.ds(j * block, block), :] = tile
        return fold(tile, jnp.maximum)
    def part_of(unit):
        i, head = unit
        return head_part(query_ref[pl.ds(i * block, block), :] * jnp.bfloat16(scale), head, size)
    tops = {0: [score_tile(units[0], part_of(units[0]), 0, 0)]}
    outs = []
    for n, (i, head) in enumerate(units):
        top = jnp.max(reduce(jnp.maximum, tops[n]), axis=0, keepdims=True)
        following = units[n + 1] if n + 1 < len(units) else None
        if following is not None:
            query_part = part_of(following)
            tops[n + 1] = []
        mixed = None
        total = None
        steps = max(i + 1, following[0] + 1 if following else 0)
        for j in range(steps):
            if following is not None and j <= following[0]:
                tops[n + 1].append(score_tile(following, query_part, j, (n + 1) % 2))
            if j <= i:
                weights = jnp.exp(held[n % 2, pl.ds(j * block, block), :] - top)
                part = dot_nn(flipped[head][:, j * block:(j + 1) * block], weights.astype(jnp.bfloat16))
                mixed = part if mixed is None else mixed + part
        total = mixed[size:size + 1]
        outs.append(mixed[:size] / total)
        rows = pl.ds(i * block, block)
        total_ref[0, head:head + 1, rows] = top + jnp.log(total)
        if head == heads - 1:
            out_ref[rows, :] = jnp.concatenate(outs[-heads:], axis=0).T.astype(out_ref.dtype)


def attend(queries, keys, values, near, size, block):
    length, width = queries.shape
    lanes = 128
    heads = lanes // size
    groups = width // lanes
    column = pl.BlockSpec((length, lanes), lambda g: (0, g))
    head_rows = pl.BlockSpec((1, heads, block), lambda g: (g, 0, 0))
    return pl.pallas_call(
        partial(attend_kernel, block=block, size=size, scale=size ** -0.5),
        grid=(groups,),
        in_specs=[column, column, column, head_rows],
        out_specs=[column, pl.BlockSpec((1, heads, length), lambda g: (g, 0, 0))],
        out_shape=[jax.ShapeDtypeStruct((length, width), jnp.bfloat16), jax.ShapeDtypeStruct((groups, heads, length), jnp.float32)],
        scratch_shapes=[pltpu.VMEM((2, length, block), jnp.float32)],
        compiler_params=pltpu.CompilerParams(vmem_limit_bytes=62 << 20),
    )(queries, keys, values, near)


def attend_back_kernel(query_ref, key_ref, value_ref, grad_ref, out_ref, total_ref, near_ref, grads_ref, dist_ref, key_acc, value_acc, *, block, size, scale):
    length, lanes = query_ref.shape
    heads = lanes // size
    count = length // block
    flipped = key_ref[...].T
    tiles = [near_tiles(near_ref, head, block) for head in range(heads)]
    near_acc = [None] * heads
    far_acc = [None] * heads
    for i in range(count):
        rows = pl.ds(i * block, block)
        query_rows = query_ref[rows, :] * jnp.bfloat16(scale)
        grad_rows = grad_ref[rows, :]
        products = (grad_rows.astype(jnp.float32) * out_ref[rows, :].astype(jnp.float32)).T
        query_parts = [head_part(query_rows, head, size) for head in range(heads)]
        grad_parts = [head_part(grad_rows, head, size) for head in range(heads)]
        inner = [jnp.sum(products[head * size:(head + 1) * size], axis=0, keepdims=True) for head in range(heads)]
        query_stack = jnp.concatenate(query_parts, axis=0)
        grad_stack = jnp.concatenate(grad_parts, axis=0)
        query_grads = [None] * heads
        for j in range(i + 1):
            cols = pl.ds(j * block, block)
            weight_list = []
            score_list = []
            for head in range(heads):
                tile = dot_nt(key_ref[cols, :], query_parts[head])
                if j == i:
                    tile = tile + tiles[head][0]
                elif j == i - 1:
                    tile = tile + tiles[head][1]
                weights = jnp.exp(tile - total_ref[0, head:head + 1, rows])
                grads = dot_nt(value_ref[cols, :], grad_parts[head])
                score_grads = weights * (grads - inner[head])
                low = score_grads.astype(jnp.bfloat16)
                weight_list.append(weights.astype(jnp.bfloat16))
                score_list.append(low)
                part = dot_nn(flipped[head * size:(head + 1) * size, j * block:(j + 1) * block], low)
                query_grads[head] = part if query_grads[head] is None else query_grads[head] + part
                if j == i:
                    near_acc[head] = score_grads if near_acc[head] is None else near_acc[head] + score_grads
                else:
                    far = score_grads
                    if j == i - 1:
                        close = jnp.where(tiles[head][2], score_grads, 0.0)
                        near_acc[head] = near_acc[head] + close
                        far = score_grads - close
                    far = jnp.sum(far, axis=0, keepdims=True)
                    far_acc[head] = far if far_acc[head] is None else far_acc[head] + far
            value_part = dot_nn(jnp.concatenate(weight_list, axis=1), grad_stack)
            key_part = dot_nn(jnp.concatenate(score_list, axis=1), query_stack)
            if j == i:
                value_acc[cols, :] = value_part
                key_acc[cols, :] = key_part
            else:
                value_acc[cols, :] += value_part
                key_acc[cols, :] += key_part
        grads_ref[0, rows, :] = (jnp.concatenate(query_grads, axis=0) * scale).T.astype(grads_ref.dtype)
    grads_ref[1] = key_acc[...].astype(grads_ref.dtype)
    grads_ref[2] = value_acc[...].astype(grads_ref.dtype)
    for head in range(heads):
        dist_ref[0, head:head + 1, :] = diagonal_sums(near_acc[head])
        dist_ref[0, heads + head:heads + head + 1, :] = far_acc[head]


def attend_back(queries, keys, values, grads, outs, totals, near, size, block):
    length, width = queries.shape
    lanes = 128
    heads = lanes // size
    groups = width // lanes
    column = pl.BlockSpec((length, lanes), lambda g: (0, g))
    head_rows = pl.BlockSpec((1, heads, block), lambda g: (g, 0, 0))
    return pl.pallas_call(
        partial(attend_back_kernel, block=block, size=size, scale=size ** -0.5),
        grid=(groups,),
        in_specs=[column] * 5 + [pl.BlockSpec((1, heads, length), lambda g: (g, 0, 0)), head_rows],
        out_specs=[pl.BlockSpec((3, length, lanes), lambda g: (0, 0, g)), pl.BlockSpec((1, 2 * heads, block), lambda g: (g, 0, 0))],
        out_shape=[jax.ShapeDtypeStruct((3, length, width), jnp.bfloat16), jax.ShapeDtypeStruct((groups, 2 * heads, block), jnp.float32)],
        scratch_shapes=[pltpu.VMEM((length, lanes), jnp.float32)] * 2,
        compiler_params=pltpu.CompilerParams(vmem_limit_bytes=62 << 20),
    )(queries, keys, values, grads, outs, totals, near)


def reverse_bits(value, count):
    out = value * 0
    for level in range(count):
        out = out * 2 + (value >> level) % 2
    return out


def project_kernel(owner_ref, inputs_ref, gain_ref, *refs, eps):
    piece_refs, weight_refs, low_ref, out_refs = refs[:4], refs[-7:-4], refs[-4], refs[-3:]
    count, half, three, _ = piece_refs[0].shape
    piece = three // 3
    owners = 2 * count
    part = owners * piece
    @pl.when(pl.program_id(0) == 0)
    def _():
        me = owner_ref[0]
        for source in range(owners):
            apart = jnp.bitwise_xor(me, source)
            near = apart % 2 == 0
            place = apart // 2
            places = (place, reverse_bits(place, owners.bit_length() - 2))
            for group in range(2):
                for line in range(half):
                    block = jnp.where(near, piece_refs[2 * group][places[group], line], piece_refs[2 * group + 1][places[group], line])
                    start = (group * half + line) * part + source * piece
                    for index in range(3):
                        weight_refs[index][start:start + piece, :] = block[index * piece:(index + 1) * piece]
    rows = inputs_ref[...].astype(jnp.float32)
    inverse = lax.rsqrt(jnp.mean(rows * rows, axis=1, keepdims=True) + eps)
    low = (rows * inverse * gain_ref[...]).astype(jnp.bfloat16)
    low_ref[...] = low
    for weight_ref, out_ref in zip(weight_refs, out_refs):
        out_ref[...] = dot_nn(low, weight_ref[...]).astype(jnp.bfloat16)


def project(owner, inputs, gain, pieces, eps, after=(), block=512):
    tokens, width = inputs.shape
    rows = pl.BlockSpec((block, width), lambda i: (i, 0))
    whole = lambda shape: pl.BlockSpec(shape, lambda i: (0,) * len(shape))
    weight = jax.ShapeDtypeStruct((width, width), jnp.bfloat16)
    return pl.pallas_call(
        partial(project_kernel, eps=eps),
        grid=(tokens // block,),
        in_specs=[pl.BlockSpec(memory_space=pltpu.SMEM), rows, whole(gain.shape)] + [whole(piece.shape) for piece in pieces] + [pl.BlockSpec(memory_space=pl.ANY)] * len(after),
        out_specs=[whole(weight.shape)] * 3 + [rows] * 4,
        out_shape=[weight] * 3 + [jax.ShapeDtypeStruct((tokens, width), jnp.bfloat16)] * 4,
        compiler_params=pltpu.CompilerParams(vmem_limit_bytes=62 << 20),
    )(owner, inputs, gain, *pieces, *after)


def settle_kernel(mixed_ref, merge_ref, inputs_ref, gain_ref, router_ref, routes_ref, slots_ref, resid_ref, low_ref, gates_ref, out_ref, held, *, eps, settling):
    step = pl.program_id(0)
    block, picking = mixed_ref.shape[0], out_ref.shape[0]
    @pl.when(step < settling)
    def _():
        resid = inputs_ref[...].astype(jnp.float32) + dot_nn(mixed_ref[...], merge_ref[...])
        resid_ref[...] = resid
        inverse = lax.rsqrt(jnp.mean(resid * resid, axis=1, keepdims=True) + eps)
        low = (resid * inverse * gain_ref[...]).astype(jnp.bfloat16)
        low_ref[...] = low
        held[pl.ds(pl.multiple_of(step * block, block), block), :] = low
        logits = dot_nt(router_ref[...], low)
        expert = lax.broadcasted_iota(jnp.int32, logits.shape, 0)
        chosen = [jnp.sum(jnp.where(routes_ref[c:c + 1, :] == expert, logits, 0.0), axis=0, keepdims=True) for c in range(2)]
        top = jnp.maximum(chosen[0], chosen[1])
        powers = [jnp.exp(value - top) for value in chosen]
        total = powers[0] + powers[1]
        for c in range(2):
            gates_ref[c:c + 1, :] = powers[c] / total
    @pl.when(step >= settling)
    def _():
        tokens = held.shape[0]
        slot = lax.broadcasted_iota(jnp.int32, (picking, tokens), 0) + (step - settling) * picking
        hot = jnp.where((slot == slots_ref[0:1, :]) | (slot == slots_ref[1:2, :]), 1.0, 0.0)
        out_ref[...] = dot_nn(hot.astype(jnp.bfloat16), held[...]).astype(out_ref.dtype)


def settle(mixed, merge, inputs, gain, router, routes, slots, count, eps, block=512):
    tokens, width = inputs.shape
    picking = count // 2
    settling = tokens // block
    early = lambda i: jnp.minimum(i, settling - 1)
    rows = pl.BlockSpec((block, width), lambda i: (early(i), 0))
    whole = lambda shape: pl.BlockSpec(shape, lambda i: (0, 0))
    small = pl.BlockSpec((2, block), lambda i: (0, early(i)))
    return pl.pallas_call(
        partial(settle_kernel, eps=eps, settling=settling),
        grid=(settling + 2,),
        in_specs=[rows, whole(merge.shape), rows, whole(gain.shape), whole(router.shape), small, whole(slots.shape)],
        out_specs=[rows, rows, small, pl.BlockSpec((picking, width), lambda i: (jnp.maximum(i - settling, 0), 0))],
        out_shape=[jax.ShapeDtypeStruct((tokens, width), jnp.float32), jax.ShapeDtypeStruct((tokens, width), jnp.bfloat16), jax.ShapeDtypeStruct((2, tokens), jnp.float32), jax.ShapeDtypeStruct((count, width), jnp.bfloat16)],
        scratch_shapes=[pltpu.VMEM((tokens, width), jnp.bfloat16)],
        compiler_params=pltpu.CompilerParams(vmem_limit_bytes=62 << 20),
    )(mixed, merge, inputs, gain, router, routes, slots)


def finish_kernel(heads_ref, query_ref, key_ref, value_ref, gain_ref, inputs_ref, resid_grad_ref, out_ref, gain_grad_ref, *, eps):
    grads = dot_nt(heads_ref[0], query_ref[...]) + dot_nt(heads_ref[1], key_ref[...]) + dot_nt(heads_ref[2], value_ref[...])
    rows = inputs_ref[...].astype(jnp.float32)
    inverse = lax.rsqrt(jnp.mean(rows * rows, axis=1, keepdims=True) + eps)
    unit = rows * inverse
    @pl.when(pl.program_id(0) == 0)
    def _():
        gain_grad_ref[...] = jnp.zeros_like(gain_grad_ref)
    gain_grad_ref[...] += jnp.sum(grads * unit, axis=0, keepdims=True)
    scaled = grads * gain_ref[...]
    inner = jnp.mean(scaled * unit, axis=1, keepdims=True)
    out_ref[...] = resid_grad_ref[...] + inverse * (scaled - unit * inner)


def finish(head_grads, query, key, value, gain, inputs, resid_grad, eps, block=256):
    tokens, width = inputs.shape
    rows = pl.BlockSpec((block, width), lambda i: (i, 0))
    whole = lambda shape: pl.BlockSpec(shape, lambda i: (0, 0))
    return pl.pallas_call(
        partial(finish_kernel, eps=eps),
        grid=(tokens // block,),
        in_specs=[pl.BlockSpec((3, block, width), lambda i: (0, i, 0))] + [whole(query.shape)] * 3 + [whole(gain.shape), rows, rows],
        out_specs=[rows, whole((1, width))],
        out_shape=[jax.ShapeDtypeStruct((tokens, width), jnp.float32), jax.ShapeDtypeStruct((1, width), jnp.float32)],
        compiler_params=pltpu.CompilerParams(vmem_limit_bytes=62 << 20),
    )(head_grads, query, key, value, gain, inputs, resid_grad)


def weight_kernel(left_ref, mixed_ref, heads_ref, branch_ref, out_ref, turned, right):
    shards, part, _ = out_ref.shape
    step = pl.program_id(0)
    last = pl.num_programs(0) - 1
    @pl.when(step == 0)
    def _():
        turned[...] = left_ref[...].T
    @pl.when(step < last)
    def _():
        right[...] = heads_ref[...]
    @pl.when(step == last)
    def _():
        turned[...] = mixed_ref[...].T
        right[...] = branch_ref[...]
    for shard in range(shards):
        grad = dot_nn(turned[shard * part:(shard + 1) * part, :], right[...])
        out_ref[shard] = grad.astype(jnp.bfloat16)


def weight_grads(left, mixed, head_grads, branch, shards):
    count, tokens, width = head_grads.shape
    part = width // shards
    fixed = pl.BlockSpec((tokens, width), lambda i: (0, 0))
    return pl.pallas_call(
        weight_kernel,
        grid=(count + 1,),
        in_specs=[fixed, fixed, pl.BlockSpec((None, tokens, width), lambda i: (jnp.minimum(i, count - 1), 0, 0)), fixed],
        out_specs=pl.BlockSpec((shards, part, width), lambda i: (0, i, 0)),
        out_shape=jax.ShapeDtypeStruct((shards, (count + 1) * part, width), jnp.bfloat16),
        scratch_shapes=[pltpu.VMEM((width, tokens), jnp.bfloat16), pltpu.VMEM((tokens, width), jnp.bfloat16)],
        compiler_params=pltpu.CompilerParams(vmem_limit_bytes=62 << 20),
    )(left, mixed, head_grads, branch)


def widen_first_kernel(rows_ref, out_ref):
    out_ref[...] = rows_ref[...].astype(jnp.float32)


def widen_first(rows):
    count, width = rows.shape
    half = pl.BlockSpec((count // 2, width), lambda i: (i, 0))
    return pl.pallas_call(
        widen_first_kernel,
        grid=(2,),
        in_specs=[half],
        out_specs=half,
        out_shape=jax.ShapeDtypeStruct((2 * count, width), jnp.float32),
        compiler_params=pltpu.CompilerParams(vmem_limit_bytes=62 << 20),
    )(rows)


def widen_rest_kernel(rows_ref, into_ref, up_ref, down_ref):
    del into_ref
    wide = rows_ref[...].astype(jnp.float32)
    step = pl.program_id(0)
    @pl.when(step < 2)
    def _():
        up_ref[...] = wide
    @pl.when(step >= 2)
    def _():
        down_ref[...] = wide


def widen_rest(rows, into):
    count, width = rows.shape[0] // 3, rows.shape[1]
    half = lambda place: pl.BlockSpec((count, width), lambda i: (place(i), 0))
    wide = jax.ShapeDtypeStruct((2 * count, width), jnp.float32)
    return pl.pallas_call(
        widen_rest_kernel,
        grid=(3,),
        in_specs=[half(lambda i: i), pl.BlockSpec(memory_space=pl.ANY)],
        out_specs=[half(lambda i: jnp.minimum(i, 1)), half(lambda i: 1)],
        out_shape=[wide, wide],
        input_output_aliases={1: 1},
        compiler_params=pltpu.CompilerParams(vmem_limit_bytes=62 << 20),
    )(rows, into)


def smalls_kernel(small_ref, near_ref, gain_one_ref, gain_two_ref, router_ref, table_ref, *, part, heads, router_at):
    shards, _, width = small_ref.shape
    group = table_ref.shape[1]
    lanes = -(-part // 128) * 128
    row = lax.broadcasted_iota(jnp.int32, (lanes, width), 0)
    column = lax.broadcasted_iota(jnp.int32, (lanes, width), 1)
    wide = None
    for shard in range(shards):
        place = jnp.where((column == row + shard * part) & (row < part), 1.0, 0.0).astype(jnp.bfloat16)
        rows = dot_nn(small_ref[shard][:, :lanes], place)
        wide = rows if wide is None else wide + rows
        near = dot_nn(small_ref[shard][:8, :128], near_ref[...])
        for head in range(heads):
            at = shard * heads + head
            table_ref[at // group, at % group:at % group + 1, :] = near[2 + head:3 + head, :]
    gain_one_ref[...] = wide[0:1]
    gain_two_ref[...] = wide[1:2]
    router_ref[...] = wide[router_at:router_at + router_ref.shape[0]].astype(jnp.bfloat16)


def spread_smalls(small, near, part, heads, group, experts, router_at):
    shards, _, width = small.shape
    f32 = jnp.float32
    return pl.pallas_call(
        partial(smalls_kernel, part=part, heads=heads, router_at=router_at),
        out_shape=[
            jax.ShapeDtypeStruct((1, width), f32),
            jax.ShapeDtypeStruct((1, width), f32),
            jax.ShapeDtypeStruct((experts, width), jnp.bfloat16),
            jax.ShapeDtypeStruct((shards * heads // group, group, near.shape[1]), f32),
        ],
    )(small, near)


OWNER = "expert"
LINE = "shard"


def exchange(rows, bit):
    count = lax.axis_size(OWNER)
    return lax.ppermute(rows, OWNER, [(i, i ^ bit) for i in range(count)])


def shift(rows, step):
    count = lax.axis_size(LINE)
    return lax.ppermute(rows, LINE, [(i, (i + step) % count) for i in range(count)])


def gather_line(rows):
    count = lax.axis_size(LINE)
    me = lax.axis_index(LINE)
    out = jnp.zeros((count,) + rows.shape, rows.dtype)
    out = lax.dynamic_update_index_in_dim(out, rows, me, 0)
    for step in range(1, count):
        got = shift(rows, step)
        out = lax.dynamic_update_index_in_dim(out, got, (me - step) % count, 0)
    return out


def add_low(left, right):
    return (left.astype(jnp.float32) + right.astype(jnp.float32)).astype(jnp.bfloat16)


def side(bit):
    return (lax.axis_index(OWNER) // bit) % 2


def halve(stack, bit):
    half = stack.shape[1] // 2
    keep = lax.dynamic_slice_in_dim(stack, side(bit) * half, half, 1)
    send = lax.dynamic_slice_in_dim(stack, (1 - side(bit)) * half, half, 1)
    got = exchange(send, bit)
    return add_low(keep, got)


def line_sum(stack):
    count = lax.axis_size(LINE)
    place = lax.axis_index(LINE)
    total = lax.dynamic_index_in_dim(stack, place, 0, False).astype(jnp.float32)
    for step in range(1, count):
        send = lax.dynamic_index_in_dim(stack, (place + step) % count, 0, False)
        total = total + shift(send, step).astype(jnp.float32)
    return total.astype(jnp.bfloat16)


def grow(piece, bit):
    other = exchange(piece, bit)
    return jnp.where(
        side(bit) == 0, jnp.concatenate([piece, other]), jnp.concatenate([other, piece])
    )


def reduce_rows(stack, bits):
    unit = 8 << (len(bits) - 1)
    cut = -(-stack.shape[1] // (2 * unit)) * unit
    parts = [stack[:, :cut], stack[:, cut:]]
    orders = [bits[1:], bits[:0:-1]]
    for level in range(len(bits) - 1):
        parts = [halve(part, order[level]) for part, order in zip(parts, orders)]
    low = parts[0].shape[1]
    piece = line_sum(jnp.concatenate(parts, axis=1))
    parts = [piece[:low], piece[low:]]
    for level in reversed(range(len(bits) - 1)):
        parts = [grow(part, order[level]) for part, order in zip(parts, orders)]
    return grow(jnp.concatenate(parts), bits[0])


def scatter_sum(grads):
    shards, rows, width = grads.shape
    grads = grads.reshape(shards * rows, width)
    return lax.psum_scatter(grads, LINE, scatter_dimension=0, tiled=True)


def share_rows(rows):
    return lax.all_to_all(rows, OWNER, 0, 0, tiled=True)


def share_large(rows):
    return pltpu.with_memory_space_constraint(share_rows(rows), pltpu.HBM)


def local(
    inputs,
    norm_gain,
    query_weight,
    key_weight,
    value_weight,
    merge_weight,
    bias_table,
    expert_gain,
    router_weight,
    up_weight,
    down_weight,
    routes,
    cotangent,
):
    f32, bf16 = jnp.float32, jnp.bfloat16
    tokens, width = inputs.shape
    owners = lax.axis_size(OWNER)
    shards = lax.axis_size(LINE)
    me = lax.axis_index(OWNER)
    part = query_weight.shape[0]
    piece = part // owners
    local_heads = bias_table.shape[1]
    heads = local_heads * shards
    size = width // heads
    experts = router_weight.shape[1]
    local_count, _, hidden = up_weight.shape
    capacity = (5 * tokens * routes.shape[1] + 4 * experts - 1) // (4 * experts)
    capacity = -(-capacity // 16) * 16
    rows = owners * capacity
    assert local_count == 2 and hidden // shards == width
    early = max(16, 2 * capacity // 5 // 16 * 16)

    router_at = 2 + local_heads + (-(2 + local_heads)) % 8

    def widen(block):
        return jnp.pad(block, ((0, 0), (0, width - block.shape[1])))

    def pack(gain_one, gain_two, table, router):
        head = jnp.concatenate([gain_one, gain_two], axis=0)
        gap = jnp.zeros((router_at - 2 - local_heads, width), bf16)
        return jnp.concatenate([widen(head), widen(table), gap, widen(router)], axis=0)

    small = pack(norm_gain[None], expert_gain[None], bias_table.T, router_weight.T)
    slices = [
        lax.dynamic_slice_in_dim(weight, me * piece, piece, 0)
        for weight in (query_weight, key_weight, value_weight)
    ]
    lined = gather_line(jnp.concatenate(slices + [small]))
    small_full = lined[:, 3 * piece :]
    bits = [1 << level for level in range(owners.bit_length() - 1)]
    pieces = []
    for index, order in enumerate((bits[1:], bits[:0:-1])):
        held = lined[index * shards // 2 : (index + 1) * shards // 2, : 3 * piece][None]
        for bit in order:
            got = exchange(held, bit)
            held = jnp.concatenate([held, got])
        pieces += [held, exchange(held, bits[0])]
    merge_full = lax.all_gather(merge_weight, LINE, axis=0, tiled=True)

    block = 256
    hot = bucket_hot(tokens)
    assert hot[block:, -1].all()
    near_hot = np.zeros((128, block), np.float32)
    near_hot[:BUCKETS] = (hot[:block] - hot[-1:]).T
    group = 128 // size
    gain_one, gain_two, router_full, near = spread_smalls(
        small_full, jnp.asarray(near_hot, bf16), part, local_heads, group, experts, router_at
    )

    routes_line = routes.T
    slots, routes_float = find_slots(routes_line, experts, local_count, owners, capacity)
    cot_rows = dispatch_first(
        slots, routes_float, cotangent, owners, capacity, early
    )

    owner = me.astype(jnp.int32).reshape(1)
    query_full, key_full, value_full, low_one, queries, keys, values = project(
        owner, inputs, gain_one, pieces, epsilon, after=(near, router_full)
    )
    cot_in = share_large(cot_rows)
    attended, totals = attend(queries, keys, values, near, size, block)
    resid, low_two, gates, send = settle(
        attended, merge_full, inputs, gain_two, router_full, routes_line, slots, rows, epsilon
    )

    rows_in = share_large(send.reshape(owners, capacity, width))
    joint = dispatch_both(
        slots, low_two, cotangent, rows, owners, capacity, early
    )
    joint_in = share_large(joint)
    act, pre, first_down, grad_in = expert_first(
        owner, rows_in, [cot_in], [(0, 0, capacity)], router_full, up_weight, 0,
        local_count, capacity, shards,
    )
    first_sum = scatter_sum(first_down)
    first_made, pair = expert_second(rows_in, grad_in, act, pre, up_weight, down_weight, 0, owners, shards, 3 * width)
    late = capacity - early
    act, pre, pair, grad_in = expert_first(
        owner, joint_in, [cot_in, joint_in], [(0, capacity, early), (1, capacity, late)],
        router_full, up_weight, 1, local_count, capacity, shards, into=pair,
    )
    low, pair = expert_slope(joint_in, grad_in, pre, down_weight, 1, shards, pair, 1)
    pair_sum = scatter_sum(pair)
    second_made = expert_last(act, low, up_weight, down_weight, 1, owners, shards)
    returned = share_rows(first_made)
    result, inner, part_grads = combine_part(slots, gates, resid, cotangent, returned)
    returned = share_rows(second_made)
    output, logit_grad = combine_out(
        slots, routes_line, gates, result, inner, cotangent, returned
    )
    router_wide = jnp.pad(router_full, ((0, 128 - experts), (0, 0)))
    resid_grad, branch, mixed_grad, gain_grad = combine_back(
        slots, logit_grad, router_wide, gain_two, resid, cotangent, merge_full,
        part_grads, returned, epsilon
    )
    router_grad = jnp.einsum("te,ti->ei", logit_grad, low_two, preferred_element_type=f32)
    head_grads, distances = attend_back(
        queries, keys, values, mixed_grad, attended, totals, near, size, block
    )
    close_sums = distances[:, :group].reshape(heads, block)
    far_sums = jnp.sum(distances[:, group:].reshape(heads, block), axis=1)
    table_grad = jnp.dot(close_sums, jnp.asarray(hot[:block]), precision=lax.Precision.HIGHEST)
    table_grad = table_grad + far_sums[:, None] * jnp.asarray(hot[-1:])
    sums = weight_grads(low_one, attended, head_grads, branch, shards)
    sums = halve(sums, bits[0])
    input_gradient, norm_grad = finish(
        head_grads, query_full, key_full, value_full, gain_one, inputs, resid_grad, epsilon
    )
    small_grad = jax.vmap(pack)(
        norm_grad.reshape(shards, 1, part).astype(bf16),
        gain_grad.reshape(shards, 1, part).astype(bf16),
        table_grad.reshape(shards, local_heads, BUCKETS).astype(bf16),
        router_grad[:experts].reshape(experts, shards, part).transpose(1, 0, 2).astype(bf16),
    )
    spare = -small_grad.shape[1] % (8 * owners)
    small_grad = halve(jnp.pad(small_grad, ((0, 0), (0, spare), (0, 0))), bits[0])
    kept = sums.shape[1]
    sums = reduce_rows(jnp.concatenate([sums, small_grad], axis=1), bits)
    half = sums.shape[0] // 2
    weights = jnp.concatenate([sums[:kept], sums[half : half + kept]]).astype(f32)
    small_sum = jnp.concatenate([sums[kept:half], sums[half + kept :]]).astype(f32)
    up_sum, down_sum = widen_rest(pair_sum, widen_first(first_sum))
    return (
        output,
        input_gradient,
        small_sum[0, :part],
        weights[:part],
        weights[part : 2 * part],
        weights[2 * part : 3 * part],
        weights[3 * part :],
        small_sum[2 : 2 + local_heads, :BUCKETS].T,
        small_sum[1, :part],
        small_sum[router_at : router_at + experts, :part].T,
        up_sum.reshape(local_count, width, width),
        down_sum.reshape(local_count, width, width),
    )


def solution(mesh):
    in_specs = (
        P((OWNER, LINE), None),
        P(LINE),
        P(LINE, None),
        P(LINE, None),
        P(LINE, None),
        P(LINE, None),
        P(None, LINE),
        P(LINE),
        P(LINE, None),
        P(OWNER, None, None),
        P(OWNER, None, None),
        P((OWNER, LINE), None),
        P((OWNER, LINE), None),
    )
    out_specs = (
        P((OWNER, LINE), None),
        P((OWNER, LINE), None),
        P(LINE),
        P(LINE, None),
        P(LINE, None),
        P(LINE, None),
        P(LINE, None),
        P(None, LINE),
        P(LINE),
        P(LINE, None),
        P(OWNER, None, LINE),
        P(OWNER, LINE, None),
    )

    return jax.shard_map(local, mesh=mesh, in_specs=in_specs, out_specs=out_specs, check_vma=False)
```

```python
from functools import partial, reduce

import jax
import jax.numpy as jnp
import numpy as np
from jax import lax
from jax.experimental import pallas as pl
from jax.experimental.pallas import tpu as pltpu
from jax.sharding import PartitionSpec as P


BUCKETS = 32
MAX_DIST = 128


epsilon = 1e-06
masked_score = -1e30


def bucket_hot(length):
    distance = np.arange(length)
    half_count = BUCKETS // 2
    clipped = np.maximum(distance, half_count)
    spread = np.log(clipped / half_count) / np.log(MAX_DIST / half_count) * (BUCKETS - half_count)
    far_bucket = np.minimum(half_count + np.floor(spread).astype(np.int32), BUCKETS - 1)
    bucket = np.where(distance < half_count, distance, far_bucket)
    return (bucket[:, None] == np.arange(BUCKETS)[None, :]).astype(np.float32)


def dot_nt(a, b):
    return lax.dot_general(a, b, (((1,), (1,)), ((), ())), preferred_element_type=jnp.float32)


def dot_nn(a, b):
    return lax.dot_general(a, b, (((1,), (0,)), ((), ())), preferred_element_type=jnp.float32)


def dot_tn(a, b):
    return lax.dot_general(a, b, (((0,), (0,)), ((), ())), preferred_element_type=jnp.float32)


def slot_kernel(routes_ref, slots_ref, float_ref, *, experts, local_count, owners, capacity):
    tokens = routes_ref.shape[1]
    expert = lax.broadcasted_iota(jnp.int32, (experts, tokens), 0)
    hits = [routes_ref[c:c + 1, :] == expert for c in range(2)]
    hot = jnp.where(hits[0] | hits[1], 1.0, 0.0).astype(jnp.bfloat16)
    earlier = lax.broadcasted_iota(jnp.int32, (tokens, tokens), 0)
    later = lax.broadcasted_iota(jnp.int32, (tokens, tokens), 1)
    before = jnp.where(earlier < later, 1.0, 0.0).astype(jnp.bfloat16)
    counts = dot_nn(hot, before)
    column = lax.broadcasted_iota(jnp.int32, (experts, 1), 0)
    base = (column % local_count * owners + column // local_count) * capacity
    counts = counts + base.astype(jnp.float32)
    for c in range(2):
        slot = jnp.sum(jnp.where(hits[c], counts, 0.0), axis=0, keepdims=True)
        slots_ref[c:c + 1, :] = slot.astype(jnp.int32)
    float_ref[...] = routes_ref[...].astype(jnp.float32)


def find_slots(routes, experts, local_count, owners, capacity):
    return pl.pallas_call(
        partial(slot_kernel, experts=experts, local_count=local_count, owners=owners, capacity=capacity),
        out_shape=[jax.ShapeDtypeStruct(routes.shape, jnp.int32), jax.ShapeDtypeStruct(routes.shape, jnp.float32)],
    )(routes)


def dispatch_both_kernel(slots_ref, rows_ref, cot_ref, *refs, start, capacity, early):
    out_ref = refs[-1]
    block, tokens = capacity, rows_ref.shape[0]
    slot = lax.broadcasted_iota(jnp.int32, (block, tokens), 0) + (pl.program_id(0) * block + start)
    hot = jnp.where((slot == slots_ref[0:1, :]) | (slot == slots_ref[1:2, :]), 1.0, 0.0)
    hot = hot.astype(jnp.bfloat16)
    out_ref[0, :capacity] = dot_nn(hot, rows_ref[...]).astype(out_ref.dtype)
    out_ref[0, capacity:] = dot_nn(hot[early:], cot_ref[...]).astype(out_ref.dtype)


def dispatch_both(slots, rows, cot, start, owners, capacity, early, after=()):
    width = rows.shape[1]
    total = 2 * capacity - early
    whole = lambda shape: pl.BlockSpec(shape, lambda i: (0, 0))
    return pl.pallas_call(
        partial(dispatch_both_kernel, start=start, capacity=capacity, early=early),
        grid=(owners,),
        in_specs=[whole(slots.shape), whole(rows.shape), whole(cot.shape)] + [pl.BlockSpec(memory_space=pl.ANY)] * len(after),
        out_specs=pl.BlockSpec((1, total, width), lambda i: (i, 0, 0)),
        out_shape=jax.ShapeDtypeStruct((owners, total, width), rows.dtype),
        compiler_params=pltpu.CompilerParams(vmem_limit_bytes=62 << 20),
    )(slots, rows, cot, *after)


def dispatch_first_kernel(slots_ref, routes_ref, rows_ref, out_ref, other_ref, *, owners, capacity):
    block, tokens = other_ref.shape[2], rows_ref.shape[0]
    row = lax.broadcasted_iota(jnp.int32, (block, tokens), 0)
    slot = row + pl.program_id(0) * capacity
    slot = slot + jnp.where(row >= capacity, (owners - 1) * capacity, 0)
    hits = [slot == slots_ref[c:c + 1, :] for c in range(2)]
    hot = jnp.where(hits[0] | hits[1], 1.0, 0.0)[:out_ref.shape[1]]
    out_ref[0] = dot_nn(hot.astype(jnp.bfloat16), rows_ref[...]).astype(out_ref.dtype)
    other = jnp.where(hits[0], routes_ref[1:2, :], jnp.where(hits[1], routes_ref[0:1, :], 0.0))
    column = jnp.sum(other, axis=1, keepdims=True)
    other_ref[0] = jnp.broadcast_to(column, (block, 128)).T[0:1, :]


def dispatch_first(slots, routes, rows, owners, capacity, early):
    width = rows.shape[1]
    total = capacity + early
    whole = lambda shape: pl.BlockSpec(shape, lambda i: (0, 0))
    return pl.pallas_call(
        partial(dispatch_first_kernel, owners=owners, capacity=capacity),
        grid=(owners,),
        in_specs=[whole(slots.shape), whole(routes.shape), whole(rows.shape)],
        out_specs=[pl.BlockSpec((1, total, width), lambda i: (i, 0, 0)), pl.BlockSpec((1, 1, 2 * capacity), lambda i: (i, 0, 0))],
        out_shape=[jax.ShapeDtypeStruct((owners, total, width), rows.dtype), jax.ShapeDtypeStruct((owners, 1, 2 * capacity), jnp.float32)],
    )(slots, routes, rows)


def gelu_half(v):
    c = np.float32(np.sqrt(2.0 / np.pi))
    square = v * v
    half = 0.5 * jnp.tanh(v * (np.float32(0.044715) * c * square + c)) + 0.5
    return half, square


def gelu_slope(v):
    c = np.float32(np.sqrt(2.0 / np.pi))
    half, square = gelu_half(v)
    return half + v * half * (1.0 - half) * (np.float32(6.0 * 0.044715) * c * square + 2.0 * c)


def arrived_spec(arrived, used=None):
    owners, count, width = arrived.shape
    return pl.BlockSpec((owners, used or count, width), lambda i: (0, 0, 0))


def first_kernel(owner_ref, rows_ref, other_ref, router_ref, up_ref, *refs, index, local_count, capacity, pieces):
    act_ref, pre_ref, down_grad_ref, grad_ref = refs[-4:]
    owners, _, width = rows_ref.shape
    rows = owners * capacity
    chunk = rows // 2
    @pl.when(pl.program_id(0) == 0)
    def _():
        logits = dot_nt(router_ref[...], rows_ref[:, :capacity].reshape(rows, width))
        expert = lax.broadcasted_iota(jnp.int32, logits.shape, 0)
        mine = owner_ref[0] * local_count + index
        own = jnp.sum(jnp.where(expert == mine, logits, 0.0), axis=0, keepdims=True)
        other = other_ref[...].astype(jnp.int32)
        other = jnp.sum(jnp.where(expert == other, logits, 0.0), axis=0, keepdims=True)
        top = jnp.maximum(own, other)
        own = jnp.exp(own - top)
        gate = own / (own + jnp.exp(other - top))
        column = jnp.broadcast_to(gate, (128, rows)).T
        for start in range(0, width, 128):
            parts = [refs[place][:, low:low + size, start:start + 128] for place, low, size in pieces]
            part = parts[0] if len(parts) == 1 else jnp.concatenate(parts, axis=1)
            part = part.reshape(rows, 128).astype(jnp.float32) * column
            grad_ref[:, start:start + 128] = part.astype(jnp.bfloat16)
    up = up_ref[0]
    for start in range(0, rows, chunk):
        part = rows_ref[start // capacity:(start + chunk) // capacity, :capacity].reshape(chunk, width)
        pre = dot_nn(part, up)
        half, _ = gelu_half(pre)
        act_ref[start:start + chunk, :] = (pre * half).astype(jnp.bfloat16)
        pre_ref[start:start + chunk, :] = pre.astype(jnp.bfloat16)
    down_grad_ref[0] = dot_tn(act_ref[...], grad_ref[...]).astype(jnp.bfloat16)


def expert_first(owner, rows_in, cots, pieces, other, router, up, index, local_count, capacity, shards, into=None):
    owners, _, width = rows_in.shape
    rows = owners * capacity
    hidden = up.shape[2]
    tile = hidden // shards
    fixed = pl.BlockSpec((rows, width), lambda i: (0, 0))
    column = pl.BlockSpec((rows, tile), lambda i: (0, i))
    operands = [owner, rows_in, other, router, up, *cots]
    place, aliases = 0, {}
    grad_shape = jax.ShapeDtypeStruct((shards, tile, width), jnp.bfloat16)
    if into is not None:
        aliases = {len(operands): 2}
        operands.append(into)
        place, grad_shape = 2, jax.ShapeDtypeStruct(into.shape, into.dtype)
    return pl.pallas_call(
        partial(first_kernel, index=index, local_count=local_count, capacity=capacity, pieces=pieces),
        grid=(shards,),
        in_specs=[
            pl.BlockSpec(memory_space=pltpu.SMEM),
            arrived_spec(rows_in, capacity),
            pl.BlockSpec((1, rows), lambda i: (0, 0)),
            pl.BlockSpec(router.shape, lambda i: (0, 0)),
            pl.BlockSpec((1, width, tile), lambda i: (index, 0, i)),
        ]
        + [arrived_spec(cot, low + size) for cot, (_, low, size) in zip(cots, pieces)]
        + [pl.BlockSpec(memory_space=pl.ANY)] * (into is not None),
        out_specs=[column, column, pl.BlockSpec((1, tile, width), lambda i: (i, place, 0)), fixed],
        out_shape=[jax.ShapeDtypeStruct((rows, hidden), jnp.bfloat16)] * 2 + [grad_shape, jax.ShapeDtypeStruct((rows, width), jnp.bfloat16)],
        input_output_aliases=aliases,
        compiler_params=pltpu.CompilerParams(vmem_limit_bytes=62 << 20),
    )(*operands)


def second_kernel(rows_ref, grad_ref, act_ref, pre_ref, up_ref, down_ref, *refs):
    made_ref, up_grad_ref, turned, made_acc, back_acc = refs[-5:]
    step = pl.program_id(0)
    owners, _, capacity, width = made_ref.shape
    @pl.when(step == 0)
    def _():
        rows, width = grad_ref.shape
        owners = rows_ref.shape[0]
        turned[...] = rows_ref[:, :rows // owners].reshape(rows, width).T
    up = up_ref[0]
    down = down_ref[0]
    grads = dot_nt(grad_ref[...], down)
    low = (gelu_slope(pre_ref[...].astype(jnp.float32)) * grads).astype(jnp.bfloat16)
    up_grad_ref[0] = dot_nn(turned[...], low).astype(jnp.bfloat16)
    back = dot_nt(low, up)
    made = dot_nn(act_ref[...], down)
    last = pl.num_programs(0) - 1
    @pl.when(step == 0)
    def _():
        made_acc[...] = made
        back_acc[...] = back
    @pl.when((step > 0) & (step < last))
    def _():
        made_acc[...] += made
        back_acc[...] += back
    @pl.when(step == last)
    def _():
        made_ref[:, 0] = (made_acc[...] + made).astype(jnp.bfloat16).reshape(owners, capacity, width)
        made_ref[:, 1] = (back_acc[...] + back).astype(jnp.bfloat16).reshape(owners, capacity, width)


def expert_second(rows_in, grad, act, pre, up, down, index, owners, shards, wide, after=()):
    rows, width = grad.shape
    hidden = up.shape[2]
    tile = hidden // shards
    fixed = pl.BlockSpec((rows, width), lambda i: (0, 0))
    column = pl.BlockSpec((rows, tile), lambda i: (0, i))
    made_shape = (owners, 2, rows // owners, width)
    return pl.pallas_call(
        second_kernel,
        grid=(shards,),
        in_specs=[arrived_spec(rows_in, rows // rows_in.shape[0]), fixed, column, column, pl.BlockSpec((1, width, tile), lambda i: (index, 0, i)), pl.BlockSpec((1, tile, width), lambda i: (index, i, 0))]
        + [pl.BlockSpec(memory_space=pl.ANY)] * len(after),
        out_specs=[pl.BlockSpec(made_shape, lambda i: (0, 0, 0, 0)), pl.BlockSpec((1, width, tile), lambda i: (i, 0, 0))],
        out_shape=[jax.ShapeDtypeStruct(made_shape, jnp.bfloat16), jax.ShapeDtypeStruct((shards, wide, tile), jnp.bfloat16)],
        scratch_shapes=[pltpu.VMEM((width, rows), jnp.bfloat16), pltpu.VMEM((rows, width), jnp.float32), pltpu.VMEM((rows, width), jnp.float32)],
        compiler_params=pltpu.CompilerParams(vmem_limit_bytes=62 << 20),
    )(rows_in, grad, act, pre, up, down, *after)


def slope_kernel(rows_ref, grad_ref, pre_ref, down_ref, into_ref, low_ref, up_grad_ref, turned):
    del into_ref
    @pl.when(pl.program_id(0) == 0)
    def _():
        rows, width = grad_ref.shape
        owners = rows_ref.shape[0]
        turned[...] = rows_ref[:, :rows // owners].reshape(rows, width).T
    grads = dot_nt(grad_ref[...], down_ref[0])
    low = (gelu_slope(pre_ref[...].astype(jnp.float32)) * grads).astype(jnp.bfloat16)
    low_ref[...] = low
    up_grad_ref[0] = dot_nn(turned[...], low).astype(jnp.bfloat16)


def expert_slope(rows_in, grad, pre, down, index, shards, into, place):
    rows, width = grad.shape
    hidden = pre.shape[1]
    tile = hidden // shards
    fixed = pl.BlockSpec((rows, width), lambda i: (0, 0))
    column = pl.BlockSpec((rows, tile), lambda i: (0, i))
    return pl.pallas_call(
        slope_kernel,
        grid=(shards,),
        in_specs=[arrived_spec(rows_in, rows // rows_in.shape[0]), fixed, column, pl.BlockSpec((1, tile, width), lambda i: (index, i, 0)), pl.BlockSpec(memory_space=pl.ANY)],
        out_specs=[column, pl.BlockSpec((1, width, tile), lambda i: (i, place, 0))],
        out_shape=[jax.ShapeDtypeStruct((rows, hidden), jnp.bfloat16), jax.ShapeDtypeStruct(into.shape, into.dtype)],
        input_output_aliases={4: 1},
        scratch_shapes=[pltpu.VMEM((width, rows), jnp.bfloat16)],
        compiler_params=pltpu.CompilerParams(vmem_limit_bytes=62 << 20),
    )(rows_in, grad, pre, down, into)


def last_kernel(act_ref, low_ref, up_ref, down_ref, made_ref, made_acc, back_acc):
    step = pl.program_id(0)
    owners, _, capacity, width = made_ref.shape
    back = dot_nt(low_ref[...], up_ref[0])
    made = dot_nn(act_ref[...], down_ref[0])
    last = pl.num_programs(0) - 1
    @pl.when(step == 0)
    def _():
        made_acc[...] = made
        back_acc[...] = back
    @pl.when((step > 0) & (step < last))
    def _():
        made_acc[...] += made
        back_acc[...] += back
    @pl.when(step == last)
    def _():
        made_ref[:, 0] = (made_acc[...] + made).astype(jnp.bfloat16).reshape(owners, capacity, width)
        made_ref[:, 1] = (back_acc[...] + back).astype(jnp.bfloat16).reshape(owners, capacity, width)


def expert_last(act, low, up, down, index, owners, shards):
    rows, hidden = act.shape
    width = up.shape[1]
    tile = hidden // shards
    column = pl.BlockSpec((rows, tile), lambda i: (0, i))
    made_shape = (owners, 2, rows // owners, width)
    return pl.pallas_call(
        last_kernel,
        grid=(shards,),
        in_specs=[column, column, pl.BlockSpec((1, width, tile), lambda i: (index, 0, i)), pl.BlockSpec((1, tile, width), lambda i: (index, i, 0))],
        out_specs=pl.BlockSpec(made_shape, lambda i: (0, 0, 0, 0)),
        out_shape=jax.ShapeDtypeStruct(made_shape, jnp.bfloat16),
        scratch_shapes=[pltpu.VMEM((rows, width), jnp.float32), pltpu.VMEM((rows, width), jnp.float32)],
        compiler_params=pltpu.CompilerParams(vmem_limit_bytes=62 << 20),
    )(act, low, up, down)


def spread(row, block):
    return jnp.broadcast_to(row, (128, block)).T


def pick(slots, lane, back_refs, first=0):
    picked = None
    for index, back_ref in enumerate(back_refs, first):
        owners, capacity, width = back_ref.shape
        half = owners * capacity
        hots = []
        for start in range(index * half, (index + 1) * half, 128):
            hit = reduce(jnp.logical_or, [slot == lane + start for slot in slots])
            hots.append(jnp.where(hit, 1.0, 0.0).astype(jnp.bfloat16))
        part = dot_nn(jnp.concatenate(hots, axis=1), back_ref[...].reshape(half, width))
        picked = part if picked is None else picked + part
    return picked


def part_kernel(slots_ref, gates_ref, resid_ref, cot_ref, made_ref, back_ref, result_ref, inner_ref, grads_ref):
    block = result_ref.shape[0]
    lane = lax.broadcasted_iota(jnp.int32, (block, 128), 1)
    cot = cot_ref[...].astype(jnp.float32)
    result = resid_ref[...]
    inner = jnp.zeros((block, 128), jnp.float32)
    slots = [spread(slots_ref[c:c + 1, :], block) for c in range(2)]
    for c in range(2):
        picked = pick([slots[c]], lane, [made_ref])
        result = result + spread(gates_ref[c:c + 1, :], block)[:, 0:1] * picked
        inner = inner + jnp.where(lane == c, jnp.sum(cot * picked, axis=1, keepdims=True), 0.0)
    result_ref[...] = result
    inner_ref[...] = inner
    grads_ref[...] = pick(slots, lane, [back_ref])


def combine_part(slots, gates, resid, cot, returned, block=256):
    tokens, width = resid.shape
    small = pl.BlockSpec((2, block), lambda i: (0, i))
    rows = pl.BlockSpec((block, width), lambda i: (i, 0))
    wide = jax.ShapeDtypeStruct((tokens, width), jnp.float32)
    return pl.pallas_call(
        part_kernel,
        grid=(tokens // block,),
        in_specs=[small, small, rows, rows, returned_spec(returned, 0), returned_spec(returned, 1)],
        out_specs=[rows, pl.BlockSpec((block, 128), lambda i: (i, 0)), rows],
        out_shape=[wide, jax.ShapeDtypeStruct((tokens, 128), jnp.float32), wide],
        compiler_params=pltpu.CompilerParams(vmem_limit_bytes=62 << 20),
    )(slots, gates, resid, cot, returned, returned)


def out_kernel(slots_ref, routes_ref, gates_ref, result_ref, inner_ref, cot_ref, made_ref, out_ref, logit_ref):
    block = out_ref.shape[0]
    lane = lax.broadcasted_iota(jnp.int32, (block, 128), 1)
    cot = cot_ref[...].astype(jnp.float32)
    result = result_ref[...]
    gates, inner = [], []
    for c in range(2):
        slot = spread(slots_ref[c:c + 1, :], block)
        gate = spread(gates_ref[c:c + 1, :], block)[:, 0:1]
        picked = pick([slot], lane, [made_ref], 1)
        result = result + gate * picked
        gates.append(gate)
        inner.append(inner_ref[:, c:c + 1] + jnp.sum(cot * picked, axis=1, keepdims=True))
    out_ref[...] = result.astype(out_ref.dtype)
    middle = gates[0] * inner[0] + gates[1] * inner[1]
    logit = jnp.zeros((block, 128), jnp.float32)
    for c in range(2):
        route = spread(routes_ref[c:c + 1, :], block)
        logit = logit + jnp.where(route == lane, gates[c] * (inner[c] - middle), 0.0)
    logit_ref[...] = logit.astype(jnp.bfloat16)


def returned_spec(returned, which):
    owners, _, capacity, width = returned.shape
    return pl.BlockSpec((owners, None, capacity, width), lambda i: (0, which, 0, 0))


def combine_out(slots, routes, gates, result, inner, cot, returned, block=256):
    tokens, width = result.shape
    small = pl.BlockSpec((2, block), lambda i: (0, i))
    rows = pl.BlockSpec((block, width), lambda i: (i, 0))
    return pl.pallas_call(
        out_kernel,
        grid=(tokens // block,),
        in_specs=[small, small, small, rows, pl.BlockSpec((block, 128), lambda i: (i, 0)), rows, returned_spec(returned, 0)],
        out_specs=[rows, pl.BlockSpec((block, 128), lambda i: (i, 0))],
        out_shape=[jax.ShapeDtypeStruct((tokens, width), jnp.bfloat16), jax.ShapeDtypeStruct((tokens, 128), jnp.bfloat16)],
        compiler_params=pltpu.CompilerParams(vmem_limit_bytes=62 << 20),
    )(slots, routes, gates, result, inner, cot, returned)


def back_kernel(slots_ref, logit_ref, router_ref, gain_ref, resid_ref, cot_ref, merge_ref, part_ref, back_ref, grad_ref, low_ref, mixed_ref, gain_grad_ref, *, eps):
    block, _ = grad_ref.shape
    lane = lax.broadcasted_iota(jnp.int32, (block, 128), 1)
    grads = part_ref[...] + pick([spread(slots_ref[c:c + 1, :], block) for c in range(2)], lane, [back_ref], 1)
    grads = grads + dot_nn(logit_ref[...], router_ref[...])
    resid = resid_ref[...]
    inverse = lax.rsqrt(jnp.mean(resid * resid, axis=1, keepdims=True) + eps)
    unit = resid * inverse
    @pl.when(pl.program_id(0) == 0)
    def _():
        gain_grad_ref[...] = jnp.zeros_like(gain_grad_ref)
    gain_grad_ref[...] += jnp.sum(grads * unit, axis=0, keepdims=True)
    scaled = grads * gain_ref[...]
    inner = jnp.mean(scaled * unit, axis=1, keepdims=True)
    total = cot_ref[...].astype(jnp.float32) + inverse * (scaled - unit * inner)
    grad_ref[...] = total
    low = total.astype(jnp.bfloat16)
    low_ref[...] = low
    mixed_ref[...] = dot_nt(low, merge_ref[...]).astype(jnp.bfloat16)


def combine_back(slots, logit, router, gain, resid, cot, merge, part, returned, eps, block=256):
    tokens, width = resid.shape
    rows = pl.BlockSpec((block, width), lambda i: (i, 0))
    whole = lambda shape: pl.BlockSpec(shape, lambda i: (0, 0))
    low = jax.ShapeDtypeStruct((tokens, width), jnp.bfloat16)
    return pl.pallas_call(
        partial(back_kernel, eps=eps),
        grid=(tokens // block,),
        in_specs=[pl.BlockSpec((2, block), lambda i: (0, i)), pl.BlockSpec((block, 128), lambda i: (i, 0)), whole(router.shape), whole(gain.shape), rows, rows, whole(merge.shape), rows, returned_spec(returned, 1)],
        out_specs=[rows, rows, rows, whole((1, width))],
        out_shape=[jax.ShapeDtypeStruct((tokens, width), jnp.float32), low, low, jax.ShapeDtypeStruct((1, width), jnp.float32)],
        compiler_params=pltpu.CompilerParams(vmem_limit_bytes=62 << 20),
    )(slots, logit, router, gain, resid, cot, merge, part, returned)


def near_tiles(near_ref, head, block):
    spread = jnp.broadcast_to(near_ref[0, head:head + 1, :], (block, block))
    spread = pltpu.roll(spread, 0, 1, stride=1, stride_axis=0)
    key_at = lax.broadcasted_iota(jnp.int32, (block, block), 0)
    query_at = lax.broadcasted_iota(jnp.int32, (block, block), 1)
    return (jnp.where(query_at >= key_at, spread, masked_score), jnp.where(query_at < key_at, spread, 0.0), query_at < key_at)


def diagonal_sums(tile):
    block = tile.shape[1]
    total = tile[:8]
    for start in range(8, block, 8):
        total = total + pltpu.roll(tile[start:start + 8], block - start, 1)
    row = lax.broadcasted_iota(jnp.int32, total.shape, 0)
    for step in (1, 2, 4):
        total = jnp.where((row & step) != 0, pltpu.roll(total, block - step, 1), total)
    return jnp.sum(total, axis=0, keepdims=True)


def head_part(rows, head, size):
    lane = lax.broadcasted_iota(jnp.int32, rows.shape, 1)
    return jnp.where((lane >= head * size) & (lane < (head + 1) * size), rows, jnp.zeros_like(rows))


def attend_kernel(query_ref, key_ref, value_ref, near_ref, out_ref, total_ref, held, *, block, size, scale):
    length, lanes = query_ref.shape
    heads = lanes // size
    count = length // block
    turned = value_ref[...].T
    ones = jnp.ones((16, length), jnp.bfloat16)
    flipped = [jnp.concatenate([turned[head * size:(head + 1) * size], ones], axis=0) for head in range(heads)]
    tiles = [near_tiles(near_ref, head, block) for head in range(heads)]
    units = [(i, head) for i in reversed(range(count)) for head in range(heads)]
    def fold(tile, op):
        parts = [tile[k:k + 8] for k in range(0, tile.shape[0], 8)]
        while len(parts) > 1:
            parts = [op(parts[k], parts[k + 1]) for k in range(0, len(parts), 2)]
        return parts[0]
    def score_tile(unit, query_part, j, slot):
        i, head = unit
        tile = dot_nt(key_ref[pl.ds(j * block, block), :], query_part)
        if j == i:
            tile = tile + tiles[head][0]
        elif j == i - 1:
            tile = tile + tiles[head][1]
        held[slot, pl.ds(j * block, block), :] = tile
        return fold(tile, jnp.maximum)
    def part_of(unit):
        i, head = unit
        return head_part(query_ref[pl.ds(i * block, block), :] * jnp.bfloat16(scale), head, size)
    first = part_of(units[0])
    tops = {0: [score_tile(units[0], first, j, 0) for j in range(units[0][0] + 1)]}
    outs = []
    for n, (i, head) in enumerate(units):
        top = jnp.max(reduce(jnp.maximum, tops[n]), axis=0, keepdims=True)
        following = units[n + 1] if n + 1 < len(units) else None
        if following is not None:
            query_part = part_of(following)
            tops[n + 1] = []
        mixed = None
        total = None
        steps = max(i + 1, following[0] + 1 if following else 0)
        for j in range(steps):
            if following is not None and j <= following[0]:
                tops[n + 1].append(score_tile(following, query_part, j, (n + 1) % 2))
            if j <= i:
                weights = jnp.exp(held[n % 2, pl.ds(j * block, block), :] - top)
                part = dot_nn(flipped[head][:, j * block:(j + 1) * block], weights.astype(jnp.bfloat16))
                mixed = part if mixed is None else mixed + part
        total = mixed[size:size + 1]
        outs.append(mixed[:size] / total)
        rows = pl.ds(i * block, block)
        total_ref[0, head:head + 1, rows] = top + jnp.log(total)
        if head == heads - 1:
            out_ref[rows, :] = jnp.concatenate(outs[-heads:], axis=0).T.astype(out_ref.dtype)


def attend(queries, keys, values, near, size, block):
    length, width = queries.shape
    lanes = 128
    heads = lanes // size
    groups = width // lanes
    column = pl.BlockSpec((length, lanes), lambda g: (0, g))
    head_rows = pl.BlockSpec((1, heads, block), lambda g: (g, 0, 0))
    return pl.pallas_call(
        partial(attend_kernel, block=block, size=size, scale=size ** -0.5),
        grid=(groups,),
        in_specs=[column, column, column, head_rows],
        out_specs=[column, pl.BlockSpec((1, heads, length), lambda g: (g, 0, 0))],
        out_shape=[jax.ShapeDtypeStruct((length, width), jnp.bfloat16), jax.ShapeDtypeStruct((groups, heads, length), jnp.float32)],
        scratch_shapes=[pltpu.VMEM((2, length, block), jnp.float32)],
        compiler_params=pltpu.CompilerParams(vmem_limit_bytes=62 << 20),
    )(queries, keys, values, near)


def attend_back_kernel(query_ref, key_ref, value_ref, grad_ref, out_ref, total_ref, near_ref, grads_ref, dist_ref, key_acc, value_acc, *, block, size, scale):
    length, lanes = query_ref.shape
    heads = lanes // size
    count = length // block
    flipped = key_ref[...].T
    tiles = [near_tiles(near_ref, head, block) for head in range(heads)]
    near_acc = [None] * heads
    far_acc = [None] * heads
    for i in range(count):
        rows = pl.ds(i * block, block)
        query_rows = query_ref[rows, :] * jnp.bfloat16(scale)
        grad_rows = grad_ref[rows, :]
        products = (grad_rows.astype(jnp.float32) * out_ref[rows, :].astype(jnp.float32)).T
        query_parts = [head_part(query_rows, head, size) for head in range(heads)]
        grad_parts = [head_part(grad_rows, head, size) for head in range(heads)]
        inner = [jnp.sum(products[head * size:(head + 1) * size], axis=0, keepdims=True) for head in range(heads)]
        query_stack = jnp.concatenate(query_parts, axis=0)
        grad_stack = jnp.concatenate(grad_parts, axis=0)
        query_grads = [None] * heads
        for j in range(i + 1):
            cols = pl.ds(j * block, block)
            weight_list = []
            score_list = []
            for head in range(heads):
                tile = dot_nt(key_ref[cols, :], query_parts[head])
                if j == i:
                    tile = tile + tiles[head][0]
                elif j == i - 1:
                    tile = tile + tiles[head][1]
                weights = jnp.exp(tile - total_ref[0, head:head + 1, rows])
                grads = dot_nt(value_ref[cols, :], grad_parts[head])
                score_grads = weights * (grads - inner[head])
                low = score_grads.astype(jnp.bfloat16)
                weight_list.append(weights.astype(jnp.bfloat16))
                score_list.append(low)
                part = dot_nn(flipped[head * size:(head + 1) * size, j * block:(j + 1) * block], low)
                query_grads[head] = part if query_grads[head] is None else query_grads[head] + part
                if j == i:
                    near_acc[head] = score_grads if near_acc[head] is None else near_acc[head] + score_grads
                else:
                    far = score_grads
                    if j == i - 1:
                        close = jnp.where(tiles[head][2], score_grads, 0.0)
                        near_acc[head] = near_acc[head] + close
                        far = score_grads - close
                    far = jnp.sum(far, axis=0, keepdims=True)
                    far_acc[head] = far if far_acc[head] is None else far_acc[head] + far
            value_part = dot_nn(jnp.concatenate(weight_list, axis=1), grad_stack)
            key_part = dot_nn(jnp.concatenate(score_list, axis=1), query_stack)
            if j == i:
                value_acc[cols, :] = value_part
                key_acc[cols, :] = key_part
            else:
                value_acc[cols, :] += value_part
                key_acc[cols, :] += key_part
        grads_ref[0, rows, :] = (jnp.concatenate(query_grads, axis=0) * scale).T.astype(grads_ref.dtype)
    grads_ref[1] = key_acc[...].astype(grads_ref.dtype)
    grads_ref[2] = value_acc[...].astype(grads_ref.dtype)
    for head in range(heads):
        dist_ref[0, head:head + 1, :] = diagonal_sums(near_acc[head])
        dist_ref[0, heads + head:heads + head + 1, :] = far_acc[head]


def attend_back(queries, keys, values, grads, outs, totals, near, size, block):
    length, width = queries.shape
    lanes = 128
    heads = lanes // size
    groups = width // lanes
    column = pl.BlockSpec((length, lanes), lambda g: (0, g))
    head_rows = pl.BlockSpec((1, heads, block), lambda g: (g, 0, 0))
    return pl.pallas_call(
        partial(attend_back_kernel, block=block, size=size, scale=size ** -0.5),
        grid=(groups,),
        in_specs=[column] * 5 + [pl.BlockSpec((1, heads, length), lambda g: (g, 0, 0)), head_rows],
        out_specs=[pl.BlockSpec((3, length, lanes), lambda g: (0, 0, g)), pl.BlockSpec((1, 2 * heads, block), lambda g: (g, 0, 0))],
        out_shape=[jax.ShapeDtypeStruct((3, length, width), jnp.bfloat16), jax.ShapeDtypeStruct((groups, 2 * heads, block), jnp.float32)],
        scratch_shapes=[pltpu.VMEM((length, lanes), jnp.float32)] * 2,
        compiler_params=pltpu.CompilerParams(vmem_limit_bytes=62 << 20),
    )(queries, keys, values, grads, outs, totals, near)


def reverse_bits(value, count):
    out = value * 0
    for level in range(count):
        out = out * 2 + (value >> level) % 2
    return out


def project_kernel(owner_ref, inputs_ref, gain_ref, *refs, eps):
    piece_refs, weight_refs, low_ref, out_refs = refs[:4], refs[-7:-4], refs[-4], refs[-3:]
    count, half, three, _ = piece_refs[0].shape
    piece = three // 3
    owners = 2 * count
    part = owners * piece
    @pl.when(pl.program_id(0) == 0)
    def _():
        me = owner_ref[0]
        for source in range(owners):
            apart = jnp.bitwise_xor(me, source)
            near = apart % 2 == 0
            place = apart // 2
            places = (place, reverse_bits(place, owners.bit_length() - 2))
            for group in range(2):
                for line in range(half):
                    block = jnp.where(near, piece_refs[2 * group][places[group], line], piece_refs[2 * group + 1][places[group], line])
                    start = (group * half + line) * part + source * piece
                    for index in range(3):
                        weight_refs[index][start:start + piece, :] = block[index * piece:(index + 1) * piece]
    rows = inputs_ref[...].astype(jnp.float32)
    inverse = lax.rsqrt(jnp.mean(rows * rows, axis=1, keepdims=True) + eps)
    low = (rows * inverse * gain_ref[...]).astype(jnp.bfloat16)
    low_ref[...] = low
    for weight_ref, out_ref in zip(weight_refs, out_refs):
        out_ref[...] = dot_nn(low, weight_ref[...]).astype(jnp.bfloat16)


def project(owner, inputs, gain, pieces, eps, after=(), block=512):
    tokens, width = inputs.shape
    rows = pl.BlockSpec((block, width), lambda i: (i, 0))
    whole = lambda shape: pl.BlockSpec(shape, lambda i: (0,) * len(shape))
    weight = jax.ShapeDtypeStruct((width, width), jnp.bfloat16)
    return pl.pallas_call(
        partial(project_kernel, eps=eps),
        grid=(tokens // block,),
        in_specs=[pl.BlockSpec(memory_space=pltpu.SMEM), rows, whole(gain.shape)] + [whole(piece.shape) for piece in pieces] + [pl.BlockSpec(memory_space=pl.ANY)] * len(after),
        out_specs=[whole(weight.shape)] * 3 + [rows] * 4,
        out_shape=[weight] * 3 + [jax.ShapeDtypeStruct((tokens, width), jnp.bfloat16)] * 4,
        compiler_params=pltpu.CompilerParams(vmem_limit_bytes=62 << 20),
    )(owner, inputs, gain, *pieces, *after)


def settle_kernel(mixed_ref, merge_ref, inputs_ref, gain_ref, router_ref, routes_ref, slots_ref, resid_ref, low_ref, gates_ref, out_ref, held, *, eps, settling):
    step = pl.program_id(0)
    block, picking = mixed_ref.shape[0], out_ref.shape[0]
    @pl.when(step < settling)
    def _():
        resid = inputs_ref[...].astype(jnp.float32) + dot_nn(mixed_ref[...], merge_ref[...])
        resid_ref[...] = resid
        inverse = lax.rsqrt(jnp.mean(resid * resid, axis=1, keepdims=True) + eps)
        low = (resid * inverse * gain_ref[...]).astype(jnp.bfloat16)
        low_ref[...] = low
        held[pl.ds(pl.multiple_of(step * block, block), block), :] = low
        logits = dot_nt(router_ref[...], low)
        expert = lax.broadcasted_iota(jnp.int32, logits.shape, 0)
        chosen = [jnp.sum(jnp.where(routes_ref[c:c + 1, :] == expert, logits, 0.0), axis=0, keepdims=True) for c in range(2)]
        top = jnp.maximum(chosen[0], chosen[1])
        powers = [jnp.exp(value - top) for value in chosen]
        total = powers[0] + powers[1]
        for c in range(2):
            gates_ref[c:c + 1, :] = powers[c] / total
    @pl.when(step >= settling)
    def _():
        tokens = held.shape[0]
        slot = lax.broadcasted_iota(jnp.int32, (picking, tokens), 0) + (step - settling) * picking
        hot = jnp.where((slot == slots_ref[0:1, :]) | (slot == slots_ref[1:2, :]), 1.0, 0.0)
        out_ref[...] = dot_nn(hot.astype(jnp.bfloat16), held[...]).astype(out_ref.dtype)


def settle(mixed, merge, inputs, gain, router, routes, slots, count, eps, block=512):
    tokens, width = inputs.shape
    picking = count // 2
    settling = tokens // block
    early = lambda i: jnp.minimum(i, settling - 1)
    rows = pl.BlockSpec((block, width), lambda i: (early(i), 0))
    whole = lambda shape: pl.BlockSpec(shape, lambda i: (0, 0))
    small = pl.BlockSpec((2, block), lambda i: (0, early(i)))
    return pl.pallas_call(
        partial(settle_kernel, eps=eps, settling=settling),
        grid=(settling + 2,),
        in_specs=[rows, whole(merge.shape), rows, whole(gain.shape), whole(router.shape), small, whole(slots.shape)],
        out_specs=[rows, rows, small, pl.BlockSpec((picking, width), lambda i: (jnp.maximum(i - settling, 0), 0))],
        out_shape=[jax.ShapeDtypeStruct((tokens, width), jnp.float32), jax.ShapeDtypeStruct((tokens, width), jnp.bfloat16), jax.ShapeDtypeStruct((2, tokens), jnp.float32), jax.ShapeDtypeStruct((count, width), jnp.bfloat16)],
        scratch_shapes=[pltpu.VMEM((tokens, width), jnp.bfloat16)],
        compiler_params=pltpu.CompilerParams(vmem_limit_bytes=62 << 20),
    )(mixed, merge, inputs, gain, router, routes, slots)


def finish_kernel(heads_ref, query_ref, key_ref, value_ref, gain_ref, inputs_ref, resid_grad_ref, out_ref, gain_grad_ref, *, eps):
    grads = dot_nt(heads_ref[0], query_ref[...]) + dot_nt(heads_ref[1], key_ref[...]) + dot_nt(heads_ref[2], value_ref[...])
    rows = inputs_ref[...].astype(jnp.float32)
    inverse = lax.rsqrt(jnp.mean(rows * rows, axis=1, keepdims=True) + eps)
    unit = rows * inverse
    @pl.when(pl.program_id(0) == 0)
    def _():
        gain_grad_ref[...] = jnp.zeros_like(gain_grad_ref)
    gain_grad_ref[...] += jnp.sum(grads * unit, axis=0, keepdims=True)
    scaled = grads * gain_ref[...]
    inner = jnp.mean(scaled * unit, axis=1, keepdims=True)
    out_ref[...] = resid_grad_ref[...] + inverse * (scaled - unit * inner)


def finish(head_grads, query, key, value, gain, inputs, resid_grad, eps, block=256):
    tokens, width = inputs.shape
    rows = pl.BlockSpec((block, width), lambda i: (i, 0))
    whole = lambda shape: pl.BlockSpec(shape, lambda i: (0, 0))
    return pl.pallas_call(
        partial(finish_kernel, eps=eps),
        grid=(tokens // block,),
        in_specs=[pl.BlockSpec((3, block, width), lambda i: (0, i, 0))] + [whole(query.shape)] * 3 + [whole(gain.shape), rows, rows],
        out_specs=[rows, whole((1, width))],
        out_shape=[jax.ShapeDtypeStruct((tokens, width), jnp.float32), jax.ShapeDtypeStruct((1, width), jnp.float32)],
        compiler_params=pltpu.CompilerParams(vmem_limit_bytes=62 << 20),
    )(head_grads, query, key, value, gain, inputs, resid_grad)


def weight_kernel(left_ref, mixed_ref, heads_ref, branch_ref, out_ref, turned, right):
    shards, part, _ = out_ref.shape
    step = pl.program_id(0)
    last = pl.num_programs(0) - 1
    @pl.when(step == 0)
    def _():
        turned[...] = left_ref[...].T
    @pl.when(step < last)
    def _():
        right[...] = heads_ref[...]
    @pl.when(step == last)
    def _():
        turned[...] = mixed_ref[...].T
        right[...] = branch_ref[...]
    for shard in range(shards):
        grad = dot_nn(turned[shard * part:(shard + 1) * part, :], right[...])
        out_ref[shard] = grad.astype(jnp.bfloat16)


def weight_grads(left, mixed, head_grads, branch, shards):
    count, tokens, width = head_grads.shape
    part = width // shards
    fixed = pl.BlockSpec((tokens, width), lambda i: (0, 0))
    return pl.pallas_call(
        weight_kernel,
        grid=(count + 1,),
        in_specs=[fixed, fixed, pl.BlockSpec((None, tokens, width), lambda i: (jnp.minimum(i, count - 1), 0, 0)), fixed],
        out_specs=pl.BlockSpec((shards, part, width), lambda i: (0, i, 0)),
        out_shape=jax.ShapeDtypeStruct((shards, (count + 1) * part, width), jnp.bfloat16),
        scratch_shapes=[pltpu.VMEM((width, tokens), jnp.bfloat16), pltpu.VMEM((tokens, width), jnp.bfloat16)],
        compiler_params=pltpu.CompilerParams(vmem_limit_bytes=62 << 20),
    )(left, mixed, head_grads, branch)


def widen_first_kernel(rows_ref, out_ref):
    out_ref[...] = rows_ref[...].astype(jnp.float32)


def widen_first(rows):
    count, width = rows.shape
    half = pl.BlockSpec((count // 2, width), lambda i: (i, 0))
    return pl.pallas_call(
        widen_first_kernel,
        grid=(2,),
        in_specs=[half],
        out_specs=half,
        out_shape=jax.ShapeDtypeStruct((2 * count, width), jnp.float32),
        compiler_params=pltpu.CompilerParams(vmem_limit_bytes=62 << 20),
    )(rows)


def widen_rest_kernel(rows_ref, into_ref, up_ref, down_ref):
    del into_ref
    wide = rows_ref[...].astype(jnp.float32)
    step = pl.program_id(0)
    @pl.when(step < 2)
    def _():
        up_ref[...] = wide
    @pl.when(step >= 2)
    def _():
        down_ref[...] = wide


def widen_rest(rows, into):
    count, width = rows.shape[0] // 3, rows.shape[1]
    half = lambda place: pl.BlockSpec((count, width), lambda i: (place(i), 0))
    wide = jax.ShapeDtypeStruct((2 * count, width), jnp.float32)
    return pl.pallas_call(
        widen_rest_kernel,
        grid=(3,),
        in_specs=[half(lambda i: i), pl.BlockSpec(memory_space=pl.ANY)],
        out_specs=[half(lambda i: jnp.minimum(i, 1)), half(lambda i: 1)],
        out_shape=[wide, wide],
        input_output_aliases={1: 1},
        compiler_params=pltpu.CompilerParams(vmem_limit_bytes=62 << 20),
    )(rows, into)


def smalls_kernel(small_ref, near_ref, gain_one_ref, gain_two_ref, router_ref, table_ref, *, part, heads, router_at):
    shards, _, width = small_ref.shape
    group = table_ref.shape[1]
    lanes = -(-part // 128) * 128
    row = lax.broadcasted_iota(jnp.int32, (lanes, width), 0)
    column = lax.broadcasted_iota(jnp.int32, (lanes, width), 1)
    wide = None
    for shard in range(shards):
        place = jnp.where((column == row + shard * part) & (row < part), 1.0, 0.0).astype(jnp.bfloat16)
        rows = dot_nn(small_ref[shard][:, :lanes], place)
        wide = rows if wide is None else wide + rows
        near = dot_nn(small_ref[shard][:8, :128], near_ref[...])
        for head in range(heads):
            at = shard * heads + head
            table_ref[at // group, at % group:at % group + 1, :] = near[2 + head:3 + head, :]
    gain_one_ref[...] = wide[0:1]
    gain_two_ref[...] = wide[1:2]
    router_ref[...] = wide[router_at:router_at + router_ref.shape[0]].astype(jnp.bfloat16)


def spread_smalls(small, near, part, heads, group, experts, router_at):
    shards, _, width = small.shape
    f32 = jnp.float32
    return pl.pallas_call(
        partial(smalls_kernel, part=part, heads=heads, router_at=router_at),
        out_shape=[
            jax.ShapeDtypeStruct((1, width), f32),
            jax.ShapeDtypeStruct((1, width), f32),
            jax.ShapeDtypeStruct((experts, width), jnp.bfloat16),
            jax.ShapeDtypeStruct((shards * heads // group, group, near.shape[1]), f32),
        ],
    )(small, near)


OWNER = "expert"
LINE = "shard"


def exchange(rows, bit):
    count = lax.axis_size(OWNER)
    return lax.ppermute(rows, OWNER, [(i, i ^ bit) for i in range(count)])


def shift(rows, step):
    count = lax.axis_size(LINE)
    return lax.ppermute(rows, LINE, [(i, (i + step) % count) for i in range(count)])


def gather_line(rows):
    count = lax.axis_size(LINE)
    me = lax.axis_index(LINE)
    out = jnp.zeros((count,) + rows.shape, rows.dtype)
    out = lax.dynamic_update_index_in_dim(out, rows, me, 0)
    for step in range(1, count):
        got = shift(rows, step)
        out = lax.dynamic_update_index_in_dim(out, got, (me - step) % count, 0)
    return out


def add_low(left, right):
    return (left.astype(jnp.float32) + right.astype(jnp.float32)).astype(jnp.bfloat16)


def side(bit):
    return (lax.axis_index(OWNER) // bit) % 2


def halve(stack, bit):
    half = stack.shape[1] // 2
    keep = lax.dynamic_slice_in_dim(stack, side(bit) * half, half, 1)
    send = lax.dynamic_slice_in_dim(stack, (1 - side(bit)) * half, half, 1)
    got = exchange(send, bit)
    return add_low(keep, got)


def line_sum(stack):
    count = lax.axis_size(LINE)
    place = lax.axis_index(LINE)
    total = lax.dynamic_index_in_dim(stack, place, 0, False).astype(jnp.float32)
    for step in range(1, count):
        send = lax.dynamic_index_in_dim(stack, (place + step) % count, 0, False)
        total = total + shift(send, step).astype(jnp.float32)
    return total.astype(jnp.bfloat16)


def grow(piece, bit):
    other = exchange(piece, bit)
    return jnp.where(
        side(bit) == 0, jnp.concatenate([piece, other]), jnp.concatenate([other, piece])
    )


def reduce_rows(stack, bits):
    unit = 8 << (len(bits) - 1)
    cut = -(-stack.shape[1] // (2 * unit)) * unit
    parts = [stack[:, :cut], stack[:, cut:]]
    orders = [bits[1:], bits[:0:-1]]
    for level in range(len(bits) - 1):
        parts = [halve(part, order[level]) for part, order in zip(parts, orders)]
    low = parts[0].shape[1]
    piece = line_sum(jnp.concatenate(parts, axis=1))
    parts = [piece[:low], piece[low:]]
    for level in reversed(range(len(bits) - 1)):
        parts = [grow(part, order[level]) for part, order in zip(parts, orders)]
    return grow(jnp.concatenate(parts), bits[0])


def scatter_sum(grads):
    shards, rows, width = grads.shape
    grads = grads.reshape(shards * rows, width)
    return lax.psum_scatter(grads, LINE, scatter_dimension=0, tiled=True)


def share_rows(rows):
    return lax.all_to_all(rows, OWNER, 0, 0, tiled=True)


def share_large(rows):
    return pltpu.with_memory_space_constraint(share_rows(rows), pltpu.HBM)


def local(
    inputs,
    norm_gain,
    query_weight,
    key_weight,
    value_weight,
    merge_weight,
    bias_table,
    expert_gain,
    router_weight,
    up_weight,
    down_weight,
    routes,
    cotangent,
):
    f32, bf16 = jnp.float32, jnp.bfloat16
    tokens, width = inputs.shape
    owners = lax.axis_size(OWNER)
    shards = lax.axis_size(LINE)
    me = lax.axis_index(OWNER)
    part = query_weight.shape[0]
    piece = part // owners
    local_heads = bias_table.shape[1]
    heads = local_heads * shards
    size = width // heads
    experts = router_weight.shape[1]
    local_count, _, hidden = up_weight.shape
    capacity = (5 * tokens * routes.shape[1] + 4 * experts - 1) // (4 * experts)
    capacity = -(-capacity // 16) * 16
    rows = owners * capacity
    assert local_count == 2 and hidden // shards == width
    early = max(16, 2 * capacity // 5 // 16 * 16)

    router_at = 2 + local_heads + (-(2 + local_heads)) % 8

    def widen(block):
        return jnp.pad(block, ((0, 0), (0, width - block.shape[1])))

    def pack(gain_one, gain_two, table, router):
        head = jnp.concatenate([gain_one, gain_two], axis=0)
        gap = jnp.zeros((router_at - 2 - local_heads, width), bf16)
        return jnp.concatenate([widen(head), widen(table), gap, widen(router)], axis=0)

    small = pack(norm_gain[None], expert_gain[None], bias_table.T, router_weight.T)
    slices = [
        lax.dynamic_slice_in_dim(weight, me * piece, piece, 0)
        for weight in (query_weight, key_weight, value_weight)
    ]
    lined = gather_line(jnp.concatenate(slices + [small]))
    small_full = lined[:, 3 * piece :]
    bits = [1 << level for level in range(owners.bit_length() - 1)]
    pieces = []
    for index, order in enumerate((bits[1:], bits[:0:-1])):
        held = lined[index * shards // 2 : (index + 1) * shards // 2, : 3 * piece][None]
        for bit in order:
            got = exchange(held, bit)
            held = jnp.concatenate([held, got])
        pieces += [held, exchange(held, bits[0])]
    merge_full = lax.all_gather(merge_weight, LINE, axis=0, tiled=True)

    block = 256
    hot = bucket_hot(tokens)
    assert hot[block:, -1].all()
    near_hot = np.zeros((128, block), np.float32)
    near_hot[:BUCKETS] = (hot[:block] - hot[-1:]).T
    group = 128 // size
    gain_one, gain_two, router_full, near = spread_smalls(
        small_full, jnp.asarray(near_hot, bf16), part, local_heads, group, experts, router_at
    )

    routes_line = routes.T
    slots, routes_float = find_slots(routes_line, experts, local_count, owners, capacity)
    cot_rows, other = dispatch_first(
        slots, routes_float, cotangent, owners, capacity, early
    )
    other = share_rows(other).reshape(owners, local_count, capacity)

    owner = me.astype(jnp.int32).reshape(1)
    query_full, key_full, value_full, low_one, queries, keys, values = project(
        owner, inputs, gain_one, pieces, epsilon, after=(near, router_full)
    )
    cot_in = share_large(cot_rows)
    attended, totals = attend(queries, keys, values, near, size, block)
    resid, low_two, gates, send = settle(
        attended, merge_full, inputs, gain_two, router_full, routes_line, slots, rows, epsilon
    )

    others = [other[:, index].reshape(1, rows) for index in range(local_count)]
    rows_in = share_large(send.reshape(owners, capacity, width))
    joint = dispatch_both(
        slots, low_two, cotangent, rows, owners, capacity, early, after=others
    )
    joint_in = share_large(joint)
    act, pre, first_down, grad_in = expert_first(
        owner, rows_in, [cot_in], [(0, 0, capacity)], others[0], router_full, up_weight,
        0, local_count, capacity, shards,
    )
    first_sum = scatter_sum(first_down)
    first_made, pair = expert_second(rows_in, grad_in, act, pre, up_weight, down_weight, 0, owners, shards, 3 * width)
    late = capacity - early
    act, pre, pair, grad_in = expert_first(
        owner, joint_in, [cot_in, joint_in], [(0, capacity, early), (1, capacity, late)],
        others[1], router_full, up_weight, 1, local_count, capacity, shards, into=pair,
    )
    low, pair = expert_slope(joint_in, grad_in, pre, down_weight, 1, shards, pair, 1)
    pair_sum = scatter_sum(pair)
    second_made = expert_last(act, low, up_weight, down_weight, 1, owners, shards)
    returned = share_rows(first_made)
    result, inner, part_grads = combine_part(slots, gates, resid, cotangent, returned)
    returned = share_rows(second_made)
    output, logit_grad = combine_out(
        slots, routes_line, gates, result, inner, cotangent, returned
    )
    router_wide = jnp.pad(router_full, ((0, 128 - experts), (0, 0)))
    resid_grad, branch, mixed_grad, gain_grad = combine_back(
        slots, logit_grad, router_wide, gain_two, resid, cotangent, merge_full,
        part_grads, returned, epsilon
    )
    router_grad = jnp.einsum("te,ti->ei", logit_grad, low_two, preferred_element_type=f32)
    head_grads, distances = attend_back(
        queries, keys, values, mixed_grad, attended, totals, near, size, block
    )
    close_sums = distances[:, :group].reshape(heads, block)
    far_sums = jnp.sum(distances[:, group:].reshape(heads, block), axis=1)
    table_grad = jnp.dot(close_sums, jnp.asarray(hot[:block]), precision=lax.Precision.HIGHEST)
    table_grad = table_grad + far_sums[:, None] * jnp.asarray(hot[-1:])
    sums = weight_grads(low_one, attended, head_grads, branch, shards)
    sums = halve(sums, bits[0])
    input_gradient, norm_grad = finish(
        head_grads, query_full, key_full, value_full, gain_one, inputs, resid_grad, epsilon
    )
    small_grad = jax.vmap(pack)(
        norm_grad.reshape(shards, 1, part).astype(bf16),
        gain_grad.reshape(shards, 1, part).astype(bf16),
        table_grad.reshape(shards, local_heads, BUCKETS).astype(bf16),
        router_grad[:experts].reshape(experts, shards, part).transpose(1, 0, 2).astype(bf16),
    )
    spare = -small_grad.shape[1] % (8 * owners)
    small_grad = halve(jnp.pad(small_grad, ((0, 0), (0, spare), (0, 0))), bits[0])
    kept = sums.shape[1]
    sums = reduce_rows(jnp.concatenate([sums, small_grad], axis=1), bits)
    half = sums.shape[0] // 2
    weights = jnp.concatenate([sums[:kept], sums[half : half + kept]]).astype(f32)
    small_sum = jnp.concatenate([sums[kept:half], sums[half + kept :]]).astype(f32)
    up_sum, down_sum = widen_rest(pair_sum, widen_first(first_sum))
    return (
        output,
        input_gradient,
        small_sum[0, :part],
        weights[:part],
        weights[part : 2 * part],
        weights[2 * part : 3 * part],
        weights[3 * part :],
        small_sum[2 : 2 + local_heads, :BUCKETS].T,
        small_sum[1, :part],
        small_sum[router_at : router_at + experts, :part].T,
        up_sum.reshape(local_count, width, width),
        down_sum.reshape(local_count, width, width),
    )


def solution(mesh):
    in_specs = (
        P((OWNER, LINE), None),
        P(LINE),
        P(LINE, None),
        P(LINE, None),
        P(LINE, None),
        P(LINE, None),
        P(None, LINE),
        P(LINE),
        P(LINE, None),
        P(OWNER, None, None),
        P(OWNER, None, None),
        P((OWNER, LINE), None),
        P((OWNER, LINE), None),
    )
    out_specs = (
        P((OWNER, LINE), None),
        P((OWNER, LINE), None),
        P(LINE),
        P(LINE, None),
        P(LINE, None),
        P(LINE, None),
        P(LINE, None),
        P(None, LINE),
        P(LINE),
        P(LINE, None),
        P(OWNER, None, LINE),
        P(OWNER, LINE, None),
    )

    return jax.shard_map(local, mesh=mesh, in_specs=in_specs, out_specs=out_specs, check_vma=False)
```

```python
from functools import partial, reduce

import jax
import jax.numpy as jnp
import numpy as np
from jax import lax
from jax.experimental import pallas as pl
from jax.experimental.pallas import tpu as pltpu
from jax.sharding import PartitionSpec as P


BUCKETS = 32
MAX_DIST = 128


epsilon = 1e-06
masked_score = -1e30


def bucket_hot(length):
    distance = np.arange(length)
    half_count = BUCKETS // 2
    clipped = np.maximum(distance, half_count)
    spread = np.log(clipped / half_count) / np.log(MAX_DIST / half_count) * (BUCKETS - half_count)
    far_bucket = np.minimum(half_count + np.floor(spread).astype(np.int32), BUCKETS - 1)
    bucket = np.where(distance < half_count, distance, far_bucket)
    return (bucket[:, None] == np.arange(BUCKETS)[None, :]).astype(np.float32)


def dot_nt(a, b):
    return lax.dot_general(a, b, (((1,), (1,)), ((), ())), preferred_element_type=jnp.float32)


def dot_nn(a, b):
    return lax.dot_general(a, b, (((1,), (0,)), ((), ())), preferred_element_type=jnp.float32)


def dot_tn(a, b):
    return lax.dot_general(a, b, (((0,), (0,)), ((), ())), preferred_element_type=jnp.float32)


def slot_kernel(routes_ref, slots_ref, float_ref, *, experts, local_count, owners, capacity):
    tokens = routes_ref.shape[1]
    expert = lax.broadcasted_iota(jnp.int32, (experts, tokens), 0)
    hits = [routes_ref[c:c + 1, :] == expert for c in range(2)]
    hot = jnp.where(hits[0] | hits[1], 1.0, 0.0).astype(jnp.bfloat16)
    earlier = lax.broadcasted_iota(jnp.int32, (tokens, tokens), 0)
    later = lax.broadcasted_iota(jnp.int32, (tokens, tokens), 1)
    before = jnp.where(earlier < later, 1.0, 0.0).astype(jnp.bfloat16)
    counts = dot_nn(hot, before)
    column = lax.broadcasted_iota(jnp.int32, (experts, 1), 0)
    base = (column % local_count * owners + column // local_count) * capacity
    counts = counts + base.astype(jnp.float32)
    for c in range(2):
        slot = jnp.sum(jnp.where(hits[c], counts, 0.0), axis=0, keepdims=True)
        slots_ref[c:c + 1, :] = slot.astype(jnp.int32)
    float_ref[...] = routes_ref[...].astype(jnp.float32)


def find_slots(routes, experts, local_count, owners, capacity):
    return pl.pallas_call(
        partial(slot_kernel, experts=experts, local_count=local_count, owners=owners, capacity=capacity),
        out_shape=[jax.ShapeDtypeStruct(routes.shape, jnp.int32), jax.ShapeDtypeStruct(routes.shape, jnp.float32)],
    )(routes)


def dispatch_both_kernel(slots_ref, rows_ref, cot_ref, *refs, start, capacity, early):
    out_ref = refs[-1]
    block, tokens = capacity, rows_ref.shape[0]
    slot = lax.broadcasted_iota(jnp.int32, (block, tokens), 0) + (pl.program_id(0) * block + start)
    hot = jnp.where((slot == slots_ref[0:1, :]) | (slot == slots_ref[1:2, :]), 1.0, 0.0)
    hot = hot.astype(jnp.bfloat16)
    out_ref[0, :capacity] = dot_nn(hot, rows_ref[...]).astype(out_ref.dtype)
    out_ref[0, capacity:] = dot_nn(hot[early:], cot_ref[...]).astype(out_ref.dtype)


def dispatch_both(slots, rows, cot, start, owners, capacity, early, after=()):
    width = rows.shape[1]
    total = 2 * capacity - early
    whole = lambda shape: pl.BlockSpec(shape, lambda i: (0, 0))
    return pl.pallas_call(
        partial(dispatch_both_kernel, start=start, capacity=capacity, early=early),
        grid=(owners,),
        in_specs=[whole(slots.shape), whole(rows.shape), whole(cot.shape)] + [pl.BlockSpec(memory_space=pl.ANY)] * len(after),
        out_specs=pl.BlockSpec((1, total, width), lambda i: (i, 0, 0)),
        out_shape=jax.ShapeDtypeStruct((owners, total, width), rows.dtype),
        compiler_params=pltpu.CompilerParams(vmem_limit_bytes=48 << 20),
    )(slots, rows, cot, *after)


def dispatch_first_kernel(slots_ref, routes_ref, rows_ref, out_ref, other_ref, *, owners, capacity):
    block, tokens = other_ref.shape[2], rows_ref.shape[0]
    row = lax.broadcasted_iota(jnp.int32, (block, tokens), 0)
    slot = row + pl.program_id(0) * capacity
    slot = slot + jnp.where(row >= capacity, (owners - 1) * capacity, 0)
    hits = [slot == slots_ref[c:c + 1, :] for c in range(2)]
    hot = jnp.where(hits[0] | hits[1], 1.0, 0.0)[:out_ref.shape[1]]
    out_ref[0] = dot_nn(hot.astype(jnp.bfloat16), rows_ref[...]).astype(out_ref.dtype)
    other = jnp.where(hits[0], routes_ref[1:2, :], jnp.where(hits[1], routes_ref[0:1, :], 0.0))
    column = jnp.sum(other, axis=1, keepdims=True)
    other_ref[0] = jnp.broadcast_to(column, (block, 128)).T[0:1, :]


def dispatch_first(slots, routes, rows, owners, capacity, early):
    width = rows.shape[1]
    total = capacity + early
    whole = lambda shape: pl.BlockSpec(shape, lambda i: (0, 0))
    return pl.pallas_call(
        partial(dispatch_first_kernel, owners=owners, capacity=capacity),
        grid=(owners,),
        in_specs=[whole(slots.shape), whole(routes.shape), whole(rows.shape)],
        out_specs=[pl.BlockSpec((1, total, width), lambda i: (i, 0, 0)), pl.BlockSpec((1, 1, 2 * capacity), lambda i: (i, 0, 0))],
        out_shape=[jax.ShapeDtypeStruct((owners, total, width), rows.dtype), jax.ShapeDtypeStruct((owners, 1, 2 * capacity), jnp.float32)],
    )(slots, routes, rows)


def gelu_half(v):
    c = np.float32(np.sqrt(2.0 / np.pi))
    square = v * v
    half = 0.5 * jnp.tanh(v * (np.float32(0.044715) * c * square + c)) + 0.5
    return half, square


def gelu_slope(v):
    c = np.float32(np.sqrt(2.0 / np.pi))
    half, square = gelu_half(v)
    return half + v * half * (1.0 - half) * (np.float32(6.0 * 0.044715) * c * square + 2.0 * c)


def arrived_spec(arrived, used=None):
    owners, count, width = arrived.shape
    return pl.BlockSpec((owners, used or count, width), lambda i: (0, 0, 0))


def first_kernel(owner_ref, rows_ref, other_ref, router_ref, up_ref, *refs, index, local_count, capacity, pieces):
    act_ref, pre_ref, down_grad_ref, grad_ref = refs[-4:]
    owners, _, width = rows_ref.shape
    rows = owners * capacity
    chunk = rows // 2
    @pl.when(pl.program_id(0) == 0)
    def _():
        logits = dot_nt(router_ref[...], rows_ref[:, :capacity].reshape(rows, width))
        expert = lax.broadcasted_iota(jnp.int32, logits.shape, 0)
        mine = owner_ref[0] * local_count + index
        own = jnp.sum(jnp.where(expert == mine, logits, 0.0), axis=0, keepdims=True)
        other = other_ref[...].astype(jnp.int32)
        other = jnp.sum(jnp.where(expert == other, logits, 0.0), axis=0, keepdims=True)
        top = jnp.maximum(own, other)
        own = jnp.exp(own - top)
        gate = own / (own + jnp.exp(other - top))
        column = jnp.broadcast_to(gate, (128, rows)).T
        for start in range(0, width, 128):
            parts = [refs[place][:, low:low + size, start:start + 128] for place, low, size in pieces]
            part = parts[0] if len(parts) == 1 else jnp.concatenate(parts, axis=1)
            part = part.reshape(rows, 128).astype(jnp.float32) * column
            grad_ref[:, start:start + 128] = part.astype(jnp.bfloat16)
    up = up_ref[0]
    for start in range(0, rows, chunk):
        part = rows_ref[start // capacity:(start + chunk) // capacity, :capacity].reshape(chunk, width)
        pre = dot_nn(part, up)
        half, _ = gelu_half(pre)
        act_ref[start:start + chunk, :] = (pre * half).astype(jnp.bfloat16)
        pre_ref[start:start + chunk, :] = pre.astype(jnp.bfloat16)
    down_grad_ref[0] = dot_tn(act_ref[...], grad_ref[...]).astype(jnp.bfloat16)


def expert_first(owner, rows_in, cots, pieces, other, router, up, index, local_count, capacity, shards, into=None):
    owners, _, width = rows_in.shape
    rows = owners * capacity
    hidden = up.shape[2]
    tile = hidden // shards
    fixed = pl.BlockSpec((rows, width), lambda i: (0, 0))
    column = pl.BlockSpec((rows, tile), lambda i: (0, i))
    operands = [owner, rows_in, other, router, up, *cots]
    place, aliases = 0, {}
    grad_shape = jax.ShapeDtypeStruct((shards, tile, width), jnp.bfloat16)
    if into is not None:
        aliases = {len(operands): 2}
        operands.append(into)
        place, grad_shape = 2, jax.ShapeDtypeStruct(into.shape, into.dtype)
    return pl.pallas_call(
        partial(first_kernel, index=index, local_count=local_count, capacity=capacity, pieces=pieces),
        grid=(shards,),
        in_specs=[
            pl.BlockSpec(memory_space=pltpu.SMEM),
            arrived_spec(rows_in, capacity),
            pl.BlockSpec((1, rows), lambda i: (0, 0)),
            pl.BlockSpec(router.shape, lambda i: (0, 0)),
            pl.BlockSpec((1, width, tile), lambda i: (index, 0, i)),
        ]
        + [arrived_spec(cot, low + size) for cot, (_, low, size) in zip(cots, pieces)]
        + [pl.BlockSpec(memory_space=pl.ANY)] * (into is not None),
        out_specs=[column, column, pl.BlockSpec((1, tile, width), lambda i: (i, place, 0)), fixed],
        out_shape=[jax.ShapeDtypeStruct((rows, hidden), jnp.bfloat16)] * 2 + [grad_shape, jax.ShapeDtypeStruct((rows, width), jnp.bfloat16)],
        input_output_aliases=aliases,
        compiler_params=pltpu.CompilerParams(vmem_limit_bytes=62 << 20),
    )(*operands)


def second_kernel(rows_ref, grad_ref, act_ref, pre_ref, up_ref, down_ref, *refs):
    made_ref, up_grad_ref, turned, made_acc, back_acc = refs[-5:]
    step = pl.program_id(0)
    owners, _, capacity, width = made_ref.shape
    @pl.when(step == 0)
    def _():
        rows, width = grad_ref.shape
        owners = rows_ref.shape[0]
        turned[...] = rows_ref[:, :rows // owners].reshape(rows, width).T
    up = up_ref[0]
    down = down_ref[0]
    grads = dot_nt(grad_ref[...], down)
    low = (gelu_slope(pre_ref[...].astype(jnp.float32)) * grads).astype(jnp.bfloat16)
    up_grad_ref[0] = dot_nn(turned[...], low).astype(jnp.bfloat16)
    back = dot_nt(low, up)
    made = dot_nn(act_ref[...], down)
    last = pl.num_programs(0) - 1
    @pl.when(step == 0)
    def _():
        made_acc[...] = made
        back_acc[...] = back
    @pl.when((step > 0) & (step < last))
    def _():
        made_acc[...] += made
        back_acc[...] += back
    @pl.when(step == last)
    def _():
        made_ref[:, 0] = (made_acc[...] + made).astype(jnp.bfloat16).reshape(owners, capacity, width)
        made_ref[:, 1] = (back_acc[...] + back).astype(jnp.bfloat16).reshape(owners, capacity, width)


def expert_second(rows_in, grad, act, pre, up, down, index, owners, shards, wide, after=()):
    rows, width = grad.shape
    hidden = up.shape[2]
    tile = hidden // shards
    fixed = pl.BlockSpec((rows, width), lambda i: (0, 0))
    column = pl.BlockSpec((rows, tile), lambda i: (0, i))
    made_shape = (owners, 2, rows // owners, width)
    return pl.pallas_call(
        second_kernel,
        grid=(shards,),
        in_specs=[arrived_spec(rows_in, rows // rows_in.shape[0]), fixed, column, column, pl.BlockSpec((1, width, tile), lambda i: (index, 0, i)), pl.BlockSpec((1, tile, width), lambda i: (index, i, 0))]
        + [pl.BlockSpec(memory_space=pl.ANY)] * len(after),
        out_specs=[pl.BlockSpec(made_shape, lambda i: (0, 0, 0, 0)), pl.BlockSpec((1, width, tile), lambda i: (i, 0, 0))],
        out_shape=[jax.ShapeDtypeStruct(made_shape, jnp.bfloat16), jax.ShapeDtypeStruct((shards, wide, tile), jnp.bfloat16)],
        scratch_shapes=[pltpu.VMEM((width, rows), jnp.bfloat16), pltpu.VMEM((rows, width), jnp.float32), pltpu.VMEM((rows, width), jnp.float32)],
        compiler_params=pltpu.CompilerParams(vmem_limit_bytes=62 << 20),
    )(rows_in, grad, act, pre, up, down, *after)


def slope_kernel(rows_ref, grad_ref, pre_ref, down_ref, into_ref, low_ref, up_grad_ref, turned):
    del into_ref
    @pl.when(pl.program_id(0) == 0)
    def _():
        rows, width = grad_ref.shape
        owners = rows_ref.shape[0]
        turned[...] = rows_ref[:, :rows // owners].reshape(rows, width).T
    grads = dot_nt(grad_ref[...], down_ref[0])
    low = (gelu_slope(pre_ref[...].astype(jnp.float32)) * grads).astype(jnp.bfloat16)
    low_ref[...] = low
    up_grad_ref[0] = dot_nn(turned[...], low).astype(jnp.bfloat16)


def expert_slope(rows_in, grad, pre, down, index, shards, into, place):
    rows, width = grad.shape
    hidden = pre.shape[1]
    tile = hidden // shards
    fixed = pl.BlockSpec((rows, width), lambda i: (0, 0))
    column = pl.BlockSpec((rows, tile), lambda i: (0, i))
    return pl.pallas_call(
        slope_kernel,
        grid=(shards,),
        in_specs=[arrived_spec(rows_in, rows // rows_in.shape[0]), fixed, column, pl.BlockSpec((1, tile, width), lambda i: (index, i, 0)), pl.BlockSpec(memory_space=pl.ANY)],
        out_specs=[column, pl.BlockSpec((1, width, tile), lambda i: (i, place, 0))],
        out_shape=[jax.ShapeDtypeStruct((rows, hidden), jnp.bfloat16), jax.ShapeDtypeStruct(into.shape, into.dtype)],
        input_output_aliases={4: 1},
        scratch_shapes=[pltpu.VMEM((width, rows), jnp.bfloat16)],
        compiler_params=pltpu.CompilerParams(vmem_limit_bytes=62 << 20),
    )(rows_in, grad, pre, down, into)


def last_kernel(act_ref, low_ref, up_ref, down_ref, made_ref, made_acc, back_acc):
    step = pl.program_id(0)
    owners, _, capacity, width = made_ref.shape
    back = dot_nt(low_ref[...], up_ref[0])
    made = dot_nn(act_ref[...], down_ref[0])
    last = pl.num_programs(0) - 1
    @pl.when(step == 0)
    def _():
        made_acc[...] = made
        back_acc[...] = back
    @pl.when((step > 0) & (step < last))
    def _():
        made_acc[...] += made
        back_acc[...] += back
    @pl.when(step == last)
    def _():
        made_ref[:, 0] = (made_acc[...] + made).astype(jnp.bfloat16).reshape(owners, capacity, width)
        made_ref[:, 1] = (back_acc[...] + back).astype(jnp.bfloat16).reshape(owners, capacity, width)


def expert_last(act, low, up, down, index, owners, shards):
    rows, hidden = act.shape
    width = up.shape[1]
    tile = hidden // shards
    column = pl.BlockSpec((rows, tile), lambda i: (0, i))
    made_shape = (owners, 2, rows // owners, width)
    return pl.pallas_call(
        last_kernel,
        grid=(shards,),
        in_specs=[column, column, pl.BlockSpec((1, width, tile), lambda i: (index, 0, i)), pl.BlockSpec((1, tile, width), lambda i: (index, i, 0))],
        out_specs=pl.BlockSpec(made_shape, lambda i: (0, 0, 0, 0)),
        out_shape=jax.ShapeDtypeStruct(made_shape, jnp.bfloat16),
        scratch_shapes=[pltpu.VMEM((rows, width), jnp.float32), pltpu.VMEM((rows, width), jnp.float32)],
        compiler_params=pltpu.CompilerParams(vmem_limit_bytes=62 << 20),
    )(act, low, up, down)


def spread(row, block):
    return jnp.broadcast_to(row, (128, block)).T


def pick(slots, lane, back_refs, first=0):
    picked = None
    for index, back_ref in enumerate(back_refs, first):
        owners, capacity, width = back_ref.shape
        half = owners * capacity
        hots = []
        for start in range(index * half, (index + 1) * half, 128):
            hit = reduce(jnp.logical_or, [slot == lane + start for slot in slots])
            hots.append(jnp.where(hit, 1.0, 0.0).astype(jnp.bfloat16))
        part = dot_nn(jnp.concatenate(hots, axis=1), back_ref[...].reshape(half, width))
        picked = part if picked is None else picked + part
    return picked


def part_kernel(slots_ref, gates_ref, resid_ref, cot_ref, made_ref, back_ref, result_ref, inner_ref, grads_ref):
    block = result_ref.shape[0]
    lane = lax.broadcasted_iota(jnp.int32, (block, 128), 1)
    cot = cot_ref[...].astype(jnp.float32)
    result = resid_ref[...]
    inner = jnp.zeros((block, 128), jnp.float32)
    slots = [spread(slots_ref[c:c + 1, :], block) for c in range(2)]
    for c in range(2):
        picked = pick([slots[c]], lane, [made_ref])
        result = result + spread(gates_ref[c:c + 1, :], block)[:, 0:1] * picked
        inner = inner + jnp.where(lane == c, jnp.sum(cot * picked, axis=1, keepdims=True), 0.0)
    result_ref[...] = result
    inner_ref[...] = inner
    grads_ref[...] = pick(slots, lane, [back_ref])


def combine_part(slots, gates, resid, cot, returned, block=256):
    tokens, width = resid.shape
    small = pl.BlockSpec((2, block), lambda i: (0, i))
    rows = pl.BlockSpec((block, width), lambda i: (i, 0))
    wide = jax.ShapeDtypeStruct((tokens, width), jnp.float32)
    return pl.pallas_call(
        part_kernel,
        grid=(tokens // block,),
        in_specs=[small, small, rows, rows, returned_spec(returned, 0), returned_spec(returned, 1)],
        out_specs=[rows, pl.BlockSpec((block, 128), lambda i: (i, 0)), rows],
        out_shape=[wide, jax.ShapeDtypeStruct((tokens, 128), jnp.float32), wide],
        compiler_params=pltpu.CompilerParams(vmem_limit_bytes=62 << 20),
    )(slots, gates, resid, cot, returned, returned)


def out_kernel(slots_ref, routes_ref, gates_ref, result_ref, inner_ref, cot_ref, made_ref, out_ref, logit_ref):
    block = out_ref.shape[0]
    lane = lax.broadcasted_iota(jnp.int32, (block, 128), 1)
    cot = cot_ref[...].astype(jnp.float32)
    result = result_ref[...]
    gates, inner = [], []
    for c in range(2):
        slot = spread(slots_ref[c:c + 1, :], block)
        gate = spread(gates_ref[c:c + 1, :], block)[:, 0:1]
        picked = pick([slot], lane, [made_ref], 1)
        result = result + gate * picked
        gates.append(gate)
        inner.append(inner_ref[:, c:c + 1] + jnp.sum(cot * picked, axis=1, keepdims=True))
    out_ref[...] = result.astype(out_ref.dtype)
    middle = gates[0] * inner[0] + gates[1] * inner[1]
    logit = jnp.zeros((block, 128), jnp.float32)
    for c in range(2):
        route = spread(routes_ref[c:c + 1, :], block)
        logit = logit + jnp.where(route == lane, gates[c] * (inner[c] - middle), 0.0)
    logit_ref[...] = logit.astype(jnp.bfloat16)


def returned_spec(returned, which):
    owners, _, capacity, width = returned.shape
    return pl.BlockSpec((owners, None, capacity, width), lambda i: (0, which, 0, 0))


def combine_out(slots, routes, gates, result, inner, cot, returned, block=256):
    tokens, width = result.shape
    small = pl.BlockSpec((2, block), lambda i: (0, i))
    rows = pl.BlockSpec((block, width), lambda i: (i, 0))
    return pl.pallas_call(
        out_kernel,
        grid=(tokens // block,),
        in_specs=[small, small, small, rows, pl.BlockSpec((block, 128), lambda i: (i, 0)), rows, returned_spec(returned, 0)],
        out_specs=[rows, pl.BlockSpec((block, 128), lambda i: (i, 0))],
        out_shape=[jax.ShapeDtypeStruct((tokens, width), jnp.bfloat16), jax.ShapeDtypeStruct((tokens, 128), jnp.bfloat16)],
        compiler_params=pltpu.CompilerParams(vmem_limit_bytes=62 << 20),
    )(slots, routes, gates, result, inner, cot, returned)


def back_kernel(slots_ref, logit_ref, router_ref, gain_ref, resid_ref, cot_ref, merge_ref, part_ref, back_ref, grad_ref, low_ref, mixed_ref, gain_grad_ref, *, eps):
    block, _ = grad_ref.shape
    lane = lax.broadcasted_iota(jnp.int32, (block, 128), 1)
    grads = part_ref[...] + pick([spread(slots_ref[c:c + 1, :], block) for c in range(2)], lane, [back_ref], 1)
    grads = grads + dot_nn(logit_ref[...], router_ref[...])
    resid = resid_ref[...]
    inverse = lax.rsqrt(jnp.mean(resid * resid, axis=1, keepdims=True) + eps)
    unit = resid * inverse
    @pl.when(pl.program_id(0) == 0)
    def _():
        gain_grad_ref[...] = jnp.zeros_like(gain_grad_ref)
    gain_grad_ref[...] += jnp.sum(grads * unit, axis=0, keepdims=True)
    scaled = grads * gain_ref[...]
    inner = jnp.mean(scaled * unit, axis=1, keepdims=True)
    total = cot_ref[...].astype(jnp.float32) + inverse * (scaled - unit * inner)
    grad_ref[...] = total
    low = total.astype(jnp.bfloat16)
    low_ref[...] = low
    mixed_ref[...] = dot_nt(low, merge_ref[...]).astype(jnp.bfloat16)


def combine_back(slots, logit, router, gain, resid, cot, merge, part, returned, eps, block=256):
    tokens, width = resid.shape
    rows = pl.BlockSpec((block, width), lambda i: (i, 0))
    whole = lambda shape: pl.BlockSpec(shape, lambda i: (0, 0))
    low = jax.ShapeDtypeStruct((tokens, width), jnp.bfloat16)
    return pl.pallas_call(
        partial(back_kernel, eps=eps),
        grid=(tokens // block,),
        in_specs=[pl.BlockSpec((2, block), lambda i: (0, i)), pl.BlockSpec((block, 128), lambda i: (i, 0)), whole(router.shape), whole(gain.shape), rows, rows, whole(merge.shape), rows, returned_spec(returned, 1)],
        out_specs=[rows, rows, rows, whole((1, width))],
        out_shape=[jax.ShapeDtypeStruct((tokens, width), jnp.float32), low, low, jax.ShapeDtypeStruct((1, width), jnp.float32)],
        compiler_params=pltpu.CompilerParams(vmem_limit_bytes=62 << 20),
    )(slots, logit, router, gain, resid, cot, merge, part, returned)


def near_tiles(near_ref, head, block):
    spread = jnp.broadcast_to(near_ref[0, head:head + 1, :], (block, block))
    spread = pltpu.roll(spread, 0, 1, stride=1, stride_axis=0)
    key_at = lax.broadcasted_iota(jnp.int32, (block, block), 0)
    query_at = lax.broadcasted_iota(jnp.int32, (block, block), 1)
    return (jnp.where(query_at >= key_at, spread, masked_score), jnp.where(query_at < key_at, spread, 0.0), query_at < key_at)


def diagonal_sums(tile):
    block = tile.shape[1]
    total = tile[:8]
    for start in range(8, block, 8):
        total = total + pltpu.roll(tile[start:start + 8], block - start, 1)
    row = lax.broadcasted_iota(jnp.int32, total.shape, 0)
    for step in (1, 2, 4):
        total = jnp.where((row & step) != 0, pltpu.roll(total, block - step, 1), total)
    return jnp.sum(total, axis=0, keepdims=True)


def head_part(rows, head, size):
    lane = lax.broadcasted_iota(jnp.int32, rows.shape, 1)
    return jnp.where((lane >= head * size) & (lane < (head + 1) * size), rows, jnp.zeros_like(rows))


def attend_kernel(query_ref, key_ref, value_ref, near_ref, out_ref, total_ref, held, *, block, size, scale):
    length, lanes = query_ref.shape
    heads = lanes // size
    count = length // block
    turned = value_ref[...].T
    ones = jnp.ones((16, length), jnp.bfloat16)
    flipped = [jnp.concatenate([turned[head * size:(head + 1) * size], ones], axis=0) for head in range(heads)]
    tiles = [near_tiles(near_ref, head, block) for head in range(heads)]
    units = [(i, head) for i in reversed(range(count)) for head in range(heads)]
    def fold(tile, op):
        parts = [tile[k:k + 8] for k in range(0, tile.shape[0], 8)]
        while len(parts) > 1:
            parts = [op(parts[k], parts[k + 1]) for k in range(0, len(parts), 2)]
        return parts[0]
    def score_tile(unit, query_part, j, slot):
        i, head = unit
        tile = dot_nt(key_ref[pl.ds(j * block, block), :], query_part)
        if j == i:
            tile = tile + tiles[head][0]
        elif j == i - 1:
            tile = tile + tiles[head][1]
        held[slot, pl.ds(j * block, block), :] = tile
        return fold(tile, jnp.maximum)
    def part_of(unit):
        i, head = unit
        return head_part(query_ref[pl.ds(i * block, block), :] * jnp.bfloat16(scale), head, size)
    first = part_of(units[0])
    tops = {0: [score_tile(units[0], first, j, 0) for j in range(units[0][0] + 1)]}
    outs = []
    for n, (i, head) in enumerate(units):
        top = jnp.max(reduce(jnp.maximum, tops[n]), axis=0, keepdims=True)
        following = units[n + 1] if n + 1 < len(units) else None
        if following is not None:
            query_part = part_of(following)
            tops[n + 1] = []
        mixed = None
        total = None
        steps = max(i + 1, following[0] + 1 if following else 0)
        for j in range(steps):
            if following is not None and j <= following[0]:
                tops[n + 1].append(score_tile(following, query_part, j, (n + 1) % 2))
            if j <= i:
                weights = jnp.exp(held[n % 2, pl.ds(j * block, block), :] - top)
                part = dot_nn(flipped[head][:, j * block:(j + 1) * block], weights.astype(jnp.bfloat16))
                mixed = part if mixed is None else mixed + part
        total = mixed[size:size + 1]
        outs.append(mixed[:size] / total)
        rows = pl.ds(i * block, block)
        total_ref[0, head:head + 1, rows] = top + jnp.log(total)
        if head == heads - 1:
            out_ref[rows, :] = jnp.concatenate(outs[-heads:], axis=0).T.astype(out_ref.dtype)


def attend(queries, keys, values, near, size, block):
    length, width = queries.shape
    lanes = 128
    heads = lanes // size
    groups = width // lanes
    column = pl.BlockSpec((length, lanes), lambda g: (0, g))
    head_rows = pl.BlockSpec((1, heads, block), lambda g: (g, 0, 0))
    return pl.pallas_call(
        partial(attend_kernel, block=block, size=size, scale=size ** -0.5),
        grid=(groups,),
        in_specs=[column, column, column, head_rows],
        out_specs=[column, pl.BlockSpec((1, heads, length), lambda g: (g, 0, 0))],
        out_shape=[jax.ShapeDtypeStruct((length, width), jnp.bfloat16), jax.ShapeDtypeStruct((groups, heads, length), jnp.float32)],
        scratch_shapes=[pltpu.VMEM((2, length, block), jnp.float32)],
        compiler_params=pltpu.CompilerParams(vmem_limit_bytes=62 << 20),
    )(queries, keys, values, near)


def attend_back_kernel(query_ref, key_ref, value_ref, grad_ref, out_ref, total_ref, near_ref, grads_ref, dist_ref, key_acc, value_acc, *, block, size, scale):
    length, lanes = query_ref.shape
    heads = lanes // size
    count = length // block
    flipped = key_ref[...].T
    tiles = [near_tiles(near_ref, head, block) for head in range(heads)]
    near_acc = [None] * heads
    far_acc = [None] * heads
    for i in range(count):
        rows = pl.ds(i * block, block)
        query_rows = query_ref[rows, :] * jnp.bfloat16(scale)
        grad_rows = grad_ref[rows, :]
        products = (grad_rows.astype(jnp.float32) * out_ref[rows, :].astype(jnp.float32)).T
        query_parts = [head_part(query_rows, head, size) for head in range(heads)]
        grad_parts = [head_part(grad_rows, head, size) for head in range(heads)]
        inner = [jnp.sum(products[head * size:(head + 1) * size], axis=0, keepdims=True) for head in range(heads)]
        query_stack = jnp.concatenate(query_parts, axis=0)
        grad_stack = jnp.concatenate(grad_parts, axis=0)
        query_grads = [None] * heads
        for j in range(i + 1):
            cols = pl.ds(j * block, block)
            weight_list = []
            score_list = []
            for head in range(heads):
                tile = dot_nt(key_ref[cols, :], query_parts[head])
                if j == i:
                    tile = tile + tiles[head][0]
                elif j == i - 1:
                    tile = tile + tiles[head][1]
                weights = jnp.exp(tile - total_ref[0, head:head + 1, rows])
                grads = dot_nt(value_ref[cols, :], grad_parts[head])
                score_grads = weights * (grads - inner[head])
                low = score_grads.astype(jnp.bfloat16)
                weight_list.append(weights.astype(jnp.bfloat16))
                score_list.append(low)
                part = dot_nn(flipped[head * size:(head + 1) * size, j * block:(j + 1) * block], low)
                query_grads[head] = part if query_grads[head] is None else query_grads[head] + part
                if j == i:
                    near_acc[head] = score_grads if near_acc[head] is None else near_acc[head] + score_grads
                else:
                    far = score_grads
                    if j == i - 1:
                        close = jnp.where(tiles[head][2], score_grads, 0.0)
                        near_acc[head] = near_acc[head] + close
                        far = score_grads - close
                    far = jnp.sum(far, axis=0, keepdims=True)
                    far_acc[head] = far if far_acc[head] is None else far_acc[head] + far
            value_part = dot_nn(jnp.concatenate(weight_list, axis=1), grad_stack)
            key_part = dot_nn(jnp.concatenate(score_list, axis=1), query_stack)
            if j == i:
                value_acc[cols, :] = value_part
                key_acc[cols, :] = key_part
            else:
                value_acc[cols, :] += value_part
                key_acc[cols, :] += key_part
        grads_ref[0, rows, :] = (jnp.concatenate(query_grads, axis=0) * scale).T.astype(grads_ref.dtype)
    grads_ref[1] = key_acc[...].astype(grads_ref.dtype)
    grads_ref[2] = value_acc[...].astype(grads_ref.dtype)
    for head in range(heads):
        dist_ref[0, head:head + 1, :] = diagonal_sums(near_acc[head])
        dist_ref[0, heads + head:heads + head + 1, :] = far_acc[head]


def attend_back(queries, keys, values, grads, outs, totals, near, size, block):
    length, width = queries.shape
    lanes = 128
    heads = lanes // size
    groups = width // lanes
    column = pl.BlockSpec((length, lanes), lambda g: (0, g))
    head_rows = pl.BlockSpec((1, heads, block), lambda g: (g, 0, 0))
    return pl.pallas_call(
        partial(attend_back_kernel, block=block, size=size, scale=size ** -0.5),
        grid=(groups,),
        in_specs=[column] * 5 + [pl.BlockSpec((1, heads, length), lambda g: (g, 0, 0)), head_rows],
        out_specs=[pl.BlockSpec((3, length, lanes), lambda g: (0, 0, g)), pl.BlockSpec((1, 2 * heads, block), lambda g: (g, 0, 0))],
        out_shape=[jax.ShapeDtypeStruct((3, length, width), jnp.bfloat16), jax.ShapeDtypeStruct((groups, 2 * heads, block), jnp.float32)],
        scratch_shapes=[pltpu.VMEM((length, lanes), jnp.float32)] * 2,
        compiler_params=pltpu.CompilerParams(vmem_limit_bytes=62 << 20),
    )(queries, keys, values, grads, outs, totals, near)


def reverse_bits(value, count):
    out = value * 0
    for level in range(count):
        out = out * 2 + (value >> level) % 2
    return out


def project_kernel(owner_ref, inputs_ref, gain_ref, *refs, eps):
    piece_refs, weight_refs, low_ref, out_refs = refs[:4], refs[-7:-4], refs[-4], refs[-3:]
    count, half, three, _ = piece_refs[0].shape
    piece = three // 3
    owners = 2 * count
    part = owners * piece
    @pl.when(pl.program_id(0) == 0)
    def _():
        me = owner_ref[0]
        for source in range(owners):
            apart = jnp.bitwise_xor(me, source)
            near = apart % 2 == 0
            place = apart // 2
            places = (place, reverse_bits(place, owners.bit_length() - 2))
            for group in range(2):
                for line in range(half):
                    block = jnp.where(near, piece_refs[2 * group][places[group], line], piece_refs[2 * group + 1][places[group], line])
                    start = (group * half + line) * part + source * piece
                    for index in range(3):
                        weight_refs[index][start:start + piece, :] = block[index * piece:(index + 1) * piece]
    rows = inputs_ref[...].astype(jnp.float32)
    inverse = lax.rsqrt(jnp.mean(rows * rows, axis=1, keepdims=True) + eps)
    low = (rows * inverse * gain_ref[...]).astype(jnp.bfloat16)
    low_ref[...] = low
    for weight_ref, out_ref in zip(weight_refs, out_refs):
        out_ref[...] = dot_nn(low, weight_ref[...]).astype(jnp.bfloat16)


def project(owner, inputs, gain, pieces, eps, after=(), block=512):
    tokens, width = inputs.shape
    rows = pl.BlockSpec((block, width), lambda i: (i, 0))
    whole = lambda shape: pl.BlockSpec(shape, lambda i: (0,) * len(shape))
    weight = jax.ShapeDtypeStruct((width, width), jnp.bfloat16)
    return pl.pallas_call(
        partial(project_kernel, eps=eps),
        grid=(tokens // block,),
        in_specs=[pl.BlockSpec(memory_space=pltpu.SMEM), rows, whole(gain.shape)] + [whole(piece.shape) for piece in pieces] + [pl.BlockSpec(memory_space=pl.ANY)] * len(after),
        out_specs=[whole(weight.shape)] * 3 + [rows] * 4,
        out_shape=[weight] * 3 + [jax.ShapeDtypeStruct((tokens, width), jnp.bfloat16)] * 4,
        compiler_params=pltpu.CompilerParams(vmem_limit_bytes=62 << 20),
    )(owner, inputs, gain, *pieces, *after)


def settle_kernel(mixed_ref, merge_ref, inputs_ref, gain_ref, router_ref, routes_ref, slots_ref, resid_ref, low_ref, gates_ref, out_ref, held, *, eps, settling):
    step = pl.program_id(0)
    block, picking = mixed_ref.shape[0], out_ref.shape[0]
    @pl.when(step < settling)
    def _():
        resid = inputs_ref[...].astype(jnp.float32) + dot_nn(mixed_ref[...], merge_ref[...])
        resid_ref[...] = resid
        inverse = lax.rsqrt(jnp.mean(resid * resid, axis=1, keepdims=True) + eps)
        low = (resid * inverse * gain_ref[...]).astype(jnp.bfloat16)
        low_ref[...] = low
        held[pl.ds(pl.multiple_of(step * block, block), block), :] = low
        logits = dot_nt(router_ref[...], low)
        expert = lax.broadcasted_iota(jnp.int32, logits.shape, 0)
        chosen = [jnp.sum(jnp.where(routes_ref[c:c + 1, :] == expert, logits, 0.0), axis=0, keepdims=True) for c in range(2)]
        top = jnp.maximum(chosen[0], chosen[1])
        powers = [jnp.exp(value - top) for value in chosen]
        total = powers[0] + powers[1]
        for c in range(2):
            gates_ref[c:c + 1, :] = powers[c] / total
    @pl.when(step >= settling)
    def _():
        tokens = held.shape[0]
        slot = lax.broadcasted_iota(jnp.int32, (picking, tokens), 0) + (step - settling) * picking
        hot = jnp.where((slot == slots_ref[0:1, :]) | (slot == slots_ref[1:2, :]), 1.0, 0.0)
        out_ref[...] = dot_nn(hot.astype(jnp.bfloat16), held[...]).astype(out_ref.dtype)


def settle(mixed, merge, inputs, gain, router, routes, slots, count, eps, block=512):
    tokens, width = inputs.shape
    picking = count // 2
    settling = tokens // block
    early = lambda i: jnp.minimum(i, settling - 1)
    rows = pl.BlockSpec((block, width), lambda i: (early(i), 0))
    whole = lambda shape: pl.BlockSpec(shape, lambda i: (0, 0))
    small = pl.BlockSpec((2, block), lambda i: (0, early(i)))
    return pl.pallas_call(
        partial(settle_kernel, eps=eps, settling=settling),
        grid=(settling + 2,),
        in_specs=[rows, whole(merge.shape), rows, whole(gain.shape), whole(router.shape), small, whole(slots.shape)],
        out_specs=[rows, rows, small, pl.BlockSpec((picking, width), lambda i: (jnp.maximum(i - settling, 0), 0))],
        out_shape=[jax.ShapeDtypeStruct((tokens, width), jnp.float32), jax.ShapeDtypeStruct((tokens, width), jnp.bfloat16), jax.ShapeDtypeStruct((2, tokens), jnp.float32), jax.ShapeDtypeStruct((count, width), jnp.bfloat16)],
        scratch_shapes=[pltpu.VMEM((tokens, width), jnp.bfloat16)],
        compiler_params=pltpu.CompilerParams(vmem_limit_bytes=62 << 20),
    )(mixed, merge, inputs, gain, router, routes, slots)


def finish_kernel(heads_ref, query_ref, key_ref, value_ref, gain_ref, inputs_ref, resid_grad_ref, out_ref, gain_grad_ref, *, eps):
    grads = dot_nt(heads_ref[0], query_ref[...]) + dot_nt(heads_ref[1], key_ref[...]) + dot_nt(heads_ref[2], value_ref[...])
    rows = inputs_ref[...].astype(jnp.float32)
    inverse = lax.rsqrt(jnp.mean(rows * rows, axis=1, keepdims=True) + eps)
    unit = rows * inverse
    @pl.when(pl.program_id(0) == 0)
    def _():
        gain_grad_ref[...] = jnp.zeros_like(gain_grad_ref)
    gain_grad_ref[...] += jnp.sum(grads * unit, axis=0, keepdims=True)
    scaled = grads * gain_ref[...]
    inner = jnp.mean(scaled * unit, axis=1, keepdims=True)
    out_ref[...] = resid_grad_ref[...] + inverse * (scaled - unit * inner)


def finish(head_grads, query, key, value, gain, inputs, resid_grad, eps, block=256):
    tokens, width = inputs.shape
    rows = pl.BlockSpec((block, width), lambda i: (i, 0))
    whole = lambda shape: pl.BlockSpec(shape, lambda i: (0, 0))
    return pl.pallas_call(
        partial(finish_kernel, eps=eps),
        grid=(tokens // block,),
        in_specs=[pl.BlockSpec((3, block, width), lambda i: (0, i, 0))] + [whole(query.shape)] * 3 + [whole(gain.shape), rows, rows],
        out_specs=[rows, whole((1, width))],
        out_shape=[jax.ShapeDtypeStruct((tokens, width), jnp.float32), jax.ShapeDtypeStruct((1, width), jnp.float32)],
        compiler_params=pltpu.CompilerParams(vmem_limit_bytes=62 << 20),
    )(head_grads, query, key, value, gain, inputs, resid_grad)


def weight_kernel(left_ref, mixed_ref, heads_ref, branch_ref, out_ref, turned, right):
    shards, part, _ = out_ref.shape
    step = pl.program_id(0)
    last = pl.num_programs(0) - 1
    @pl.when(step == 0)
    def _():
        turned[...] = left_ref[...].T
    @pl.when(step < last)
    def _():
        right[...] = heads_ref[...]
    @pl.when(step == last)
    def _():
        turned[...] = mixed_ref[...].T
        right[...] = branch_ref[...]
    for shard in range(shards):
        grad = dot_nn(turned[shard * part:(shard + 1) * part, :], right[...])
        out_ref[shard] = grad.astype(jnp.bfloat16)


def weight_grads(left, mixed, head_grads, branch, shards):
    count, tokens, width = head_grads.shape
    part = width // shards
    fixed = pl.BlockSpec((tokens, width), lambda i: (0, 0))
    return pl.pallas_call(
        weight_kernel,
        grid=(count + 1,),
        in_specs=[fixed, fixed, pl.BlockSpec((None, tokens, width), lambda i: (jnp.minimum(i, count - 1), 0, 0)), fixed],
        out_specs=pl.BlockSpec((shards, part, width), lambda i: (0, i, 0)),
        out_shape=jax.ShapeDtypeStruct((shards, (count + 1) * part, width), jnp.bfloat16),
        scratch_shapes=[pltpu.VMEM((width, tokens), jnp.bfloat16), pltpu.VMEM((tokens, width), jnp.bfloat16)],
        compiler_params=pltpu.CompilerParams(vmem_limit_bytes=62 << 20),
    )(left, mixed, head_grads, branch)


def widen_first_kernel(rows_ref, out_ref):
    out_ref[...] = rows_ref[...].astype(jnp.float32)


def widen_first(rows):
    count, width = rows.shape
    half = pl.BlockSpec((count // 2, width), lambda i: (i, 0))
    return pl.pallas_call(
        widen_first_kernel,
        grid=(2,),
        in_specs=[half],
        out_specs=half,
        out_shape=jax.ShapeDtypeStruct((2 * count, width), jnp.float32),
        compiler_params=pltpu.CompilerParams(vmem_limit_bytes=62 << 20),
    )(rows)


def widen_rest_kernel(rows_ref, into_ref, up_ref, down_ref):
    del into_ref
    wide = rows_ref[...].astype(jnp.float32)
    step = pl.program_id(0)
    @pl.when(step < 2)
    def _():
        up_ref[...] = wide
    @pl.when(step >= 2)
    def _():
        down_ref[...] = wide


def widen_rest(rows, into):
    count, width = rows.shape[0] // 3, rows.shape[1]
    half = lambda place: pl.BlockSpec((count, width), lambda i: (place(i), 0))
    wide = jax.ShapeDtypeStruct((2 * count, width), jnp.float32)
    return pl.pallas_call(
        widen_rest_kernel,
        grid=(3,),
        in_specs=[half(lambda i: i), pl.BlockSpec(memory_space=pl.ANY)],
        out_specs=[half(lambda i: jnp.minimum(i, 1)), half(lambda i: 1)],
        out_shape=[wide, wide],
        input_output_aliases={1: 1},
        compiler_params=pltpu.CompilerParams(vmem_limit_bytes=62 << 20),
    )(rows, into)


def smalls_kernel(small_ref, near_ref, gain_one_ref, gain_two_ref, router_ref, table_ref, *, part, heads, router_at):
    shards, _, width = small_ref.shape
    group = table_ref.shape[1]
    lanes = -(-part // 128) * 128
    row = lax.broadcasted_iota(jnp.int32, (lanes, width), 0)
    column = lax.broadcasted_iota(jnp.int32, (lanes, width), 1)
    wide = None
    for shard in range(shards):
        place = jnp.where((column == row + shard * part) & (row < part), 1.0, 0.0).astype(jnp.bfloat16)
        rows = dot_nn(small_ref[shard][:, :lanes], place)
        wide = rows if wide is None else wide + rows
        near = dot_nn(small_ref[shard][:8, :128], near_ref[...])
        for head in range(heads):
            at = shard * heads + head
            table_ref[at // group, at % group:at % group + 1, :] = near[2 + head:3 + head, :]
    gain_one_ref[...] = wide[0:1]
    gain_two_ref[...] = wide[1:2]
    router_ref[...] = wide[router_at:router_at + router_ref.shape[0]].astype(jnp.bfloat16)


def spread_smalls(small, near, part, heads, group, experts, router_at):
    shards, _, width = small.shape
    f32 = jnp.float32
    return pl.pallas_call(
        partial(smalls_kernel, part=part, heads=heads, router_at=router_at),
        out_shape=[
            jax.ShapeDtypeStruct((1, width), f32),
            jax.ShapeDtypeStruct((1, width), f32),
            jax.ShapeDtypeStruct((experts, width), jnp.bfloat16),
            jax.ShapeDtypeStruct((shards * heads // group, group, near.shape[1]), f32),
        ],
    )(small, near)


def pack_kernel(owner_ref, query_ref, key_ref, value_ref, one_ref, two_ref, table_ref, router_ref, out_ref, tall, *, router_at):
    del owner_ref
    piece = query_ref.shape[0]
    experts, part = router_ref.shape
    heads, buckets = table_ref.shape
    tall[...] = jnp.zeros_like(tall)
    tall[0:1, :part] = one_ref[...].astype(jnp.float32).reshape(1, part)
    tall[1:2, :part] = two_ref[...].astype(jnp.float32).reshape(1, part)
    tall[2:2 + heads, :buckets] = table_ref[...].astype(jnp.float32)
    tall[router_at:router_at + experts, :part] = router_ref[...].astype(jnp.float32)
    for index, ref in enumerate((query_ref, key_ref, value_ref)):
        out_ref[index * piece:(index + 1) * piece, :] = ref[...]
    out_ref[3 * piece:, :] = tall[...].astype(out_ref.dtype)


def pack_first(owner, weights, one, two, table, router, piece, small_rows, router_at):
    width = weights[0].shape[1]
    if piece % 8 == 0:
        rows = pl.BlockSpec((piece, width), lambda i, owner: (owner[0], 0))
    else:
        weights = [lax.dynamic_slice_in_dim(weight, owner[0] * piece, piece, 0) for weight in weights]
        rows = pl.BlockSpec((piece, width), lambda i, owner: (0, 0))
    whole = lambda shape: pl.BlockSpec(shape, lambda i, owner: (0,) * len(shape))
    return pl.pallas_call(
        partial(pack_kernel, router_at=router_at),
        grid_spec=pltpu.PrefetchScalarGridSpec(
            num_scalar_prefetch=1,
            grid=(1,),
            in_specs=[rows, rows, rows, whole(one.shape), whole(two.shape), whole(table.shape), whole(router.shape)],
            out_specs=whole((3 * piece + small_rows, width)),
            scratch_shapes=[pltpu.VMEM((small_rows, width), jnp.float32)],
        ),
        out_shape=jax.ShapeDtypeStruct((3 * piece + small_rows, width), weights[0].dtype),
    )(owner, *weights, one, two, table, router)


OWNER = "expert"
LINE = "shard"


def exchange(rows, bit):
    count = lax.axis_size(OWNER)
    return lax.ppermute(rows, OWNER, [(i, i ^ bit) for i in range(count)])


def shift(rows, step):
    count = lax.axis_size(LINE)
    return lax.ppermute(rows, LINE, [(i, (i + step) % count) for i in range(count)])


def gather_line(rows):
    count = lax.axis_size(LINE)
    me = lax.axis_index(LINE)
    out = jnp.zeros((count,) + rows.shape, rows.dtype)
    out = lax.dynamic_update_index_in_dim(out, rows, me, 0)
    for step in range(1, count):
        got = shift(rows, step)
        out = lax.dynamic_update_index_in_dim(out, got, (me - step) % count, 0)
    return out


def add_low(left, right):
    return (left.astype(jnp.float32) + right.astype(jnp.float32)).astype(jnp.bfloat16)


def side(bit):
    return (lax.axis_index(OWNER) // bit) % 2


def halve(stack, bit):
    half = stack.shape[1] // 2
    keep = lax.dynamic_slice_in_dim(stack, side(bit) * half, half, 1)
    send = lax.dynamic_slice_in_dim(stack, (1 - side(bit)) * half, half, 1)
    got = exchange(send, bit)
    return add_low(keep, got)


def line_sum(stack):
    count = lax.axis_size(LINE)
    place = lax.axis_index(LINE)
    total = lax.dynamic_index_in_dim(stack, place, 0, False).astype(jnp.float32)
    for step in range(1, count):
        send = lax.dynamic_index_in_dim(stack, (place + step) % count, 0, False)
        total = total + shift(send, step).astype(jnp.float32)
    return total.astype(jnp.bfloat16)


def grow(piece, bit):
    other = exchange(piece, bit)
    return jnp.where(
        side(bit) == 0, jnp.concatenate([piece, other]), jnp.concatenate([other, piece])
    )


def reduce_rows(stack, bits):
    unit = 8 << (len(bits) - 1)
    cut = -(-stack.shape[1] // (2 * unit)) * unit
    parts = [stack[:, :cut], stack[:, cut:]]
    orders = [bits[1:], bits[:0:-1]]
    for level in range(len(bits) - 1):
        parts = [halve(part, order[level]) for part, order in zip(parts, orders)]
    low = parts[0].shape[1]
    piece = line_sum(jnp.concatenate(parts, axis=1))
    parts = [piece[:low], piece[low:]]
    for level in reversed(range(len(bits) - 1)):
        parts = [grow(part, order[level]) for part, order in zip(parts, orders)]
    return grow(jnp.concatenate(parts), bits[0])


def scatter_sum(grads):
    shards, rows, width = grads.shape
    grads = grads.reshape(shards * rows, width)
    return lax.psum_scatter(grads, LINE, scatter_dimension=0, tiled=True)


def share_rows(rows):
    return lax.all_to_all(rows, OWNER, 0, 0, tiled=True)


def share_large(rows):
    return pltpu.with_memory_space_constraint(share_rows(rows), pltpu.HBM)


def local(
    inputs,
    norm_gain,
    query_weight,
    key_weight,
    value_weight,
    merge_weight,
    bias_table,
    expert_gain,
    router_weight,
    up_weight,
    down_weight,
    routes,
    cotangent,
):
    f32, bf16 = jnp.float32, jnp.bfloat16
    tokens, width = inputs.shape
    owners = lax.axis_size(OWNER)
    shards = lax.axis_size(LINE)
    me = lax.axis_index(OWNER)
    part = query_weight.shape[0]
    piece = part // owners
    local_heads = bias_table.shape[1]
    heads = local_heads * shards
    size = width // heads
    experts = router_weight.shape[1]
    local_count, _, hidden = up_weight.shape
    capacity = (5 * tokens * routes.shape[1] + 4 * experts - 1) // (4 * experts)
    capacity = -(-capacity // 16) * 16
    rows = owners * capacity
    assert local_count == 2 and hidden // shards == width
    early = max(16, 2 * capacity // 5 // 16 * 16)

    router_at = 2 + local_heads + (-(2 + local_heads)) % 8

    def widen(block):
        return jnp.pad(block, ((0, 0), (0, width - block.shape[1])))

    def pack(gain_one, gain_two, table, router):
        head = jnp.concatenate([gain_one, gain_two], axis=0)
        gap = jnp.zeros((router_at - 2 - local_heads, width), bf16)
        return jnp.concatenate([widen(head), widen(table), gap, widen(router)], axis=0)

    owner = me.astype(jnp.int32).reshape(1)
    first = pack_first(
        owner, [query_weight, key_weight, value_weight], norm_gain, expert_gain,
        bias_table.T, router_weight.T, piece, router_at + experts, router_at,
    )
    lined = gather_line(first)
    small_full = lined[:, 3 * piece :]
    bits = [1 << level for level in range(owners.bit_length() - 1)]
    pieces = []
    for index, order in enumerate((bits[1:], bits[:0:-1])):
        held = lined[index * shards // 2 : (index + 1) * shards // 2, : 3 * piece][None]
        for bit in order:
            got = exchange(held, bit)
            held = jnp.concatenate([held, got])
        pieces += [held, exchange(held, bits[0])]
    merge_full = lax.all_gather(merge_weight, LINE, axis=0, tiled=True)

    block = 256
    hot = bucket_hot(tokens)
    assert hot[block:, -1].all()
    near_hot = np.zeros((128, block), np.float32)
    near_hot[:BUCKETS] = (hot[:block] - hot[-1:]).T
    group = 128 // size
    gain_one, gain_two, router_full, near = spread_smalls(
        small_full, jnp.asarray(near_hot, bf16), part, local_heads, group, experts, router_at
    )

    routes_line = routes.T
    slots, routes_float = find_slots(routes_line, experts, local_count, owners, capacity)
    cot_rows, other = dispatch_first(
        slots, routes_float, cotangent, owners, capacity, early
    )
    other = share_rows(other).reshape(owners, local_count, capacity)

    query_full, key_full, value_full, low_one, queries, keys, values = project(
        owner, inputs, gain_one, pieces, epsilon, after=(near, router_full)
    )
    cot_in = share_large(cot_rows)
    attended, totals = attend(queries, keys, values, near, size, block)
    resid, low_two, gates, send = settle(
        attended, merge_full, inputs, gain_two, router_full, routes_line, slots, rows, epsilon
    )

    others = [other[:, index].reshape(1, rows) for index in range(local_count)]
    rows_in = share_large(send.reshape(owners, capacity, width))
    joint = dispatch_both(
        slots, low_two, cotangent, rows, owners, capacity, early, after=others
    )
    joint_in = share_large(joint)
    act, pre, first_down, grad_in = expert_first(
        owner, rows_in, [cot_in], [(0, 0, capacity)], others[0], router_full, up_weight,
        0, local_count, capacity, shards,
    )
    first_sum = scatter_sum(first_down)
    first_made, pair = expert_second(rows_in, grad_in, act, pre, up_weight, down_weight, 0, owners, shards, 3 * width)
    late = capacity - early
    act, pre, pair, grad_in = expert_first(
        owner, joint_in, [cot_in, joint_in], [(0, capacity, early), (1, capacity, late)],
        others[1], router_full, up_weight, 1, local_count, capacity, shards, into=pair,
    )
    low, pair = expert_slope(joint_in, grad_in, pre, down_weight, 1, shards, pair, 1)
    pair_sum = scatter_sum(pair)
    second_made = expert_last(act, low, up_weight, down_weight, 1, owners, shards)
    returned = share_rows(first_made)
    result, inner, part_grads = combine_part(slots, gates, resid, cotangent, returned)
    returned = share_rows(second_made)
    output, logit_grad = combine_out(
        slots, routes_line, gates, result, inner, cotangent, returned
    )
    router_wide = jnp.pad(router_full, ((0, 128 - experts), (0, 0)))
    resid_grad, branch, mixed_grad, gain_grad = combine_back(
        slots, logit_grad, router_wide, gain_two, resid, cotangent, merge_full,
        part_grads, returned, epsilon
    )
    router_grad = jnp.einsum("te,ti->ei", logit_grad, low_two, preferred_element_type=f32)
    head_grads, distances = attend_back(
        queries, keys, values, mixed_grad, attended, totals, near, size, block
    )
    close_sums = distances[:, :group].reshape(heads, block)
    far_sums = jnp.sum(distances[:, group:].reshape(heads, block), axis=1)
    table_grad = jnp.dot(close_sums, jnp.asarray(hot[:block]), precision=lax.Precision.HIGHEST)
    table_grad = table_grad + far_sums[:, None] * jnp.asarray(hot[-1:])
    sums = weight_grads(low_one, attended, head_grads, branch, shards)
    sums = halve(sums, bits[0])
    input_gradient, norm_grad = finish(
        head_grads, query_full, key_full, value_full, gain_one, inputs, resid_grad, epsilon
    )
    small_grad = jax.vmap(pack)(
        norm_grad.reshape(shards, 1, part).astype(bf16),
        gain_grad.reshape(shards, 1, part).astype(bf16),
        table_grad.reshape(shards, local_heads, BUCKETS).astype(bf16),
        router_grad[:experts].reshape(experts, shards, part).transpose(1, 0, 2).astype(bf16),
    )
    spare = -small_grad.shape[1] % (8 * owners)
    small_grad = halve(jnp.pad(small_grad, ((0, 0), (0, spare), (0, 0))), bits[0])
    kept = sums.shape[1]
    sums = reduce_rows(jnp.concatenate([sums, small_grad], axis=1), bits)
    half = sums.shape[0] // 2
    weights = jnp.concatenate([sums[:kept], sums[half : half + kept]]).astype(f32)
    small_sum = jnp.concatenate([sums[kept:half], sums[half + kept :]]).astype(f32)
    up_sum, down_sum = widen_rest(pair_sum, widen_first(first_sum))
    return (
        output,
        input_gradient,
        small_sum[0, :part],
        weights[:part],
        weights[part : 2 * part],
        weights[2 * part : 3 * part],
        weights[3 * part :],
        small_sum[2 : 2 + local_heads, :BUCKETS].T,
        small_sum[1, :part],
        small_sum[router_at : router_at + experts, :part].T,
        up_sum.reshape(local_count, width, width),
        down_sum.reshape(local_count, width, width),
    )


def solution(mesh):
    in_specs = (
        P((OWNER, LINE), None),
        P(LINE),
        P(LINE, None),
        P(LINE, None),
        P(LINE, None),
        P(LINE, None),
        P(None, LINE),
        P(LINE),
        P(LINE, None),
        P(OWNER, None, None),
        P(OWNER, None, None),
        P((OWNER, LINE), None),
        P((OWNER, LINE), None),
    )
    out_specs = (
        P((OWNER, LINE), None),
        P((OWNER, LINE), None),
        P(LINE),
        P(LINE, None),
        P(LINE, None),
        P(LINE, None),
        P(LINE, None),
        P(None, LINE),
        P(LINE),
        P(LINE, None),
        P(OWNER, None, LINE),
        P(OWNER, LINE, None),
    )

    return jax.shard_map(local, mesh=mesh, in_specs=in_specs, out_specs=out_specs, check_vma=False)
```

```python
from functools import partial, reduce

import jax
import jax.numpy as jnp
import numpy as np
from jax import lax
from jax.experimental import pallas as pl
from jax.experimental.pallas import tpu as pltpu
from jax.sharding import PartitionSpec as P


BUCKETS = 32
MAX_DIST = 128


epsilon = 1e-06
masked_score = -1e30


def bucket_hot(length):
    distance = np.arange(length)
    half_count = BUCKETS // 2
    clipped = np.maximum(distance, half_count)
    spread = np.log(clipped / half_count) / np.log(MAX_DIST / half_count) * (BUCKETS - half_count)
    far_bucket = np.minimum(half_count + np.floor(spread).astype(np.int32), BUCKETS - 1)
    bucket = np.where(distance < half_count, distance, far_bucket)
    return (bucket[:, None] == np.arange(BUCKETS)[None, :]).astype(np.float32)


def dot_nt(a, b):
    return lax.dot_general(a, b, (((1,), (1,)), ((), ())), preferred_element_type=jnp.float32)


def dot_nn(a, b):
    return lax.dot_general(a, b, (((1,), (0,)), ((), ())), preferred_element_type=jnp.float32)


def dot_tn(a, b):
    return lax.dot_general(a, b, (((0,), (0,)), ((), ())), preferred_element_type=jnp.float32)


def slot_kernel(routes_ref, slots_ref, float_ref, *, experts, local_count, owners, capacity):
    tokens = routes_ref.shape[1]
    expert = lax.broadcasted_iota(jnp.int32, (experts, tokens), 0)
    hits = [routes_ref[c:c + 1, :] == expert for c in range(2)]
    hot = jnp.where(hits[0] | hits[1], 1.0, 0.0).astype(jnp.bfloat16)
    earlier = lax.broadcasted_iota(jnp.int32, (tokens, tokens), 0)
    later = lax.broadcasted_iota(jnp.int32, (tokens, tokens), 1)
    before = jnp.where(earlier < later, 1.0, 0.0).astype(jnp.bfloat16)
    counts = dot_nn(hot, before)
    column = lax.broadcasted_iota(jnp.int32, (experts, 1), 0)
    base = (column % local_count * owners + column // local_count) * capacity
    counts = counts + base.astype(jnp.float32)
    for c in range(2):
        slot = jnp.sum(jnp.where(hits[c], counts, 0.0), axis=0, keepdims=True)
        slots_ref[c:c + 1, :] = slot.astype(jnp.int32)
    float_ref[...] = routes_ref[...].astype(jnp.float32)


def find_slots(routes, experts, local_count, owners, capacity):
    return pl.pallas_call(
        partial(slot_kernel, experts=experts, local_count=local_count, owners=owners, capacity=capacity),
        out_shape=[jax.ShapeDtypeStruct(routes.shape, jnp.int32), jax.ShapeDtypeStruct(routes.shape, jnp.float32)],
    )(routes)


def dispatch_both_kernel(slots_ref, rows_ref, cot_ref, *refs, start, capacity, early):
    out_ref = refs[-1]
    block, tokens = capacity, rows_ref.shape[0]
    slot = lax.broadcasted_iota(jnp.int32, (block, tokens), 0) + (pl.program_id(0) * block + start)
    hot = jnp.where((slot == slots_ref[0:1, :]) | (slot == slots_ref[1:2, :]), 1.0, 0.0)
    hot = hot.astype(jnp.bfloat16)
    out_ref[0, :capacity] = dot_nn(hot, rows_ref[...]).astype(out_ref.dtype)
    out_ref[0, capacity:] = dot_nn(hot[early:], cot_ref[...]).astype(out_ref.dtype)


def dispatch_both(slots, rows, cot, start, owners, capacity, early, after=()):
    width = rows.shape[1]
    total = 2 * capacity - early
    whole = lambda shape: pl.BlockSpec(shape, lambda i: (0, 0))
    return pl.pallas_call(
        partial(dispatch_both_kernel, start=start, capacity=capacity, early=early),
        grid=(owners,),
        in_specs=[whole(slots.shape), whole(rows.shape), whole(cot.shape)] + [pl.BlockSpec(memory_space=pl.ANY)] * len(after),
        out_specs=pl.BlockSpec((1, total, width), lambda i: (i, 0, 0)),
        out_shape=jax.ShapeDtypeStruct((owners, total, width), rows.dtype),
        compiler_params=pltpu.CompilerParams(vmem_limit_bytes=48 << 20),
    )(slots, rows, cot, *after)


def dispatch_first_kernel(slots_ref, routes_ref, rows_ref, out_ref, other_ref, *, owners, capacity):
    per, total, _ = out_ref.shape
    block, tokens = other_ref.shape[2], rows_ref.shape[0]
    row = lax.broadcasted_iota(jnp.int32, (block, tokens), 0)
    row = row + jnp.where(row >= capacity, (owners - 1) * capacity, 0)
    hots = []
    for index in range(per):
        slot = row + (pl.program_id(0) * per + index) * capacity
        hits = [slot == slots_ref[c:c + 1, :] for c in range(2)]
        hots.append(jnp.where(hits[0] | hits[1], 1.0, 0.0)[:total].astype(jnp.bfloat16))
        other = jnp.where(hits[0], routes_ref[1:2, :], jnp.where(hits[1], routes_ref[0:1, :], 0.0))
        column = jnp.sum(other, axis=1, keepdims=True)
        other_ref[index] = jnp.broadcast_to(column, (block, 128)).T[0:1, :]
    picked = dot_nn(jnp.concatenate(hots, axis=0), rows_ref[...]).astype(out_ref.dtype)
    for index in range(per):
        out_ref[index] = picked[index * total:(index + 1) * total]


def dispatch_first(slots, routes, rows, owners, capacity, early, per=4):
    width = rows.shape[1]
    total = capacity + early
    whole = lambda shape: pl.BlockSpec(shape, lambda i: (0, 0))
    return pl.pallas_call(
        partial(dispatch_first_kernel, owners=owners, capacity=capacity),
        grid=(owners // per,),
        in_specs=[whole(slots.shape), whole(routes.shape), whole(rows.shape)],
        out_specs=[pl.BlockSpec((per, total, width), lambda i: (i, 0, 0)), pl.BlockSpec((per, 1, 2 * capacity), lambda i: (i, 0, 0))],
        out_shape=[jax.ShapeDtypeStruct((owners, total, width), rows.dtype), jax.ShapeDtypeStruct((owners, 1, 2 * capacity), jnp.float32)],
    )(slots, routes, rows)


def gelu_half(v):
    c = np.float32(np.sqrt(2.0 / np.pi))
    square = v * v
    half = 0.5 * jnp.tanh(v * (np.float32(0.044715) * c * square + c)) + 0.5
    return half, square


def gelu_slope(v):
    c = np.float32(np.sqrt(2.0 / np.pi))
    half, square = gelu_half(v)
    return half + v * half * (1.0 - half) * (np.float32(6.0 * 0.044715) * c * square + 2.0 * c)


def arrived_spec(arrived, used=None):
    owners, count, width = arrived.shape
    return pl.BlockSpec((owners, used or count, width), lambda i: (0, 0, 0))


def first_kernel(owner_ref, rows_ref, other_ref, router_ref, up_ref, *refs, index, local_count, capacity, pieces):
    act_ref, pre_ref, down_grad_ref, grad_ref = refs[-4:]
    owners, _, width = rows_ref.shape
    rows = owners * capacity
    chunk = rows // 2
    @pl.when(pl.program_id(0) == 0)
    def _():
        logits = dot_nt(router_ref[...], rows_ref[:, :capacity].reshape(rows, width))
        expert = lax.broadcasted_iota(jnp.int32, logits.shape, 0)
        mine = owner_ref[0] * local_count + index
        own = jnp.sum(jnp.where(expert == mine, logits, 0.0), axis=0, keepdims=True)
        other = other_ref[...].astype(jnp.int32)
        other = jnp.sum(jnp.where(expert == other, logits, 0.0), axis=0, keepdims=True)
        top = jnp.maximum(own, other)
        own = jnp.exp(own - top)
        gate = own / (own + jnp.exp(other - top))
        column = jnp.broadcast_to(gate, (128, rows)).T
        for start in range(0, width, 128):
            parts = [refs[place][:, low:low + size, start:start + 128] for place, low, size in pieces]
            part = parts[0] if len(parts) == 1 else jnp.concatenate(parts, axis=1)
            part = part.reshape(rows, 128).astype(jnp.float32) * column
            grad_ref[:, start:start + 128] = part.astype(jnp.bfloat16)
    up = up_ref[0]
    for start in range(0, rows, chunk):
        part = rows_ref[start // capacity:(start + chunk) // capacity, :capacity].reshape(chunk, width)
        pre = dot_nn(part, up)
        half, _ = gelu_half(pre)
        act_ref[start:start + chunk, :] = (pre * half).astype(jnp.bfloat16)
        pre_ref[start:start + chunk, :] = pre.astype(jnp.bfloat16)
    down_grad_ref[0] = dot_tn(act_ref[...], grad_ref[...]).astype(jnp.bfloat16)


def expert_first(owner, rows_in, cots, pieces, other, router, up, index, local_count, capacity, shards, into=None):
    owners, _, width = rows_in.shape
    rows = owners * capacity
    hidden = up.shape[2]
    tile = hidden // shards
    fixed = pl.BlockSpec((rows, width), lambda i: (0, 0))
    column = pl.BlockSpec((rows, tile), lambda i: (0, i))
    operands = [owner, rows_in, other, router, up, *cots]
    place, aliases = 0, {}
    grad_shape = jax.ShapeDtypeStruct((shards, tile, width), jnp.bfloat16)
    if into is not None:
        aliases = {len(operands): 2}
        operands.append(into)
        place, grad_shape = 2, jax.ShapeDtypeStruct(into.shape, into.dtype)
    return pl.pallas_call(
        partial(first_kernel, index=index, local_count=local_count, capacity=capacity, pieces=pieces),
        grid=(shards,),
        in_specs=[
            pl.BlockSpec(memory_space=pltpu.SMEM),
            arrived_spec(rows_in, capacity),
            pl.BlockSpec((1, rows), lambda i: (0, 0)),
            pl.BlockSpec(router.shape, lambda i: (0, 0)),
            pl.BlockSpec((1, width, tile), lambda i: (index, 0, i)),
        ]
        + [arrived_spec(cot, low + size) for cot, (_, low, size) in zip(cots, pieces)]
        + [pl.BlockSpec(memory_space=pl.ANY)] * (into is not None),
        out_specs=[column, column, pl.BlockSpec((1, tile, width), lambda i: (i, place, 0)), fixed],
        out_shape=[jax.ShapeDtypeStruct((rows, hidden), jnp.bfloat16)] * 2 + [grad_shape, jax.ShapeDtypeStruct((rows, width), jnp.bfloat16)],
        input_output_aliases=aliases,
        compiler_params=pltpu.CompilerParams(vmem_limit_bytes=62 << 20),
    )(*operands)


def second_kernel(rows_ref, grad_ref, act_ref, pre_ref, up_ref, down_ref, *refs):
    made_ref, up_grad_ref, turned, made_acc, back_acc = refs[-5:]
    step = pl.program_id(0)
    owners, _, capacity, width = made_ref.shape
    @pl.when(step == 0)
    def _():
        rows, width = grad_ref.shape
        owners = rows_ref.shape[0]
        turned[...] = rows_ref[:, :rows // owners].reshape(rows, width).T
    up = up_ref[0]
    down = down_ref[0]
    grads = dot_nt(grad_ref[...], down)
    low = (gelu_slope(pre_ref[...].astype(jnp.float32)) * grads).astype(jnp.bfloat16)
    up_grad_ref[0] = dot_nn(turned[...], low).astype(jnp.bfloat16)
    back = dot_nt(low, up)
    made = dot_nn(act_ref[...], down)
    last = pl.num_programs(0) - 1
    @pl.when(step == 0)
    def _():
        made_acc[...] = made
        back_acc[...] = back
    @pl.when((step > 0) & (step < last))
    def _():
        made_acc[...] += made
        back_acc[...] += back
    @pl.when(step == last)
    def _():
        made_ref[:, 0] = (made_acc[...] + made).astype(jnp.bfloat16).reshape(owners, capacity, width)
        made_ref[:, 1] = (back_acc[...] + back).astype(jnp.bfloat16).reshape(owners, capacity, width)


def expert_second(rows_in, grad, act, pre, up, down, index, owners, shards, wide, after=()):
    rows, width = grad.shape
    hidden = up.shape[2]
    tile = hidden // shards
    fixed = pl.BlockSpec((rows, width), lambda i: (0, 0))
    column = pl.BlockSpec((rows, tile), lambda i: (0, i))
    made_shape = (owners, 2, rows // owners, width)
    return pl.pallas_call(
        second_kernel,
        grid=(shards,),
        in_specs=[arrived_spec(rows_in, rows // rows_in.shape[0]), fixed, column, column, pl.BlockSpec((1, width, tile), lambda i: (index, 0, i)), pl.BlockSpec((1, tile, width), lambda i: (index, i, 0))]
        + [pl.BlockSpec(memory_space=pl.ANY)] * len(after),
        out_specs=[pl.BlockSpec(made_shape, lambda i: (0, 0, 0, 0)), pl.BlockSpec((1, width, tile), lambda i: (i, 0, 0))],
        out_shape=[jax.ShapeDtypeStruct(made_shape, jnp.bfloat16), jax.ShapeDtypeStruct((shards, wide, tile), jnp.bfloat16)],
        scratch_shapes=[pltpu.VMEM((width, rows), jnp.bfloat16), pltpu.VMEM((rows, width), jnp.float32), pltpu.VMEM((rows, width), jnp.float32)],
        compiler_params=pltpu.CompilerParams(vmem_limit_bytes=62 << 20),
    )(rows_in, grad, act, pre, up, down, *after)


def slope_kernel(rows_ref, grad_ref, pre_ref, down_ref, into_ref, low_ref, up_grad_ref, turned):
    del into_ref
    @pl.when(pl.program_id(0) == 0)
    def _():
        rows, width = grad_ref.shape
        owners = rows_ref.shape[0]
        turned[...] = rows_ref[:, :rows // owners].reshape(rows, width).T
    grads = dot_nt(grad_ref[...], down_ref[0])
    low = (gelu_slope(pre_ref[...].astype(jnp.float32)) * grads).astype(jnp.bfloat16)
    low_ref[...] = low
    up_grad_ref[0] = dot_nn(turned[...], low).astype(jnp.bfloat16)


def expert_slope(rows_in, grad, pre, down, index, shards, into, place):
    rows, width = grad.shape
    hidden = pre.shape[1]
    tile = hidden // shards
    fixed = pl.BlockSpec((rows, width), lambda i: (0, 0))
    column = pl.BlockSpec((rows, tile), lambda i: (0, i))
    return pl.pallas_call(
        slope_kernel,
        grid=(shards,),
        in_specs=[arrived_spec(rows_in, rows // rows_in.shape[0]), fixed, column, pl.BlockSpec((1, tile, width), lambda i: (index, i, 0)), pl.BlockSpec(memory_space=pl.ANY)],
        out_specs=[column, pl.BlockSpec((1, width, tile), lambda i: (i, place, 0))],
        out_shape=[jax.ShapeDtypeStruct((rows, hidden), jnp.bfloat16), jax.ShapeDtypeStruct(into.shape, into.dtype)],
        input_output_aliases={4: 1},
        scratch_shapes=[pltpu.VMEM((width, rows), jnp.bfloat16)],
        compiler_params=pltpu.CompilerParams(vmem_limit_bytes=62 << 20),
    )(rows_in, grad, pre, down, into)


def last_kernel(act_ref, low_ref, up_ref, down_ref, made_ref, made_acc, back_acc):
    step = pl.program_id(0)
    owners, _, capacity, width = made_ref.shape
    back = dot_nt(low_ref[...], up_ref[0])
    made = dot_nn(act_ref[...], down_ref[0])
    last = pl.num_programs(0) - 1
    @pl.when(step == 0)
    def _():
        made_acc[...] = made
        back_acc[...] = back
    @pl.when((step > 0) & (step < last))
    def _():
        made_acc[...] += made
        back_acc[...] += back
    @pl.when(step == last)
    def _():
        made_ref[:, 0] = (made_acc[...] + made).astype(jnp.bfloat16).reshape(owners, capacity, width)
        made_ref[:, 1] = (back_acc[...] + back).astype(jnp.bfloat16).reshape(owners, capacity, width)


def expert_last(act, low, up, down, index, owners, shards):
    rows, hidden = act.shape
    width = up.shape[1]
    tile = hidden // shards
    column = pl.BlockSpec((rows, tile), lambda i: (0, i))
    made_shape = (owners, 2, rows // owners, width)
    return pl.pallas_call(
        last_kernel,
        grid=(shards,),
        in_specs=[column, column, pl.BlockSpec((1, width, tile), lambda i: (index, 0, i)), pl.BlockSpec((1, tile, width), lambda i: (index, i, 0))],
        out_specs=pl.BlockSpec(made_shape, lambda i: (0, 0, 0, 0)),
        out_shape=jax.ShapeDtypeStruct(made_shape, jnp.bfloat16),
        scratch_shapes=[pltpu.VMEM((rows, width), jnp.float32), pltpu.VMEM((rows, width), jnp.float32)],
        compiler_params=pltpu.CompilerParams(vmem_limit_bytes=62 << 20),
    )(act, low, up, down)


def spread(row, block):
    return jnp.broadcast_to(row, (128, block)).T


def pick(slots, lane, back_refs, first=0):
    picked = None
    for index, back_ref in enumerate(back_refs, first):
        owners, capacity, width = back_ref.shape
        half = owners * capacity
        hots = []
        for start in range(index * half, (index + 1) * half, 128):
            hit = reduce(jnp.logical_or, [slot == lane + start for slot in slots])
            hots.append(jnp.where(hit, 1.0, 0.0).astype(jnp.bfloat16))
        part = dot_nn(jnp.concatenate(hots, axis=1), back_ref[...].reshape(half, width))
        picked = part if picked is None else picked + part
    return picked


def part_kernel(slots_ref, gates_ref, resid_ref, cot_ref, made_ref, back_ref, result_ref, inner_ref, grads_ref):
    block = result_ref.shape[0]
    lane = lax.broadcasted_iota(jnp.int32, (block, 128), 1)
    cot = cot_ref[...].astype(jnp.float32)
    result = resid_ref[...]
    inner = jnp.zeros((block, 128), jnp.float32)
    slots = [spread(slots_ref[c:c + 1, :], block) for c in range(2)]
    for c in range(2):
        picked = pick([slots[c]], lane, [made_ref])
        result = result + spread(gates_ref[c:c + 1, :], block)[:, 0:1] * picked
        inner = inner + jnp.where(lane == c, jnp.sum(cot * picked, axis=1, keepdims=True), 0.0)
    result_ref[...] = result
    inner_ref[...] = inner
    grads_ref[...] = pick(slots, lane, [back_ref])


def combine_part(slots, gates, resid, cot, returned, block=256):
    tokens, width = resid.shape
    small = pl.BlockSpec((2, block), lambda i: (0, i))
    rows = pl.BlockSpec((block, width), lambda i: (i, 0))
    wide = jax.ShapeDtypeStruct((tokens, width), jnp.float32)
    return pl.pallas_call(
        part_kernel,
        grid=(tokens // block,),
        in_specs=[small, small, rows, rows, returned_spec(returned, 0), returned_spec(returned, 1)],
        out_specs=[rows, pl.BlockSpec((block, 128), lambda i: (i, 0)), rows],
        out_shape=[wide, jax.ShapeDtypeStruct((tokens, 128), jnp.float32), wide],
        compiler_params=pltpu.CompilerParams(vmem_limit_bytes=62 << 20),
    )(slots, gates, resid, cot, returned, returned)


def out_kernel(slots_ref, routes_ref, gates_ref, result_ref, inner_ref, cot_ref, made_ref, out_ref, logit_ref):
    block = out_ref.shape[0]
    lane = lax.broadcasted_iota(jnp.int32, (block, 128), 1)
    cot = cot_ref[...].astype(jnp.float32)
    result = result_ref[...]
    gates, inner = [], []
    for c in range(2):
        slot = spread(slots_ref[c:c + 1, :], block)
        gate = spread(gates_ref[c:c + 1, :], block)[:, 0:1]
        picked = pick([slot], lane, [made_ref], 1)
        result = result + gate * picked
        gates.append(gate)
        inner.append(inner_ref[:, c:c + 1] + jnp.sum(cot * picked, axis=1, keepdims=True))
    out_ref[...] = result.astype(out_ref.dtype)
    middle = gates[0] * inner[0] + gates[1] * inner[1]
    logit = jnp.zeros((block, 128), jnp.float32)
    for c in range(2):
        route = spread(routes_ref[c:c + 1, :], block)
        logit = logit + jnp.where(route == lane, gates[c] * (inner[c] - middle), 0.0)
    logit_ref[...] = logit.astype(jnp.bfloat16)


def returned_spec(returned, which):
    owners, _, capacity, width = returned.shape
    return pl.BlockSpec((owners, None, capacity, width), lambda i: (0, which, 0, 0))


def combine_out(slots, routes, gates, result, inner, cot, returned, block=256):
    tokens, width = result.shape
    small = pl.BlockSpec((2, block), lambda i: (0, i))
    rows = pl.BlockSpec((block, width), lambda i: (i, 0))
    return pl.pallas_call(
        out_kernel,
        grid=(tokens // block,),
        in_specs=[small, small, small, rows, pl.BlockSpec((block, 128), lambda i: (i, 0)), rows, returned_spec(returned, 0)],
        out_specs=[rows, pl.BlockSpec((block, 128), lambda i: (i, 0))],
        out_shape=[jax.ShapeDtypeStruct((tokens, width), jnp.bfloat16), jax.ShapeDtypeStruct((tokens, 128), jnp.bfloat16)],
        compiler_params=pltpu.CompilerParams(vmem_limit_bytes=62 << 20),
    )(slots, routes, gates, result, inner, cot, returned)


def back_kernel(slots_ref, logit_ref, router_ref, gain_ref, resid_ref, cot_ref, merge_ref, part_ref, back_ref, grad_ref, low_ref, mixed_ref, gain_grad_ref, *, eps):
    block, _ = grad_ref.shape
    lane = lax.broadcasted_iota(jnp.int32, (block, 128), 1)
    grads = part_ref[...] + pick([spread(slots_ref[c:c + 1, :], block) for c in range(2)], lane, [back_ref], 1)
    grads = grads + dot_nn(logit_ref[...], router_ref[...])
    resid = resid_ref[...]
    inverse = lax.rsqrt(jnp.mean(resid * resid, axis=1, keepdims=True) + eps)
    unit = resid * inverse
    @pl.when(pl.program_id(0) == 0)
    def _():
        gain_grad_ref[...] = jnp.zeros_like(gain_grad_ref)
    gain_grad_ref[...] += jnp.sum(grads * unit, axis=0, keepdims=True)
    scaled = grads * gain_ref[...]
    inner = jnp.mean(scaled * unit, axis=1, keepdims=True)
    total = cot_ref[...].astype(jnp.float32) + inverse * (scaled - unit * inner)
    grad_ref[...] = total
    low = total.astype(jnp.bfloat16)
    low_ref[...] = low
    mixed_ref[...] = dot_nt(low, merge_ref[...]).astype(jnp.bfloat16)


def combine_back(slots, logit, router, gain, resid, cot, merge, part, returned, eps, block=256):
    tokens, width = resid.shape
    rows = pl.BlockSpec((block, width), lambda i: (i, 0))
    whole = lambda shape: pl.BlockSpec(shape, lambda i: (0, 0))
    low = jax.ShapeDtypeStruct((tokens, width), jnp.bfloat16)
    return pl.pallas_call(
        partial(back_kernel, eps=eps),
        grid=(tokens // block,),
        in_specs=[pl.BlockSpec((2, block), lambda i: (0, i)), pl.BlockSpec((block, 128), lambda i: (i, 0)), whole(router.shape), whole(gain.shape), rows, rows, whole(merge.shape), rows, returned_spec(returned, 1)],
        out_specs=[rows, rows, rows, whole((1, width))],
        out_shape=[jax.ShapeDtypeStruct((tokens, width), jnp.float32), low, low, jax.ShapeDtypeStruct((1, width), jnp.float32)],
        compiler_params=pltpu.CompilerParams(vmem_limit_bytes=62 << 20),
    )(slots, logit, router, gain, resid, cot, merge, part, returned)


def near_tiles(near_ref, head, block):
    spread = jnp.broadcast_to(near_ref[0, head:head + 1, :], (block, block))
    spread = pltpu.roll(spread, 0, 1, stride=1, stride_axis=0)
    key_at = lax.broadcasted_iota(jnp.int32, (block, block), 0)
    query_at = lax.broadcasted_iota(jnp.int32, (block, block), 1)
    return (jnp.where(query_at >= key_at, spread, masked_score), jnp.where(query_at < key_at, spread, 0.0), query_at < key_at)


def diagonal_sums(tile):
    block = tile.shape[1]
    total = tile[:8]
    for start in range(8, block, 8):
        total = total + pltpu.roll(tile[start:start + 8], block - start, 1)
    row = lax.broadcasted_iota(jnp.int32, total.shape, 0)
    for step in (1, 2, 4):
        total = jnp.where((row & step) != 0, pltpu.roll(total, block - step, 1), total)
    return jnp.sum(total, axis=0, keepdims=True)


def head_part(rows, head, size):
    lane = lax.broadcasted_iota(jnp.int32, rows.shape, 1)
    return jnp.where((lane >= head * size) & (lane < (head + 1) * size), rows, jnp.zeros_like(rows))


def attend_kernel(query_ref, key_ref, value_ref, near_ref, out_ref, total_ref, held, *, block, size, scale):
    length, lanes = query_ref.shape
    heads = lanes // size
    count = length // block
    turned = value_ref[...].T
    ones = jnp.ones((16, length), jnp.bfloat16)
    flipped = [jnp.concatenate([turned[head * size:(head + 1) * size], ones], axis=0) for head in range(heads)]
    tiles = [near_tiles(near_ref, head, block) for head in range(heads)]
    units = [(i, head) for i in reversed(range(count)) for head in range(heads)]
    def fold(tile, op):
        parts = [tile[k:k + 8] for k in range(0, tile.shape[0], 8)]
        while len(parts) > 1:
            parts = [op(parts[k], parts[k + 1]) for k in range(0, len(parts), 2)]
        return parts[0]
    def score_tile(unit, query_part, j, slot):
        i, head = unit
        tile = dot_nt(key_ref[pl.ds(j * block, block), :], query_part)
        if j == i:
            tile = tile + tiles[head][0]
        elif j == i - 1:
            tile = tile + tiles[head][1]
        held[slot, pl.ds(j * block, block), :] = tile
        return fold(tile, jnp.maximum)
    def part_of(unit):
        i, head = unit
        return head_part(query_ref[pl.ds(i * block, block), :] * jnp.bfloat16(scale), head, size)
    first = part_of(units[0])
    tops = {0: [score_tile(units[0], first, j, 0) for j in range(units[0][0] + 1)]}
    outs = []
    for n, (i, head) in enumerate(units):
        top = jnp.max(reduce(jnp.maximum, tops[n]), axis=0, keepdims=True)
        following = units[n + 1] if n + 1 < len(units) else None
        if following is not None:
            query_part = part_of(following)
            tops[n + 1] = []
        mixed = None
        total = None
        steps = max(i + 1, following[0] + 1 if following else 0)
        for j in range(steps):
            if following is not None and j <= following[0]:
                tops[n + 1].append(score_tile(following, query_part, j, (n + 1) % 2))
            if j <= i:
                weights = jnp.exp(held[n % 2, pl.ds(j * block, block), :] - top)
                part = dot_nn(flipped[head][:, j * block:(j + 1) * block], weights.astype(jnp.bfloat16))
                mixed = part if mixed is None else mixed + part
        total = mixed[size:size + 1]
        outs.append(mixed[:size] / total)
        rows = pl.ds(i * block, block)
        total_ref[0, head:head + 1, rows] = top + jnp.log(total)
        if head == heads - 1:
            out_ref[rows, :] = jnp.concatenate(outs[-heads:], axis=0).T.astype(out_ref.dtype)


def attend(queries, keys, values, near, size, block):
    length, width = queries.shape
    lanes = 128
    heads = lanes // size
    groups = width // lanes
    column = pl.BlockSpec((length, lanes), lambda g: (0, g))
    head_rows = pl.BlockSpec((1, heads, block), lambda g: (g, 0, 0))
    return pl.pallas_call(
        partial(attend_kernel, block=block, size=size, scale=size ** -0.5),
        grid=(groups,),
        in_specs=[column, column, column, head_rows],
        out_specs=[column, pl.BlockSpec((1, heads, length), lambda g: (g, 0, 0))],
        out_shape=[jax.ShapeDtypeStruct((length, width), jnp.bfloat16), jax.ShapeDtypeStruct((groups, heads, length), jnp.float32)],
        scratch_shapes=[pltpu.VMEM((2, length, block), jnp.float32)],
        compiler_params=pltpu.CompilerParams(vmem_limit_bytes=62 << 20),
    )(queries, keys, values, near)


def attend_back_kernel(query_ref, key_ref, value_ref, grad_ref, out_ref, total_ref, near_ref, grads_ref, dist_ref, key_acc, value_acc, *, block, size, scale):
    length, lanes = query_ref.shape
    heads = lanes // size
    count = length // block
    flipped = key_ref[...].T
    tiles = [near_tiles(near_ref, head, block) for head in range(heads)]
    near_acc = [None] * heads
    far_acc = [None] * heads
    for i in range(count):
        rows = pl.ds(i * block, block)
        query_rows = query_ref[rows, :] * jnp.bfloat16(scale)
        grad_rows = grad_ref[rows, :]
        products = (grad_rows.astype(jnp.float32) * out_ref[rows, :].astype(jnp.float32)).T
        query_parts = [head_part(query_rows, head, size) for head in range(heads)]
        grad_parts = [head_part(grad_rows, head, size) for head in range(heads)]
        inner = [jnp.sum(products[head * size:(head + 1) * size], axis=0, keepdims=True) for head in range(heads)]
        query_stack = jnp.concatenate(query_parts, axis=0)
        grad_stack = jnp.concatenate(grad_parts, axis=0)
        query_grads = [None] * heads
        for j in range(i + 1):
            cols = pl.ds(j * block, block)
            weight_list = []
            score_list = []
            for head in range(heads):
                tile = dot_nt(key_ref[cols, :], query_parts[head])
                if j == i:
                    tile = tile + tiles[head][0]
                elif j == i - 1:
                    tile = tile + tiles[head][1]
                weights = jnp.exp(tile - total_ref[0, head:head + 1, rows])
                grads = dot_nt(value_ref[cols, :], grad_parts[head])
                score_grads = weights * (grads - inner[head])
                low = score_grads.astype(jnp.bfloat16)
                weight_list.append(weights.astype(jnp.bfloat16))
                score_list.append(low)
                part = dot_nn(flipped[head * size:(head + 1) * size, j * block:(j + 1) * block], low)
                query_grads[head] = part if query_grads[head] is None else query_grads[head] + part
                if j == i:
                    near_acc[head] = score_grads if near_acc[head] is None else near_acc[head] + score_grads
                else:
                    far = score_grads
                    if j == i - 1:
                        close = jnp.where(tiles[head][2], score_grads, 0.0)
                        near_acc[head] = near_acc[head] + close
                        far = score_grads - close
                    far = jnp.sum(far, axis=0, keepdims=True)
                    far_acc[head] = far if far_acc[head] is None else far_acc[head] + far
            value_part = dot_nn(jnp.concatenate(weight_list, axis=1), grad_stack)
            key_part = dot_nn(jnp.concatenate(score_list, axis=1), query_stack)
            if j == i:
                value_acc[cols, :] = value_part
                key_acc[cols, :] = key_part
            else:
                value_acc[cols, :] += value_part
                key_acc[cols, :] += key_part
        grads_ref[0, rows, :] = (jnp.concatenate(query_grads, axis=0) * scale).T.astype(grads_ref.dtype)
    grads_ref[1] = key_acc[...].astype(grads_ref.dtype)
    grads_ref[2] = value_acc[...].astype(grads_ref.dtype)
    for head in range(heads):
        dist_ref[0, head:head + 1, :] = diagonal_sums(near_acc[head])
        dist_ref[0, heads + head:heads + head + 1, :] = far_acc[head]


def attend_back(queries, keys, values, grads, outs, totals, near, size, block):
    length, width = queries.shape
    lanes = 128
    heads = lanes // size
    groups = width // lanes
    column = pl.BlockSpec((length, lanes), lambda g: (0, g))
    head_rows = pl.BlockSpec((1, heads, block), lambda g: (g, 0, 0))
    return pl.pallas_call(
        partial(attend_back_kernel, block=block, size=size, scale=size ** -0.5),
        grid=(groups,),
        in_specs=[column] * 5 + [pl.BlockSpec((1, heads, length), lambda g: (g, 0, 0)), head_rows],
        out_specs=[pl.BlockSpec((3, length, lanes), lambda g: (0, 0, g)), pl.BlockSpec((1, 2 * heads, block), lambda g: (g, 0, 0))],
        out_shape=[jax.ShapeDtypeStruct((3, length, width), jnp.bfloat16), jax.ShapeDtypeStruct((groups, 2 * heads, block), jnp.float32)],
        scratch_shapes=[pltpu.VMEM((length, lanes), jnp.float32)] * 2,
        compiler_params=pltpu.CompilerParams(vmem_limit_bytes=62 << 20),
    )(queries, keys, values, grads, outs, totals, near)


def reverse_bits(value, count):
    out = value * 0
    for level in range(count):
        out = out * 2 + (value >> level) % 2
    return out


def project_kernel(owner_ref, inputs_ref, gain_ref, *refs, eps):
    piece_refs, weight_refs, low_ref, out_refs = refs[:4], refs[-7:-4], refs[-4], refs[-3:]
    count, half, three, _ = piece_refs[0].shape
    piece = three // 3
    owners = 2 * count
    part = owners * piece
    @pl.when(pl.program_id(0) == 0)
    def _():
        me = owner_ref[0]
        for source in range(owners):
            apart = jnp.bitwise_xor(me, source)
            near = apart % 2 == 0
            place = apart // 2
            places = (place, reverse_bits(place, owners.bit_length() - 2))
            for group in range(2):
                for line in range(half):
                    block = jnp.where(near, piece_refs[2 * group][places[group], line], piece_refs[2 * group + 1][places[group], line])
                    start = (group * half + line) * part + source * piece
                    for index in range(3):
                        weight_refs[index][start:start + piece, :] = block[index * piece:(index + 1) * piece]
    rows = inputs_ref[...].astype(jnp.float32)
    inverse = lax.rsqrt(jnp.mean(rows * rows, axis=1, keepdims=True) + eps)
    low = (rows * inverse * gain_ref[...]).astype(jnp.bfloat16)
    low_ref[...] = low
    for weight_ref, out_ref in zip(weight_refs, out_refs):
        out_ref[...] = dot_nn(low, weight_ref[...]).astype(jnp.bfloat16)


def project(owner, inputs, gain, pieces, eps, after=(), block=512):
    tokens, width = inputs.shape
    rows = pl.BlockSpec((block, width), lambda i: (i, 0))
    whole = lambda shape: pl.BlockSpec(shape, lambda i: (0,) * len(shape))
    weight = jax.ShapeDtypeStruct((width, width), jnp.bfloat16)
    return pl.pallas_call(
        partial(project_kernel, eps=eps),
        grid=(tokens // block,),
        in_specs=[pl.BlockSpec(memory_space=pltpu.SMEM), rows, whole(gain.shape)] + [whole(piece.shape) for piece in pieces] + [pl.BlockSpec(memory_space=pl.ANY)] * len(after),
        out_specs=[whole(weight.shape)] * 3 + [rows] * 4,
        out_shape=[weight] * 3 + [jax.ShapeDtypeStruct((tokens, width), jnp.bfloat16)] * 4,
        compiler_params=pltpu.CompilerParams(vmem_limit_bytes=62 << 20),
    )(owner, inputs, gain, *pieces, *after)


def settle_kernel(mixed_ref, merge_ref, inputs_ref, gain_ref, router_ref, routes_ref, slots_ref, resid_ref, low_ref, gates_ref, out_ref, held, *, eps, settling):
    step = pl.program_id(0)
    block, picking = mixed_ref.shape[0], out_ref.shape[0]
    @pl.when(step < settling)
    def _():
        resid = inputs_ref[...].astype(jnp.float32) + dot_nn(mixed_ref[...], merge_ref[...])
        resid_ref[...] = resid
        inverse = lax.rsqrt(jnp.mean(resid * resid, axis=1, keepdims=True) + eps)
        low = (resid * inverse * gain_ref[...]).astype(jnp.bfloat16)
        low_ref[...] = low
        held[pl.ds(pl.multiple_of(step * block, block), block), :] = low
        logits = dot_nt(router_ref[...], low)
        expert = lax.broadcasted_iota(jnp.int32, logits.shape, 0)
        chosen = [jnp.sum(jnp.where(routes_ref[c:c + 1, :] == expert, logits, 0.0), axis=0, keepdims=True) for c in range(2)]
        top = jnp.maximum(chosen[0], chosen[1])
        powers = [jnp.exp(value - top) for value in chosen]
        total = powers[0] + powers[1]
        for c in range(2):
            gates_ref[c:c + 1, :] = powers[c] / total
    @pl.when(step >= settling)
    def _():
        tokens = held.shape[0]
        slot = lax.broadcasted_iota(jnp.int32, (picking, tokens), 0) + (step - settling) * picking
        hot = jnp.where((slot == slots_ref[0:1, :]) | (slot == slots_ref[1:2, :]), 1.0, 0.0)
        out_ref[...] = dot_nn(hot.astype(jnp.bfloat16), held[...]).astype(out_ref.dtype)


def settle(mixed, merge, inputs, gain, router, routes, slots, count, eps, block=512):
    tokens, width = inputs.shape
    picking = count // 2
    settling = tokens // block
    early = lambda i: jnp.minimum(i, settling - 1)
    rows = pl.BlockSpec((block, width), lambda i: (early(i), 0))
    whole = lambda shape: pl.BlockSpec(shape, lambda i: (0, 0))
    small = pl.BlockSpec((2, block), lambda i: (0, early(i)))
    return pl.pallas_call(
        partial(settle_kernel, eps=eps, settling=settling),
        grid=(settling + 2,),
        in_specs=[rows, whole(merge.shape), rows, whole(gain.shape), whole(router.shape), small, whole(slots.shape)],
        out_specs=[rows, rows, small, pl.BlockSpec((picking, width), lambda i: (jnp.maximum(i - settling, 0), 0))],
        out_shape=[jax.ShapeDtypeStruct((tokens, width), jnp.float32), jax.ShapeDtypeStruct((tokens, width), jnp.bfloat16), jax.ShapeDtypeStruct((2, tokens), jnp.float32), jax.ShapeDtypeStruct((count, width), jnp.bfloat16)],
        scratch_shapes=[pltpu.VMEM((tokens, width), jnp.bfloat16)],
        compiler_params=pltpu.CompilerParams(vmem_limit_bytes=62 << 20),
    )(mixed, merge, inputs, gain, router, routes, slots)


def finish_kernel(heads_ref, query_ref, key_ref, value_ref, gain_ref, inputs_ref, resid_grad_ref, out_ref, gain_grad_ref, *, eps):
    grads = dot_nt(heads_ref[0], query_ref[...]) + dot_nt(heads_ref[1], key_ref[...]) + dot_nt(heads_ref[2], value_ref[...])
    rows = inputs_ref[...].astype(jnp.float32)
    inverse = lax.rsqrt(jnp.mean(rows * rows, axis=1, keepdims=True) + eps)
    unit = rows * inverse
    @pl.when(pl.program_id(0) == 0)
    def _():
        gain_grad_ref[...] = jnp.zeros_like(gain_grad_ref)
    gain_grad_ref[...] += jnp.sum(grads * unit, axis=0, keepdims=True)
    scaled = grads * gain_ref[...]
    inner = jnp.mean(scaled * unit, axis=1, keepdims=True)
    out_ref[...] = resid_grad_ref[...] + inverse * (scaled - unit * inner)


def finish(head_grads, query, key, value, gain, inputs, resid_grad, eps, block=256):
    tokens, width = inputs.shape
    rows = pl.BlockSpec((block, width), lambda i: (i, 0))
    whole = lambda shape: pl.BlockSpec(shape, lambda i: (0, 0))
    return pl.pallas_call(
        partial(finish_kernel, eps=eps),
        grid=(tokens // block,),
        in_specs=[pl.BlockSpec((3, block, width), lambda i: (0, i, 0))] + [whole(query.shape)] * 3 + [whole(gain.shape), rows, rows],
        out_specs=[rows, whole((1, width))],
        out_shape=[jax.ShapeDtypeStruct((tokens, width), jnp.float32), jax.ShapeDtypeStruct((1, width), jnp.float32)],
        compiler_params=pltpu.CompilerParams(vmem_limit_bytes=62 << 20),
    )(head_grads, query, key, value, gain, inputs, resid_grad)


def weight_kernel(left_ref, mixed_ref, heads_ref, branch_ref, out_ref, turned, right):
    shards, part, _ = out_ref.shape
    step = pl.program_id(0)
    last = pl.num_programs(0) - 1
    @pl.when(step == 0)
    def _():
        turned[...] = left_ref[...].T
    @pl.when(step < last)
    def _():
        right[...] = heads_ref[...]
    @pl.when(step == last)
    def _():
        turned[...] = mixed_ref[...].T
        right[...] = branch_ref[...]
    for shard in range(shards):
        grad = dot_nn(turned[shard * part:(shard + 1) * part, :], right[...])
        out_ref[shard] = grad.astype(jnp.bfloat16)


def weight_grads(left, mixed, head_grads, branch, shards):
    count, tokens, width = head_grads.shape
    part = width // shards
    fixed = pl.BlockSpec((tokens, width), lambda i: (0, 0))
    return pl.pallas_call(
        weight_kernel,
        grid=(count + 1,),
        in_specs=[fixed, fixed, pl.BlockSpec((None, tokens, width), lambda i: (jnp.minimum(i, count - 1), 0, 0)), fixed],
        out_specs=pl.BlockSpec((shards, part, width), lambda i: (0, i, 0)),
        out_shape=jax.ShapeDtypeStruct((shards, (count + 1) * part, width), jnp.bfloat16),
        scratch_shapes=[pltpu.VMEM((width, tokens), jnp.bfloat16), pltpu.VMEM((tokens, width), jnp.bfloat16)],
        compiler_params=pltpu.CompilerParams(vmem_limit_bytes=62 << 20),
    )(left, mixed, head_grads, branch)


def widen_first_kernel(rows_ref, out_ref):
    out_ref[...] = rows_ref[...].astype(jnp.float32)


def widen_first(rows):
    count, width = rows.shape
    half = pl.BlockSpec((count // 2, width), lambda i: (i, 0))
    return pl.pallas_call(
        widen_first_kernel,
        grid=(2,),
        in_specs=[half],
        out_specs=half,
        out_shape=jax.ShapeDtypeStruct((2 * count, width), jnp.float32),
        compiler_params=pltpu.CompilerParams(vmem_limit_bytes=62 << 20),
    )(rows)


def widen_rest_kernel(rows_ref, into_ref, up_ref, down_ref):
    del into_ref
    wide = rows_ref[...].astype(jnp.float32)
    step = pl.program_id(0)
    @pl.when(step < 2)
    def _():
        up_ref[...] = wide
    @pl.when(step >= 2)
    def _():
        down_ref[...] = wide


def widen_rest(rows, into):
    count, width = rows.shape[0] // 3, rows.shape[1]
    half = lambda place: pl.BlockSpec((count, width), lambda i: (place(i), 0))
    wide = jax.ShapeDtypeStruct((2 * count, width), jnp.float32)
    return pl.pallas_call(
        widen_rest_kernel,
        grid=(3,),
        in_specs=[half(lambda i: i), pl.BlockSpec(memory_space=pl.ANY)],
        out_specs=[half(lambda i: jnp.minimum(i, 1)), half(lambda i: 1)],
        out_shape=[wide, wide],
        input_output_aliases={1: 1},
        compiler_params=pltpu.CompilerParams(vmem_limit_bytes=62 << 20),
    )(rows, into)


def smalls_kernel(small_ref, near_ref, gain_one_ref, gain_two_ref, router_ref, table_ref, *, part, heads, router_at):
    shards, _, width = small_ref.shape
    group = table_ref.shape[1]
    lanes = -(-part // 128) * 128
    row = lax.broadcasted_iota(jnp.int32, (lanes, width), 0)
    column = lax.broadcasted_iota(jnp.int32, (lanes, width), 1)
    wide = None
    for shard in range(shards):
        place = jnp.where((column == row + shard * part) & (row < part), 1.0, 0.0).astype(jnp.bfloat16)
        rows = dot_nn(small_ref[shard][:, :lanes], place)
        wide = rows if wide is None else wide + rows
        near = dot_nn(small_ref[shard][:8, :128], near_ref[...])
        for head in range(heads):
            at = shard * heads + head
            table_ref[at // group, at % group:at % group + 1, :] = near[2 + head:3 + head, :]
    gain_one_ref[...] = wide[0:1]
    gain_two_ref[...] = wide[1:2]
    router_ref[...] = wide[router_at:router_at + router_ref.shape[0]].astype(jnp.bfloat16)


def spread_smalls(small, near, part, heads, group, experts, router_at):
    shards, _, width = small.shape
    f32 = jnp.float32
    return pl.pallas_call(
        partial(smalls_kernel, part=part, heads=heads, router_at=router_at),
        out_shape=[
            jax.ShapeDtypeStruct((1, width), f32),
            jax.ShapeDtypeStruct((1, width), f32),
            jax.ShapeDtypeStruct((experts, width), jnp.bfloat16),
            jax.ShapeDtypeStruct((shards * heads // group, group, near.shape[1]), f32),
        ],
    )(small, near)


def pack_kernel(owner_ref, query_ref, key_ref, value_ref, one_ref, two_ref, table_ref, router_ref, out_ref, tall, *, router_at):
    del owner_ref
    piece = query_ref.shape[0]
    experts, part = router_ref.shape
    heads, buckets = table_ref.shape
    tall[...] = jnp.zeros_like(tall)
    tall[0:1, :part] = one_ref[...].astype(jnp.float32).reshape(1, part)
    tall[1:2, :part] = two_ref[...].astype(jnp.float32).reshape(1, part)
    tall[2:2 + heads, :buckets] = table_ref[...].astype(jnp.float32)
    tall[router_at:router_at + experts, :part] = router_ref[...].astype(jnp.float32)
    for index, ref in enumerate((query_ref, key_ref, value_ref)):
        out_ref[index * piece:(index + 1) * piece, :] = ref[...]
    out_ref[3 * piece:, :] = tall[...].astype(out_ref.dtype)


def pack_first(owner, weights, one, two, table, router, piece, small_rows, router_at):
    width = weights[0].shape[1]
    if piece % 8 == 0:
        rows = pl.BlockSpec((piece, width), lambda i, owner: (owner[0], 0))
    else:
        weights = [lax.dynamic_slice_in_dim(weight, owner[0] * piece, piece, 0) for weight in weights]
        rows = pl.BlockSpec((piece, width), lambda i, owner: (0, 0))
    whole = lambda shape: pl.BlockSpec(shape, lambda i, owner: (0,) * len(shape))
    return pl.pallas_call(
        partial(pack_kernel, router_at=router_at),
        grid_spec=pltpu.PrefetchScalarGridSpec(
            num_scalar_prefetch=1,
            grid=(1,),
            in_specs=[rows, rows, rows, whole(one.shape), whole(two.shape), whole(table.shape), whole(router.shape)],
            out_specs=whole((3 * piece + small_rows, width)),
            scratch_shapes=[pltpu.VMEM((small_rows, width), jnp.float32)],
        ),
        out_shape=jax.ShapeDtypeStruct((3 * piece + small_rows, width), weights[0].dtype),
    )(owner, *weights, one, two, table, router)


OWNER = "expert"
LINE = "shard"


def exchange(rows, bit):
    count = lax.axis_size(OWNER)
    return lax.ppermute(rows, OWNER, [(i, i ^ bit) for i in range(count)])


def shift(rows, step):
    count = lax.axis_size(LINE)
    return lax.ppermute(rows, LINE, [(i, (i + step) % count) for i in range(count)])


def gather_line(rows):
    count = lax.axis_size(LINE)
    me = lax.axis_index(LINE)
    out = jnp.zeros((count,) + rows.shape, rows.dtype)
    out = lax.dynamic_update_index_in_dim(out, rows, me, 0)
    for step in range(1, count):
        got = shift(rows, step)
        out = lax.dynamic_update_index_in_dim(out, got, (me - step) % count, 0)
    return out


def add_low(left, right):
    return (left.astype(jnp.float32) + right.astype(jnp.float32)).astype(jnp.bfloat16)


def side(bit):
    return (lax.axis_index(OWNER) // bit) % 2


def halve(stack, bit):
    half = stack.shape[1] // 2
    keep = lax.dynamic_slice_in_dim(stack, side(bit) * half, half, 1)
    send = lax.dynamic_slice_in_dim(stack, (1 - side(bit)) * half, half, 1)
    got = exchange(send, bit)
    return add_low(keep, got)


def line_sum(stack):
    count = lax.axis_size(LINE)
    place = lax.axis_index(LINE)
    total = lax.dynamic_index_in_dim(stack, place, 0, False).astype(jnp.float32)
    for step in range(1, count):
        send = lax.dynamic_index_in_dim(stack, (place + step) % count, 0, False)
        total = total + shift(send, step).astype(jnp.float32)
    return total.astype(jnp.bfloat16)


def grow(piece, bit):
    other = exchange(piece, bit)
    return jnp.where(
        side(bit) == 0, jnp.concatenate([piece, other]), jnp.concatenate([other, piece])
    )


def reduce_rows(stack, bits):
    unit = 8 << (len(bits) - 1)
    cut = -(-stack.shape[1] // (2 * unit)) * unit
    parts = [stack[:, :cut], stack[:, cut:]]
    orders = [bits[1:], bits[:0:-1]]
    for level in range(len(bits) - 1):
        parts = [halve(part, order[level]) for part, order in zip(parts, orders)]
    low = parts[0].shape[1]
    piece = line_sum(jnp.concatenate(parts, axis=1))
    parts = [piece[:low], piece[low:]]
    for level in reversed(range(len(bits) - 1)):
        parts = [grow(part, order[level]) for part, order in zip(parts, orders)]
    return grow(jnp.concatenate(parts), bits[0])


def scatter_sum(grads):
    shards, rows, width = grads.shape
    grads = grads.reshape(shards * rows, width)
    return lax.psum_scatter(grads, LINE, scatter_dimension=0, tiled=True)


def share_rows(rows):
    return lax.all_to_all(rows, OWNER, 0, 0, tiled=True)


def share_large(rows):
    return pltpu.with_memory_space_constraint(share_rows(rows), pltpu.HBM)


def local(
    inputs,
    norm_gain,
    query_weight,
    key_weight,
    value_weight,
    merge_weight,
    bias_table,
    expert_gain,
    router_weight,
    up_weight,
    down_weight,
    routes,
    cotangent,
):
    f32, bf16 = jnp.float32, jnp.bfloat16
    tokens, width = inputs.shape
    owners = lax.axis_size(OWNER)
    shards = lax.axis_size(LINE)
    me = lax.axis_index(OWNER)
    part = query_weight.shape[0]
    piece = part // owners
    local_heads = bias_table.shape[1]
    heads = local_heads * shards
    size = width // heads
    experts = router_weight.shape[1]
    local_count, _, hidden = up_weight.shape
    capacity = (5 * tokens * routes.shape[1] + 4 * experts - 1) // (4 * experts)
    capacity = -(-capacity // 16) * 16
    rows = owners * capacity
    assert local_count == 2 and hidden // shards == width
    early = max(16, 2 * capacity // 5 // 16 * 16)

    router_at = 2 + local_heads + (-(2 + local_heads)) % 8

    def widen(block):
        return jnp.pad(block, ((0, 0), (0, width - block.shape[1])))

    def pack(gain_one, gain_two, table, router):
        head = jnp.concatenate([gain_one, gain_two], axis=0)
        gap = jnp.zeros((router_at - 2 - local_heads, width), bf16)
        return jnp.concatenate([widen(head), widen(table), gap, widen(router)], axis=0)

    owner = me.astype(jnp.int32).reshape(1)
    first = pack_first(
        owner, [query_weight, key_weight, value_weight], norm_gain, expert_gain,
        bias_table.T, router_weight.T, piece, router_at + experts, router_at,
    )
    lined = gather_line(first)
    small_full = lined[:, 3 * piece :]
    bits = [1 << level for level in range(owners.bit_length() - 1)]
    pieces = []
    for index, order in enumerate((bits[1:], bits[:0:-1])):
        held = lined[index * shards // 2 : (index + 1) * shards // 2, : 3 * piece][None]
        for bit in order:
            got = exchange(held, bit)
            held = jnp.concatenate([held, got])
        pieces += [held, exchange(held, bits[0])]
    merge_full = lax.all_gather(merge_weight, LINE, axis=0, tiled=True)

    block = 256
    hot = bucket_hot(tokens)
    assert hot[block:, -1].all()
    near_hot = np.zeros((128, block), np.float32)
    near_hot[:BUCKETS] = (hot[:block] - hot[-1:]).T
    group = 128 // size
    gain_one, gain_two, router_full, near = spread_smalls(
        small_full, jnp.asarray(near_hot, bf16), part, local_heads, group, experts, router_at
    )

    routes_line = routes.T
    slots, routes_float = find_slots(routes_line, experts, local_count, owners, capacity)
    cot_rows, other = dispatch_first(
        slots, routes_float, cotangent, owners, capacity, early
    )
    other = share_rows(other).reshape(owners, local_count, capacity)

    query_full, key_full, value_full, low_one, queries, keys, values = project(
        owner, inputs, gain_one, pieces, epsilon, after=(near, router_full)
    )
    cot_in = share_large(cot_rows)
    attended, totals = attend(queries, keys, values, near, size, block)
    resid, low_two, gates, send = settle(
        attended, merge_full, inputs, gain_two, router_full, routes_line, slots, rows, epsilon
    )

    others = [other[:, index].reshape(1, rows) for index in range(local_count)]
    rows_in = share_large(send.reshape(owners, capacity, width))
    joint = dispatch_both(
        slots, low_two, cotangent, rows, owners, capacity, early, after=others
    )
    joint_in = share_large(joint)
    act, pre, first_down, grad_in = expert_first(
        owner, rows_in, [cot_in], [(0, 0, capacity)], others[0], router_full, up_weight,
        0, local_count, capacity, shards,
    )
    first_sum = scatter_sum(first_down)
    first_made, pair = expert_second(rows_in, grad_in, act, pre, up_weight, down_weight, 0, owners, shards, 3 * width)
    late = capacity - early
    act, pre, pair, grad_in = expert_first(
        owner, joint_in, [cot_in, joint_in], [(0, capacity, early), (1, capacity, late)],
        others[1], router_full, up_weight, 1, local_count, capacity, shards, into=pair,
    )
    low, pair = expert_slope(joint_in, grad_in, pre, down_weight, 1, shards, pair, 1)
    pair_sum = scatter_sum(pair)
    second_made = expert_last(act, low, up_weight, down_weight, 1, owners, shards)
    returned = share_rows(first_made)
    result, inner, part_grads = combine_part(slots, gates, resid, cotangent, returned)
    returned = share_rows(second_made)
    output, logit_grad = combine_out(
        slots, routes_line, gates, result, inner, cotangent, returned
    )
    router_wide = jnp.pad(router_full, ((0, 128 - experts), (0, 0)))
    resid_grad, branch, mixed_grad, gain_grad = combine_back(
        slots, logit_grad, router_wide, gain_two, resid, cotangent, merge_full,
        part_grads, returned, epsilon
    )
    router_grad = jnp.einsum("te,ti->ei", logit_grad, low_two, preferred_element_type=f32)
    head_grads, distances = attend_back(
        queries, keys, values, mixed_grad, attended, totals, near, size, block
    )
    close_sums = distances[:, :group].reshape(heads, block)
    far_sums = jnp.sum(distances[:, group:].reshape(heads, block), axis=1)
    table_grad = jnp.dot(close_sums, jnp.asarray(hot[:block]), precision=lax.Precision.HIGHEST)
    table_grad = table_grad + far_sums[:, None] * jnp.asarray(hot[-1:])
    sums = weight_grads(low_one, attended, head_grads, branch, shards)
    sums = halve(sums, bits[0])
    input_gradient, norm_grad = finish(
        head_grads, query_full, key_full, value_full, gain_one, inputs, resid_grad, epsilon
    )
    small_grad = jax.vmap(pack)(
        norm_grad.reshape(shards, 1, part).astype(bf16),
        gain_grad.reshape(shards, 1, part).astype(bf16),
        table_grad.reshape(shards, local_heads, BUCKETS).astype(bf16),
        router_grad[:experts].reshape(experts, shards, part).transpose(1, 0, 2).astype(bf16),
    )
    spare = -small_grad.shape[1] % (8 * owners)
    small_grad = halve(jnp.pad(small_grad, ((0, 0), (0, spare), (0, 0))), bits[0])
    kept = sums.shape[1]
    sums = reduce_rows(jnp.concatenate([sums, small_grad], axis=1), bits)
    half = sums.shape[0] // 2
    weights = jnp.concatenate([sums[:kept], sums[half : half + kept]]).astype(f32)
    small_sum = jnp.concatenate([sums[kept:half], sums[half + kept :]]).astype(f32)
    up_sum, down_sum = widen_rest(pair_sum, widen_first(first_sum))
    return (
        output,
        input_gradient,
        small_sum[0, :part],
        weights[:part],
        weights[part : 2 * part],
        weights[2 * part : 3 * part],
        weights[3 * part :],
        small_sum[2 : 2 + local_heads, :BUCKETS].T,
        small_sum[1, :part],
        small_sum[router_at : router_at + experts, :part].T,
        up_sum.reshape(local_count, width, width),
        down_sum.reshape(local_count, width, width),
    )


def solution(mesh):
    in_specs = (
        P((OWNER, LINE), None),
        P(LINE),
        P(LINE, None),
        P(LINE, None),
        P(LINE, None),
        P(LINE, None),
        P(None, LINE),
        P(LINE),
        P(LINE, None),
        P(OWNER, None, None),
        P(OWNER, None, None),
        P((OWNER, LINE), None),
        P((OWNER, LINE), None),
    )
    out_specs = (
        P((OWNER, LINE), None),
        P((OWNER, LINE), None),
        P(LINE),
        P(LINE, None),
        P(LINE, None),
        P(LINE, None),
        P(LINE, None),
        P(None, LINE),
        P(LINE),
        P(LINE, None),
        P(OWNER, None, LINE),
        P(OWNER, LINE, None),
    )

    return jax.shard_map(local, mesh=mesh, in_specs=in_specs, out_specs=out_specs, check_vma=False)
```
